32 devices in a mesh: seq: 16 (over z, x, core), head: 2 (over y).
Axes of the slice: x: 2, y: 2, z: 4, core: 2. Of those that a mesh axis runs over, the one named last changes fastest.
Arguments:
- inputs: bfloat16 [8192, 1152], P('seq'), may hold values from -6 to 6
- segment_ids: int32 [8192], P('seq'), may hold values from 0 to 15, never falling along the last dimension, each value on 1 to 1025 neighbouring positions
- w_query: bfloat16 [1152, 1024], P(None, 'head'), may hold values from -0.1875 to 0.1875
- w_key: bfloat16 [1152, 256], replicated, may hold values from -0.1875 to 0.1875
- w_value: bfloat16 [1152, 256], replicated, may hold values from -0.1875 to 0.1875
- w_out: bfloat16 [1024, 1152], P('head'), may hold values from -0.1875 to 0.1875
- w_gate: bfloat16 [1152, 6912], P(None, 'head'), may hold values from -0.1875 to 0.1875
- w_up: bfloat16 [1152, 6912], P(None, 'head'), may hold values from -0.1875 to 0.1875
- w_down: bfloat16 [6912, 1152], P('head'), may hold values from -0.078125 to 0.078125
- gain_in: float32 [1152], replicated, may hold values from 0.5 to 1.5
- gain_query: float32 [256], replicated, may hold values from 0.5 to 1.5
- gain_key: float32 [256], replicated, may hold values from 0.5 to 1.5
- gain_post_attn: float32 [1152], replicated, may hold values from 0.5 to 1.5
- gain_pre_ffn: float32 [1152], replicated, may hold values from 0.5 to 1.5
- gain_post_ffn: float32 [1152], replicated, may hold values from 0.5 to 1.5
- cotangent: bfloat16 [8192, 1152], P('seq'), may hold values from -6 to 6
Outputs:
- output: bfloat16 [8192, 1152], P('seq')
- grad_inputs: bfloat16 [8192, 1152], P('seq')
- grad_w_query: float32 [1152, 1024], P('seq', 'head')
- grad_w_key: float32 [1152, 256], P('seq')
- grad_w_value: float32 [1152, 256], P('seq')
- grad_w_out: float32 [1024, 1152], P('head', 'seq')
- grad_w_gate: float32 [1152, 6912], P('seq', 'head')
- grad_w_up: float32 [1152, 6912], P('seq', 'head')
- grad_w_down: float32 [6912, 1152], P('head', 'seq')
- grad_gain_in: float32 [1152], P('seq')
- grad_gain_query: float32 [256], P('seq')
- grad_gain_key: float32 [256], P('seq')
- grad_gain_post_attn: float32 [1152], P('seq')
- grad_gain_pre_ffn: float32 [1152], P('seq')
- grad_gain_post_ffn: float32 [1152], P('seq')
The draws below stay inside these ranges and needn't reach their ends.
Inputs may be any that keep to these rules, and one draw needn't show every extreme that they name: `segment_ids`: segment ids never fall along the row; every document has 1 to 1025 tokens, and one has exactly 1025.
All inputs are finite; a program needn't handle non-finite values.
Results may differ from the reference program's by a relative error of at most 0.018.
Values may be sent and summed in bfloat16 or wider, within the bound.
A program may use at most 320 MiB of HBM per device.

```python
import math
import jax
import jax.numpy as jnp
import numpy as np
from jax import lax

D = 1152
HEADS = 4
HD = 256
FF = 6912
TOK_DEV = 512
TOKENS = 8192
DOC_MAX = 1025


def with_spikes(result, key, source, target, parts, factor):
    def block_of(position):
        return (jnp.arange(result.shape[position]) // (result.shape[position] // parts)).reshape((-1,) + (1,) * (result.ndim - 1 - position))

    first = jax.random.permutation(key, parts)[block_of(target)]
    far = (block_of(target) + parts // 2) % parts
    return jnp.where((block_of(source) == first) | (block_of(source) == far), factor * result, result)


def steps_of(rng, extent, pieces, low, top_value):
    level = 1.0
    for dim, shards_of in pieces:
        steps = jax.random.uniform(jax.random.fold_in(jax.random.fold_in(rng, 6), dim), (shards_of,), jnp.float32, low / len(pieces), top_value / len(pieces))
        level = level * jnp.repeat(jnp.exp(steps), extent[dim] // shards_of).reshape((-1,) + (1,) * (len(extent) - 1 - dim))
    return level


def length_profile(amount, total, limit, skew):
    loads = [(1 << 20) // math.isqrt(rank ** skew) + 1 for rank in range(2, amount + 1)]
    spare, given = total - limit - (amount - 1), [1] * (amount - 1)
    while spare > 0:
        candidates = [i for i in range(amount - 1) if given[i] < limit]
        mass, remaining = sum([loads[i] for i in candidates]), spare
        for i in candidates:
            extra = min(limit - given[i], max(1, remaining * loads[i] // mass), spare)
            given[i] = given[i] + extra
            spare = spare - extra
    return np.array([limit] + given)


def uneven_parts(stream_key, number_of, total, bound, slope):
    if number_of == 2:
        one = jax.random.randint(stream_key, (), max(1, total - bound), min(bound, total - 1) + 1)
        return jnp.stack([one, total - one])
    lengths = jnp.asarray(length_profile(number_of, total, bound, slope), jnp.int32)
    twos = (number_of - 1) // 2
    giver, sink = lengths[1:1 + 2 * twos:2], lengths[2:2 + 2 * twos:2]
    room = jnp.minimum(giver - 1, bound - sink)
    moved = jax.random.randint(jax.random.fold_in(stream_key, 1), (twos,), 0, 1 << 20) % (room + 1)
    lengths = lengths.at[1:1 + 2 * twos:2].set(giver - moved).at[2:2 + 2 * twos:2].set(sink + moved)
    return lengths[jax.random.permutation(jax.random.fold_in(stream_key, 2), number_of)]


def normal_values(rng, extent, spread, limit, cuts=(), held_as=jnp.bfloat16):
    entries = spread * jax.random.normal(rng, extent, jnp.float32)
    if cuts:
        entries = entries * steps_of(rng, extent, cuts, -0.22, 0.18)
    return jnp.clip(entries, -limit, limit).astype(held_as)


def heavy_noise(key, dims, scale, most, split, heavy, held_as=jnp.bfloat16):
    values = scale * jax.random.normal(key, dims, jnp.float32)
    if split:
        values = values * steps_of(key, dims, split, -0.22, 0.18)
    return jnp.clip(with_spikes(values, jax.random.fold_in(key, 3), *heavy), -most, most).astype(held_as)


def setup_inputs(seed: int = 0) -> dict:
    splits = jax.random.split(jax.random.key(seed), 17)
    return {
        "inputs": heavy_noise(splits[0], (TOKENS, D), 1.0, 6.0, ((0, 16),), (0, 1, 16, 2.0)),
        "segment_ids": jnp.searchsorted(jnp.cumsum(uneven_parts(splits[1], TOKENS // TOK_DEV, TOKENS, DOC_MAX, 2)), jnp.arange(TOKENS), side="right").astype(jnp.int32),
        "w_query": normal_values(splits[2], (D, HEADS * HD), D ** -0.5, 0.1875, ((1, 2),)),
        "w_key": normal_values(splits[3], (D, HD), D ** -0.5, 0.1875),
        "w_value": normal_values(splits[4], (D, HD), D ** -0.5, 0.1875),
        "w_out": normal_values(splits[5], (HEADS * HD, D), (HEADS * HD) ** -0.5, 0.1875, ((0, 2),)),
        "w_gate": normal_values(splits[6], (D, FF), D ** -0.5, 0.1875, ((1, 2),)),
        "w_up": normal_values(splits[7], (D, FF), D ** -0.5, 0.1875, ((1, 2),)),
        "w_down": normal_values(splits[8], (FF, D), FF ** -0.5, 0.078125, ((0, 2),)),
        "gain_in": jnp.clip(1.0 + 0.1 * jax.random.normal(splits[9], (D,), jnp.float32), 0.5, 1.5),
        "gain_query": jnp.clip(1.0 + 0.1 * jax.random.normal(splits[10], (HD,), jnp.float32), 0.5, 1.5),
        "gain_key": jnp.clip(1.0 + 0.1 * jax.random.normal(splits[11], (HD,), jnp.float32), 0.5, 1.5),
        "gain_post_attn": jnp.clip(1.0 + 0.1 * jax.random.normal(splits[12], (D,), jnp.float32), 0.5, 1.5),
        "gain_pre_ffn": jnp.clip(1.0 + 0.1 * jax.random.normal(splits[13], (D,), jnp.float32), 0.5, 1.5),
        "gain_post_ffn": jnp.clip(1.0 + 0.1 * jax.random.normal(splits[14], (D,), jnp.float32), 0.5, 1.5),
        "cotangent": heavy_noise(splits[15], (TOKENS, D), 1.0, 6.0, ((0, 16),), (0, 1, 16, 2.0)),
    }


EPS = 1e-06
QUERY_SCALE = 0.0625
HIGH = lax.Precision.HIGHEST

@jax.custom_vjp
def low(v):
    return lax.optimization_barrier(v.astype(jnp.bfloat16)).astype(jnp.float32)

@jax.custom_vjp
def low_back(v):
    return v

def low_keep(v):
    return (low(v), None)

def low_pass(kept, grad):
    return (grad,)

def back_keep(v):
    return (v, None)

def back_low(kept, grad):
    return (low(grad),)
low.defvjp(low_keep, low_pass)
low_back.defvjp(back_keep, back_low)

def rms_scale(values, gain):
    return values * lax.rsqrt(lax.optimization_barrier(jnp.mean(values * values, axis=-1, keepdims=True)) + EPS) * gain

def rope_angles(positions, width):
    half_width = width // 2
    frequency = jnp.exp(jnp.arange(half_width, dtype=jnp.float32) * (-2.0 * math.log(1000000.0) / width))
    angles = positions.astype(jnp.float32)[:, None] * frequency[None, :]
    return (jnp.cos(angles), jnp.sin(angles))

def rotate(values, cosine, sine):
    half_width = values.shape[-1] // 2
    first_half = values[..., :half_width]
    second_half = values[..., half_width:]
    cos_rows = cosine[:, None, :]
    sin_rows = sine[:, None, :]
    return jnp.concatenate([first_half * cos_rows - second_half * sin_rows, second_half * cos_rows + first_half * sin_rows], axis=-1)

def prepare(values, gain, cosine, sine, factor):
    return rotate(rms_scale(values, gain), cosine, sine) * factor

def gelu_tanh(values):
    return 0.5 * values * (1.0 + jnp.tanh(0.7978845608028654 * (values + 0.044715 * values * values * values)))

def doc_positions(segment_ids):
    token_index = jnp.arange(segment_ids.shape[0], dtype=jnp.int32)
    fresh = jnp.concatenate([jnp.ones((1,), jnp.bool_), segment_ids[1:] != segment_ids[:-1]])
    run_begin = lax.cummax(jnp.where(fresh, token_index, 0).astype(jnp.int32))
    return token_index - run_begin

def reference(inputs, segment_ids, w_query, w_key, w_value, w_out, w_gate, w_up, w_down, gain_in, gain_query, gain_key, gain_post_attn, gain_pre_ffn, gain_post_ffn, cotangent):
    positions = doc_positions(segment_ids)
    cosine, sine = rope_angles(positions, HD)
    row_block = math.gcd(4096, TOKENS)

    def forward(inputs_f, wq_f, wk_f, wv_f, wo_f, wg_f, wu_f, wd_f, g_in, g_query, g_key, g_post_attn, g_pre_ffn, g_post_ffn):
        hidden_in = low(rms_scale(inputs_f, g_in))
        query_proj = low_back(jnp.dot(hidden_in, wq_f, precision=HIGH))
        key_proj = low_back(jnp.dot(hidden_in, wk_f, precision=HIGH))
        value_proj = low_back(jnp.dot(hidden_in, wv_f, precision=HIGH))
        queries = low(prepare(query_proj.reshape(TOKENS, HEADS, HD), g_query, cosine, sine, QUERY_SCALE))
        key_rows = low(prepare(key_proj[:, None, :], g_key, cosine, sine, 1.0)[:, 0, :])
        value_rows = low(value_proj)
        padding = jnp.zeros((2 * TOK_DEV, HD), jnp.float32)
        keys_padded = jnp.concatenate([padding, key_rows], axis=0)
        values_padded = jnp.concatenate([padding, value_rows], axis=0)

        def attend(block_index):
            block_begin = (block_index * TOK_DEV).astype(jnp.int32)
            block_queries = lax.dynamic_slice_in_dim(queries, block_begin, TOK_DEV, 0)
            block_keys = lax.dynamic_slice_in_dim(keys_padded, block_begin, 3 * TOK_DEV, 0)
            block_values = lax.dynamic_slice_in_dim(values_padded, block_begin, 3 * TOK_DEV, 0)
            block_positions = lax.dynamic_slice_in_dim(positions, block_begin, TOK_DEV, 0)
            query_index = block_begin + jnp.arange(TOK_DEV, dtype=jnp.int32)
            key_index = block_begin - 2 * TOK_DEV + jnp.arange(3 * TOK_DEV, dtype=jnp.int32)
            distance = query_index[:, None] - key_index[None, :]
            visible = (distance >= 0) & (distance <= block_positions[:, None])
            scores = low_back(jnp.einsum('ihd,jd->hij', block_queries, block_keys, precision=HIGH))
            scores = jnp.where(visible[None], scores, -1e+30)
            row_max = lax.optimization_barrier(jnp.max(scores, axis=-1, keepdims=True))
            expo = jnp.exp(scores - row_max)
            attn_probs = expo / lax.optimization_barrier(jnp.sum(expo, axis=-1, keepdims=True))
            attended = jnp.einsum('hij,jd->ihd', low(attn_probs), block_values, precision=HIGH)
            return low(low_back(attended)).reshape(TOK_DEV, HEADS * HD)
        blocks = jnp.arange(TOKENS // TOK_DEV, dtype=jnp.int32)
        attended_all = lax.map(jax.checkpoint(attend), blocks).reshape(TOKENS, HEADS * HD)
        attn_branch = low_back(jnp.dot(attended_all, wo_f, precision=HIGH))
        residual_mid = inputs_f + rms_scale(attn_branch, g_post_attn)

        def feed_forward(rows_in):
            hidden_mid = low(rms_scale(rows_in, g_pre_ffn))
            gate_act = low_back(jnp.dot(hidden_mid, wg_f, precision=HIGH))
            up_proj = low_back(jnp.dot(hidden_mid, wu_f, precision=HIGH))
            mixed = low(gelu_tanh(gate_act) * up_proj)
            ffn_branch = low_back(jnp.dot(mixed, wd_f, precision=HIGH))
            return rows_in + rms_scale(ffn_branch, g_post_ffn)
        output_rows = lax.map(jax.checkpoint(feed_forward), residual_mid.reshape(TOKENS // row_block, row_block, D))
        return output_rows.reshape(TOKENS, D)
    output_f, backward = jax.vjp(forward, inputs.astype(jnp.float32), w_query.astype(jnp.float32), w_key.astype(jnp.float32), w_value.astype(jnp.float32), w_out.astype(jnp.float32), w_gate.astype(jnp.float32), w_up.astype(jnp.float32), w_down.astype(jnp.float32), gain_in.astype(jnp.float32), gain_query.astype(jnp.float32), gain_key.astype(jnp.float32), gain_post_attn.astype(jnp.float32), gain_pre_ffn.astype(jnp.float32), gain_post_ffn.astype(jnp.float32))
    grads = backward(cotangent.astype(jnp.float32))
    return (output_f.astype(jnp.bfloat16), grads[0].astype(jnp.bfloat16), grads[1], grads[2], grads[3], grads[4], grads[5], grads[6], grads[7], grads[8], grads[9], grads[10], grads[11], grads[12], grads[13])
```

```python
import math

import jax
import jax.numpy as jnp
from jax import lax
from jax.sharding import PartitionSpec as P

EPS = 1e-06
QUERY_SCALE = 0.0625


def from_behind(block, axis, distance):
    devices = range(lax.axis_size(axis))
    route = [(i - distance, i) for i in devices if i - distance in devices]
    return lax.ppermute(block, axis, route)


def rms_scale(values, gain):
    return values * lax.rsqrt(jnp.mean(values * values, axis=-1, keepdims=True) + EPS) * gain


def rope_angles(positions, width):
    half_width = width // 2
    frequency = jnp.exp(
        jnp.arange(half_width, dtype=jnp.float32) * (-2.0 * math.log(1000000.0) / width)
    )
    angles = positions.astype(jnp.float32)[:, None] * frequency[None, :]
    return (jnp.cos(angles), jnp.sin(angles))


def rotate(values, cosine, sine):
    half_width = values.shape[-1] // 2
    first_half = values[..., :half_width]
    second_half = values[..., half_width:]
    cos_rows = cosine[:, None, :]
    sin_rows = sine[:, None, :]
    return jnp.concatenate(
        [
            first_half * cos_rows - second_half * sin_rows,
            second_half * cos_rows + first_half * sin_rows,
        ],
        axis=-1,
    )


def prepare(values, gain, cosine, sine, factor):
    return rotate(rms_scale(values, gain), cosine, sine) * factor


def gelu_tanh(values):
    return (
        0.5
        * values
        * (1.0 + jnp.tanh(0.7978845608028654 * (values + 0.044715 * values * values * values)))
    )


def gated(gate_act, up_proj):
    return gelu_tanh(gate_act) * up_proj


def over_head(part):
    low = part.astype(jnp.bfloat16)
    other = lax.ppermute(low, "head", [(0, 1), (1, 0)])
    return low.astype(jnp.float32) + other.astype(jnp.float32)


def per_device(
    inputs,
    segment_ids,
    w_query,
    w_key,
    w_value,
    w_out,
    w_gate,
    w_up,
    w_down,
    gain_in,
    gain_query,
    gain_key,
    gain_post_attn,
    gain_pre_ffn,
    gain_post_ffn,
    cotangent,
):
    rows = inputs.shape[0]
    head_dim = w_key.shape[1]
    local_heads = w_query.shape[1] // head_dim
    place = lax.axis_index("seq")
    local_index = jnp.arange(rows, dtype=jnp.int32)
    ids_parts = [
        jnp.where(place >= distance, from_behind(segment_ids, "seq", distance), -1)
        for distance in (2, 1)
    ]
    window_ids = jnp.concatenate(ids_parts + [segment_ids], axis=0)
    window_index = jnp.arange(3 * rows, dtype=jnp.int32) - 2 * rows
    same = segment_ids[:, None] == window_ids[None, :]
    visible = same & (window_index[None, :] <= local_index[:, None])
    positions = jnp.sum(visible.astype(jnp.int32), axis=1) - 1
    cosine, sine = rope_angles(positions, head_dim)
    inputs_f = inputs.astype(jnp.float32)
    hidden_in = rms_scale(inputs_f, gain_in).astype(jnp.bfloat16)
    query_proj = jnp.dot(hidden_in, w_query, preferred_element_type=jnp.float32)
    key_proj = jnp.dot(hidden_in, w_key, preferred_element_type=jnp.float32)
    value_proj = jnp.dot(hidden_in, w_value, preferred_element_type=jnp.float32)

    def query_side(projection, gain):
        return prepare(
            projection.reshape(rows, local_heads, head_dim), gain, cosine, sine, QUERY_SCALE
        )

    def key_side(projection, gain):
        return prepare(projection[:, None, :], gain, cosine, sine, 1.0)[:, 0, :]

    queries = query_side(query_proj, gain_query).astype(jnp.bfloat16)
    own_keys = key_side(key_proj, gain_key).astype(jnp.bfloat16)
    own_values = value_proj.astype(jnp.bfloat16)
    key_parts = []
    value_parts = []
    for distance in (2, 1):
        moved_keys, moved_values = from_behind((own_keys, own_values), "seq", distance)
        key_parts.append(moved_keys)
        value_parts.append(moved_values)
    all_keys = jnp.concatenate(key_parts + [own_keys], axis=0)
    all_values = jnp.concatenate(value_parts + [own_values], axis=0)
    def raw_scores():
        return jnp.einsum("ihd,jd->hij", queries, all_keys, preferred_element_type=jnp.float32)

    scores = jnp.where(visible[None], raw_scores(), -1e30)
    row_max = jnp.max(scores, axis=-1, keepdims=True)
    expo = jnp.exp(scores - row_max)
    total = jnp.sum(expo, axis=-1, keepdims=True)
    attn_probs = expo / total
    log_total = row_max + jnp.log(total)
    attended = jnp.einsum(
        "hij,jd->ihd",
        attn_probs.astype(jnp.bfloat16),
        all_values,
        preferred_element_type=jnp.float32,
    )
    attended = attended.reshape(rows, local_heads * head_dim).astype(jnp.bfloat16)
    attn_branch = over_head(jnp.dot(attended, w_out, preferred_element_type=jnp.float32))
    residual_mid = inputs_f + rms_scale(attn_branch, gain_post_attn)
    hidden_mid = rms_scale(residual_mid, gain_pre_ffn).astype(jnp.bfloat16)
    gate_act = jnp.dot(hidden_mid, w_gate, preferred_element_type=jnp.float32)
    up_proj = jnp.dot(hidden_mid, w_up, preferred_element_type=jnp.float32)
    mixed_low = gated(gate_act, up_proj).astype(jnp.bfloat16)
    ffn_branch = over_head(jnp.dot(mixed_low, w_down, preferred_element_type=jnp.float32))
    output_f = residual_mid + rms_scale(ffn_branch, gain_post_ffn)
    grad_output = cotangent.astype(jnp.float32)
    unused_post, post_back = jax.vjp(rms_scale, ffn_branch, gain_post_ffn)
    grad_ffn, grad_g_post_ffn = post_back(grad_output)
    grad_ffn_low = grad_ffn.astype(jnp.bfloat16)
    grad_w_down = jnp.dot(mixed_low.T, grad_ffn_low, preferred_element_type=jnp.float32)
    grad_mixed = jnp.dot(grad_ffn_low, w_down.T, preferred_element_type=jnp.float32)
    unused_gate, gate_back = jax.vjp(gated, gate_act, up_proj)
    grad_gate, grad_up = gate_back(grad_mixed)
    grad_gate_low = grad_gate.astype(jnp.bfloat16)
    grad_up_low = grad_up.astype(jnp.bfloat16)
    grad_w_gate = jnp.dot(hidden_mid.T, grad_gate_low, preferred_element_type=jnp.float32)
    grad_w_up = jnp.dot(hidden_mid.T, grad_up_low, preferred_element_type=jnp.float32)
    grad_hidden_part = jnp.dot(
        grad_gate_low, w_gate.T, preferred_element_type=jnp.float32
    ) + jnp.dot(grad_up_low, w_up.T, preferred_element_type=jnp.float32)
    grad_hidden_mid = over_head(grad_hidden_part)
    unused_pre, pre_back = jax.vjp(rms_scale, residual_mid, gain_pre_ffn)
    grad_res_part, grad_g_pre_ffn = pre_back(grad_hidden_mid)
    grad_residual = grad_output + grad_res_part
    unused_attn, attn_post_back = jax.vjp(rms_scale, attn_branch, gain_post_attn)
    grad_attn, grad_g_post_attn = attn_post_back(grad_residual)
    grad_attn_low = grad_attn.astype(jnp.bfloat16)
    grad_w_out = jnp.dot(attended.T, grad_attn_low, preferred_element_type=jnp.float32)
    grad_attended = jnp.dot(grad_attn_low, w_out.T, preferred_element_type=jnp.float32).astype(
        jnp.bfloat16
    )
    grad_attended = grad_attended.reshape(rows, local_heads, head_dim)
    probs_again = jnp.where(visible[None], jnp.exp(raw_scores() - log_total), 0.0)
    grad_probs = jnp.einsum(
        "ihd,jd->hij", grad_attended, all_values, preferred_element_type=jnp.float32
    )
    grad_scores = (
        probs_again * (grad_probs - jnp.sum(probs_again * grad_probs, axis=-1, keepdims=True))
    ).astype(jnp.bfloat16)
    grad_queries = jnp.einsum(
        "hij,jd->ihd", grad_scores, all_keys, preferred_element_type=jnp.float32
    )
    grad_keys_all = jnp.einsum(
        "hij,ihd->jd", grad_scores, queries, preferred_element_type=jnp.float32
    )
    grad_values_all = jnp.einsum(
        "hij,ihd->jd",
        probs_again.astype(jnp.bfloat16),
        grad_attended,
        preferred_element_type=jnp.float32,
    )
    grad_keys = grad_keys_all[2 * rows :]
    grad_values = grad_values_all[2 * rows :]
    for distance in (2, 1):
        piece_begin = (2 - distance) * rows
        returned_keys, returned_values = (
            from_behind(
                grad_keys_all[piece_begin : piece_begin + rows].astype(jnp.bfloat16),
                "seq",
                -distance,
            ).astype(jnp.float32),
            from_behind(
                grad_values_all[piece_begin : piece_begin + rows].astype(jnp.bfloat16),
                "seq",
                -distance,
            ).astype(jnp.float32),
        )
        grad_keys = grad_keys + returned_keys
        grad_values = grad_values + returned_values
    unused_query, query_back = jax.vjp(query_side, query_proj, gain_query)
    grad_query_proj, grad_g_query_part = query_back(grad_queries)
    grad_query_low = grad_query_proj.astype(jnp.bfloat16)
    grad_w_query = jnp.dot(hidden_in.T, grad_query_low, preferred_element_type=jnp.float32)
    grad_hidden_query = jnp.dot(grad_query_low, w_query.T, preferred_element_type=jnp.float32)
    keys_summed, values_summed, hidden_summed, grad_g_query = (
        over_head(grad_keys),
        over_head(grad_values),
        over_head(grad_hidden_query),
        over_head(grad_g_query_part),
    )
    unused_key, key_back = jax.vjp(key_side, key_proj, gain_key)
    grad_key_proj, grad_g_key = key_back(keys_summed)
    grad_key_low = grad_key_proj.astype(jnp.bfloat16)
    grad_value_low = values_summed.astype(jnp.bfloat16)
    grad_w_key = jnp.dot(hidden_in.T, grad_key_low, preferred_element_type=jnp.float32)
    grad_w_value = jnp.dot(hidden_in.T, grad_value_low, preferred_element_type=jnp.float32)
    grad_hidden_in = (
        hidden_summed
        + jnp.dot(grad_key_low, w_key.T, preferred_element_type=jnp.float32)
        + jnp.dot(grad_value_low, w_value.T, preferred_element_type=jnp.float32)
    )
    unused_in, in_back = jax.vjp(rms_scale, inputs_f, gain_in)
    grad_in_part, grad_g_in = in_back(grad_hidden_in)
    grad_inputs = (grad_residual + grad_in_part).astype(jnp.bfloat16)
    def scatter(grad, dim):
        return lax.psum_scatter(
            grad.astype(jnp.bfloat16), "seq", scatter_dimension=dim, tiled=True
        ).astype(jnp.float32)

    gains = (grad_g_in, grad_g_query, grad_g_key, grad_g_post_attn, grad_g_pre_ffn, grad_g_post_ffn)
    gain_rows = jnp.concatenate(
        [g.reshape(lax.axis_size("seq"), -1) for g in gains], axis=1
    )
    gain_sum = lax.psum_scatter(gain_rows, "seq", scatter_dimension=0, tiled=True)[0]
    gain_out = []
    start = 0
    for g in gains:
        size = g.shape[0] // lax.axis_size("seq")
        gain_out.append(gain_sum[start : start + size])
        start += size
    every_grad = (
        scatter(grad_w_query, 0),
        scatter(grad_w_key, 0),
        scatter(grad_w_value, 0),
        scatter(grad_w_out, 1),
        scatter(grad_w_gate, 0),
        scatter(grad_w_up, 0),
        scatter(grad_w_down, 1),
        *gain_out,
    )
    (
        summed_query,
        summed_key,
        summed_value,
        summed_out,
        summed_gate,
        summed_up,
        summed_down,
        summed_g_in,
        summed_g_query,
        summed_g_key,
        summed_g_post_attn,
        summed_g_pre_ffn,
        summed_g_post_ffn,
    ) = every_grad
    return (
        output_f.astype(jnp.bfloat16),
        grad_inputs,
        summed_query,
        summed_key,
        summed_value,
        summed_out,
        summed_gate,
        summed_up,
        summed_down,
        summed_g_in,
        summed_g_query,
        summed_g_key,
        summed_g_post_attn,
        summed_g_pre_ffn,
        summed_g_post_ffn,
    )


def solution(mesh):
    placed = (
        P("seq", None),
        P("seq"),
        P(None, "head"),
        P(),
        P(),
        P("head", None),
        P(None, "head"),
        P(None, "head"),
        P("head", None),
        P(),
        P(),
        P(),
        P(),
        P(),
        P(),
        P("seq", None),
    )
    return jax.shard_map(
        per_device,
        mesh=mesh,
        in_specs=placed,
        out_specs=(
            P("seq", None),
            P("seq", None),
            P("seq", "head"),
            P("seq", None),
            P("seq", None),
            P("head", "seq"),
            P("seq", "head"),
            P("seq", "head"),
            P("head", "seq"),
            P("seq"),
            P("seq"),
            P("seq"),
            P("seq"),
            P("seq"),
            P("seq"),
        ),
        check_vma=False,
    )
```

```python
import math

import jax
import jax.numpy as jnp
from jax import lax
from jax.sharding import PartitionSpec as P

EPS = 1e-06
QUERY_SCALE = 0.0625


def from_behind(block, axis, distance):
    devices = range(lax.axis_size(axis))
    route = [(i - distance, i) for i in devices if i - distance in devices]
    return lax.ppermute(block, axis, route)


def rms_scale(values, gain):
    return values * lax.rsqrt(jnp.mean(values * values, axis=-1, keepdims=True) + EPS) * gain


def rope_angles(positions, width):
    half_width = width // 2
    frequency = jnp.exp(
        jnp.arange(half_width, dtype=jnp.float32) * (-2.0 * math.log(1000000.0) / width)
    )
    angles = positions.astype(jnp.float32)[:, None] * frequency[None, :]
    return (jnp.cos(angles), jnp.sin(angles))


def rotate(values, cosine, sine):
    half_width = values.shape[-1] // 2
    first_half = values[..., :half_width]
    second_half = values[..., half_width:]
    cos_rows = cosine[:, None, :]
    sin_rows = sine[:, None, :]
    return jnp.concatenate(
        [
            first_half * cos_rows - second_half * sin_rows,
            second_half * cos_rows + first_half * sin_rows,
        ],
        axis=-1,
    )


def prepare(values, gain, cosine, sine, factor):
    return rotate(rms_scale(values, gain), cosine, sine) * factor


def gelu_tanh(values):
    return (
        0.5
        * values
        * (1.0 + jnp.tanh(0.7978845608028654 * (values + 0.044715 * values * values * values)))
    )


def gated(gate_act, up_proj):
    return gelu_tanh(gate_act) * up_proj


def over_head(part):
    low = part.astype(jnp.bfloat16)
    other = lax.ppermute(low, "head", [(0, 1), (1, 0)])
    return low.astype(jnp.float32) + other.astype(jnp.float32)


def scatter_rows(grad):
    count = lax.axis_size("seq")
    if count != 16:
        return lax.psum_scatter(grad, "seq", scatter_dimension=0, tiled=True).astype(jnp.float32)
    place = lax.axis_index("seq")
    core, side, level = place % 2, place // 2 % 2, place // 4
    columns = grad.shape[1]
    wide = jnp.float32
    halves = grad.reshape(2, -1, columns)
    other = lax.ppermute(
        lax.dynamic_index_in_dim(halves, 1 - core, 0, False),
        "seq",
        [(i, i ^ 1) for i in range(count)],
    )
    mine = lax.dynamic_index_in_dim(halves, core, 0, False)
    pair = (mine.astype(wide) + other.astype(wide)).astype(jnp.bfloat16)
    quarters = pair.reshape(2, 2, -1, columns)
    other = lax.ppermute(
        lax.dynamic_index_in_dim(quarters, 1 - side, 1, False),
        "seq",
        [(i, i ^ 2) for i in range(count)],
    )
    mine = lax.dynamic_index_in_dim(quarters, side, 1, False)
    four = (mine.astype(wide) + other.astype(wide)).astype(jnp.bfloat16)
    blocks = four.reshape(4, -1, columns)
    total = None
    for lap in range(4):
        route = []
        for i in range(count):
            block = (i // 4) ^ lap
            target_level = 2 * (i % 2) + block // 2
            route.append((i, target_level * 4 + (i // 2 % 2) * 2 + block % 2))
        part = lax.ppermute(
            lax.dynamic_index_in_dim(blocks, level ^ lap, 0, False), "seq", route
        ).astype(wide)
        total = part if total is None else total + part
    return total


def per_device(
    inputs,
    segment_ids,
    w_query,
    w_key,
    w_value,
    w_out,
    w_gate,
    w_up,
    w_down,
    gain_in,
    gain_query,
    gain_key,
    gain_post_attn,
    gain_pre_ffn,
    gain_post_ffn,
    cotangent,
):
    rows = inputs.shape[0]
    head_dim = w_key.shape[1]
    local_heads = w_query.shape[1] // head_dim
    place = lax.axis_index("seq")
    local_index = jnp.arange(rows, dtype=jnp.int32)
    ids_parts = [
        jnp.where(place >= distance, from_behind(segment_ids, "seq", distance), -1)
        for distance in (2, 1)
    ]
    window_ids = jnp.concatenate(ids_parts + [segment_ids], axis=0)
    window_index = jnp.arange(3 * rows, dtype=jnp.int32) - 2 * rows
    same = segment_ids[:, None] == window_ids[None, :]
    visible = same & (window_index[None, :] <= local_index[:, None])
    positions = jnp.sum(visible.astype(jnp.int32), axis=1) - 1
    cosine, sine = rope_angles(positions, head_dim)
    inputs_f = inputs.astype(jnp.float32)
    hidden_in = rms_scale(inputs_f, gain_in).astype(jnp.bfloat16)
    query_proj = jnp.dot(hidden_in, w_query, preferred_element_type=jnp.float32)
    key_proj = jnp.dot(hidden_in, w_key, preferred_element_type=jnp.float32)
    value_proj = jnp.dot(hidden_in, w_value, preferred_element_type=jnp.float32)

    def query_side(projection, gain):
        return prepare(
            projection.reshape(rows, local_heads, head_dim), gain, cosine, sine, QUERY_SCALE
        )

    def key_side(projection, gain):
        return prepare(projection[:, None, :], gain, cosine, sine, 1.0)[:, 0, :]

    queries = query_side(query_proj, gain_query).astype(jnp.bfloat16)
    own_keys = key_side(key_proj, gain_key).astype(jnp.bfloat16)
    own_values = value_proj.astype(jnp.bfloat16)
    key_parts = []
    value_parts = []
    for distance in (2, 1):
        moved_keys, moved_values = from_behind((own_keys, own_values), "seq", distance)
        key_parts.append(moved_keys)
        value_parts.append(moved_values)
    all_keys = jnp.concatenate(key_parts + [own_keys], axis=0)
    all_values = jnp.concatenate(value_parts + [own_values], axis=0)
    def raw_scores():
        return jnp.einsum("ihd,jd->hij", queries, all_keys, preferred_element_type=jnp.float32)

    scores = jnp.where(visible[None], raw_scores(), -1e30)
    row_max = jnp.max(scores, axis=-1, keepdims=True)
    expo = jnp.exp(scores - row_max)
    total = jnp.sum(expo, axis=-1, keepdims=True)
    attn_probs = expo / total
    log_total = row_max + jnp.log(total)
    attended = jnp.einsum(
        "hij,jd->ihd",
        attn_probs.astype(jnp.bfloat16),
        all_values,
        preferred_element_type=jnp.float32,
    )
    attended = attended.reshape(rows, local_heads * head_dim).astype(jnp.bfloat16)
    attn_branch = over_head(jnp.dot(attended, w_out, preferred_element_type=jnp.float32))
    residual_mid = inputs_f + rms_scale(attn_branch, gain_post_attn)
    hidden_mid = rms_scale(residual_mid, gain_pre_ffn).astype(jnp.bfloat16)
    gate_act = jnp.dot(hidden_mid, w_gate, preferred_element_type=jnp.float32)
    up_proj = jnp.dot(hidden_mid, w_up, preferred_element_type=jnp.float32)
    mixed_low = gated(gate_act, up_proj).astype(jnp.bfloat16)
    ffn_branch = over_head(jnp.dot(mixed_low, w_down, preferred_element_type=jnp.float32))
    output_f = residual_mid + rms_scale(ffn_branch, gain_post_ffn)
    grad_output = cotangent.astype(jnp.float32)
    unused_post, post_back = jax.vjp(rms_scale, ffn_branch, gain_post_ffn)
    grad_ffn, grad_g_post_ffn = post_back(grad_output)
    grad_ffn_low = grad_ffn.astype(jnp.bfloat16)
    grad_w_down = jnp.dot(grad_ffn_low.T, mixed_low, preferred_element_type=jnp.float32)
    summed_down = scatter_rows(grad_w_down.astype(jnp.bfloat16))
    grad_mixed = jnp.dot(grad_ffn_low, w_down.T, preferred_element_type=jnp.float32)
    unused_gate, gate_back = jax.vjp(gated, gate_act, up_proj)
    grad_gate, grad_up = gate_back(grad_mixed)
    grad_gate_low = grad_gate.astype(jnp.bfloat16)
    grad_up_low = grad_up.astype(jnp.bfloat16)
    grad_w_gate = jnp.dot(hidden_mid.T, grad_gate_low, preferred_element_type=jnp.float32)
    grad_w_up = jnp.dot(hidden_mid.T, grad_up_low, preferred_element_type=jnp.float32)
    summed_gate = scatter_rows(grad_w_gate.astype(jnp.bfloat16))
    summed_up = scatter_rows(grad_w_up.astype(jnp.bfloat16))
    grad_hidden_part = jnp.dot(
        grad_gate_low, w_gate.T, preferred_element_type=jnp.float32
    ) + jnp.dot(grad_up_low, w_up.T, preferred_element_type=jnp.float32)
    grad_hidden_mid = over_head(grad_hidden_part)
    unused_pre, pre_back = jax.vjp(rms_scale, residual_mid, gain_pre_ffn)
    grad_res_part, grad_g_pre_ffn = pre_back(grad_hidden_mid)
    grad_residual = grad_output + grad_res_part
    unused_attn, attn_post_back = jax.vjp(rms_scale, attn_branch, gain_post_attn)
    grad_attn, grad_g_post_attn = attn_post_back(grad_residual)
    grad_attn_low = grad_attn.astype(jnp.bfloat16)
    grad_w_out = jnp.dot(grad_attn_low.T, attended, preferred_element_type=jnp.float32)
    grad_attended = jnp.dot(grad_attn_low, w_out.T, preferred_element_type=jnp.float32).astype(
        jnp.bfloat16
    )
    grad_attended = grad_attended.reshape(rows, local_heads, head_dim)
    probs_again = jnp.where(visible[None], jnp.exp(raw_scores() - log_total), 0.0)
    grad_probs = jnp.einsum(
        "ihd,jd->hij", grad_attended, all_values, preferred_element_type=jnp.float32
    )
    grad_scores = (
        probs_again * (grad_probs - jnp.sum(probs_again * grad_probs, axis=-1, keepdims=True))
    ).astype(jnp.bfloat16)
    grad_queries = jnp.einsum(
        "hij,jd->ihd", grad_scores, all_keys, preferred_element_type=jnp.float32
    )
    grad_keys_all = jnp.einsum(
        "hij,ihd->jd", grad_scores, queries, preferred_element_type=jnp.float32
    )
    grad_values_all = jnp.einsum(
        "hij,ihd->jd",
        probs_again.astype(jnp.bfloat16),
        grad_attended,
        preferred_element_type=jnp.float32,
    )
    grad_keys = grad_keys_all[2 * rows :]
    grad_values = grad_values_all[2 * rows :]
    for distance in (2, 1):
        piece_begin = (2 - distance) * rows
        returned_keys, returned_values = (
            from_behind(
                grad_keys_all[piece_begin : piece_begin + rows].astype(jnp.bfloat16),
                "seq",
                -distance,
            ).astype(jnp.float32),
            from_behind(
                grad_values_all[piece_begin : piece_begin + rows].astype(jnp.bfloat16),
                "seq",
                -distance,
            ).astype(jnp.float32),
        )
        grad_keys = grad_keys + returned_keys
        grad_values = grad_values + returned_values
    unused_query, query_back = jax.vjp(query_side, query_proj, gain_query)
    grad_query_proj, grad_g_query_part = query_back(grad_queries)
    grad_query_low = grad_query_proj.astype(jnp.bfloat16)
    grad_w_query = jnp.dot(hidden_in.T, grad_query_low, preferred_element_type=jnp.float32)
    grad_hidden_query = jnp.dot(grad_query_low, w_query.T, preferred_element_type=jnp.float32)
    keys_summed, values_summed, hidden_summed, grad_g_query = (
        over_head(grad_keys),
        over_head(grad_values),
        over_head(grad_hidden_query),
        over_head(grad_g_query_part),
    )
    unused_key, key_back = jax.vjp(key_side, key_proj, gain_key)
    grad_key_proj, grad_g_key = key_back(keys_summed)
    grad_key_low = grad_key_proj.astype(jnp.bfloat16)
    grad_value_low = values_summed.astype(jnp.bfloat16)
    grad_w_key = jnp.dot(hidden_in.T, grad_key_low, preferred_element_type=jnp.float32)
    grad_w_value = jnp.dot(hidden_in.T, grad_value_low, preferred_element_type=jnp.float32)
    grad_hidden_in = (
        hidden_summed
        + jnp.dot(grad_key_low, w_key.T, preferred_element_type=jnp.float32)
        + jnp.dot(grad_value_low, w_value.T, preferred_element_type=jnp.float32)
    )
    unused_in, in_back = jax.vjp(rms_scale, inputs_f, gain_in)
    grad_in_part, grad_g_in = in_back(grad_hidden_in)
    grad_inputs = (grad_residual + grad_in_part).astype(jnp.bfloat16)
    count = lax.axis_size("seq")
    gain_columns = jnp.stack(
        [grad_g_in, grad_g_post_attn, grad_g_pre_ffn, grad_g_post_ffn], axis=1
    )
    side = jnp.concatenate(
        [grad_g_query.reshape(count, -1), grad_g_key.reshape(count, -1)], axis=1
    )
    side_rows = jnp.repeat(side, inputs.shape[1] // count, axis=0)
    extra = jnp.concatenate([gain_columns, side_rows], axis=1)
    extra = jnp.pad(extra, ((0, 0), (0, -extra.shape[1] % 128)))
    widths = [g.shape[1] for g in (grad_w_query, grad_w_out, grad_w_key, grad_w_value)]
    attn_sum = scatter_rows(
        jnp.concatenate(
            [
                g.astype(jnp.bfloat16)
                for g in (grad_w_query, grad_w_out, grad_w_key, grad_w_value, extra)
            ],
            axis=1,
        )
    )
    edges = [sum(widths[:i]) for i in range(5)]
    summed_query, summed_out, summed_key, summed_value = (
        attn_sum[:, edges[i] : edges[i + 1]] for i in range(4)
    )
    gain_sum = attn_sum[:, edges[4] :]
    summed_g_in, summed_g_post_attn, summed_g_pre_ffn, summed_g_post_ffn = (
        gain_sum[:, i] for i in range(4)
    )
    own = head_dim // count
    summed_g_query = gain_sum[0, 4 : 4 + own]
    summed_g_key = gain_sum[0, 4 + own : 4 + 2 * own]
    summed_out = summed_out.T
    summed_down = summed_down.T
    return (
        output_f.astype(jnp.bfloat16),
        grad_inputs,
        summed_query,
        summed_key,
        summed_value,
        summed_out,
        summed_gate,
        summed_up,
        summed_down,
        summed_g_in,
        summed_g_query,
        summed_g_key,
        summed_g_post_attn,
        summed_g_pre_ffn,
        summed_g_post_ffn,
    )


def solution(mesh):
    placed = (
        P("seq", None),
        P("seq"),
        P(None, "head"),
        P(),
        P(),
        P("head", None),
        P(None, "head"),
        P(None, "head"),
        P("head", None),
        P(),
        P(),
        P(),
        P(),
        P(),
        P(),
        P("seq", None),
    )
    return jax.shard_map(
        per_device,
        mesh=mesh,
        in_specs=placed,
        out_specs=(
            P("seq", None),
            P("seq", None),
            P("seq", "head"),
            P("seq", None),
            P("seq", None),
            P("head", "seq"),
            P("seq", "head"),
            P("seq", "head"),
            P("head", "seq"),
            P("seq"),
            P("seq"),
            P("seq"),
            P("seq"),
            P("seq"),
            P("seq"),
        ),
        check_vma=False,
    )
```

```python
import functools
import math

import jax
import jax.numpy as jnp
from jax import lax
from jax.experimental import pallas as pl
from jax.experimental.pallas import tpu as pltpu
from jax.sharding import PartitionSpec as P

MESH = pl.DeviceIdType.MESH
WIDE = 384
BLOCK = 72

EPS = 1e-06
QUERY_SCALE = 0.0625


def from_behind(block, axis, distance):
    devices = range(lax.axis_size(axis))
    route = [(i - distance, i) for i in devices if i - distance in devices]
    return lax.ppermute(block, axis, route)


def rms_scale(values, gain):
    return values * lax.rsqrt(jnp.mean(values * values, axis=-1, keepdims=True) + EPS) * gain


def rope_angles(positions, width):
    half_width = width // 2
    frequency = jnp.exp(
        jnp.arange(half_width, dtype=jnp.float32) * (-2.0 * math.log(1000000.0) / width)
    )
    angles = positions.astype(jnp.float32)[:, None] * frequency[None, :]
    return (jnp.cos(angles), jnp.sin(angles))


def rotate(values, cosine, sine):
    half_width = values.shape[-1] // 2
    first_half = values[..., :half_width]
    second_half = values[..., half_width:]
    cos_rows = cosine[:, None, :]
    sin_rows = sine[:, None, :]
    return jnp.concatenate(
        [
            first_half * cos_rows - second_half * sin_rows,
            second_half * cos_rows + first_half * sin_rows,
        ],
        axis=-1,
    )


def prepare(values, gain, cosine, sine, factor):
    return rotate(rms_scale(values, gain), cosine, sine) * factor


def gelu_tanh(values):
    return (
        0.5
        * values
        * (1.0 + jnp.tanh(0.7978845608028654 * (values + 0.044715 * values * values * values)))
    )


def gated(gate_act, up_proj):
    return gelu_tanh(gate_act) * up_proj


def over_head(part):
    low = part.astype(jnp.bfloat16)
    other = lax.ppermute(low, "head", [(0, 1), (1, 0)])
    return low.astype(jnp.float32) + other.astype(jnp.float32)


def place_of():
    seq = lax.axis_index("seq")
    return seq, lax.axis_index("head"), seq % 2, seq // 2 % 2, seq // 4


def gradient_kernel(
    steps, lag_x, lag_z, lhs, rhs, extra, out,
    held, sent, core_in, x_in, z_out, z_in, rhs_slots,
    rhs_sem, core_send, core_recv, x_send, x_recv, z_send, z_recv,
):
    seq, head, core, side, level = place_of()
    wide = jnp.float32
    low = jnp.bfloat16
    ring = held.shape[0]

    barrier = pltpu.get_barrier_semaphore()
    partners = [seq ^ 1, seq ^ 2]
    targets = []
    for k in range(4):
        target_level = 2 * core + k // 2
        targets.append((target_level * 4 + side * 2 + k % 2, target_level, k % 2))
    sources = []
    for z in range(4):
        sources.append(z * 4 + side * 2 + level // 2)
    for partner in partners:
        pl.semaphore_signal(barrier, inc=1, device_id=(partner, head), device_id_type=MESH)
    for z in range(4):
        for c in range(2):
            other = z * 4 + side * 2 + c

            @pl.when(other != seq)
            def _():
                pl.semaphore_signal(barrier, inc=1, device_id=(other, head), device_id_type=MESH)

    pl.semaphore_wait(barrier, 9)

    def rhs_copy(t):
        slot = lax.rem(t, 2)
        return pltpu.make_async_copy(rhs.at[t], rhs_slots.at[slot], rhs_sem.at[slot])

    def core_copy(t):
        return pltpu.make_async_remote_copy(
            src_ref=sent.at[lax.rem(t, 2)],
            dst_ref=core_in.at[t],
            send_sem=core_send.at[t],
            recv_sem=core_recv.at[t],
            device_id=(seq ^ 1, head),
            device_id_type=MESH,
        )

    def x_copy(t):
        return pltpu.make_async_remote_copy(
            src_ref=held.at[lax.rem(t, ring), 1 - side],
            dst_ref=x_in.at[t],
            send_sem=x_send.at[t],
            recv_sem=x_recv.at[t],
            device_id=(seq ^ 2, head),
            device_id_type=MESH,
        )

    def z_copy(t, k):
        return pltpu.make_async_remote_copy(
            src_ref=z_out.at[lax.rem(t, ring), k],
            dst_ref=z_in.at[t, level],
            send_sem=z_send.at[t, k],
            recv_sem=z_recv.at[t, level],
            device_id=(targets[k][0], head),
            device_id_type=MESH,
        )

    def z_arrival(t, z):
        return pltpu.make_async_remote_copy(
            src_ref=z_out.at[0, 0],
            dst_ref=z_in.at[t, z],
            send_sem=z_send.at[t, 0],
            recv_sem=z_recv.at[t, z],
            device_id=(sources[z], head),
            device_id_type=MESH,
        )

    def to_self(k):
        return targets[k][0] == seq

    def produce(t):
        @pl.when(t + 1 < steps)
        def _():
            rhs_copy(t + 1).start()

        rhs_copy(t).wait()

        @pl.when(t >= 2)
        def _():
            core_copy(t - 2).wait_send()

        @pl.when(t >= ring)
        def _():
            x_copy(t - ring).wait_send()

        which = (t >= 9).astype(jnp.int32) + (t >= 27).astype(jnp.int32) + (t >= 30).astype(jnp.int32)
        tile = rhs_slots[lax.rem(t, 2)]

        def half(start):
            rows = lhs[which, pl.ds(pl.multiple_of(start, 576), 576), :]
            return jnp.dot(rows, tile, preferred_element_type=wide)

        away = half((1 - core) * 576)
        for k in range(8):
            sent[lax.rem(t, 2), k // 4, k % 4] = away[k * BLOCK : (k + 1) * BLOCK].astype(low)

        @pl.when(t == 29)
        def _():
            for k in range(8):
                sent[lax.rem(t, 2), k // 4, k % 4, :, 256:] = extra[1 - core, k]

        core_copy(t).start()
        home = half(core * 576)
        for k in range(8):
            held[lax.rem(t, ring), k // 4, k % 4] = home[k * BLOCK : (k + 1) * BLOCK].astype(low)

        @pl.when(t == 29)
        def _():
            for k in range(8):
                held[lax.rem(t, ring), k // 4, k % 4, :, 256:] = extra[core, k]

    def core_stage(t):
        core_copy(t).wait_recv()
        slot = lax.rem(t, ring)
        for part in (1 - side, side):
            for k in range(4):
                held[slot, part, k] = (
                    held[slot, part, k].astype(wide) + core_in[t, part, k].astype(wide)
                ).astype(low)
            if part is not side:
                x_copy(t).start()

    def x_stage(t):
        x_copy(t).wait_recv()
        slot = lax.rem(t, ring)

        @pl.when(t >= ring)
        def _():
            for k in range(4):
                @pl.when(jnp.logical_not(to_self(k)))
                def _():
                    z_copy(t - ring, k).wait_send()

        for k in range(4):
            total = (held[slot, side, k].astype(wide) + x_in[t, k].astype(wide)).astype(low)

            @pl.when(to_self(k))
            def _():
                z_in[t, level] = total

            @pl.when(jnp.logical_not(to_self(k)))
            def _():
                z_out[slot, k] = total
                z_copy(t, k).start()

    def z_stage(t):
        for z in range(4):
            @pl.when(sources[z] != seq)
            def _():
                z_arrival(t, z).wait_recv()

        total = z_in[t, 0].astype(wide)
        for z in range(1, 4):
            total = total + z_in[t, z].astype(wide)
        out[t] = total

    rhs_copy(0).start()

    def step(i, carry):
        @pl.when(i < steps)
        def _():
            produce(i)

        @pl.when((i >= 1) & (i - 1 < steps))
        def _():
            core_stage(i - 1)

        @pl.when((i >= lag_x) & (i - lag_x < steps))
        def _():
            x_stage(i - lag_x)

        @pl.when((i >= lag_z) & (i - lag_z < steps))
        def _():
            z_stage(i - lag_z)

        return carry

    lax.fori_loop(0, steps + lag_z, step, 0)

    def drain(i, carry):
        @pl.when(i >= steps - 2)
        def _():
            core_copy(i).wait_send()

        x_copy(i).wait_send()
        for k in range(4):
            @pl.when(jnp.logical_not(to_self(k)))
            def _():
                z_copy(i, k).wait_send()

        return carry

    lax.fori_loop(steps - ring, steps, drain, 0)


def block_order(rows):
    return rows.reshape(2, 2, 2, 2 * BLOCK, -1).transpose(0, 2, 1, 3, 4).reshape(rows.shape[0], -1)


def summed_gradients(lhs, rhs, extra):
    steps, tokens, wide = rhs.shape
    ring, lag_x, lag_z = 6, 3, 5
    low, f32 = jnp.bfloat16, jnp.float32
    dma = pltpu.SemaphoreType.DMA
    return pl.pallas_call(
        functools.partial(gradient_kernel, steps, lag_x, lag_z),
        out_shape=jax.ShapeDtypeStruct((steps, BLOCK, wide), f32),
        in_specs=[
            pl.BlockSpec(memory_space=pltpu.VMEM),
            pl.BlockSpec(memory_space=pl.ANY),
            pl.BlockSpec(memory_space=pltpu.VMEM),
        ],
        out_specs=pl.BlockSpec(memory_space=pltpu.VMEM),
        scratch_shapes=[
            pltpu.VMEM((ring, 2, 4, BLOCK, wide), low),
            pltpu.VMEM((2, 2, 4, BLOCK, wide), low),
            pltpu.VMEM((steps, 2, 4, BLOCK, wide), low),
            pltpu.VMEM((steps, 4, BLOCK, wide), low),
            pltpu.VMEM((ring, 4, BLOCK, wide), low),
            pltpu.VMEM((steps, 4, BLOCK, wide), low),
            pltpu.VMEM((2, tokens, wide), low),
            dma((2,)),
            dma((steps,)),
            dma((steps,)),
            dma((steps,)),
            dma((steps,)),
            dma((steps, 4)),
            dma((steps, 4)),
        ],
        compiler_params=pltpu.CompilerParams(
            collective_id=1, has_side_effects=True, vmem_limit_bytes=58 << 20
        ),
        name="gradients",
    )(lhs, rhs, extra)


def scatter_rows(grad):
    return lax.psum_scatter(
        grad.astype(jnp.bfloat16), "seq", scatter_dimension=0, tiled=True
    ).astype(jnp.float32)


def tiles(rhs):
    padded = jnp.pad(rhs, ((0, 0), (0, -rhs.shape[1] % WIDE)))
    return padded.reshape(rhs.shape[0], -1, WIDE).transpose(1, 0, 2)


def per_device(
    inputs,
    segment_ids,
    w_query,
    w_key,
    w_value,
    w_out,
    w_gate,
    w_up,
    w_down,
    gain_in,
    gain_query,
    gain_key,
    gain_post_attn,
    gain_pre_ffn,
    gain_post_ffn,
    cotangent,
):
    rows = inputs.shape[0]
    head_dim = w_key.shape[1]
    local_heads = w_query.shape[1] // head_dim
    place = lax.axis_index("seq")
    local_index = jnp.arange(rows, dtype=jnp.int32)
    ids_parts = [
        jnp.where(place >= distance, from_behind(segment_ids, "seq", distance), -1)
        for distance in (2, 1)
    ]
    window_ids = jnp.concatenate(ids_parts + [segment_ids], axis=0)
    window_index = jnp.arange(3 * rows, dtype=jnp.int32) - 2 * rows
    same = segment_ids[:, None] == window_ids[None, :]
    visible = same & (window_index[None, :] <= local_index[:, None])
    positions = jnp.sum(visible.astype(jnp.int32), axis=1) - 1
    cosine, sine = rope_angles(positions, head_dim)
    inputs_f = inputs.astype(jnp.float32)
    hidden_in = rms_scale(inputs_f, gain_in).astype(jnp.bfloat16)
    query_proj = jnp.dot(hidden_in, w_query, preferred_element_type=jnp.float32)
    key_proj = jnp.dot(hidden_in, w_key, preferred_element_type=jnp.float32)
    value_proj = jnp.dot(hidden_in, w_value, preferred_element_type=jnp.float32)

    def query_side(projection, gain):
        return prepare(
            projection.reshape(rows, local_heads, head_dim), gain, cosine, sine, QUERY_SCALE
        )

    def key_side(projection, gain):
        return prepare(projection[:, None, :], gain, cosine, sine, 1.0)[:, 0, :]

    queries = query_side(query_proj, gain_query).astype(jnp.bfloat16)
    own_keys = key_side(key_proj, gain_key).astype(jnp.bfloat16)
    own_values = value_proj.astype(jnp.bfloat16)
    key_parts = []
    value_parts = []
    for distance in (2, 1):
        moved_keys, moved_values = from_behind((own_keys, own_values), "seq", distance)
        key_parts.append(moved_keys)
        value_parts.append(moved_values)
    all_keys = jnp.concatenate(key_parts + [own_keys], axis=0)
    all_values = jnp.concatenate(value_parts + [own_values], axis=0)
    def raw_scores():
        return jnp.einsum("ihd,jd->hij", queries, all_keys, preferred_element_type=jnp.float32)

    scores = jnp.where(visible[None], raw_scores(), -1e30)
    row_max = jnp.max(scores, axis=-1, keepdims=True)
    expo = jnp.exp(scores - row_max)
    total = jnp.sum(expo, axis=-1, keepdims=True)
    attn_probs = expo / total
    log_total = row_max + jnp.log(total)
    attended = jnp.einsum(
        "hij,jd->ihd",
        attn_probs.astype(jnp.bfloat16),
        all_values,
        preferred_element_type=jnp.float32,
    )
    attended = attended.reshape(rows, local_heads * head_dim).astype(jnp.bfloat16)
    attn_branch = over_head(jnp.dot(attended, w_out, preferred_element_type=jnp.float32))
    residual_mid = inputs_f + rms_scale(attn_branch, gain_post_attn)
    hidden_mid = rms_scale(residual_mid, gain_pre_ffn).astype(jnp.bfloat16)
    gate_act = jnp.dot(hidden_mid, w_gate, preferred_element_type=jnp.float32)
    up_proj = jnp.dot(hidden_mid, w_up, preferred_element_type=jnp.float32)
    mixed_low = gated(gate_act, up_proj).astype(jnp.bfloat16)
    ffn_branch = over_head(jnp.dot(mixed_low, w_down, preferred_element_type=jnp.float32))
    output_f = residual_mid + rms_scale(ffn_branch, gain_post_ffn)
    grad_output = cotangent.astype(jnp.float32)
    unused_post, post_back = jax.vjp(rms_scale, ffn_branch, gain_post_ffn)
    grad_ffn, grad_g_post_ffn = post_back(grad_output)
    grad_ffn_low = grad_ffn.astype(jnp.bfloat16)
    grad_mixed = jnp.dot(grad_ffn_low, w_down.T, preferred_element_type=jnp.float32)
    unused_gate, gate_back = jax.vjp(gated, gate_act, up_proj)
    grad_gate, grad_up = gate_back(grad_mixed)
    grad_gate_low = grad_gate.astype(jnp.bfloat16)
    grad_up_low = grad_up.astype(jnp.bfloat16)
    grad_hidden_part = jnp.dot(
        grad_gate_low, w_gate.T, preferred_element_type=jnp.float32
    ) + jnp.dot(grad_up_low, w_up.T, preferred_element_type=jnp.float32)
    grad_hidden_mid = over_head(grad_hidden_part)
    unused_pre, pre_back = jax.vjp(rms_scale, residual_mid, gain_pre_ffn)
    grad_res_part, grad_g_pre_ffn = pre_back(grad_hidden_mid)
    grad_residual = grad_output + grad_res_part
    unused_attn, attn_post_back = jax.vjp(rms_scale, attn_branch, gain_post_attn)
    grad_attn, grad_g_post_attn = attn_post_back(grad_residual)
    grad_attn_low = grad_attn.astype(jnp.bfloat16)
    grad_attended = jnp.dot(grad_attn_low, w_out.T, preferred_element_type=jnp.float32).astype(
        jnp.bfloat16
    )
    grad_attended = grad_attended.reshape(rows, local_heads, head_dim)
    probs_again = jnp.where(visible[None], jnp.exp(raw_scores() - log_total), 0.0)
    grad_probs = jnp.einsum(
        "ihd,jd->hij", grad_attended, all_values, preferred_element_type=jnp.float32
    )
    grad_scores = (
        probs_again * (grad_probs - jnp.sum(probs_again * grad_probs, axis=-1, keepdims=True))
    ).astype(jnp.bfloat16)
    grad_queries = jnp.einsum(
        "hij,jd->ihd", grad_scores, all_keys, preferred_element_type=jnp.float32
    )
    grad_keys_all = jnp.einsum(
        "hij,ihd->jd", grad_scores, queries, preferred_element_type=jnp.float32
    )
    grad_values_all = jnp.einsum(
        "hij,ihd->jd",
        probs_again.astype(jnp.bfloat16),
        grad_attended,
        preferred_element_type=jnp.float32,
    )
    grad_keys = grad_keys_all[2 * rows :]
    grad_values = grad_values_all[2 * rows :]
    for distance in (2, 1):
        piece_begin = (2 - distance) * rows
        returned_keys, returned_values = (
            from_behind(
                grad_keys_all[piece_begin : piece_begin + rows].astype(jnp.bfloat16),
                "seq",
                -distance,
            ).astype(jnp.float32),
            from_behind(
                grad_values_all[piece_begin : piece_begin + rows].astype(jnp.bfloat16),
                "seq",
                -distance,
            ).astype(jnp.float32),
        )
        grad_keys = grad_keys + returned_keys
        grad_values = grad_values + returned_values
    unused_query, query_back = jax.vjp(query_side, query_proj, gain_query)
    grad_query_proj, grad_g_query_part = query_back(grad_queries)
    grad_query_low = grad_query_proj.astype(jnp.bfloat16)
    grad_hidden_query = jnp.dot(grad_query_low, w_query.T, preferred_element_type=jnp.float32)
    keys_summed, values_summed, hidden_summed, grad_g_query = (
        over_head(grad_keys),
        over_head(grad_values),
        over_head(grad_hidden_query),
        over_head(grad_g_query_part),
    )
    unused_key, key_back = jax.vjp(key_side, key_proj, gain_key)
    grad_key_proj, grad_g_key = key_back(keys_summed)
    grad_key_low = grad_key_proj.astype(jnp.bfloat16)
    grad_value_low = values_summed.astype(jnp.bfloat16)
    grad_hidden_in = (
        hidden_summed
        + jnp.dot(grad_key_low, w_key.T, preferred_element_type=jnp.float32)
        + jnp.dot(grad_value_low, w_value.T, preferred_element_type=jnp.float32)
    )
    unused_in, in_back = jax.vjp(rms_scale, inputs_f, gain_in)
    grad_in_part, grad_g_in = in_back(grad_hidden_in)
    grad_inputs = (grad_residual + grad_in_part).astype(jnp.bfloat16)
    count = lax.axis_size("seq")
    gain_columns = jnp.stack(
        [grad_g_in, grad_g_post_attn, grad_g_pre_ffn, grad_g_post_ffn], axis=1
    )
    side = jnp.concatenate(
        [grad_g_query.reshape(count, -1), grad_g_key.reshape(count, -1)], axis=1
    )
    side_rows = jnp.repeat(side, inputs.shape[1] // count, axis=0)
    extra = jnp.concatenate([gain_columns, side_rows], axis=1)
    extra = jnp.pad(extra, ((0, 0), (0, -extra.shape[1] % 128)))
    lefts = (grad_ffn_low.T, hidden_mid.T, hidden_in.T, grad_attn_low.T)
    sides = jnp.concatenate([grad_query_low, grad_key_low, grad_value_low], axis=1)
    groups = ((0, mixed_low), (1, grad_gate_low), (1, grad_up_low), (2, sides), (3, attended))
    if count == 16:
        total = summed_gradients(
            jnp.stack([block_order(left) for left in lefts]),
            jnp.concatenate([tiles(rhs) for _, rhs in groups]),
            block_order(extra.astype(jnp.bfloat16)).reshape(2, 8, BLOCK, -1),
        )

        def joined(first, amount):
            part = total[first : first + amount]
            return part.transpose(1, 0, 2).reshape(BLOCK, -1)

        summed = [joined(*span) for span in ((0, 9), (9, 9), (18, 9), (27, 3), (30, 2))]
        gain_sum = summed[3][:, sides.shape[1] :]
    else:
        summed = [
            scatter_rows(jnp.dot(lefts[i], rhs, preferred_element_type=jnp.float32))
            for i, rhs in groups
        ]
        gain_sum = scatter_rows(extra)
    summed_down, summed_gate, summed_up = summed[0].T, summed[1], summed[2]
    query_width = grad_query_low.shape[1]
    summed_query = summed[3][:, :query_width]
    summed_key = summed[3][:, query_width : query_width + head_dim]
    summed_value = summed[3][:, query_width + head_dim : query_width + 2 * head_dim]
    summed_out = summed[4][:, : attended.shape[1]].T
    summed_g_in, summed_g_post_attn, summed_g_pre_ffn, summed_g_post_ffn = (
        gain_sum[:, i] for i in range(4)
    )
    own = head_dim // count
    summed_g_query = gain_sum[0, 4 : 4 + own]
    summed_g_key = gain_sum[0, 4 + own : 4 + 2 * own]
    return (
        output_f.astype(jnp.bfloat16),
        grad_inputs,
        summed_query,
        summed_key,
        summed_value,
        summed_out,
        summed_gate,
        summed_up,
        summed_down,
        summed_g_in,
        summed_g_query,
        summed_g_key,
        summed_g_post_attn,
        summed_g_pre_ffn,
        summed_g_post_ffn,
    )


def solution(mesh):
    placed = (
        P("seq", None),
        P("seq"),
        P(None, "head"),
        P(),
        P(),
        P("head", None),
        P(None, "head"),
        P(None, "head"),
        P("head", None),
        P(),
        P(),
        P(),
        P(),
        P(),
        P(),
        P("seq", None),
    )
    return jax.shard_map(
        per_device,
        mesh=mesh,
        in_specs=placed,
        out_specs=(
            P("seq", None),
            P("seq", None),
            P("seq", "head"),
            P("seq", None),
            P("seq", None),
            P("head", "seq"),
            P("seq", "head"),
            P("seq", "head"),
            P("head", "seq"),
            P("seq"),
            P("seq"),
            P("seq"),
            P("seq"),
            P("seq"),
            P("seq"),
        ),
        check_vma=False,
    )
```

```python
import functools
import math
import types

import jax
import jax.numpy as jnp
from jax import lax
from jax.experimental import pallas as pl
from jax.experimental.pallas import tpu as pltpu
from jax.sharding import PartitionSpec as P

MESH = pl.DeviceIdType.MESH
WIDE = 384
BLOCK = 72

EPS = 1e-06
QUERY_SCALE = 0.0625


def from_behind(block, axis, distance):
    devices = range(lax.axis_size(axis))
    route = [(i - distance, i) for i in devices if i - distance in devices]
    return lax.ppermute(block, axis, route)


def rms_scale(values, gain):
    return values * lax.rsqrt(jnp.mean(values * values, axis=-1, keepdims=True) + EPS) * gain


def rope_angles(positions, width):
    half_width = width // 2
    frequency = jnp.exp(
        jnp.arange(half_width, dtype=jnp.float32) * (-2.0 * math.log(1000000.0) / width)
    )
    angles = positions.astype(jnp.float32)[:, None] * frequency[None, :]
    return (jnp.cos(angles), jnp.sin(angles))


def rotate(values, cosine, sine):
    half_width = values.shape[-1] // 2
    first_half = values[..., :half_width]
    second_half = values[..., half_width:]
    cos_rows = cosine[:, None, :]
    sin_rows = sine[:, None, :]
    return jnp.concatenate(
        [
            first_half * cos_rows - second_half * sin_rows,
            second_half * cos_rows + first_half * sin_rows,
        ],
        axis=-1,
    )


def prepare(values, gain, cosine, sine, factor):
    return rotate(rms_scale(values, gain), cosine, sine) * factor


def gelu_tanh(values):
    return (
        0.5
        * values
        * (1.0 + jnp.tanh(0.7978845608028654 * (values + 0.044715 * values * values * values)))
    )


def gated(gate_act, up_proj):
    return gelu_tanh(gate_act) * up_proj


def over_head(part):
    low = part.astype(jnp.bfloat16)
    other = lax.ppermute(low, "head", [(0, 1), (1, 0)])
    return low.astype(jnp.float32) + other.astype(jnp.float32)


def place_of():
    seq = lax.axis_index("seq")
    return seq, lax.axis_index("head"), seq % 2, seq // 2 % 2, seq // 4


def dot_nt(left, right):
    return lax.dot_general(left, right, (((1,), (1,)), ((), ())), preferred_element_type=jnp.float32)


def dot_tn(left, right):
    return lax.dot_general(left, right, (((0,), (0,)), ((), ())), preferred_element_type=jnp.float32)


def rotate_back(grad, cosine, sine):
    half = grad.shape[-1] // 2
    first, second = grad[:, :half], grad[:, half:]
    return jnp.concatenate(
        [first * cosine + second * sine, second * cosine - first * sine], axis=-1
    )


def norm_parts(values):
    scale = lax.rsqrt(jnp.mean(values * values, axis=-1, keepdims=True) + EPS)
    return scale, values * scale


def norm_back(grad, gain, scale, normed):
    inner = grad * gain
    back = scale * (inner - normed * jnp.mean(inner * normed, axis=-1, keepdims=True))
    return back, jnp.sum(grad * normed, axis=0, keepdims=True)


RING = 6
STEPS = 32
FIRST_SIDE = 27
LAG_X = 3
LAG_Z = 5


def backward_kernel(names, *refs):
    r = types.SimpleNamespace(**dict(zip(names, refs)))
    seq, head, core, side, level = place_of()
    last_seq = lax.axis_size("seq") - 1
    f32, low = jnp.float32, jnp.bfloat16
    rows = r.grad_ffn.shape[0]
    width = r.grad_ffn.shape[1]

    barrier = pltpu.get_barrier_semaphore()

    def greet(to_seq, to_head):
        pl.semaphore_signal(barrier, inc=1, device_id=(to_seq, to_head), device_id_type=MESH)

    greet(seq ^ 1, head)
    greet(seq ^ 2, head)
    greet(seq, 1 - head)
    for z in range(4):
        for c in range(2):
            other = z * 4 + side * 2 + c

            @pl.when(other != seq)
            def _():
                greet(other, head)

    expected = jnp.int32(10)
    for distance in (1, 2):
        @pl.when(seq >= distance)
        def _():
            greet(seq - distance, head)

        @pl.when(seq + distance <= last_seq)
        def _():
            greet(seq + distance, head)

        expected = (
            expected
            + (seq >= distance).astype(jnp.int32)
            + (seq + distance <= last_seq).astype(jnp.int32)
        )
    pl.semaphore_wait(barrier, expected)

    def remote(src, dst, send, recv, to_seq, to_head):
        return pltpu.make_async_remote_copy(
            src_ref=src,
            dst_ref=dst,
            send_sem=send,
            recv_sem=recv,
            device_id=(to_seq, to_head),
            device_id_type=MESH,
        )

    targets = [((2 * core + k // 2) * 4 + side * 2 + k % 2) for k in range(4)]
    sources = [z * 4 + side * 2 + level // 2 for z in range(4)]

    def core_copy(t):
        slot = lax.rem(t, RING)
        return remote(
            r.sent.at[lax.rem(t, 2)], r.core_in.at[slot], r.core_send.at[t], r.core_recv.at[t],
            seq ^ 1, head,
        )

    def x_copy(t):
        slot = lax.rem(t, RING)
        return remote(
            r.held.at[slot, 1 - side], r.x_in.at[slot], r.x_send.at[t], r.x_recv.at[t],
            seq ^ 2, head,
        )

    def z_copy(t, k):
        return remote(
            r.z_out.at[lax.rem(t, RING), k], r.z_in.at[t, level],
            r.z_send.at[t, k], r.z_recv.at[t, level], targets[k], head,
        )

    def z_arrival(t, z):
        return remote(
            r.z_out.at[0, 0], r.z_in.at[t, z], r.z_send.at[t, 0], r.z_recv.at[t, z],
            sources[z], head,
        )

    def produce(t):
        @pl.when(t >= 2)
        def _():
            core_copy(t - 2).wait_send()

        @pl.when(t >= RING)
        def _():
            x_copy(t - RING).wait_send()

        which = jnp.where(t < 9, 0, jnp.where(t < FIRST_SIDE, 1, jnp.where(t < 30, 2, 0)))
        place = jnp.where(
            t < 9, lax.rem(t, 2), jnp.where(t < FIRST_SIDE, t - 7, t - (FIRST_SIDE - 2))
        )
        tile = r.tiles[place]

        def half(start):
            left = r.lefts[which, pl.ds(pl.multiple_of(start, 576), 576), :]
            return jnp.dot(left, tile, preferred_element_type=f32)

        away = half((1 - core) * 576)
        for k in range(8):
            r.sent[lax.rem(t, 2), k // 4, k % 4] = away[k * BLOCK : (k + 1) * BLOCK].astype(low)

        @pl.when(t >= RING)
        def _():
            pl.semaphore_wait(r.core_free, 1)

        core_copy(t).start()
        home = half(core * 576)
        for k in range(8):
            r.held[lax.rem(t, RING), k // 4, k % 4] = home[k * BLOCK : (k + 1) * BLOCK].astype(low)

    def core_stage(t):
        core_copy(t).wait_recv()
        slot = lax.rem(t, RING)

        def add(part):
            for k in range(4):
                r.held[slot, part, k] = (
                    r.held[slot, part, k].astype(f32) + r.core_in[slot, part, k].astype(f32)
                ).astype(low)

        add(1 - side)

        @pl.when(t >= RING)
        def _():
            pl.semaphore_wait(r.x_free, 1)

        x_copy(t).start()
        add(side)

        @pl.when(t + RING < STEPS)
        def _():
            pl.semaphore_signal(r.core_free, inc=1, device_id=(seq ^ 1, head), device_id_type=MESH)

    def x_stage(t):
        x_copy(t).wait_recv()
        slot = lax.rem(t, RING)

        @pl.when(t >= RING)
        def _():
            for k in range(4):
                @pl.when(targets[k] != seq)
                def _():
                    z_copy(t - RING, k).wait_send()

        for k in range(4):
            total = (r.held[slot, side, k].astype(f32) + r.x_in[slot, k].astype(f32)).astype(low)

            @pl.when(targets[k] == seq)
            def _():
                r.z_in[t, level] = total

            @pl.when(targets[k] != seq)
            def _():
                r.z_out[slot, k] = total
                z_copy(t, k).start()

        @pl.when(t + RING < STEPS)
        def _():
            pl.semaphore_signal(r.x_free, inc=1, device_id=(seq ^ 2, head), device_id_type=MESH)

    def out_copy(t, kind):
        slot = lax.rem(t, 2)
        at = pl.multiple_of(lax.rem(t, 9) * WIDE, WIDE)
        if kind == "down":
            return pltpu.make_async_copy(
                r.turned.at[slot], r.down_out.at[pl.ds(at, WIDE), :], r.out_sem.at[t]
            )
        if kind == "side":
            return pltpu.make_async_copy(
                r.flat.at[slot], r.side_out.at[t - FIRST_SIDE], r.out_sem.at[t]
            )
        target = r.gate_out if kind == "gate" else r.up_out
        return pltpu.make_async_copy(
            r.flat.at[slot], target.at[:, pl.ds(at, WIDE)], r.out_sem.at[t]
        )

    KINDS = (("down", 0, 9), ("gate", 9, 18), ("up", 18, 27), ("side", 27, 32))

    def out_wait(t):
        for kind, first, end in KINDS:
            @pl.when((t >= first) & (t < end))
            def _():
                out_copy(t, kind).wait()

    def z_stage(t):
        for z in range(4):
            @pl.when(sources[z] != seq)
            def _():
                z_arrival(t, z).wait_recv()

        total = r.z_in[t, 0].astype(f32)
        for z in range(1, 4):
            total = total + r.z_in[t, z].astype(f32)

        @pl.when(t >= 2)
        def _():
            out_wait(t - 2)

        slot = lax.rem(t, 2)
        for kind, first, end in KINDS:
            @pl.when((t >= first) & (t < end))
            def _():
                if kind == "down":
                    r.turned[slot] = total.T
                else:
                    r.flat[slot] = total
                out_copy(t, kind).start()

        @pl.when(t == FIRST_SIDE + 1)
        def _():
            r.kv_own[:, :256] = total[:, 128:]

        @pl.when(t == FIRST_SIDE + 2)
        def _():
            r.kv_own[:, 256:] = total[:, :256]

    def pump(i):
        @pl.when(i < STEPS)
        def _():
            produce(i)

        @pl.when((i >= 1) & (i - 1 < STEPS))
        def _():
            core_stage(i - 1)

        @pl.when((i >= LAG_X) & (i - LAG_X < STEPS))
        def _():
            x_stage(i - LAG_X)

        @pl.when((i >= LAG_Z) & (i - LAG_Z < STEPS))
        def _():
            z_stage(i - LAG_Z)

    def y_copy(n):
        return remote(
            r.y_out, r.y_in.at[n], r.y_send.at[n], r.y_recv.at[n], seq, 1 - head
        )

    def feed_forward(grad, wd, wg, wu, gate, up, acc, sems, grad_sem, left_sem):
        def copies(j):
            slot = lax.rem(j, 2)
            at = pl.ds(pl.multiple_of(j * WIDE, WIDE), WIDE)
            pairs = (
                (r.w_down.at[at, :], wd),
                (r.w_gate.at[:, at], wg),
                (r.w_up.at[:, at], wu),
                (r.gate_act.at[:, at], gate),
                (r.up_proj.at[:, at], up),
            )
            return [
                pltpu.make_async_copy(src, dst.at[slot], sems.at[n, slot])
                for n, (src, dst) in enumerate(pairs)
            ]

        first = [pltpu.make_async_copy(r.grad_ffn, grad, grad_sem)] + [
            pltpu.make_async_copy(left, r.lefts.at[n], left_sem.at[n])
            for n, left in enumerate((r.left_ffn, r.left_mid, r.left_in))
        ]
        for copy in first:
            copy.start()
        for copy in copies(0):
            copy.start()
        for copy in first:
            copy.wait()
        acc[...] = jnp.zeros_like(acc)

        def step(i, carry):
            @pl.when(i + 1 < 9)
            def _():
                for copy in copies(i + 1):
                    copy.start()

            for copy in copies(i):
                copy.wait()
            slot = lax.rem(i, 2)
            grad_mixed = dot_nt(grad[...], wd[slot])
            v, u = gate[slot], up[slot]
            square = v * v
            curve = jnp.tanh(0.7978845608028654 * v * (1.0 + 0.044715 * square))
            gelu = 0.5 * v * (1.0 + curve)
            slope = 0.5 * (1.0 + curve) + 0.5 * v * (1.0 - curve * curve) * (
                0.7978845608028654 * (1.0 + 3.0 * 0.044715 * square)
            )
            r.tiles[slot] = (gelu * u).astype(low)
            grad_gate = (grad_mixed * u * slope).astype(low)
            grad_up = (grad_mixed * gelu).astype(low)
            r.tiles[2 + i] = grad_gate
            r.tiles[11 + i] = grad_up
            acc[...] += dot_nt(grad_gate, wg[slot])
            acc[...] += dot_nt(grad_up, wu[slot])
            pump(i)
            return carry

        lax.fori_loop(0, 9, step, 0)
        r.y_out[...] = acc[...].astype(low)
        y_copy(0).start()

    dma = pltpu.SemaphoreType.DMA
    pl.run_scoped(
        feed_forward,
        pltpu.VMEM((rows, width), low),
        pltpu.VMEM((2, WIDE, width), low),
        pltpu.VMEM((2, width, WIDE), low),
        pltpu.VMEM((2, width, WIDE), low),
        pltpu.VMEM((2, rows, WIDE), f32),
        pltpu.VMEM((2, rows, WIDE), f32),
        pltpu.VMEM((rows, width), f32),
        dma((5, 2)),
        dma(()),
        dma((3,)),
    )

    def attention(*scoped):
        b = types.SimpleNamespace(**dict(zip(ATTENTION_NAMES, scoped)))
        loads = {
            name: pltpu.make_async_copy(getattr(r, name), getattr(b, name), b.sems.at[n])
            for n, name in enumerate(ATTENTION_LOADS)
        }
        for copy in loads.values():
            copy.start()
        heads = r.queries.shape[1] // 256

        def gains_copy(n):
            to_seq, to_head = ((seq, 1 - head), (seq ^ 1, head), (seq ^ 2, head))[n]
            return remote(
                r.gains.at[n], r.gains_in.at[n], r.gains_send.at[n], r.gains_recv.at[n],
                to_seq, to_head,
            )

        def gains_level(z):
            return remote(
                r.gains.at[3], r.gains_z.at[level], r.level_send.at[z], r.level_recv.at[level],
                z * 4 + side * 2 + core, head,
            )

        def gains_from(z):
            return remote(
                r.gains.at[3], r.gains_z.at[z], r.level_send.at[z], r.level_recv.at[z],
                z * 4 + side * 2 + core, head,
            )

        def norms():
            y_copy(0).wait_recv()
            y_copy(0).wait_send()
            for name in ("residual_mid", "attn_branch", "cotangent", "gain_rows", "head_gains"):
                loads[name].wait()
            loads["gain_start"].wait()
            gain_post, gain_pre = b.gain_rows[1:2, :], b.gain_rows[2:3, :]
            size = 128

            def chunk(c, sums):
                at = pl.ds(pl.multiple_of(c * size, size), size)
                grad_mid = r.y_out[at, :].astype(f32) + r.y_in[0, at, :].astype(f32)
                scale, normed = norm_parts(b.residual_mid[at, :])
                back, pre = norm_back(grad_mid, gain_pre, scale, normed)
                grad_residual = b.cotangent[at, :].astype(f32) + back
                b.residual_mid[at, :] = grad_residual
                scale, normed = norm_parts(b.attn_branch[at, :])
                back, post = norm_back(grad_residual, gain_post, scale, normed)
                r.y_out[at, :] = back.astype(low)
                return sums[0] + post, sums[1] + pre

            zero = jnp.zeros((1, width), f32)
            post, pre = lax.fori_loop(0, rows // size, chunk, (zero, zero))
            r.gains[0] = b.gain_start[...]
            r.gains[0, 1:2, :] = post
            r.gains[0, 2:3, :] = pre

        def through_out():
            for name in ("w_out", "attended", "lse"):
                loads[name].wait()
            b.grad_attended[...] = dot_nt(r.y_out[...], b.w_out[...]).astype(low)
            for h in range(heads):
                at = slice(256 * h, 256 * h + 256)
                delta = jnp.sum(
                    b.grad_attended[:, at].astype(f32) * b.attended[:, at], axis=1, keepdims=True
                )
                b.delta[h : h + 1, :] = jnp.broadcast_to(delta, (rows, 128)).T[:1]
            turned = r.y_out[...].astype(f32).T.astype(low)
            for half in range(2):
                for x in range(2):
                    for f in range(2):
                        source = 144 * ((2 * half + f) * 2 + x)
                        to = 144 * (half * 4 + x * 2 + f)
                        r.lefts[0, to : to + 144, :] = turned[source : source + 144]
            r.tiles[5] = b.attended[:, :WIDE].astype(low)
            r.tiles[6, :, :128] = b.attended[:, WIDE:].astype(low)
            r.tiles[6, :, 128:] = jnp.zeros((rows, WIDE - 128), low)

        def attend(block):
            if block == 0:
                for name in ("queries", "keys", "values", "segment_row", "segment_column"):
                    loads[name].wait()
                b.grad_queries[...] = jnp.zeros_like(b.grad_queries)
            size = 256

            def chunk(c, carry):
                local = pl.multiple_of(c * size, size)
                at = pl.ds(pl.multiple_of(block * rows + c * size, size), size)
                keys, values = b.keys[at, :], b.values[at, :]
                seen = b.segment_column[at, :] == b.segment_row[...]
                if block == 2:
                    key_at = lax.broadcasted_iota(jnp.int32, (size, rows), 0) + local
                    query_at = lax.broadcasted_iota(jnp.int32, (size, rows), 1)
                    seen = seen & (key_at <= query_at)
                grad_keys = jnp.zeros((size, 256), f32)
                grad_values = jnp.zeros((size, 256), f32)
                for h in range(heads):
                    head_at = slice(256 * h, 256 * h + 256)
                    q, grad_out = b.queries[:, head_at], b.grad_attended[:, head_at]
                    probs = jnp.where(
                        seen, jnp.exp(dot_nt(keys, q) - b.lse[h : h + 1, :]), 0.0
                    )
                    grad_probs = dot_nt(values, grad_out)
                    grad_scores = (probs * (grad_probs - b.delta[h : h + 1, :])).astype(low)
                    grad_keys += jnp.dot(grad_scores, q, preferred_element_type=f32)
                    grad_values += jnp.dot(
                        probs.astype(low), grad_out, preferred_element_type=f32
                    )
                    b.grad_queries[:, head_at] += dot_tn(grad_scores, keys)
                to = pl.ds(local, size)
                if block == 2:
                    b.grad_own[0, to, :] = grad_keys
                    b.grad_own[1, to, :] = grad_values
                else:
                    r.halo_out[block, 0, to, :] = grad_keys.astype(low)
                    r.halo_out[block, 1, to, :] = grad_values.astype(low)
                return carry

            lax.fori_loop(0, rows // size, chunk, 0)
            if block < 2:
                @pl.when(seq >= 2 - block)
                def _():
                    halo_copy(block).start()

        def halo_copy(block):
            return remote(
                r.halo_out.at[block], r.halo_in.at[block],
                r.halo_send.at[block], r.halo_recv.at[block], seq - (2 - block), head,
            )

        def query_side():
            for name in ("query_proj", "cosine", "sine", "w_query"):
                loads[name].wait()
            total = jnp.zeros((1, 256), f32)
            for h in range(heads):
                at = slice(256 * h, 256 * h + 256)
                grad = rotate_back(
                    b.grad_queries[:, at] * QUERY_SCALE, b.cosine[...], b.sine[...]
                )
                scale, normed = norm_parts(b.query_proj[:, at])
                back, gain = norm_back(grad, b.head_gains[0:1, :], scale, normed)
                total += gain
                back = back.astype(low)
                if h == 0:
                    r.tiles[2, :, :256] = back
                else:
                    r.tiles[2, :, 256:] = back[:, :128]
                    r.tiles[3, :, :128] = back[:, 128:]
                part = dot_nt(back, b.w_query[:, at])
                if h == 0:
                    b.attn_branch[...] = part
                else:
                    b.attn_branch[...] += part
            r.gains[0, 4:5, :256] = total

        def key_side():
            for name in ("key_proj", "w_key", "w_value", "inputs"):
                loads[name].wait()
            for block in range(2):
                @pl.when(seq + (2 - block) <= last_seq)
                def _():
                    halo_copy(block).wait_recv()
                    for n in range(2):
                        b.grad_own[n] += r.halo_in[block, n].astype(f32)

            grad = rotate_back(b.grad_own[0], b.cosine[...], b.sine[...])
            scale, normed = norm_parts(b.key_proj[...])
            back, gain = norm_back(grad, b.head_gains[1:2, :], scale, normed)
            r.gains[0, 4:5, 256:512] = gain
            grad_key, grad_value = back.astype(low), b.grad_own[1].astype(low)
            r.tiles[3, :, 128:] = grad_key
            r.tiles[4, :, :256] = grad_value
            r.tiles[4, :, 256:] = jnp.zeros((rows, 128), low)
            b.attn_branch[...] += dot_nt(grad_key, b.w_key[...])
            b.attn_branch[...] += dot_nt(grad_value, b.w_value[...])
            size = 128

            def chunk(c, total):
                at = pl.ds(pl.multiple_of(c * size, size), size)
                part = b.attn_branch[at, :]
                scale, normed = norm_parts(b.inputs[at, :].astype(f32))
                r.y_out[at, :] = part.astype(low)
                return total + jnp.sum(part * normed, axis=0, keepdims=True)

            zero = jnp.zeros((1, width), f32)
            r.gains[0, 0:1, :] = lax.fori_loop(0, rows // size, chunk, zero)
            y_copy(1).start()
            gains_copy(0).start()

        def gains_stage(n):
            gains_copy(n).wait_recv()
            own, other = r.gains[n], r.gains_in[n]
            if n == 0:
                row = lax.broadcasted_iota(jnp.int32, own.shape, 0)
                other = jnp.where((row == 0) | (row == 4), other, 0.0)
            r.gains[n + 1] = own + other
            if n < 2:
                gains_copy(n + 1).start()
            else:
                for z in range(4):
                    @pl.when(level == z)
                    def _():
                        r.gains_z[z] = r.gains[3]

                    @pl.when(level != z)
                    def _():
                        gains_level(z).start()

        def gains_end():
            for z in range(4):
                @pl.when(level != z)
                def _():
                    gains_from(z).wait_recv()

            r.gains_out[...] = (r.gains_z[0] + r.gains_z[1]) + (r.gains_z[2] + r.gains_z[3])

        def finish_inputs():
            y_copy(1).wait_recv()
            size = 128

            def chunk(c, carry):
                at = pl.ds(pl.multiple_of(c * size, size), size)
                grad = r.y_out[at, :].astype(f32) + r.y_in[1, at, :].astype(f32)
                scale, normed = norm_parts(b.inputs[at, :].astype(f32))
                back, _ = norm_back(grad, b.gain_rows[0:1, :], scale, normed)
                r.inputs_out[at, :] = (b.residual_mid[at, :] + back).astype(low)
                return carry

            lax.fori_loop(0, rows // size, chunk, 0)

        def kv_copy():
            return remote(r.kv_own, r.kv_in, r.kv_send, r.kv_recv, seq, 1 - head)

        pieces = {
            14: norms,
            15: through_out,
            16: lambda: attend(0),
            17: lambda: attend(1),
            18: lambda: attend(2),
            19: query_side,
            20: key_side,
            21: lambda: gains_stage(0),
            22: lambda: gains_stage(1),
            23: lambda: gains_stage(2),
            25: gains_end,
            26: finish_inputs,
            35: lambda: kv_copy().start(),
        }

        def step(i, carry):
            for k, piece in pieces.items():
                @pl.when(i == k)
                def _():
                    piece()

            pump(i)
            return carry

        lax.fori_loop(9, STEPS + LAG_Z, step, 0)
        kv_copy().wait()
        r.kv_out[...] = r.kv_own[...] + r.kv_in[...]
        y_copy(1).wait_send()
        for n in range(3):
            gains_copy(n).wait_send()
        for z in range(4):
            @pl.when(level != z)
            def _():
                gains_level(z).wait_send()

        for block in range(2):
            @pl.when(seq >= 2 - block)
            def _():
                halo_copy(block).wait_send()

    heads_width = r.queries.shape[1]
    shapes = {
        "residual_mid": ((rows, width), f32),
        "attn_branch": ((rows, width), f32),
        "cotangent": ((rows, width), low),
        "inputs": ((rows, width), low),
        "gain_rows": ((8, width), f32),
        "head_gains": ((8, 256), f32),
        "gain_start": ((8, width), f32),
        "w_out": ((heads_width, width), low),
        "attended": ((rows, heads_width), f32),
        "lse": ((8, rows), f32),
        "queries": ((rows, heads_width), low),
        "keys": ((3 * rows, 256), low),
        "values": ((3 * rows, 256), low),
        "segment_row": ((1, rows), jnp.int32),
        "segment_column": ((3 * rows, 1), jnp.int32),
        "query_proj": ((rows, heads_width), f32),
        "key_proj": ((rows, 256), f32),
        "cosine": ((rows, 128), f32),
        "sine": ((rows, 128), f32),
        "w_query": ((width, heads_width), low),
        "w_key": ((width, 256), low),
        "w_value": ((width, 256), low),
        "grad_attended": ((rows, heads_width), low),
        "delta": ((8, rows), f32),
        "grad_queries": ((rows, heads_width), f32),
        "grad_own": ((2, rows, 256), f32),
    }
    pl.run_scoped(
        attention,
        *(pltpu.VMEM(*shapes[name]) for name in ATTENTION_NAMES[:-1]),
        dma((len(ATTENTION_LOADS),)),
    )

    def drain(i, carry):
        @pl.when(i >= STEPS - 2)
        def _():
            core_copy(i).wait_send()
            out_wait(i)

        x_copy(i).wait_send()
        for k in range(4):
            @pl.when(targets[k] != seq)
            def _():
                z_copy(i, k).wait_send()

        return carry

    lax.fori_loop(STEPS - RING, STEPS, drain, 0)


ATTENTION_LOADS = (
    "residual_mid", "attn_branch", "cotangent", "gain_rows", "head_gains", "gain_start",
    "w_out", "attended", "lse", "queries", "keys", "values", "segment_row", "segment_column",
    "query_proj", "cosine", "sine", "w_query", "key_proj", "w_key", "w_value", "inputs",
)
ATTENTION_NAMES = ATTENTION_LOADS + (
    "grad_attended", "delta", "grad_queries", "grad_own", "sems",
)


def block_order(rows):
    return rows.reshape(2, 2, 2, 2 * BLOCK, -1).transpose(0, 2, 1, 3, 4).reshape(rows.shape[0], -1)


def backward(operands):
    low, f32 = jnp.bfloat16, jnp.float32
    dma = pltpu.SemaphoreType.DMA
    rows, width = operands["grad_ffn"].shape
    hidden = operands["w_gate"].shape[1]
    anywhere = pl.BlockSpec(memory_space=pl.ANY)
    vmem = pl.BlockSpec(memory_space=pltpu.VMEM)
    outs = {
        "down_out": (jax.ShapeDtypeStruct((hidden, BLOCK), f32), anywhere),
        "gate_out": (jax.ShapeDtypeStruct((BLOCK, hidden), f32), anywhere),
        "up_out": (jax.ShapeDtypeStruct((BLOCK, hidden), f32), anywhere),
        "side_out": (jax.ShapeDtypeStruct((STEPS - FIRST_SIDE, BLOCK, WIDE), f32), anywhere),
        "kv_out": (jax.ShapeDtypeStruct((BLOCK, 512), f32), vmem),
        "gains_out": (jax.ShapeDtypeStruct((8, width), f32), vmem),
        "inputs_out": (jax.ShapeDtypeStruct((rows, width), low), vmem),
    }
    scratch = {
        "held": pltpu.VMEM((RING, 2, 4, BLOCK, WIDE), low),
        "sent": pltpu.VMEM((2, 2, 4, BLOCK, WIDE), low),
        "core_in": pltpu.VMEM((RING, 2, 4, BLOCK, WIDE), low),
        "x_in": pltpu.VMEM((RING, 4, BLOCK, WIDE), low),
        "z_out": pltpu.VMEM((RING, 4, BLOCK, WIDE), low),
        "z_in": pltpu.VMEM((STEPS, 4, BLOCK, WIDE), low),
        "tiles": pltpu.VMEM((20, rows, WIDE), low),
        "lefts": pltpu.VMEM((3, width, rows), low),
        "y_out": pltpu.VMEM((rows, width), low),
        "y_in": pltpu.VMEM((2, rows, width), low),
        "halo_out": pltpu.VMEM((2, 2, rows, 256), low),
        "halo_in": pltpu.VMEM((2, 2, rows, 256), low),
        "gains": pltpu.VMEM((4, 8, width), f32),
        "gains_in": pltpu.VMEM((3, 8, width), f32),
        "gains_z": pltpu.VMEM((4, 8, width), f32),
        "kv_own": pltpu.VMEM((BLOCK, 512), f32),
        "kv_in": pltpu.VMEM((BLOCK, 512), f32),
        "turned": pltpu.VMEM((2, WIDE, BLOCK), f32),
        "flat": pltpu.VMEM((2, BLOCK, WIDE), f32),
        "core_send": dma((STEPS,)),
        "core_recv": dma((STEPS,)),
        "x_send": dma((STEPS,)),
        "x_recv": dma((STEPS,)),
        "z_send": dma((STEPS, 4)),
        "z_recv": dma((STEPS, 4)),
        "out_sem": dma((STEPS,)),
        "y_send": dma((2,)),
        "y_recv": dma((2,)),
        "halo_send": dma((2,)),
        "halo_recv": dma((2,)),
        "gains_send": dma((3,)),
        "gains_recv": dma((3,)),
        "level_send": dma((4,)),
        "level_recv": dma((4,)),
        "kv_send": dma(()),
        "kv_recv": dma(()),
        "core_free": pltpu.SemaphoreType.REGULAR,
        "x_free": pltpu.SemaphoreType.REGULAR,
    }
    names = (*operands, *outs, *scratch)
    results = pl.pallas_call(
        functools.partial(backward_kernel, names),
        out_shape=[shape for shape, _ in outs.values()],
        in_specs=[anywhere] * len(operands),
        out_specs=[spec for _, spec in outs.values()],
        scratch_shapes=list(scratch.values()),
        compiler_params=pltpu.CompilerParams(
            collective_id=1, has_side_effects=True, vmem_limit_bytes=62 << 20
        ),
        name="backward",
    )(*operands.values())
    return dict(zip(outs, results))


def scatter_rows(grad):
    return lax.psum_scatter(grad, "seq", scatter_dimension=0, tiled=True).astype(jnp.float32)


def per_device(
    inputs,
    segment_ids,
    w_query,
    w_key,
    w_value,
    w_out,
    w_gate,
    w_up,
    w_down,
    gain_in,
    gain_query,
    gain_key,
    gain_post_attn,
    gain_pre_ffn,
    gain_post_ffn,
    cotangent,
):
    rows = inputs.shape[0]
    head_dim = w_key.shape[1]
    local_heads = w_query.shape[1] // head_dim
    place = lax.axis_index("seq")
    local_index = jnp.arange(rows, dtype=jnp.int32)
    ids_parts = [
        jnp.where(place >= distance, from_behind(segment_ids, "seq", distance), -1)
        for distance in (2, 1)
    ]
    window_ids = jnp.concatenate(ids_parts + [segment_ids], axis=0)
    window_index = jnp.arange(3 * rows, dtype=jnp.int32) - 2 * rows
    same = segment_ids[:, None] == window_ids[None, :]
    visible = same & (window_index[None, :] <= local_index[:, None])
    positions = jnp.sum(visible.astype(jnp.int32), axis=1) - 1
    cosine, sine = rope_angles(positions, head_dim)
    inputs_f = inputs.astype(jnp.float32)
    hidden_in = rms_scale(inputs_f, gain_in).astype(jnp.bfloat16)
    query_proj = jnp.dot(hidden_in, w_query, preferred_element_type=jnp.float32)
    key_proj = jnp.dot(hidden_in, w_key, preferred_element_type=jnp.float32)
    value_proj = jnp.dot(hidden_in, w_value, preferred_element_type=jnp.float32)

    def query_side(projection, gain):
        return prepare(
            projection.reshape(rows, local_heads, head_dim), gain, cosine, sine, QUERY_SCALE
        )

    def key_side(projection, gain):
        return prepare(projection[:, None, :], gain, cosine, sine, 1.0)[:, 0, :]

    queries = query_side(query_proj, gain_query).astype(jnp.bfloat16)
    own_keys = key_side(key_proj, gain_key).astype(jnp.bfloat16)
    own_values = value_proj.astype(jnp.bfloat16)
    key_parts = []
    value_parts = []
    for distance in (2, 1):
        moved_keys, moved_values = from_behind((own_keys, own_values), "seq", distance)
        key_parts.append(moved_keys)
        value_parts.append(moved_values)
    all_keys = jnp.concatenate(key_parts + [own_keys], axis=0)
    all_values = jnp.concatenate(value_parts + [own_values], axis=0)
    def raw_scores():
        return jnp.einsum("ihd,jd->hij", queries, all_keys, preferred_element_type=jnp.float32)

    scores = jnp.where(visible[None], raw_scores(), -1e30)
    row_max = jnp.max(scores, axis=-1, keepdims=True)
    expo = jnp.exp(scores - row_max)
    total = jnp.sum(expo, axis=-1, keepdims=True)
    attn_probs = expo / total
    log_total = row_max + jnp.log(total)
    attended = jnp.einsum(
        "hij,jd->ihd",
        attn_probs.astype(jnp.bfloat16),
        all_values,
        preferred_element_type=jnp.float32,
    )
    attended_f = attended.reshape(rows, local_heads * head_dim)
    attended = attended_f.astype(jnp.bfloat16)
    attn_branch = over_head(jnp.dot(attended, w_out, preferred_element_type=jnp.float32))
    residual_mid = inputs_f + rms_scale(attn_branch, gain_post_attn)
    hidden_mid = rms_scale(residual_mid, gain_pre_ffn).astype(jnp.bfloat16)
    gate_act = jnp.dot(hidden_mid, w_gate, preferred_element_type=jnp.float32)
    up_proj = jnp.dot(hidden_mid, w_up, preferred_element_type=jnp.float32)
    mixed_low = gated(gate_act, up_proj).astype(jnp.bfloat16)
    ffn_branch = over_head(jnp.dot(mixed_low, w_down, preferred_element_type=jnp.float32))
    output_f = residual_mid + rms_scale(ffn_branch, gain_post_ffn)
    grad_output = cotangent.astype(jnp.float32)
    unused_post, post_back = jax.vjp(rms_scale, ffn_branch, gain_post_ffn)
    grad_ffn, grad_g_post_ffn = post_back(grad_output)
    grad_ffn_low = grad_ffn.astype(jnp.bfloat16)
    count = lax.axis_size("seq")
    if count == 16:
        zero_row = jnp.zeros((1, inputs.shape[1]), jnp.float32)
        made = backward(
            {
                "grad_ffn": grad_ffn_low,
                "left_ffn": block_order(grad_ffn_low.T),
                "left_mid": block_order(hidden_mid.T),
                "left_in": block_order(hidden_in.T),
                "gate_act": gate_act,
                "up_proj": up_proj,
                "w_down": w_down,
                "w_gate": w_gate,
                "w_up": w_up,
                "residual_mid": residual_mid,
                "attn_branch": attn_branch,
                "cotangent": cotangent,
                "gain_rows": jnp.concatenate(
                    [gain_in[None], gain_post_attn[None], gain_pre_ffn[None]] + [zero_row] * 5
                ),
                "head_gains": jnp.stack([gain_query, gain_key] + [gain_key] * 6),
                "gain_start": jnp.concatenate(
                    [zero_row] * 3 + [grad_g_post_ffn[None]] + [zero_row] * 4
                ),
                "w_out": w_out,
                "attended": attended_f,
                "lse": jnp.pad(log_total[:, :, 0], ((0, 8 - local_heads), (0, 0))),
                "queries": queries.reshape(rows, -1),
                "keys": all_keys,
                "values": all_values,
                "segment_row": segment_ids[None, :],
                "segment_column": window_ids[:, None],
                "query_proj": query_proj,
                "cosine": cosine,
                "sine": sine,
                "w_query": w_query,
                "key_proj": key_proj,
                "w_key": w_key,
                "w_value": w_value,
                "inputs": inputs,
            }
        )
        side = made["side_out"]
        wide_query = w_query.shape[1]
        summed_query = jnp.concatenate([side[0], side[1][:, : wide_query - WIDE]], axis=1)
        summed_out = jnp.concatenate([side[3], side[4][:, : wide_query - WIDE]], axis=1).T
        place_gains = lax.dynamic_slice_in_dim(made["gains_out"], place * BLOCK, BLOCK, 1)
        own = head_dim // count
        gain_q = lax.dynamic_slice_in_dim(made["gains_out"], place * own, own, 1)[4]
        gain_k = lax.dynamic_slice_in_dim(made["gains_out"], head_dim + place * own, own, 1)[4]
        return (
            output_f.astype(jnp.bfloat16),
            made["inputs_out"],
            summed_query,
            made["kv_out"][:, :head_dim],
            made["kv_out"][:, head_dim:],
            summed_out,
            made["gate_out"],
            made["up_out"],
            made["down_out"],
            place_gains[0],
            gain_q,
            gain_k,
            place_gains[1],
            place_gains[2],
            place_gains[3],
        )
    grad_w_down = jnp.dot(grad_ffn_low.T, mixed_low, preferred_element_type=jnp.float32)
    summed_down = scatter_rows(grad_w_down.astype(jnp.bfloat16))
    grad_mixed = jnp.dot(grad_ffn_low, w_down.T, preferred_element_type=jnp.float32)
    unused_gate, gate_back = jax.vjp(gated, gate_act, up_proj)
    grad_gate, grad_up = gate_back(grad_mixed)
    grad_gate_low = grad_gate.astype(jnp.bfloat16)
    grad_up_low = grad_up.astype(jnp.bfloat16)
    grad_w_gate = jnp.dot(hidden_mid.T, grad_gate_low, preferred_element_type=jnp.float32)
    grad_w_up = jnp.dot(hidden_mid.T, grad_up_low, preferred_element_type=jnp.float32)
    summed_gate = scatter_rows(grad_w_gate.astype(jnp.bfloat16))
    summed_up = scatter_rows(grad_w_up.astype(jnp.bfloat16))
    grad_hidden_part = jnp.dot(
        grad_gate_low, w_gate.T, preferred_element_type=jnp.float32
    ) + jnp.dot(grad_up_low, w_up.T, preferred_element_type=jnp.float32)
    grad_hidden_mid = over_head(grad_hidden_part)
    unused_pre, pre_back = jax.vjp(rms_scale, residual_mid, gain_pre_ffn)
    grad_res_part, grad_g_pre_ffn = pre_back(grad_hidden_mid)
    grad_residual = grad_output + grad_res_part
    unused_attn, attn_post_back = jax.vjp(rms_scale, attn_branch, gain_post_attn)
    grad_attn, grad_g_post_attn = attn_post_back(grad_residual)
    grad_attn_low = grad_attn.astype(jnp.bfloat16)
    grad_w_out = jnp.dot(grad_attn_low.T, attended, preferred_element_type=jnp.float32)
    grad_attended = jnp.dot(grad_attn_low, w_out.T, preferred_element_type=jnp.float32).astype(
        jnp.bfloat16
    )
    grad_attended = grad_attended.reshape(rows, local_heads, head_dim)
    probs_again = jnp.where(visible[None], jnp.exp(raw_scores() - log_total), 0.0)
    grad_probs = jnp.einsum(
        "ihd,jd->hij", grad_attended, all_values, preferred_element_type=jnp.float32
    )
    grad_scores = (
        probs_again * (grad_probs - jnp.sum(probs_again * grad_probs, axis=-1, keepdims=True))
    ).astype(jnp.bfloat16)
    grad_queries = jnp.einsum(
        "hij,jd->ihd", grad_scores, all_keys, preferred_element_type=jnp.float32
    )
    grad_keys_all = jnp.einsum(
        "hij,ihd->jd", grad_scores, queries, preferred_element_type=jnp.float32
    )
    grad_values_all = jnp.einsum(
        "hij,ihd->jd",
        probs_again.astype(jnp.bfloat16),
        grad_attended,
        preferred_element_type=jnp.float32,
    )
    grad_keys = grad_keys_all[2 * rows :]
    grad_values = grad_values_all[2 * rows :]
    for distance in (2, 1):
        piece_begin = (2 - distance) * rows
        returned_keys, returned_values = (
            from_behind(
                grad_keys_all[piece_begin : piece_begin + rows].astype(jnp.bfloat16),
                "seq",
                -distance,
            ).astype(jnp.float32),
            from_behind(
                grad_values_all[piece_begin : piece_begin + rows].astype(jnp.bfloat16),
                "seq",
                -distance,
            ).astype(jnp.float32),
        )
        grad_keys = grad_keys + returned_keys
        grad_values = grad_values + returned_values
    unused_query, query_back = jax.vjp(query_side, query_proj, gain_query)
    grad_query_proj, grad_g_query_part = query_back(grad_queries)
    grad_query_low = grad_query_proj.astype(jnp.bfloat16)
    grad_w_query = jnp.dot(hidden_in.T, grad_query_low, preferred_element_type=jnp.float32)
    grad_hidden_query = jnp.dot(grad_query_low, w_query.T, preferred_element_type=jnp.float32)
    keys_summed, values_summed, hidden_summed, grad_g_query = (
        over_head(grad_keys),
        over_head(grad_values),
        over_head(grad_hidden_query),
        over_head(grad_g_query_part),
    )
    unused_key, key_back = jax.vjp(key_side, key_proj, gain_key)
    grad_key_proj, grad_g_key = key_back(keys_summed)
    grad_key_low = grad_key_proj.astype(jnp.bfloat16)
    grad_value_low = values_summed.astype(jnp.bfloat16)
    grad_w_key = jnp.dot(hidden_in.T, grad_key_low, preferred_element_type=jnp.float32)
    grad_w_value = jnp.dot(hidden_in.T, grad_value_low, preferred_element_type=jnp.float32)
    grad_hidden_in = (
        hidden_summed
        + jnp.dot(grad_key_low, w_key.T, preferred_element_type=jnp.float32)
        + jnp.dot(grad_value_low, w_value.T, preferred_element_type=jnp.float32)
    )
    unused_in, in_back = jax.vjp(rms_scale, inputs_f, gain_in)
    grad_in_part, grad_g_in = in_back(grad_hidden_in)
    grad_inputs = (grad_residual + grad_in_part).astype(jnp.bfloat16)
    gain_columns = jnp.stack(
        [grad_g_in, grad_g_post_attn, grad_g_pre_ffn, grad_g_post_ffn], axis=1
    )
    side = jnp.concatenate(
        [grad_g_query.reshape(count, -1), grad_g_key.reshape(count, -1)], axis=1
    )
    side_rows = jnp.repeat(side, inputs.shape[1] // count, axis=0)
    extra = jnp.concatenate([gain_columns, side_rows], axis=1)
    extra = jnp.pad(extra, ((0, 0), (0, -extra.shape[1] % 128)))
    widths = [g.shape[1] for g in (grad_w_query, grad_w_out, grad_w_key, grad_w_value)]
    attn_sum = scatter_rows(
        jnp.concatenate(
            [
                g.astype(jnp.bfloat16)
                for g in (grad_w_query, grad_w_out, grad_w_key, grad_w_value, extra)
            ],
            axis=1,
        )
    )
    edges = [sum(widths[:i]) for i in range(5)]
    summed_query, summed_out, summed_key, summed_value = (
        attn_sum[:, edges[i] : edges[i + 1]] for i in range(4)
    )
    gain_sum = attn_sum[:, edges[4] :]
    summed_g_in, summed_g_post_attn, summed_g_pre_ffn, summed_g_post_ffn = (
        gain_sum[:, i] for i in range(4)
    )
    own = head_dim // count
    summed_g_query = gain_sum[0, 4 : 4 + own]
    summed_g_key = gain_sum[0, 4 + own : 4 + 2 * own]
    summed_out = summed_out.T
    summed_down = summed_down.T
    return (
        output_f.astype(jnp.bfloat16),
        grad_inputs,
        summed_query,
        summed_key,
        summed_value,
        summed_out,
        summed_gate,
        summed_up,
        summed_down,
        summed_g_in,
        summed_g_query,
        summed_g_key,
        summed_g_post_attn,
        summed_g_pre_ffn,
        summed_g_post_ffn,
    )


def solution(mesh):
    placed = (
        P("seq", None),
        P("seq"),
        P(None, "head"),
        P(),
        P(),
        P("head", None),
        P(None, "head"),
        P(None, "head"),
        P("head", None),
        P(),
        P(),
        P(),
        P(),
        P(),
        P(),
        P("seq", None),
    )
    return jax.shard_map(
        per_device,
        mesh=mesh,
        in_specs=placed,
        out_specs=(
            P("seq", None),
            P("seq", None),
            P("seq", "head"),
            P("seq", None),
            P("seq", None),
            P("head", "seq"),
            P("seq", "head"),
            P("seq", "head"),
            P("head", "seq"),
            P("seq"),
            P("seq"),
            P("seq"),
            P("seq"),
            P("seq"),
            P("seq"),
        ),
        check_vma=False,
    )
```

```python
import functools
import math
import types

import jax
import jax.numpy as jnp
from jax import lax
from jax.experimental import pallas as pl
from jax.experimental.pallas import tpu as pltpu
from jax.sharding import PartitionSpec as P

MESH = pl.DeviceIdType.MESH
WIDE = 384
BLOCK = 72

EPS = 1e-06
QUERY_SCALE = 0.0625


def from_behind(block, axis, distance):
    devices = range(lax.axis_size(axis))
    route = [(i - distance, i) for i in devices if i - distance in devices]
    return lax.ppermute(block, axis, route)


def rms_scale(values, gain):
    return values * lax.rsqrt(jnp.mean(values * values, axis=-1, keepdims=True) + EPS) * gain


def rope_angles(positions, width):
    half_width = width // 2
    frequency = jnp.exp(
        jnp.arange(half_width, dtype=jnp.float32) * (-2.0 * math.log(1000000.0) / width)
    )
    angles = positions.astype(jnp.float32)[:, None] * frequency[None, :]
    return (jnp.cos(angles), jnp.sin(angles))


def rotate(values, cosine, sine):
    half_width = values.shape[-1] // 2
    first_half = values[..., :half_width]
    second_half = values[..., half_width:]
    cos_rows = cosine[:, None, :]
    sin_rows = sine[:, None, :]
    return jnp.concatenate(
        [
            first_half * cos_rows - second_half * sin_rows,
            second_half * cos_rows + first_half * sin_rows,
        ],
        axis=-1,
    )


def prepare(values, gain, cosine, sine, factor):
    return rotate(rms_scale(values, gain), cosine, sine) * factor


def gelu_tanh(values):
    return (
        0.5
        * values
        * (1.0 + jnp.tanh(0.7978845608028654 * (values + 0.044715 * values * values * values)))
    )


def gated(gate_act, up_proj):
    return gelu_tanh(gate_act) * up_proj


def over_head(part):
    low = part.astype(jnp.bfloat16)
    other = lax.ppermute(low, "head", [(0, 1), (1, 0)])
    return low.astype(jnp.float32) + other.astype(jnp.float32)


def place_of():
    seq = lax.axis_index("seq")
    return seq, lax.axis_index("head"), seq % 2, seq // 2 % 2, seq // 4


def dot_nt(left, right):
    return lax.dot_general(left, right, (((1,), (1,)), ((), ())), preferred_element_type=jnp.float32)


def dot_tn(left, right):
    return lax.dot_general(left, right, (((0,), (0,)), ((), ())), preferred_element_type=jnp.float32)


def rotate_back(grad, cosine, sine):
    half = grad.shape[-1] // 2
    first, second = grad[:, :half], grad[:, half:]
    return jnp.concatenate(
        [first * cosine + second * sine, second * cosine - first * sine], axis=-1
    )


def norm_parts(values):
    scale = lax.rsqrt(jnp.mean(values * values, axis=-1, keepdims=True) + EPS)
    return scale, values * scale


def norm_back(grad, gain, scale, normed):
    inner = grad * gain
    back = scale * (inner - normed * jnp.mean(inner * normed, axis=-1, keepdims=True))
    return back, jnp.sum(grad * normed, axis=0, keepdims=True)


CHUNKS = 2


def turn(values, cosine, sine):
    half = values.shape[-1] // 2
    first, second = values[:, :half], values[:, half:]
    return jnp.concatenate(
        [first * cosine - second * sine, second * cosine + first * sine], axis=-1
    )


def to_blocks(target, values, columns):
    turned = values.astype(jnp.float32).T.astype(jnp.bfloat16)
    for half in range(2):
        for x in range(2):
            for f in range(2):
                source = 144 * ((2 * half + f) * 2 + x)
                to = 144 * (half * 4 + x * 2 + f)
                target[to : to + 144, columns] = turned[source : source + 144]


def forward_kernel(names, *refs):
    r = types.SimpleNamespace(**dict(zip(names, refs)))
    seq, head, core, side, level = place_of()
    last_seq = lax.axis_size("seq") - 1
    f32, low = jnp.float32, jnp.bfloat16
    rows, width = r.inputs.shape
    heads = r.w_query.shape[1] // 256
    hidden = r.w_gate.shape[1]
    size = rows // CHUNKS
    even = core == 0

    barrier = pltpu.get_barrier_semaphore()

    def greet(to_seq, to_head):
        pl.semaphore_signal(barrier, inc=1, device_id=(to_seq, to_head), device_id_type=MESH)

    def load(n, src, dst):
        copy = pltpu.make_async_copy(src, dst, r.load_sem.at[n])
        copy.start()
        return copy

    in_copy = load(0, r.inputs, r.x)
    gain_copy = load(1, r.gain_rows, r.gains)
    kv_copies = (load(2, r.w_key, r.wk), load(3, r.w_value, r.wv))
    more_gains = (load(4, r.head_gains, r.head_gain), load(5, r.frequency, r.freq))
    ids_copy = load(6, r.segment_row, r.ids.at[2])
    query_copy = load(7, r.w_query, r.wq)
    out_copy = load(8, r.w_out, r.wo.at[head])
    ffn_copies = (
        load(9, r.w_gate, r.wg), load(10, r.w_up, r.wu), load(11, r.w_down, r.wd),
    )
    cot_copy = load(12, r.cotangent, r.cot)

    greet(seq ^ 1, head)
    greet(seq, 1 - head)
    expected = jnp.int32(2)
    for distance in (1, 2):
        @pl.when(seq >= distance)
        def _():
            greet(seq - distance, head)

        @pl.when(seq + distance <= last_seq)
        def _():
            greet(seq + distance, head)

        expected = (
            expected
            + (seq >= distance).astype(jnp.int32)
            + (seq + distance <= last_seq).astype(jnp.int32)
        )
    pl.semaphore_wait(barrier, expected)

    def remote(src, dst, send, recv, to_seq, to_head):
        return pltpu.make_async_remote_copy(
            src_ref=src,
            dst_ref=dst,
            send_sem=send,
            recv_sem=recv,
            device_id=(to_seq, to_head),
            device_id_type=MESH,
        )

    share = r.w_out.shape[0] // 2

    def out_share(which):
        return pl.ds(pl.multiple_of(which * share, share), share)

    def w_out_y():
        mine = out_share(core)
        return remote(
            r.w_out.at[mine, :], r.wo.at[head, mine, :], r.wo_send.at[0], r.wo_recv.at[0],
            seq, 1 - head,
        )

    def w_out_core():
        mine = out_share(core)
        part = r.wo.at[1 - head, mine, :]
        return remote(part, part, r.wo_send.at[1], r.wo_recv.at[1], seq ^ 1, head)

    def ids_send(distance):
        return remote(
            r.ids.at[2], r.ids.at[2 - distance], r.ids_send.at[distance - 1],
            r.ids_recv.at[distance - 1], seq + distance, head,
        )

    def halo(n, distance, hand_on=False):
        kind = r.window.at[n]
        source = kind.at[pl.ds((1 if hand_on else 2) * rows, rows), :]
        target = kind.at[pl.ds((2 - distance) * rows, rows), :]
        place = 2 if hand_on else distance - 1
        return remote(
            source, target, r.halo_send.at[n, place], r.halo_recv.at[n, distance - 1],
            seq + (1 if hand_on else distance), head,
        )

    ids_copy.wait()
    for distance in (1, 2):
        @pl.when(seq + distance <= last_seq)
        def _():
            ids_send(distance).start()

    w_out_y().start()

    in_copy.wait()
    gain_copy.wait()

    def norm_in(c, carry):
        at = pl.ds(pl.multiple_of(c * 128, 128), 128)
        _, normed = norm_parts(r.x[at, :].astype(f32))
        r.normed_in[at, :] = (normed * r.gains[0:1, :]).astype(low)
        return carry

    lax.fori_loop(0, rows // 128, norm_in, 0)
    for copy in kv_copies:
        copy.wait()
    r.key_raw[...] = jnp.dot(r.normed_in[...], r.wk[...], preferred_element_type=f32)
    r.window[1, 2 * rows :, :] = jnp.dot(
        r.normed_in[...], r.wv[...], preferred_element_type=f32
    ).astype(low)

    def value_halo(distance):
        return halo(1, distance)

    @pl.when(seq + 1 <= last_seq)
    def _():
        value_halo(1).start()

    @pl.when(even & (seq + 2 <= last_seq))
    def _():
        value_halo(2).start()

    for distance in (1, 2):
        @pl.when(seq >= distance)
        def _():
            remote(
                r.ids.at[2], r.ids.at[2 - distance], r.ids_send.at[distance - 1],
                r.ids_recv.at[distance - 1], seq ^ 1, head,
            ).wait_recv()

        @pl.when(seq < distance)
        def _():
            r.ids[2 - distance] = jnp.full((8, rows), -1.0, f32)

    ids_row = jnp.concatenate([r.ids[b][:1] for b in range(3)], axis=1)
    r.ids_flat[...] = jnp.broadcast_to(ids_row, (8, 3 * rows))
    ids_column = jnp.broadcast_to(r.ids[2][:1], (128, rows)).T
    r.ids_turned[...] = ids_column
    for copy in more_gains:
        copy.wait()

    def angles(c, carry):
        at = pl.ds(pl.multiple_of(c * 128, 128), 128)
        here = lax.broadcasted_iota(jnp.int32, (128, 3 * rows), 0) + (2 * rows + c * 128)
        there = lax.broadcasted_iota(jnp.int32, (128, 3 * rows), 1)
        same = (r.ids_turned[at, :1] == r.ids_flat[:1, :]) & (there < here)
        position = jnp.sum(same.astype(f32), axis=1, keepdims=True)
        angle = position * r.freq[:1, :]
        r.cosine[at, :] = jnp.cos(angle)
        r.sine[at, :] = jnp.sin(angle)
        return carry

    lax.fori_loop(0, rows // 128, angles, 0)
    _, normed = norm_parts(r.key_raw[...])
    r.window[0, 2 * rows :, :] = turn(
        normed * r.head_gain[1:2, :], r.cosine[...], r.sine[...]
    ).astype(low)

    @pl.when(seq + 1 <= last_seq)
    def _():
        halo(0, 1).start()

    @pl.when(even & (seq + 2 <= last_seq))
    def _():
        halo(0, 2).start()

    query_copy.wait()
    r.query_raw[...] = jnp.dot(r.normed_in[...], r.wq[...], preferred_element_type=f32)
    for h in range(heads):
        at = slice(256 * h, 256 * h + 256)
        _, normed = norm_parts(r.query_raw[:, at])
        r.q[:, at] = (
            turn(normed * r.head_gain[0:1, :], r.cosine[...], r.sine[...]) * QUERY_SCALE
        ).astype(low)

    def store(n, src, dst):
        copy = pltpu.make_async_copy(src, dst, r.store_sem.at[n])
        copy.start()
        return copy

    to_blocks(r.turned, r.normed_in[...], slice(0, rows))
    stores = [
        store(1, r.key_raw, r.key_proj),
        store(2, r.query_raw, r.query_proj),
        store(3, r.q, r.queries),
        store(4, r.cosine, r.cosine_out),
        store(5, r.sine, r.sine_out),
        store(6, r.ids_flat, r.ids_out),
    ]
    turned_store = store(0, r.turned, r.left_in)

    out_copy.wait()
    w_out_y().wait()
    w_out_core().start()

    def arrival(n, distance):
        return halo(n, distance)

    for n in (1, 0):
        @pl.when(seq >= 1)
        def _():
            arrival(n, 1).wait_recv()

        @pl.when(even & (seq >= 2))
        def _():
            halo(n, 2, True).start()

    for n in (1, 0):
        @pl.when(seq >= 2)
        def _():
            arrival(n, 2).wait_recv()

    for distance in (1, 2):
        @pl.when(seq < distance)
        def _():
            for n in range(2):
                r.window[n, (2 - distance) * rows : (3 - distance) * rows, :] = jnp.zeros(
                    (rows, 256), low
                )

    def head_exchange(c):
        part = r.heads_all.at[head, pl.ds(c * size, size), :]
        return remote(part, part, r.y_send.at[c], r.y_recv.at[c], seq, 1 - head)

    def branch_exchange(c):
        at = pl.ds(c * size, size)
        return remote(
            r.y_out.at[at, :], r.y_in.at[at, :], r.y_send.at[CHUNKS + c], r.y_recv.at[CHUNKS + c],
            seq, 1 - head,
        )

    def attend(c):
        first = c * size
        span = 2 * rows + size
        at = slice(first, first + size)
        key_at = slice(first, first + span)
        here = lax.broadcasted_iota(jnp.int32, (size, span), 0) + 2 * rows
        there = lax.broadcasted_iota(jnp.int32, (size, span), 1)
        seen = (r.ids_turned[at, :1] == r.ids_flat[:1, key_at]) & (there <= here)
        for h in range(heads):
            head_at = slice(256 * h, 256 * h + 256)
            scores = jnp.where(seen, dot_nt(r.q[at, head_at], r.window[0, key_at, :]), -1e30)
            top = jnp.max(scores, axis=1, keepdims=True)
            expo = jnp.exp(scores - top)
            total = jnp.sum(expo, axis=1, keepdims=True)
            probs = (expo / total).astype(low)
            out = jnp.dot(probs, r.window[1, key_at, :], preferred_element_type=f32)
            r.heads_f[at, head_at] = out
            r.heads_all[head, at, head_at] = out.astype(low)
            r.lse_rows[h : h + 1, at] = jnp.broadcast_to(top + jnp.log(total), (size, 128)).T[:1]
        head_exchange(c).start()

    for c in range(CHUNKS):
        attend(c)
    stores += [
        store(7, r.heads_f, r.attended),
        store(8, r.lse_rows, r.lse),
        store(9, r.window.at[0], r.keys),
        store(10, r.window.at[1], r.values),
    ]
    w_out_core().wait()
    turned_store.wait()
    for copy in ffn_copies:
        copy.wait()

    def tile_stores(c, j):
        slot = lax.rem(j, 2)
        at = pl.ds(pl.multiple_of(j * WIDE, WIDE), WIDE)
        here = pl.ds(c * size, size)
        return (
            pltpu.make_async_copy(
                r.gate_tile.at[slot], r.gate_act.at[here, at], r.tile_sem.at[0, slot]
            ),
            pltpu.make_async_copy(
                r.up_tile.at[slot], r.up_proj.at[here, at], r.tile_sem.at[1, slot]
            ),
        )

    steps = hidden // WIDE

    def feed(c):
        at = pl.ds(c * size, size)
        head_exchange(c).wait_recv()
        branch = jnp.dot(r.heads_all[0, at, :], r.wo[0], preferred_element_type=f32) + jnp.dot(
            r.heads_all[1, at, :], r.wo[1], preferred_element_type=f32
        )
        r.branch[at, :] = branch
        _, normed = norm_parts(branch)
        middle = r.x[at, :].astype(f32) + normed * r.gains[1:2, :]
        r.middle[at, :] = middle
        _, normed = norm_parts(middle)
        r.normed_mid[at, :] = (normed * r.gains[2:3, :]).astype(low)

        def tile(j, carry):
            slot = lax.rem(j, 2)
            columns = pl.ds(pl.multiple_of(j * WIDE, WIDE), WIDE)
            left = r.normed_mid[at, :]
            gate = jnp.dot(left, r.wg[:, columns], preferred_element_type=f32)
            up = jnp.dot(left, r.wu[:, columns], preferred_element_type=f32)

            @pl.when(j >= 2)
            def _():
                for copy in tile_stores(c, j - 2):
                    copy.wait()

            r.gate_tile[slot] = gate
            r.up_tile[slot] = up
            for copy in tile_stores(c, j):
                copy.start()
            curve = jnp.tanh(0.7978845608028654 * gate * (1.0 + 0.044715 * gate * gate))
            mixed = (0.5 * gate * (1.0 + curve) * up).astype(low)
            part = jnp.dot(mixed, r.wd[columns, :], preferred_element_type=f32)

            @pl.when(j == 0)
            def _():
                r.acc[...] = part

            @pl.when(j > 0)
            def _():
                r.acc[...] += part

            return carry

        lax.fori_loop(0, steps, tile, 0)
        for j in (steps - 2, steps - 1):
            for copy in tile_stores(c, jnp.int32(j)):
                copy.wait()
        r.y_out[at, :] = r.acc[...].astype(low)
        branch_exchange(c).start()

    for c in range(CHUNKS):
        feed(c)
    stores += [store(11, r.branch, r.attn_branch), store(12, r.middle, r.residual_mid)]
    to_blocks(r.turned, r.normed_mid[...], slice(0, rows))
    mid_store = store(0, r.turned, r.left_mid)
    cot_copy.wait()
    gain_sum = jnp.zeros((1, width), f32)
    for c in range(CHUNKS):
        branch_exchange(c).wait_recv()

        def end(n, total):
            at = pl.ds(pl.multiple_of(c * size + n * 128, 128), 128)
            branch = r.y_out[at, :].astype(f32) + r.y_in[at, :].astype(f32)
            scale, normed = norm_parts(branch)
            r.result[at, :] = (r.middle[at, :] + normed * r.gains[3:4, :]).astype(low)
            back, gain = norm_back(r.cot[at, :].astype(f32), r.gains[3:4, :], scale, normed)
            r.cot[at, :] = back.astype(low)
            return total + gain

        gain_sum = lax.fori_loop(0, size // 128, end, gain_sum)
        if c == 0:
            mid_store.wait()
        at = slice(c * size, (c + 1) * size)
        to_blocks(r.turned, r.cot[at, :], at)
    stores += [
        store(0, r.turned, r.left_ffn),
        store(13, r.cot, r.grad_ffn),
        store(14, r.result, r.output),
    ]
    r.gain_tile[...] = jnp.zeros_like(r.gain_tile)
    r.gain_tile[3:4, :] = gain_sum
    stores.append(store(15, r.gain_tile, r.gain_start))
    for copy in stores:
        copy.wait()
    for distance in (1, 2):
        @pl.when(seq + distance <= last_seq)
        def _():
            ids_send(distance).wait_send()

    for n in range(2):
        @pl.when(seq + 1 <= last_seq)
        def _():
            halo(n, 1).wait_send()

        @pl.when(even & (seq + 2 <= last_seq))
        def _():
            halo(n, 2).wait_send()

        @pl.when(even & (seq >= 2))
        def _():
            halo(n, 2, True).wait_send()

    for c in range(CHUNKS):
        head_exchange(c).wait_send()
        branch_exchange(c).wait_send()


def forward(operands):
    low, f32 = jnp.bfloat16, jnp.float32
    dma = pltpu.SemaphoreType.DMA
    rows, width = operands["inputs"].shape
    hidden = operands["w_gate"].shape[1]
    wide = operands["w_query"].shape[1]
    shape = jax.ShapeDtypeStruct
    anywhere = pl.BlockSpec(memory_space=pl.ANY)
    outs = dict(
        left_in=shape((width, rows), low),
        left_mid=shape((width, rows), low),
        left_ffn=shape((width, rows), low),
        key_proj=shape((rows, 256), f32),
        query_proj=shape((rows, wide), f32),
        queries=shape((rows, wide), low),
        cosine_out=shape((rows, 128), f32),
        sine_out=shape((rows, 128), f32),
        ids_out=shape((8, 3 * rows), f32),
        attended=shape((rows, wide), f32),
        lse=shape((8, rows), f32),
        keys=shape((3 * rows, 256), low),
        values=shape((3 * rows, 256), low),
        attn_branch=shape((rows, width), f32),
        residual_mid=shape((rows, width), f32),
        gate_act=shape((rows, hidden), f32),
        up_proj=shape((rows, hidden), f32),
        grad_ffn=shape((rows, width), low),
        output=shape((rows, width), low),
        gain_start=shape((8, width), f32),
    )
    size = rows // CHUNKS
    vmem = pltpu.VMEM
    scratch = dict(
        x=vmem((rows, width), low),
        gains=vmem((8, width), f32),
        wk=vmem((width, 256), low),
        wv=vmem((width, 256), low),
        head_gain=vmem((8, 256), f32),
        freq=vmem((8, 128), f32),
        ids=vmem((3, 8, rows), f32),
        ids_flat=vmem((8, 3 * rows), f32),
        ids_turned=vmem((rows, 128), f32),
        wq=vmem((width, wide), low),
        wo=vmem((2, wide, width), low),
        wg=vmem((width, hidden), low),
        wu=vmem((width, hidden), low),
        wd=vmem((hidden, width), low),
        cot=vmem((rows, width), low),
        normed_in=vmem((rows, width), low),
        normed_mid=vmem((rows, width), low),
        key_raw=vmem((rows, 256), f32),
        query_raw=vmem((rows, wide), f32),
        q=vmem((rows, wide), low),
        window=vmem((2, 3 * rows, 256), low),
        cosine=vmem((rows, 128), f32),
        sine=vmem((rows, 128), f32),
        turned=vmem((width, rows), low),
        heads_f=vmem((rows, wide), f32),
        heads_all=vmem((2, rows, wide), low),
        lse_rows=vmem((8, rows), f32),
        branch=vmem((rows, width), f32),
        middle=vmem((rows, width), f32),
        gate_tile=vmem((2, size, WIDE), f32),
        up_tile=vmem((2, size, WIDE), f32),
        acc=vmem((size, width), f32),
        y_out=vmem((rows, width), low),
        y_in=vmem((rows, width), low),
        result=vmem((rows, width), low),
        gain_tile=vmem((8, width), f32),
        load_sem=dma((13,)),
        store_sem=dma((16,)),
        tile_sem=dma((2, 2)),
        wo_send=dma((2,)),
        wo_recv=dma((2,)),
        ids_send=dma((2,)),
        ids_recv=dma((2,)),
        halo_send=dma((2, 3)),
        halo_recv=dma((2, 2)),
        y_send=dma((2 * CHUNKS,)),
        y_recv=dma((2 * CHUNKS,)),
    )
    names = (*operands, *outs, *scratch)
    results = pl.pallas_call(
        functools.partial(forward_kernel, names),
        out_shape=list(outs.values()),
        in_specs=[anywhere] * len(operands),
        out_specs=[anywhere] * len(outs),
        scratch_shapes=list(scratch.values()),
        compiler_params=pltpu.CompilerParams(
            collective_id=2, has_side_effects=True, vmem_limit_bytes=62 << 20
        ),
        name="forward",
    )(*operands.values())
    return dict(zip(outs, results))


DOWN, GATE, UP, SIDE = range(4)
RING = 6
STEPS = 32
FIRST_SIDE = 27
LAG_X = 3
LAG_Z = 5


def backward_kernel(names, *refs):
    r = types.SimpleNamespace(**dict(zip(names, refs)))
    seq, head, core, side, level = place_of()
    last_seq = lax.axis_size("seq") - 1
    f32, low = jnp.float32, jnp.bfloat16
    rows = r.grad_ffn.shape[0]
    width = r.grad_ffn.shape[1]

    barrier = pltpu.get_barrier_semaphore()

    def greet(to_seq, to_head):
        pl.semaphore_signal(barrier, inc=1, device_id=(to_seq, to_head), device_id_type=MESH)

    greet(seq ^ 1, head)
    greet(seq ^ 2, head)
    greet(seq, 1 - head)
    for z in range(4):
        for c in range(2):
            other = z * 4 + side * 2 + c

            @pl.when(other != seq)
            def _():
                greet(other, head)

    expected = jnp.int32(10)
    for distance in (1, 2):
        @pl.when(seq >= distance)
        def _():
            greet(seq - distance, head)

        @pl.when(seq + distance <= last_seq)
        def _():
            greet(seq + distance, head)

        expected = (
            expected
            + (seq >= distance).astype(jnp.int32)
            + (seq + distance <= last_seq).astype(jnp.int32)
        )
    pl.semaphore_wait(barrier, expected)

    def remote(src, dst, send, recv, to_seq, to_head):
        return pltpu.make_async_remote_copy(
            src_ref=src,
            dst_ref=dst,
            send_sem=send,
            recv_sem=recv,
            device_id=(to_seq, to_head),
            device_id_type=MESH,
        )

    targets = [((2 * core + k // 2) * 4 + side * 2 + k % 2) for k in range(4)]
    sources = [z * 4 + side * 2 + level // 2 for z in range(4)]

    def core_copy(t):
        slot = lax.rem(t, RING)
        return remote(
            r.sent.at[lax.rem(t, 2)], r.core_in.at[slot], r.core_send.at[t], r.core_recv.at[t],
            seq ^ 1, head,
        )

    def x_copy(t):
        slot = lax.rem(t, RING)
        return remote(
            r.held.at[slot, 1 - side], r.x_in.at[slot], r.x_send.at[t], r.x_recv.at[t],
            seq ^ 2, head,
        )

    def z_copy(t, k):
        return remote(
            r.z_out.at[lax.rem(t, RING), k], r.z_in.at[t, level],
            r.z_send.at[t, k], r.z_recv.at[t, level], targets[k], head,
        )

    def z_arrival(t, z):
        return remote(
            r.z_out.at[0, 0], r.z_in.at[t, z], r.z_send.at[t, 0], r.z_recv.at[t, z],
            sources[z], head,
        )

    def produce(t):
        @pl.when(t >= 2)
        def _():
            core_copy(t - 2).wait_send()

        @pl.when(t >= RING)
        def _():
            x_copy(t - RING).wait_send()

        which = jnp.where(t < 9, 0, jnp.where(t < FIRST_SIDE, 1, jnp.where(t < 30, 2, 0)))
        place = jnp.where(
            t < 9, lax.rem(t, 2), jnp.where(t < FIRST_SIDE, t - 7, t - (FIRST_SIDE - 2))
        )
        tile = r.tiles[place]

        def half(start):
            left = r.lefts[which, pl.ds(pl.multiple_of(start, 576), 576), :]
            return jnp.dot(left, tile, preferred_element_type=f32)

        away = half((1 - core) * 576)
        for k in range(8):
            r.sent[lax.rem(t, 2), k // 4, k % 4] = away[k * BLOCK : (k + 1) * BLOCK].astype(low)

        @pl.when(t >= RING)
        def _():
            pl.semaphore_wait(r.core_free, 1)

        core_copy(t).start()
        home = half(core * 576)
        for k in range(8):
            r.held[lax.rem(t, RING), k // 4, k % 4] = home[k * BLOCK : (k + 1) * BLOCK].astype(low)

    def core_stage(t):
        core_copy(t).wait_recv()
        slot = lax.rem(t, RING)

        def add(part):
            for k in range(4):
                r.held[slot, part, k] = (
                    r.held[slot, part, k].astype(f32) + r.core_in[slot, part, k].astype(f32)
                ).astype(low)

        add(1 - side)

        @pl.when(t >= RING)
        def _():
            pl.semaphore_wait(r.x_free, 1)

        x_copy(t).start()
        add(side)

        @pl.when(t + RING < STEPS)
        def _():
            pl.semaphore_signal(r.core_free, inc=1, device_id=(seq ^ 1, head), device_id_type=MESH)

    def x_stage(t):
        x_copy(t).wait_recv()
        slot = lax.rem(t, RING)

        @pl.when(t >= RING)
        def _():
            for k in range(4):
                @pl.when(targets[k] != seq)
                def _():
                    z_copy(t - RING, k).wait_send()

        for k in range(4):
            total = (r.held[slot, side, k].astype(f32) + r.x_in[slot, k].astype(f32)).astype(low)

            @pl.when(targets[k] == seq)
            def _():
                r.z_in[t, level] = total

            @pl.when(targets[k] != seq)
            def _():
                r.z_out[slot, k] = total
                z_copy(t, k).start()

        @pl.when(t + RING < STEPS)
        def _():
            pl.semaphore_signal(r.x_free, inc=1, device_id=(seq ^ 2, head), device_id_type=MESH)

    def out_copy(t, kind):
        slot = lax.rem(t, 2)
        at = pl.multiple_of(lax.rem(t, 9) * WIDE, WIDE)
        if kind == DOWN:
            return pltpu.make_async_copy(
                r.turned.at[slot], r.down_out.at[pl.ds(at, WIDE), :], r.out_sem.at[t]
            )
        if kind == SIDE:
            return pltpu.make_async_copy(
                r.flat.at[slot], r.side_out.at[t - FIRST_SIDE], r.out_sem.at[t]
            )
        target = r.gate_out if kind == GATE else r.up_out
        return pltpu.make_async_copy(
            r.flat.at[slot], target.at[:, pl.ds(at, WIDE)], r.out_sem.at[t]
        )

    KINDS = ((DOWN, 0, 9), (GATE, 9, 18), (UP, 18, 27), (SIDE, 27, 32))

    def out_wait(t):
        for kind, first, end in KINDS:
            @pl.when((t >= first) & (t < end))
            def _():
                out_copy(t, kind).wait()

    def z_stage(t):
        for z in range(4):
            @pl.when(sources[z] != seq)
            def _():
                z_arrival(t, z).wait_recv()

        total = r.z_in[t, 0].astype(f32)
        for z in range(1, 4):
            total = total + r.z_in[t, z].astype(f32)

        @pl.when(t >= 2)
        def _():
            out_wait(t - 2)

        slot = lax.rem(t, 2)
        for kind, first, end in KINDS:
            @pl.when((t >= first) & (t < end))
            def _():
                if kind == DOWN:
                    r.turned[slot] = total.T
                else:
                    r.flat[slot] = total
                out_copy(t, kind).start()

        @pl.when(t == FIRST_SIDE + 1)
        def _():
            r.kv_own[:, :256] = total[:, 128:]

        @pl.when(t == FIRST_SIDE + 2)
        def _():
            r.kv_own[:, 256:] = total[:, :256]

    def pump(i):
        @pl.when(i < STEPS)
        def _():
            produce(i)

        @pl.when((i >= 1) & (i - 1 < STEPS))
        def _():
            core_stage(i - 1)

        @pl.when((i >= LAG_X) & (i - LAG_X < STEPS))
        def _():
            x_stage(i - LAG_X)

        @pl.when((i >= LAG_Z) & (i - LAG_Z < STEPS))
        def _():
            z_stage(i - LAG_Z)

    def y_copy(n):
        return remote(
            r.y_out, r.y_in.at[n], r.y_send.at[n], r.y_recv.at[n], seq, 1 - head
        )

    def feed_forward(grad, wd, wg, wu, gate, up, acc, sems, grad_sem, left_sem):
        def copies(j):
            slot = lax.rem(j, 2)
            at = pl.ds(pl.multiple_of(j * WIDE, WIDE), WIDE)
            pairs = (
                (r.w_down.at[at, :], wd),
                (r.w_gate.at[:, at], wg),
                (r.w_up.at[:, at], wu),
                (r.gate_act.at[:, at], gate),
                (r.up_proj.at[:, at], up),
            )
            return [
                pltpu.make_async_copy(src, dst.at[slot], sems.at[n, slot])
                for n, (src, dst) in enumerate(pairs)
            ]

        first = [pltpu.make_async_copy(r.grad_ffn, grad, grad_sem)] + [
            pltpu.make_async_copy(left, r.lefts.at[n], left_sem.at[n])
            for n, left in enumerate((r.left_ffn, r.left_mid, r.left_in))
        ]
        for copy in first:
            copy.start()
        for copy in copies(0):
            copy.start()
        for copy in first:
            copy.wait()
        acc[...] = jnp.zeros_like(acc)

        def step(i, carry):
            @pl.when(i + 1 < 9)
            def _():
                for copy in copies(i + 1):
                    copy.start()

            for copy in copies(i):
                copy.wait()
            slot = lax.rem(i, 2)
            grad_mixed = dot_nt(grad[...], wd[slot])
            v, u = gate[slot], up[slot]
            square = v * v
            curve = jnp.tanh(0.7978845608028654 * v * (1.0 + 0.044715 * square))
            gelu = 0.5 * v * (1.0 + curve)
            slope = 0.5 * (1.0 + curve) + 0.5 * v * (1.0 - curve * curve) * (
                0.7978845608028654 * (1.0 + 3.0 * 0.044715 * square)
            )
            r.tiles[slot] = (gelu * u).astype(low)
            grad_gate = (grad_mixed * u * slope).astype(low)
            grad_up = (grad_mixed * gelu).astype(low)
            r.tiles[2 + i] = grad_gate
            r.tiles[11 + i] = grad_up
            acc[...] += dot_nt(grad_gate, wg[slot])
            acc[...] += dot_nt(grad_up, wu[slot])
            pump(i)
            return carry

        lax.fori_loop(0, 9, step, 0)
        r.y_out[...] = acc[...].astype(low)
        y_copy(0).start()

    dma = pltpu.SemaphoreType.DMA
    pl.run_scoped(
        feed_forward,
        pltpu.VMEM((rows, width), low),
        pltpu.VMEM((2, WIDE, width), low),
        pltpu.VMEM((2, width, WIDE), low),
        pltpu.VMEM((2, width, WIDE), low),
        pltpu.VMEM((2, rows, WIDE), f32),
        pltpu.VMEM((2, rows, WIDE), f32),
        pltpu.VMEM((rows, width), f32),
        dma((5, 2)),
        dma(()),
        dma((3,)),
    )

    def attention(loaded, names, *scoped):
        b = types.SimpleNamespace(**dict(zip(names, scoped)))
        made = {
            name: pltpu.make_async_copy(getattr(r, name), getattr(b, name), b.sems.at[n])
            for n, name in enumerate(loaded)
        }
        for copy in made.values():
            copy.start()
        loads = types.SimpleNamespace(**made)
        heads = r.queries.shape[1] // 256

        def gains_copy(n):
            to_seq, to_head = ((seq, 1 - head), (seq ^ 1, head), (seq ^ 2, head))[n]
            return remote(
                r.gains.at[n], r.gains_in.at[n], r.gains_send.at[n], r.gains_recv.at[n],
                to_seq, to_head,
            )

        def gains_level(z):
            return remote(
                r.gains.at[3], r.gains_z.at[level], r.level_send.at[z], r.level_recv.at[level],
                z * 4 + side * 2 + core, head,
            )

        def gains_from(z):
            return remote(
                r.gains.at[3], r.gains_z.at[z], r.level_send.at[z], r.level_recv.at[z],
                z * 4 + side * 2 + core, head,
            )

        def norms():
            y_copy(0).wait_recv()
            y_copy(0).wait_send()
            for copy in (loads.residual_mid, loads.attn_branch, loads.cotangent, loads.gain_rows, loads.head_gains):
                copy.wait()
            loads.gain_start.wait()
            gain_post, gain_pre = b.gain_rows[1:2, :], b.gain_rows[2:3, :]
            size = 128

            def chunk(c, sums):
                at = pl.ds(pl.multiple_of(c * size, size), size)
                grad_mid = r.y_out[at, :].astype(f32) + r.y_in[0, at, :].astype(f32)
                scale, normed = norm_parts(b.residual_mid[at, :])
                back, pre = norm_back(grad_mid, gain_pre, scale, normed)
                grad_residual = b.cotangent[at, :].astype(f32) + back
                b.residual_mid[at, :] = grad_residual
                scale, normed = norm_parts(b.attn_branch[at, :])
                back, post = norm_back(grad_residual, gain_post, scale, normed)
                r.y_out[at, :] = back.astype(low)
                return sums[0] + post, sums[1] + pre

            zero = jnp.zeros((1, width), f32)
            post, pre = lax.fori_loop(0, rows // size, chunk, (zero, zero))
            r.gains[0] = b.gain_start[...]
            r.gains[0, 1:2, :] = post
            r.gains[0, 2:3, :] = pre

        def through_out():
            for copy in (loads.w_out, loads.attended, loads.lse):
                copy.wait()
            b.grad_attended[...] = dot_nt(r.y_out[...], b.w_out[...]).astype(low)
            for h in range(heads):
                at = slice(256 * h, 256 * h + 256)
                delta = jnp.sum(
                    b.grad_attended[:, at].astype(f32) * b.attended[:, at], axis=1, keepdims=True
                )
                b.delta[h : h + 1, :] = jnp.broadcast_to(delta, (rows, 128)).T[:1]
            to_blocks(r.lefts.at[0], r.y_out[...], slice(0, rows))
            r.tiles[5] = b.attended[:, :WIDE].astype(low)
            r.tiles[6, :, :128] = b.attended[:, WIDE:].astype(low)
            r.tiles[6, :, 128:] = jnp.zeros((rows, WIDE - 128), low)

        def attend(block):
            if block == 0:
                for copy in (loads.queries, loads.keys, loads.values, loads.ids_out):
                    copy.wait()
                b.grad_queries[...] = jnp.zeros_like(b.grad_queries)
                b.ids_turned[...] = jnp.broadcast_to(b.ids_out[:1], (128, 3 * rows)).T
            size = 256

            def chunk(c, carry):
                local = pl.multiple_of(c * size, size)
                at = pl.ds(pl.multiple_of(block * rows + c * size, size), size)
                keys, values = b.keys[at, :], b.values[at, :]
                seen = b.ids_turned[at, :1] == b.ids_out[:1, 2 * rows :]
                if block == 2:
                    key_at = lax.broadcasted_iota(jnp.int32, (size, rows), 0) + local
                    query_at = lax.broadcasted_iota(jnp.int32, (size, rows), 1)
                    seen = seen & (key_at <= query_at)
                grad_keys = jnp.zeros((size, 256), f32)
                grad_values = jnp.zeros((size, 256), f32)
                for h in range(heads):
                    head_at = slice(256 * h, 256 * h + 256)
                    q, grad_out = b.queries[:, head_at], b.grad_attended[:, head_at]
                    probs = jnp.where(
                        seen, jnp.exp(dot_nt(keys, q) - b.lse[h : h + 1, :]), 0.0
                    )
                    grad_probs = dot_nt(values, grad_out)
                    grad_scores = (probs * (grad_probs - b.delta[h : h + 1, :])).astype(low)
                    grad_keys += jnp.dot(grad_scores, q, preferred_element_type=f32)
                    grad_values += jnp.dot(
                        probs.astype(low), grad_out, preferred_element_type=f32
                    )
                    b.grad_queries[:, head_at] += dot_tn(grad_scores, keys)
                to = pl.ds(local, size)
                if block == 2:
                    b.grad_own[0, to, :] = grad_keys
                    b.grad_own[1, to, :] = grad_values
                else:
                    r.halo_out[block, 0, to, :] = grad_keys.astype(low)
                    r.halo_out[block, 1, to, :] = grad_values.astype(low)
                return carry

            lax.fori_loop(0, rows // size, chunk, 0)
            if block < 2:
                @pl.when(seq >= 2 - block)
                def _():
                    halo_copy(block).start()

        def halo_copy(block):
            return remote(
                r.halo_out.at[block], r.halo_in.at[block],
                r.halo_send.at[block], r.halo_recv.at[block], seq - (2 - block), head,
            )

        def query_side():
            for copy in (loads.query_proj, loads.cosine_out, loads.sine_out, loads.w_query):
                copy.wait()
            total = jnp.zeros((1, 256), f32)
            for h in range(heads):
                at = slice(256 * h, 256 * h + 256)
                grad = rotate_back(
                    b.grad_queries[:, at] * QUERY_SCALE, b.cosine_out[...], b.sine_out[...]
                )
                scale, normed = norm_parts(b.query_proj[:, at])
                back, gain = norm_back(grad, b.head_gains[0:1, :], scale, normed)
                total += gain
                back = back.astype(low)
                if h == 0:
                    r.tiles[2, :, :256] = back
                else:
                    r.tiles[2, :, 256:] = back[:, :128]
                    r.tiles[3, :, :128] = back[:, 128:]
                part = dot_nt(back, b.w_query[:, at])
                if h == 0:
                    b.attn_branch[...] = part
                else:
                    b.attn_branch[...] += part
            r.gains[0, 4:5, :256] = total

        def key_side():
            for copy in (loads.key_proj, loads.w_key, loads.w_value, loads.inputs):
                copy.wait()
            for block in range(2):
                @pl.when(seq + (2 - block) <= last_seq)
                def _():
                    halo_copy(block).wait_recv()
                    for n in range(2):
                        b.grad_own[n] += r.halo_in[block, n].astype(f32)

            grad = rotate_back(b.grad_own[0], b.cosine_out[...], b.sine_out[...])
            scale, normed = norm_parts(b.key_proj[...])
            back, gain = norm_back(grad, b.head_gains[1:2, :], scale, normed)
            r.gains[0, 4:5, 256:512] = gain
            grad_key, grad_value = back.astype(low), b.grad_own[1].astype(low)
            r.tiles[3, :, 128:] = grad_key
            r.tiles[4, :, :256] = grad_value
            r.tiles[4, :, 256:] = jnp.zeros((rows, 128), low)
            b.attn_branch[...] += dot_nt(grad_key, b.w_key[...])
            b.attn_branch[...] += dot_nt(grad_value, b.w_value[...])
            size = 128

            def chunk(c, total):
                at = pl.ds(pl.multiple_of(c * size, size), size)
                part = b.attn_branch[at, :]
                scale, normed = norm_parts(b.inputs[at, :].astype(f32))
                r.y_out[at, :] = part.astype(low)
                return total + jnp.sum(part * normed, axis=0, keepdims=True)

            zero = jnp.zeros((1, width), f32)
            r.gains[0, 0:1, :] = lax.fori_loop(0, rows // size, chunk, zero)
            y_copy(1).start()
            gains_copy(0).start()

        def gains_stage(n):
            gains_copy(n).wait_recv()
            own, other = r.gains[n], r.gains_in[n]
            if n == 0:
                row = lax.broadcasted_iota(jnp.int32, own.shape, 0)
                other = jnp.where((row == 0) | (row == 4), other, 0.0)
            r.gains[n + 1] = own + other
            if n < 2:
                gains_copy(n + 1).start()
            else:
                for z in range(4):
                    @pl.when(level == z)
                    def _():
                        r.gains_z[z] = r.gains[3]

                    @pl.when(level != z)
                    def _():
                        gains_level(z).start()

        def gains_end():
            for z in range(4):
                @pl.when(level != z)
                def _():
                    gains_from(z).wait_recv()

            r.gains_out[...] = (r.gains_z[0] + r.gains_z[1]) + (r.gains_z[2] + r.gains_z[3])

        def finish_inputs():
            y_copy(1).wait_recv()
            size = 128

            def chunk(c, carry):
                at = pl.ds(pl.multiple_of(c * size, size), size)
                grad = r.y_out[at, :].astype(f32) + r.y_in[1, at, :].astype(f32)
                scale, normed = norm_parts(b.inputs[at, :].astype(f32))
                back, _ = norm_back(grad, b.gain_rows[0:1, :], scale, normed)
                r.inputs_out[at, :] = (b.residual_mid[at, :] + back).astype(low)
                return carry

            lax.fori_loop(0, rows // size, chunk, 0)

        def kv_copy():
            return remote(r.kv_own, r.kv_in, r.kv_send, r.kv_recv, seq, 1 - head)

        pieces = {
            14: norms,
            15: through_out,
            16: lambda: attend(0),
            17: lambda: attend(1),
            18: lambda: attend(2),
            19: query_side,
            20: key_side,
            21: lambda: gains_stage(0),
            22: lambda: gains_stage(1),
            23: lambda: gains_stage(2),
            25: gains_end,
            26: finish_inputs,
            35: lambda: kv_copy().start(),
        }

        def step(i, carry):
            for k, piece in pieces.items():
                @pl.when(i == k)
                def _():
                    piece()

            pump(i)
            return carry

        lax.fori_loop(9, STEPS + LAG_Z, step, 0)
        kv_copy().wait()
        r.kv_out[...] = r.kv_own[...] + r.kv_in[...]
        y_copy(1).wait_send()
        for n in range(3):
            gains_copy(n).wait_send()
        for z in range(4):
            @pl.when(level != z)
            def _():
                gains_level(z).wait_send()

        for block in range(2):
            @pl.when(seq >= 2 - block)
            def _():
                halo_copy(block).wait_send()

    heads_width = r.queries.shape[1]
    def shape(size, kind):
        return pltpu.VMEM(size, kind)

    loaded = dict(
        residual_mid=shape((rows, width), f32),
        attn_branch=shape((rows, width), f32),
        cotangent=shape((rows, width), low),
        inputs=shape((rows, width), low),
        gain_rows=shape((8, width), f32),
        head_gains=shape((8, 256), f32),
        gain_start=shape((8, width), f32),
        w_out=shape((heads_width, width), low),
        attended=shape((rows, heads_width), f32),
        lse=shape((8, rows), f32),
        queries=shape((rows, heads_width), low),
        keys=shape((3 * rows, 256), low),
        values=shape((3 * rows, 256), low),
        ids_out=shape((8, 3 * rows), f32),
        query_proj=shape((rows, heads_width), f32),
        key_proj=shape((rows, 256), f32),
        cosine_out=shape((rows, 128), f32),
        sine_out=shape((rows, 128), f32),
        w_query=shape((width, heads_width), low),
        w_key=shape((width, 256), low),
        w_value=shape((width, 256), low),
    )
    scoped = dict(
        loaded,
        grad_attended=shape((rows, heads_width), low),
        delta=shape((8, rows), f32),
        grad_queries=shape((rows, heads_width), f32),
        grad_own=shape((2, rows, 256), f32),
        ids_turned=shape((3 * rows, 128), f32),
        sems=dma((len(loaded),)),
    )
    pl.run_scoped(functools.partial(attention, tuple(loaded), tuple(scoped)), *scoped.values())

    def drain(i, carry):
        @pl.when(i >= STEPS - 2)
        def _():
            core_copy(i).wait_send()
            out_wait(i)

        x_copy(i).wait_send()
        for k in range(4):
            @pl.when(targets[k] != seq)
            def _():
                z_copy(i, k).wait_send()

        return carry

    lax.fori_loop(STEPS - RING, STEPS, drain, 0)


def backward(operands):
    low, f32 = jnp.bfloat16, jnp.float32
    dma = pltpu.SemaphoreType.DMA
    rows, width = operands["grad_ffn"].shape
    hidden = operands["w_gate"].shape[1]
    anywhere = pl.BlockSpec(memory_space=pl.ANY)
    vmem = pl.BlockSpec(memory_space=pltpu.VMEM)
    outs = dict(
        down_out=(jax.ShapeDtypeStruct((hidden, BLOCK), f32), anywhere),
        gate_out=(jax.ShapeDtypeStruct((BLOCK, hidden), f32), anywhere),
        up_out=(jax.ShapeDtypeStruct((BLOCK, hidden), f32), anywhere),
        side_out=(jax.ShapeDtypeStruct((STEPS - FIRST_SIDE, BLOCK, WIDE), f32), anywhere),
        kv_out=(jax.ShapeDtypeStruct((BLOCK, 512), f32), vmem),
        gains_out=(jax.ShapeDtypeStruct((8, width), f32), vmem),
        inputs_out=(jax.ShapeDtypeStruct((rows, width), low), vmem),
    )
    scratch = dict(
        held=pltpu.VMEM((RING, 2, 4, BLOCK, WIDE), low),
        sent=pltpu.VMEM((2, 2, 4, BLOCK, WIDE), low),
        core_in=pltpu.VMEM((RING, 2, 4, BLOCK, WIDE), low),
        x_in=pltpu.VMEM((RING, 4, BLOCK, WIDE), low),
        z_out=pltpu.VMEM((RING, 4, BLOCK, WIDE), low),
        z_in=pltpu.VMEM((STEPS, 4, BLOCK, WIDE), low),
        tiles=pltpu.VMEM((20, rows, WIDE), low),
        lefts=pltpu.VMEM((3, width, rows), low),
        y_out=pltpu.VMEM((rows, width), low),
        y_in=pltpu.VMEM((2, rows, width), low),
        halo_out=pltpu.VMEM((2, 2, rows, 256), low),
        halo_in=pltpu.VMEM((2, 2, rows, 256), low),
        gains=pltpu.VMEM((4, 8, width), f32),
        gains_in=pltpu.VMEM((3, 8, width), f32),
        gains_z=pltpu.VMEM((4, 8, width), f32),
        kv_own=pltpu.VMEM((BLOCK, 512), f32),
        kv_in=pltpu.VMEM((BLOCK, 512), f32),
        turned=pltpu.VMEM((2, WIDE, BLOCK), f32),
        flat=pltpu.VMEM((2, BLOCK, WIDE), f32),
        core_send=dma((STEPS,)),
        core_recv=dma((STEPS,)),
        x_send=dma((STEPS,)),
        x_recv=dma((STEPS,)),
        z_send=dma((STEPS, 4)),
        z_recv=dma((STEPS, 4)),
        out_sem=dma((STEPS,)),
        y_send=dma((2,)),
        y_recv=dma((2,)),
        halo_send=dma((2,)),
        halo_recv=dma((2,)),
        gains_send=dma((3,)),
        gains_recv=dma((3,)),
        level_send=dma((4,)),
        level_recv=dma((4,)),
        kv_send=dma(()),
        kv_recv=dma(()),
        core_free=pltpu.SemaphoreType.REGULAR,
        x_free=pltpu.SemaphoreType.REGULAR,
    )
    names = (*operands, *outs, *scratch)
    results = pl.pallas_call(
        functools.partial(backward_kernel, names),
        out_shape=[shape for shape, _ in outs.values()],
        in_specs=[anywhere] * len(operands),
        out_specs=[spec for _, spec in outs.values()],
        scratch_shapes=list(scratch.values()),
        compiler_params=pltpu.CompilerParams(
            collective_id=1, has_side_effects=True, vmem_limit_bytes=62 << 20
        ),
        name="backward",
    )(*operands.values())
    return dict(zip(outs, results))


def fast_device(
    inputs,
    segment_ids,
    w_query,
    w_key,
    w_value,
    w_out,
    w_gate,
    w_up,
    w_down,
    gain_in,
    gain_query,
    gain_key,
    gain_post_attn,
    gain_pre_ffn,
    gain_post_ffn,
    cotangent,
):
    rows, width = inputs.shape
    head_dim = w_key.shape[1]
    wide = w_query.shape[1]
    place, count = lax.axis_index("seq"), lax.axis_size("seq")
    f32 = jnp.float32
    gain_rows = jnp.concatenate(
        [g[None] for g in (gain_in, gain_post_attn, gain_pre_ffn, gain_post_ffn)]
        + [jnp.zeros((4, width), f32)]
    )
    head_gains = jnp.concatenate(
        [gain_query[None], gain_key[None], jnp.zeros((6, head_dim), f32)]
    )
    frequency = jnp.exp(
        jnp.arange(head_dim // 2, dtype=f32) * (-2.0 * math.log(1000000.0) / head_dim)
    )
    shared = dict(
        inputs=inputs, cotangent=cotangent, gain_rows=gain_rows, head_gains=head_gains,
        w_query=w_query, w_key=w_key, w_value=w_value, w_out=w_out,
        w_gate=w_gate, w_up=w_up, w_down=w_down,
    )
    first = forward(
        dict(
            shared,
            segment_row=jnp.broadcast_to(segment_ids.astype(f32)[None, :], (8, rows)),
            frequency=jnp.broadcast_to(frequency[None, :], (8, head_dim // 2)),
        )
    )
    output = first.pop("output")
    made = types.SimpleNamespace(**backward(dict(shared, **first)))
    side = made.side_out
    summed_query = jnp.concatenate([side[0], side[1][:, : wide - WIDE]], axis=1)
    summed_out = jnp.concatenate([side[3], side[4][:, : wide - WIDE]], axis=1).T
    gains = lax.dynamic_slice_in_dim(made.gains_out, place * BLOCK, BLOCK, 1)
    own = head_dim // count
    gain_q = lax.dynamic_slice_in_dim(made.gains_out, place * own, own, 1)[4]
    gain_k = lax.dynamic_slice_in_dim(made.gains_out, head_dim + place * own, own, 1)[4]
    return (
        output,
        made.inputs_out,
        summed_query,
        made.kv_out[:, :head_dim],
        made.kv_out[:, head_dim:],
        summed_out,
        made.gate_out,
        made.up_out,
        made.down_out,
        gains[0],
        gain_q,
        gain_k,
        gains[1],
        gains[2],
        gains[3],
    )


def scatter_rows(grad):
    return lax.psum_scatter(grad, "seq", scatter_dimension=0, tiled=True).astype(jnp.float32)


def per_device(
    inputs,
    segment_ids,
    w_query,
    w_key,
    w_value,
    w_out,
    w_gate,
    w_up,
    w_down,
    gain_in,
    gain_query,
    gain_key,
    gain_post_attn,
    gain_pre_ffn,
    gain_post_ffn,
    cotangent,
):
    rows = inputs.shape[0]
    head_dim = w_key.shape[1]
    local_heads = w_query.shape[1] // head_dim
    place = lax.axis_index("seq")
    local_index = jnp.arange(rows, dtype=jnp.int32)
    ids_parts = [
        jnp.where(place >= distance, from_behind(segment_ids, "seq", distance), -1)
        for distance in (2, 1)
    ]
    window_ids = jnp.concatenate(ids_parts + [segment_ids], axis=0)
    window_index = jnp.arange(3 * rows, dtype=jnp.int32) - 2 * rows
    same = segment_ids[:, None] == window_ids[None, :]
    visible = same & (window_index[None, :] <= local_index[:, None])
    positions = jnp.sum(visible.astype(jnp.int32), axis=1) - 1
    cosine, sine = rope_angles(positions, head_dim)
    inputs_f = inputs.astype(jnp.float32)
    hidden_in = rms_scale(inputs_f, gain_in).astype(jnp.bfloat16)
    query_proj = jnp.dot(hidden_in, w_query, preferred_element_type=jnp.float32)
    key_proj = jnp.dot(hidden_in, w_key, preferred_element_type=jnp.float32)
    value_proj = jnp.dot(hidden_in, w_value, preferred_element_type=jnp.float32)

    def query_side(projection, gain):
        return prepare(
            projection.reshape(rows, local_heads, head_dim), gain, cosine, sine, QUERY_SCALE
        )

    def key_side(projection, gain):
        return prepare(projection[:, None, :], gain, cosine, sine, 1.0)[:, 0, :]

    queries = query_side(query_proj, gain_query).astype(jnp.bfloat16)
    own_keys = key_side(key_proj, gain_key).astype(jnp.bfloat16)
    own_values = value_proj.astype(jnp.bfloat16)
    key_parts = []
    value_parts = []
    for distance in (2, 1):
        moved_keys, moved_values = from_behind((own_keys, own_values), "seq", distance)
        key_parts.append(moved_keys)
        value_parts.append(moved_values)
    all_keys = jnp.concatenate(key_parts + [own_keys], axis=0)
    all_values = jnp.concatenate(value_parts + [own_values], axis=0)
    def raw_scores():
        return jnp.einsum("ihd,jd->hij", queries, all_keys, preferred_element_type=jnp.float32)

    scores = jnp.where(visible[None], raw_scores(), -1e30)
    row_max = jnp.max(scores, axis=-1, keepdims=True)
    expo = jnp.exp(scores - row_max)
    total = jnp.sum(expo, axis=-1, keepdims=True)
    attn_probs = expo / total
    log_total = row_max + jnp.log(total)
    attended = jnp.einsum(
        "hij,jd->ihd",
        attn_probs.astype(jnp.bfloat16),
        all_values,
        preferred_element_type=jnp.float32,
    )
    attended = attended.reshape(rows, local_heads * head_dim).astype(jnp.bfloat16)
    attn_branch = over_head(jnp.dot(attended, w_out, preferred_element_type=jnp.float32))
    residual_mid = inputs_f + rms_scale(attn_branch, gain_post_attn)
    hidden_mid = rms_scale(residual_mid, gain_pre_ffn).astype(jnp.bfloat16)
    gate_act = jnp.dot(hidden_mid, w_gate, preferred_element_type=jnp.float32)
    up_proj = jnp.dot(hidden_mid, w_up, preferred_element_type=jnp.float32)
    mixed_low = gated(gate_act, up_proj).astype(jnp.bfloat16)
    ffn_branch = over_head(jnp.dot(mixed_low, w_down, preferred_element_type=jnp.float32))
    output_f = residual_mid + rms_scale(ffn_branch, gain_post_ffn)
    grad_output = cotangent.astype(jnp.float32)
    unused_post, post_back = jax.vjp(rms_scale, ffn_branch, gain_post_ffn)
    grad_ffn, grad_g_post_ffn = post_back(grad_output)
    grad_ffn_low = grad_ffn.astype(jnp.bfloat16)
    grad_w_down = jnp.dot(grad_ffn_low.T, mixed_low, preferred_element_type=jnp.float32)
    summed_down = scatter_rows(grad_w_down.astype(jnp.bfloat16))
    grad_mixed = jnp.dot(grad_ffn_low, w_down.T, preferred_element_type=jnp.float32)
    unused_gate, gate_back = jax.vjp(gated, gate_act, up_proj)
    grad_gate, grad_up = gate_back(grad_mixed)
    grad_gate_low = grad_gate.astype(jnp.bfloat16)
    grad_up_low = grad_up.astype(jnp.bfloat16)
    grad_w_gate = jnp.dot(hidden_mid.T, grad_gate_low, preferred_element_type=jnp.float32)
    grad_w_up = jnp.dot(hidden_mid.T, grad_up_low, preferred_element_type=jnp.float32)
    summed_gate = scatter_rows(grad_w_gate.astype(jnp.bfloat16))
    summed_up = scatter_rows(grad_w_up.astype(jnp.bfloat16))
    grad_hidden_part = jnp.dot(
        grad_gate_low, w_gate.T, preferred_element_type=jnp.float32
    ) + jnp.dot(grad_up_low, w_up.T, preferred_element_type=jnp.float32)
    grad_hidden_mid = over_head(grad_hidden_part)
    unused_pre, pre_back = jax.vjp(rms_scale, residual_mid, gain_pre_ffn)
    grad_res_part, grad_g_pre_ffn = pre_back(grad_hidden_mid)
    grad_residual = grad_output + grad_res_part
    unused_attn, attn_post_back = jax.vjp(rms_scale, attn_branch, gain_post_attn)
    grad_attn, grad_g_post_attn = attn_post_back(grad_residual)
    grad_attn_low = grad_attn.astype(jnp.bfloat16)
    grad_w_out = jnp.dot(grad_attn_low.T, attended, preferred_element_type=jnp.float32)
    grad_attended = jnp.dot(grad_attn_low, w_out.T, preferred_element_type=jnp.float32).astype(
        jnp.bfloat16
    )
    grad_attended = grad_attended.reshape(rows, local_heads, head_dim)
    probs_again = jnp.where(visible[None], jnp.exp(raw_scores() - log_total), 0.0)
    grad_probs = jnp.einsum(
        "ihd,jd->hij", grad_attended, all_values, preferred_element_type=jnp.float32
    )
    grad_scores = (
        probs_again * (grad_probs - jnp.sum(probs_again * grad_probs, axis=-1, keepdims=True))
    ).astype(jnp.bfloat16)
    grad_queries = jnp.einsum(
        "hij,jd->ihd", grad_scores, all_keys, preferred_element_type=jnp.float32
    )
    grad_keys_all = jnp.einsum(
        "hij,ihd->jd", grad_scores, queries, preferred_element_type=jnp.float32
    )
    grad_values_all = jnp.einsum(
        "hij,ihd->jd",
        probs_again.astype(jnp.bfloat16),
        grad_attended,
        preferred_element_type=jnp.float32,
    )
    grad_keys = grad_keys_all[2 * rows :]
    grad_values = grad_values_all[2 * rows :]
    for distance in (2, 1):
        piece_begin = (2 - distance) * rows
        returned_keys, returned_values = (
            from_behind(
                grad_keys_all[piece_begin : piece_begin + rows].astype(jnp.bfloat16),
                "seq",
                -distance,
            ).astype(jnp.float32),
            from_behind(
                grad_values_all[piece_begin : piece_begin + rows].astype(jnp.bfloat16),
                "seq",
                -distance,
            ).astype(jnp.float32),
        )
        grad_keys = grad_keys + returned_keys
        grad_values = grad_values + returned_values
    unused_query, query_back = jax.vjp(query_side, query_proj, gain_query)
    grad_query_proj, grad_g_query_part = query_back(grad_queries)
    grad_query_low = grad_query_proj.astype(jnp.bfloat16)
    grad_w_query = jnp.dot(hidden_in.T, grad_query_low, preferred_element_type=jnp.float32)
    grad_hidden_query = jnp.dot(grad_query_low, w_query.T, preferred_element_type=jnp.float32)
    keys_summed, values_summed, hidden_summed, grad_g_query = (
        over_head(grad_keys),
        over_head(grad_values),
        over_head(grad_hidden_query),
        over_head(grad_g_query_part),
    )
    unused_key, key_back = jax.vjp(key_side, key_proj, gain_key)
    grad_key_proj, grad_g_key = key_back(keys_summed)
    grad_key_low = grad_key_proj.astype(jnp.bfloat16)
    grad_value_low = values_summed.astype(jnp.bfloat16)
    grad_w_key = jnp.dot(hidden_in.T, grad_key_low, preferred_element_type=jnp.float32)
    grad_w_value = jnp.dot(hidden_in.T, grad_value_low, preferred_element_type=jnp.float32)
    grad_hidden_in = (
        hidden_summed
        + jnp.dot(grad_key_low, w_key.T, preferred_element_type=jnp.float32)
        + jnp.dot(grad_value_low, w_value.T, preferred_element_type=jnp.float32)
    )
    unused_in, in_back = jax.vjp(rms_scale, inputs_f, gain_in)
    grad_in_part, grad_g_in = in_back(grad_hidden_in)
    grad_inputs = (grad_residual + grad_in_part).astype(jnp.bfloat16)
    count = lax.axis_size("seq")
    gain_columns = jnp.stack(
        [grad_g_in, grad_g_post_attn, grad_g_pre_ffn, grad_g_post_ffn], axis=1
    )
    side = jnp.concatenate(
        [grad_g_query.reshape(count, -1), grad_g_key.reshape(count, -1)], axis=1
    )
    side_rows = jnp.repeat(side, inputs.shape[1] // count, axis=0)
    extra = jnp.concatenate([gain_columns, side_rows], axis=1)
    extra = jnp.pad(extra, ((0, 0), (0, -extra.shape[1] % 128)))
    widths = [g.shape[1] for g in (grad_w_query, grad_w_out, grad_w_key, grad_w_value)]
    attn_sum = scatter_rows(
        jnp.concatenate(
            [
                g.astype(jnp.bfloat16)
                for g in (grad_w_query, grad_w_out, grad_w_key, grad_w_value, extra)
            ],
            axis=1,
        )
    )
    edges = [sum(widths[:i]) for i in range(5)]
    summed_query, summed_out, summed_key, summed_value = (
        attn_sum[:, edges[i] : edges[i + 1]] for i in range(4)
    )
    gain_sum = attn_sum[:, edges[4] :]
    summed_g_in, summed_g_post_attn, summed_g_pre_ffn, summed_g_post_ffn = (
        gain_sum[:, i] for i in range(4)
    )
    own = head_dim // count
    summed_g_query = gain_sum[0, 4 : 4 + own]
    summed_g_key = gain_sum[0, 4 + own : 4 + 2 * own]
    summed_out = summed_out.T
    summed_down = summed_down.T
    return (
        output_f.astype(jnp.bfloat16),
        grad_inputs,
        summed_query,
        summed_key,
        summed_value,
        summed_out,
        summed_gate,
        summed_up,
        summed_down,
        summed_g_in,
        summed_g_query,
        summed_g_key,
        summed_g_post_attn,
        summed_g_pre_ffn,
        summed_g_post_ffn,
    )


def solution(mesh):
    placed = (
        P("seq", None),
        P("seq"),
        P(None, "head"),
        P(),
        P(),
        P("head", None),
        P(None, "head"),
        P(None, "head"),
        P("head", None),
        P(),
        P(),
        P(),
        P(),
        P(),
        P(),
        P("seq", None),
    )
    return jax.shard_map(
        fast_device if mesh.shape["seq"] == 16 else per_device,
        mesh=mesh,
        in_specs=placed,
        out_specs=(
            P("seq", None),
            P("seq", None),
            P("seq", "head"),
            P("seq", None),
            P("seq", None),
            P("head", "seq"),
            P("seq", "head"),
            P("seq", "head"),
            P("head", "seq"),
            P("seq"),
            P("seq"),
            P("seq"),
            P("seq"),
            P("seq"),
            P("seq"),
        ),
        check_vma=False,
    )
```

```python
import functools
import math
import types

import jax
import jax.numpy as jnp
from jax import lax
from jax.experimental import pallas as pl
from jax.experimental.pallas import tpu as pltpu
from jax.sharding import PartitionSpec as P

MESH = pl.DeviceIdType.MESH
WIDE = 384
BLOCK = 72

EPS = 1e-06
QUERY_SCALE = 0.0625


def from_behind(block, axis, distance):
    devices = range(lax.axis_size(axis))
    route = [(i - distance, i) for i in devices if i - distance in devices]
    return lax.ppermute(block, axis, route)


def rms_scale(values, gain):
    return values * lax.rsqrt(jnp.mean(values * values, axis=-1, keepdims=True) + EPS) * gain


def rope_angles(positions, width):
    half_width = width // 2
    frequency = jnp.exp(
        jnp.arange(half_width, dtype=jnp.float32) * (-2.0 * math.log(1000000.0) / width)
    )
    angles = positions.astype(jnp.float32)[:, None] * frequency[None, :]
    return (jnp.cos(angles), jnp.sin(angles))


def rotate(values, cosine, sine):
    half_width = values.shape[-1] // 2
    first_half = values[..., :half_width]
    second_half = values[..., half_width:]
    cos_rows = cosine[:, None, :]
    sin_rows = sine[:, None, :]
    return jnp.concatenate(
        [
            first_half * cos_rows - second_half * sin_rows,
            second_half * cos_rows + first_half * sin_rows,
        ],
        axis=-1,
    )


def prepare(values, gain, cosine, sine, factor):
    return rotate(rms_scale(values, gain), cosine, sine) * factor


def gelu_tanh(values):
    return (
        0.5
        * values
        * (1.0 + jnp.tanh(0.7978845608028654 * (values + 0.044715 * values * values * values)))
    )


def gated(gate_act, up_proj):
    return gelu_tanh(gate_act) * up_proj


def over_head(part):
    low = part.astype(jnp.bfloat16)
    other = lax.ppermute(low, "head", [(0, 1), (1, 0)])
    return low.astype(jnp.float32) + other.astype(jnp.float32)


def place_of():
    seq = lax.axis_index("seq")
    return seq, lax.axis_index("head"), seq % 2, seq // 2 % 2, seq // 4


def dot_nt(left, right):
    return lax.dot_general(left, right, (((1,), (1,)), ((), ())), preferred_element_type=jnp.float32)


def dot_tn(left, right):
    return lax.dot_general(left, right, (((0,), (0,)), ((), ())), preferred_element_type=jnp.float32)


def rotate_back(grad, cosine, sine):
    half = grad.shape[-1] // 2
    first, second = grad[:, :half], grad[:, half:]
    return jnp.concatenate(
        [first * cosine + second * sine, second * cosine - first * sine], axis=-1
    )


def norm_parts(values):
    scale = lax.rsqrt(jnp.mean(values * values, axis=-1, keepdims=True) + EPS)
    return scale, values * scale


def norm_back(grad, gain, scale, normed):
    inner = grad * gain
    back = scale * (inner - normed * jnp.mean(inner * normed, axis=-1, keepdims=True))
    return back, jnp.sum(grad * normed, axis=0, keepdims=True)


CHUNKS = 2


def turn(values, cosine, sine):
    half = values.shape[-1] // 2
    first, second = values[:, :half], values[:, half:]
    return jnp.concatenate(
        [first * cosine - second * sine, second * cosine + first * sine], axis=-1
    )


def to_blocks(target, values, columns):
    turned = values.astype(jnp.float32).T.astype(jnp.bfloat16)
    for half in range(2):
        for x in range(2):
            for f in range(2):
                source = 144 * ((2 * half + f) * 2 + x)
                to = 144 * (half * 4 + x * 2 + f)
                target[to : to + 144, columns] = turned[source : source + 144]


def forward_kernel(names, *refs):
    r = types.SimpleNamespace(**dict(zip(names, refs)))
    seq, head, core, side, level = place_of()
    last_seq = lax.axis_size("seq") - 1
    f32, low = jnp.float32, jnp.bfloat16
    rows, width = r.inputs.shape
    heads = r.w_query.shape[1] // 256
    hidden = r.w_gate.shape[1]
    size = rows // CHUNKS
    even = core == 0

    barrier = pltpu.get_barrier_semaphore()

    def greet(to_seq, to_head):
        pl.semaphore_signal(barrier, inc=1, device_id=(to_seq, to_head), device_id_type=MESH)

    def load(n, src, dst):
        copy = pltpu.make_async_copy(src, dst, r.load_sem.at[n])
        copy.start()
        return copy

    in_copy = load(0, r.inputs, r.x)
    kv_copies = (load(2, r.w_key, r.wk), load(3, r.w_value, r.wv))
    query_copy = load(7, r.w_query, r.wq)
    out_copy = load(8, r.w_out, r.wo.at[head])
    ffn_copies = (
        load(9, r.w_gate, r.wg), load(10, r.w_up, r.wu), load(11, r.w_down, r.wd),
    )
    cot_copy = load(12, r.cotangent, r.cot)

    greet(seq ^ 1, head)
    greet(seq, 1 - head)
    expected = jnp.int32(2)
    for distance in (1, 2):
        @pl.when(seq >= distance)
        def _():
            greet(seq - distance, head)

        @pl.when(seq + distance <= last_seq)
        def _():
            greet(seq + distance, head)

        expected = (
            expected
            + (seq >= distance).astype(jnp.int32)
            + (seq + distance <= last_seq).astype(jnp.int32)
        )
    pl.semaphore_wait(barrier, expected)

    def remote(src, dst, send, recv, to_seq, to_head):
        return pltpu.make_async_remote_copy(
            src_ref=src,
            dst_ref=dst,
            send_sem=send,
            recv_sem=recv,
            device_id=(to_seq, to_head),
            device_id_type=MESH,
        )

    share = r.w_out.shape[0] // 2

    def out_share(which):
        return pl.ds(pl.multiple_of(which * share, share), share)

    def w_out_y():
        mine = out_share(core)
        return remote(
            r.w_out.at[mine, :], r.wo.at[head, mine, :], r.wo_send.at[0], r.wo_recv.at[0],
            seq, 1 - head,
        )

    def w_out_core():
        mine = out_share(core)
        part = r.wo.at[1 - head, mine, :]
        return remote(part, part, r.wo_send.at[1], r.wo_recv.at[1], seq ^ 1, head)

    def ids_send(distance):
        return remote(
            r.ids.at[2], r.ids.at[2 - distance], r.ids_send.at[distance - 1],
            r.ids_recv.at[distance - 1], seq + distance, head,
        )

    def halo(n, distance, hand_on=False):
        kind = r.window.at[n]
        source = kind.at[pl.ds((1 if hand_on else 2) * rows, rows), :]
        target = kind.at[pl.ds((2 - distance) * rows, rows), :]
        place = 2 if hand_on else distance - 1
        return remote(
            source, target, r.halo_send.at[n, place], r.halo_recv.at[n, distance - 1],
            seq + (1 if hand_on else distance), head,
        )

    ids = r.segment_ids[...].astype(f32).reshape(1, rows)
    r.ids[2] = jnp.broadcast_to(ids, (8, rows))
    for distance in (1, 2):
        @pl.when(seq + distance <= last_seq)
        def _():
            ids_send(distance).start()

    w_out_y().start()

    r.gains[...] = jnp.zeros_like(r.gains)
    r.head_gain[...] = jnp.zeros_like(r.head_gain)
    for n, gain in enumerate((r.gain_in, r.gain_post_attn, r.gain_pre_ffn, r.gain_post_ffn)):
        r.gains[n : n + 1, :] = gain[...].reshape(1, width)
    for n, gain in enumerate((r.gain_query, r.gain_key)):
        r.head_gain[n : n + 1, :] = gain[...].reshape(1, 256)
    in_copy.wait()

    def norm_in(c, carry):
        at = pl.ds(pl.multiple_of(c * 128, 128), 128)
        _, normed = norm_parts(r.x[at, :].astype(f32))
        r.normed_in[at, :] = (normed * r.gains[0:1, :]).astype(low)
        return carry

    lax.fori_loop(0, rows // 128, norm_in, 0)
    for copy in kv_copies:
        copy.wait()
    r.key_raw[...] = jnp.dot(r.normed_in[...], r.wk[...], preferred_element_type=f32)
    r.window[1, 2 * rows :, :] = jnp.dot(
        r.normed_in[...], r.wv[...], preferred_element_type=f32
    ).astype(low)

    def value_halo(distance):
        return halo(1, distance)

    @pl.when(seq + 1 <= last_seq)
    def _():
        value_halo(1).start()

    @pl.when(even & (seq + 2 <= last_seq))
    def _():
        value_halo(2).start()

    for distance in (1, 2):
        @pl.when(seq >= distance)
        def _():
            remote(
                r.ids.at[2], r.ids.at[2 - distance], r.ids_send.at[distance - 1],
                r.ids_recv.at[distance - 1], seq ^ 1, head,
            ).wait_recv()

        @pl.when(seq < distance)
        def _():
            r.ids[2 - distance] = jnp.full((8, rows), -1.0, f32)

    ids_row = jnp.concatenate([r.ids[b][:1] for b in range(3)], axis=1)
    r.ids_flat[...] = jnp.broadcast_to(ids_row, (8, 3 * rows))
    ids_column = jnp.broadcast_to(r.ids[2][:1], (128, rows)).T
    r.ids_turned[...] = ids_column
    column = lax.broadcasted_iota(jnp.int32, (8, 128), 1).astype(f32)
    frequency = jnp.exp(column * (-2.0 * math.log(1000000.0) / 256))[:1]

    def angles(c, carry):
        at = pl.ds(pl.multiple_of(c * 128, 128), 128)
        here = lax.broadcasted_iota(jnp.int32, (128, 3 * rows), 0) + (2 * rows + c * 128)
        there = lax.broadcasted_iota(jnp.int32, (128, 3 * rows), 1)
        same = (r.ids_turned[at, :1] == r.ids_flat[:1, :]) & (there < here)
        position = jnp.sum(same.astype(f32), axis=1, keepdims=True)
        angle = position * frequency
        r.cosine[at, :] = jnp.cos(angle)
        r.sine[at, :] = jnp.sin(angle)
        return carry

    lax.fori_loop(0, rows // 128, angles, 0)
    _, normed = norm_parts(r.key_raw[...])
    r.window[0, 2 * rows :, :] = turn(
        normed * r.head_gain[1:2, :], r.cosine[...], r.sine[...]
    ).astype(low)

    @pl.when(seq + 1 <= last_seq)
    def _():
        halo(0, 1).start()

    @pl.when(even & (seq + 2 <= last_seq))
    def _():
        halo(0, 2).start()

    query_copy.wait()
    r.query_raw[...] = jnp.dot(r.normed_in[...], r.wq[...], preferred_element_type=f32)
    for h in range(heads):
        at = slice(256 * h, 256 * h + 256)
        _, normed = norm_parts(r.query_raw[:, at])
        r.q[:, at] = (
            turn(normed * r.head_gain[0:1, :], r.cosine[...], r.sine[...]) * QUERY_SCALE
        ).astype(low)

    def store(n, src, dst):
        copy = pltpu.make_async_copy(src, dst, r.store_sem.at[n])
        copy.start()
        return copy

    to_blocks(r.turned, r.normed_in[...], slice(0, rows))
    stores = [
        store(1, r.key_raw, r.key_proj),
        store(2, r.query_raw, r.query_proj),
        store(3, r.q, r.queries),
        store(4, r.cosine, r.cosine_out),
        store(5, r.sine, r.sine_out),
        store(6, r.ids_flat, r.ids_out),
        store(16, r.gains, r.gain_rows),
        store(17, r.head_gain, r.head_gains),
    ]
    turned_store = store(0, r.turned, r.left_in)

    out_copy.wait()
    w_out_y().wait()
    w_out_core().start()

    def arrival(n, distance):
        return halo(n, distance)

    for n in (1, 0):
        @pl.when(seq >= 1)
        def _():
            arrival(n, 1).wait_recv()

        @pl.when(even & (seq >= 2))
        def _():
            halo(n, 2, True).start()

    for n in (1, 0):
        @pl.when(seq >= 2)
        def _():
            arrival(n, 2).wait_recv()

    for distance in (1, 2):
        @pl.when(seq < distance)
        def _():
            for n in range(2):
                r.window[n, (2 - distance) * rows : (3 - distance) * rows, :] = jnp.zeros(
                    (rows, 256), low
                )

    def head_exchange(c):
        part = r.heads_all.at[head, pl.ds(c * size, size), :]
        return remote(part, part, r.y_send.at[c], r.y_recv.at[c], seq, 1 - head)

    def branch_exchange(c):
        at = pl.ds(c * size, size)
        return remote(
            r.y_out.at[at, :], r.y_in.at[at, :], r.y_send.at[CHUNKS + c], r.y_recv.at[CHUNKS + c],
            seq, 1 - head,
        )

    def attend(c):
        first = c * size
        span = 2 * rows + size
        at = slice(first, first + size)
        key_at = slice(first, first + span)
        here = lax.broadcasted_iota(jnp.int32, (size, span), 0) + 2 * rows
        there = lax.broadcasted_iota(jnp.int32, (size, span), 1)
        seen = (r.ids_turned[at, :1] == r.ids_flat[:1, key_at]) & (there <= here)
        for h in range(heads):
            head_at = slice(256 * h, 256 * h + 256)
            scores = jnp.where(seen, dot_nt(r.q[at, head_at], r.window[0, key_at, :]), -1e30)
            top = jnp.max(scores, axis=1, keepdims=True)
            expo = jnp.exp(scores - top)
            total = jnp.sum(expo, axis=1, keepdims=True)
            probs = (expo / total).astype(low)
            out = jnp.dot(probs, r.window[1, key_at, :], preferred_element_type=f32)
            r.heads_f[at, head_at] = out
            r.heads_all[head, at, head_at] = out.astype(low)
            r.lse_rows[h : h + 1, at] = jnp.broadcast_to(top + jnp.log(total), (size, 128)).T[:1]
        head_exchange(c).start()

    for c in range(CHUNKS):
        attend(c)
    stores += [
        store(7, r.heads_f, r.attended),
        store(8, r.lse_rows, r.lse),
        store(9, r.window.at[0], r.keys),
        store(10, r.window.at[1], r.values),
    ]
    w_out_core().wait()
    turned_store.wait()
    for copy in ffn_copies:
        copy.wait()

    def tile_stores(c, j):
        slot = lax.rem(j, 2)
        at = pl.ds(pl.multiple_of(j * WIDE, WIDE), WIDE)
        here = pl.ds(c * size, size)
        return (
            pltpu.make_async_copy(
                r.gate_tile.at[slot], r.gate_act.at[here, at], r.tile_sem.at[0, slot]
            ),
            pltpu.make_async_copy(
                r.up_tile.at[slot], r.up_proj.at[here, at], r.tile_sem.at[1, slot]
            ),
            pltpu.make_async_copy(
                r.mixed_tile.at[slot], r.mixed.at[here, at], r.tile_sem.at[2, slot]
            ),
        )

    steps = hidden // WIDE

    def feed(c):
        at = pl.ds(c * size, size)
        head_exchange(c).wait_recv()
        branch = jnp.dot(r.heads_all[0, at, :], r.wo[0], preferred_element_type=f32) + jnp.dot(
            r.heads_all[1, at, :], r.wo[1], preferred_element_type=f32
        )
        r.branch[at, :] = branch
        _, normed = norm_parts(branch)
        middle = r.x[at, :].astype(f32) + normed * r.gains[1:2, :]
        r.middle[at, :] = middle
        _, normed = norm_parts(middle)
        r.normed_mid[at, :] = (normed * r.gains[2:3, :]).astype(low)

        def tile(j, carry):
            slot = lax.rem(j, 2)
            columns = pl.ds(pl.multiple_of(j * WIDE, WIDE), WIDE)
            left = r.normed_mid[at, :]
            gate = jnp.dot(left, r.wg[:, columns], preferred_element_type=f32)
            up = jnp.dot(left, r.wu[:, columns], preferred_element_type=f32)

            @pl.when(j >= 2)
            def _():
                for copy in tile_stores(c, j - 2):
                    copy.wait()

            r.gate_tile[slot] = gate
            r.up_tile[slot] = up
            curve = jnp.tanh(0.7978845608028654 * gate * (1.0 + 0.044715 * gate * gate))
            mixed = (0.5 * gate * (1.0 + curve) * up).astype(low)
            r.mixed_tile[slot] = mixed
            for copy in tile_stores(c, j):
                copy.start()
            part = jnp.dot(mixed, r.wd[columns, :], preferred_element_type=f32)

            @pl.when(j == 0)
            def _():
                r.acc[...] = part

            @pl.when(j > 0)
            def _():
                r.acc[...] += part

            return carry

        lax.fori_loop(0, steps, tile, 0)
        for j in (steps - 2, steps - 1):
            for copy in tile_stores(c, jnp.int32(j)):
                copy.wait()
        r.y_out[at, :] = r.acc[...].astype(low)
        branch_exchange(c).start()

    for c in range(CHUNKS):
        feed(c)
    stores += [store(11, r.branch, r.attn_branch), store(12, r.middle, r.residual_mid)]
    to_blocks(r.turned, r.normed_mid[...], slice(0, rows))
    mid_store = store(0, r.turned, r.left_mid)
    cot_copy.wait()
    gain_sum = jnp.zeros((1, width), f32)
    for c in range(CHUNKS):
        branch_exchange(c).wait_recv()

        def end(n, total):
            at = pl.ds(pl.multiple_of(c * size + n * 128, 128), 128)
            branch = r.y_out[at, :].astype(f32) + r.y_in[at, :].astype(f32)
            scale, normed = norm_parts(branch)
            r.result[at, :] = (r.middle[at, :] + normed * r.gains[3:4, :]).astype(low)
            back, gain = norm_back(r.cot[at, :].astype(f32), r.gains[3:4, :], scale, normed)
            r.cot[at, :] = back.astype(low)
            return total + gain

        gain_sum = lax.fori_loop(0, size // 128, end, gain_sum)
        if c == 0:
            mid_store.wait()
        at = slice(c * size, (c + 1) * size)
        to_blocks(r.turned, r.cot[at, :], at)
    stores += [
        store(0, r.turned, r.left_ffn),
        store(13, r.cot, r.grad_ffn),
        store(14, r.result, r.output),
    ]
    r.gain_tile[...] = jnp.zeros_like(r.gain_tile)
    r.gain_tile[3:4, :] = gain_sum
    stores.append(store(15, r.gain_tile, r.gain_start))
    for copy in stores:
        copy.wait()
    for distance in (1, 2):
        @pl.when(seq + distance <= last_seq)
        def _():
            ids_send(distance).wait_send()

    for n in range(2):
        @pl.when(seq + 1 <= last_seq)
        def _():
            halo(n, 1).wait_send()

        @pl.when(even & (seq + 2 <= last_seq))
        def _():
            halo(n, 2).wait_send()

        @pl.when(even & (seq >= 2))
        def _():
            halo(n, 2, True).wait_send()

    for c in range(CHUNKS):
        head_exchange(c).wait_send()
        branch_exchange(c).wait_send()


def forward(operands):
    low, f32 = jnp.bfloat16, jnp.float32
    dma = pltpu.SemaphoreType.DMA
    rows, width = operands["inputs"].shape
    hidden = operands["w_gate"].shape[1]
    wide = operands["w_query"].shape[1]
    shape = jax.ShapeDtypeStruct
    anywhere = pl.BlockSpec(memory_space=pl.ANY)
    outs = dict(
        left_in=shape((width, rows), low),
        left_mid=shape((width, rows), low),
        left_ffn=shape((width, rows), low),
        key_proj=shape((rows, 256), f32),
        query_proj=shape((rows, wide), f32),
        queries=shape((rows, wide), low),
        cosine_out=shape((rows, 128), f32),
        sine_out=shape((rows, 128), f32),
        ids_out=shape((8, 3 * rows), f32),
        attended=shape((rows, wide), f32),
        lse=shape((8, rows), f32),
        keys=shape((3 * rows, 256), low),
        values=shape((3 * rows, 256), low),
        attn_branch=shape((rows, width), f32),
        residual_mid=shape((rows, width), f32),
        gate_act=shape((rows, hidden), f32),
        up_proj=shape((rows, hidden), f32),
        mixed=shape((rows, hidden), low),
        grad_ffn=shape((rows, width), low),
        output=shape((rows, width), low),
        gain_start=shape((8, width), f32),
        gain_rows=shape((8, width), f32),
        head_gains=shape((8, 256), f32),
    )
    size = rows // CHUNKS
    vmem = pltpu.VMEM
    scratch = dict(
        x=vmem((rows, width), low),
        gains=vmem((8, width), f32),
        wk=vmem((width, 256), low),
        wv=vmem((width, 256), low),
        head_gain=vmem((8, 256), f32),
        ids=vmem((3, 8, rows), f32),
        ids_flat=vmem((8, 3 * rows), f32),
        ids_turned=vmem((rows, 128), f32),
        wq=vmem((width, wide), low),
        wo=vmem((2, wide, width), low),
        wg=vmem((width, hidden), low),
        wu=vmem((width, hidden), low),
        wd=vmem((hidden, width), low),
        cot=vmem((rows, width), low),
        normed_in=vmem((rows, width), low),
        normed_mid=vmem((rows, width), low),
        key_raw=vmem((rows, 256), f32),
        query_raw=vmem((rows, wide), f32),
        q=vmem((rows, wide), low),
        window=vmem((2, 3 * rows, 256), low),
        cosine=vmem((rows, 128), f32),
        sine=vmem((rows, 128), f32),
        turned=vmem((width, rows), low),
        heads_f=vmem((rows, wide), f32),
        heads_all=vmem((2, rows, wide), low),
        lse_rows=vmem((8, rows), f32),
        branch=vmem((rows, width), f32),
        middle=vmem((rows, width), f32),
        gate_tile=vmem((2, size, WIDE), f32),
        up_tile=vmem((2, size, WIDE), f32),
        mixed_tile=vmem((2, size, WIDE), low),
        acc=vmem((size, width), f32),
        y_out=vmem((rows, width), low),
        y_in=vmem((rows, width), low),
        result=vmem((rows, width), low),
        gain_tile=vmem((8, width), f32),
        load_sem=dma((13,)),
        store_sem=dma((18,)),
        tile_sem=dma((3, 2)),
        wo_send=dma((2,)),
        wo_recv=dma((2,)),
        ids_send=dma((2,)),
        ids_recv=dma((2,)),
        halo_send=dma((2, 3)),
        halo_recv=dma((2, 2)),
        y_send=dma((2 * CHUNKS,)),
        y_recv=dma((2 * CHUNKS,)),
    )
    names = (*operands, *outs, *scratch)
    results = pl.pallas_call(
        functools.partial(forward_kernel, names),
        out_shape=list(outs.values()),
        in_specs=[
            pl.BlockSpec(memory_space=pltpu.VMEM) if len(a.shape) == 1 else anywhere
            for a in operands.values()
        ],
        out_specs=[anywhere] * len(outs),
        scratch_shapes=list(scratch.values()),
        compiler_params=pltpu.CompilerParams(
            collective_id=2, has_side_effects=True, vmem_limit_bytes=62 << 20
        ),
        name="forward",
    )(*operands.values())
    return dict(zip(outs, results))


DOWN, GATE, UP, QUERY, QUERY_END, OUT, OUT_END = range(7)
RING = 6
Y_PARTS = 8
STEPS = 31
FIRST_SIDE = 27
LAG_X = 4
LAG_M = 6
LAG_Z = 8


def backward_kernel(names, *refs):
    r = types.SimpleNamespace(**dict(zip(names, refs)))
    seq, head, core, side, level = place_of()
    last_seq = lax.axis_size("seq") - 1
    f32, low = jnp.float32, jnp.bfloat16
    rows = r.grad_ffn.shape[0]
    width = r.grad_ffn.shape[1]

    barrier = pltpu.get_barrier_semaphore()

    def greet(to_seq, to_head):
        pl.semaphore_signal(barrier, inc=1, device_id=(to_seq, to_head), device_id_type=MESH)

    greet(seq ^ 1, head)
    greet(seq ^ 2, head)
    greet(seq, 1 - head)
    for z in range(4):
        for c in range(2):
            other = z * 4 + side * 2 + c

            @pl.when(other != seq)
            def _():
                greet(other, head)

    expected = jnp.int32(10)
    for distance in (1, 2):
        @pl.when(seq >= distance)
        def _():
            greet(seq - distance, head)

        @pl.when(seq + distance <= last_seq)
        def _():
            greet(seq + distance, head)

        expected = (
            expected
            + (seq >= distance).astype(jnp.int32)
            + (seq + distance <= last_seq).astype(jnp.int32)
        )
    pl.semaphore_wait(barrier, expected)

    def remote(src, dst, send, recv, to_seq, to_head):
        return pltpu.make_async_remote_copy(
            src_ref=src,
            dst_ref=dst,
            send_sem=send,
            recv_sem=recv,
            device_id=(to_seq, to_head),
            device_id_type=MESH,
        )

    targets = [((2 * core + k // 2) * 4 + side * 2 + k % 2) for k in range(4)]
    sources = [z * 4 + side * 2 + level // 2 for z in range(4)]
    starts_far = (level == 3 * (1 - core))
    hands_on = (level == 2 - core)
    near = (2 - core) * 4 + side * 2 + core
    far = (3 - 3 * core) * 4 + side * 2 + core
    far_level = 3 * core

    def is_far(k):
        return core == k // 2

    def unheard(z):
        return (level == 3 - z) if z in (0, 3) else False

    def core_copy(t):
        slot = lax.rem(t, RING)
        return remote(
            r.sent.at[lax.rem(t, 2)], r.core_in.at[slot], r.core_send.at[t], r.core_recv.at[t],
            seq ^ 1, head,
        )

    def x_copy(t):
        slot = lax.rem(t, RING)
        return remote(
            r.held.at[slot, 1 - side], r.x_in.at[slot], r.x_send.at[t], r.x_recv.at[t],
            seq ^ 2, head,
        )

    def z_copy(t, k):
        return remote(
            r.z_out.at[lax.rem(t, RING), k], r.z_in.at[t, level],
            r.z_send.at[t, k], r.z_recv.at[t, level], targets[k], head,
        )

    def near_copy(t, k):
        return remote(
            r.z_out.at[lax.rem(t, RING), k], r.m_in.at[lax.rem(t, RING), k % 2],
            r.z_send.at[t, k], r.m_recv.at[t, k % 2], near, head,
        )

    def far_copy(t, g):
        return remote(
            r.z_out.at[lax.rem(t, RING), 2 * core + g], r.z_in.at[t, level],
            r.z_send.at[t, 2 * core + g], r.z_recv.at[t, level],
            far_level * 4 + side * 2 + g, head,
        )

    def z_arrival(t, z):
        return remote(
            r.z_out.at[0, 0], r.z_in.at[t, z], r.z_send.at[t, 0], r.z_recv.at[t, z],
            sources[z], head,
        )

    def produce(t):
        @pl.when(t >= 2)
        def _():
            core_copy(t - 2).wait_send()

        @pl.when(t >= RING)
        def _():
            x_copy(t - RING).wait_send()

        which = jnp.where(t < 9, 0, jnp.where(t < FIRST_SIDE, 1, jnp.where(t < 30, 2, 0)))
        place = jnp.where(
            t < 9, lax.rem(t, 2), jnp.where(t < FIRST_SIDE, t - 7, t - (FIRST_SIDE - 2))
        )
        tile = r.tiles[place]

        def half(start):
            left = r.lefts[which, pl.ds(pl.multiple_of(start, 576), 576), :]
            return jnp.dot(left, tile, preferred_element_type=f32)

        away = half((1 - core) * 576)
        for k in range(8):
            r.sent[lax.rem(t, 2), k // 4, k % 4] = away[k * BLOCK : (k + 1) * BLOCK].astype(low)

        @pl.when(t >= RING)
        def _():
            pl.semaphore_wait(r.core_free, 1)

        def second(start):
            left = r.lefts[0, pl.ds(pl.multiple_of(start, 576), 576), :]
            return jnp.dot(left, tile[:, 256:], preferred_element_type=f32)

        @pl.when(t == FIRST_SIDE + 2)
        def _():
            more = second((1 - core) * 576)
            for k in range(8):
                r.sent[lax.rem(t, 2), k // 4, k % 4, :, 256:] = more[
                    k * BLOCK : (k + 1) * BLOCK
                ].astype(low)

        core_copy(t).start()
        home = half(core * 576)
        for k in range(8):
            r.held[lax.rem(t, RING), k // 4, k % 4] = home[k * BLOCK : (k + 1) * BLOCK].astype(low)

        @pl.when(t == FIRST_SIDE + 2)
        def _():
            more = second(core * 576)
            for k in range(8):
                r.held[lax.rem(t, RING), k // 4, k % 4, :, 256:] = more[
                    k * BLOCK : (k + 1) * BLOCK
                ].astype(low)

    def core_stage(t):
        core_copy(t).wait_recv()
        slot = lax.rem(t, RING)

        def add(part):
            for k in range(4):
                r.held[slot, part, k] = (
                    r.held[slot, part, k].astype(f32) + r.core_in[slot, part, k].astype(f32)
                ).astype(low)

        add(1 - side)

        @pl.when(t >= RING)
        def _():
            pl.semaphore_wait(r.x_free, 1)

        x_copy(t).start()
        add(side)

        @pl.when(t + RING < STEPS)
        def _():
            pl.semaphore_signal(r.core_free, inc=1, device_id=(seq ^ 1, head), device_id_type=MESH)

    def x_stage(t):
        x_copy(t).wait_recv()
        slot = lax.rem(t, RING)

        @pl.when(t >= RING)
        def _():
            for k in range(4):
                @pl.when(targets[k] != seq)
                def _():
                    z_copy(t - RING, k).wait_send()

        @pl.when(starts_far & (t >= RING))
        def _():
            pl.semaphore_wait(r.m_free, 1)

        for k in range(4):
            total = (r.held[slot, side, k].astype(f32) + r.x_in[slot, k].astype(f32)).astype(low)

            @pl.when(targets[k] == seq)
            def _():
                r.z_in[t, level] = total

            @pl.when(targets[k] != seq)
            def _():
                r.z_out[slot, k] = total

                @pl.when(starts_far & is_far(k))
                def _():
                    near_copy(t, k).start()

                @pl.when(jnp.logical_not((starts_far | hands_on) & is_far(k)))
                def _():
                    z_copy(t, k).start()

        @pl.when(t + RING < STEPS)
        def _():
            pl.semaphore_signal(r.x_free, inc=1, device_id=(seq ^ 2, head), device_id_type=MESH)

    def m_stage(t):
        slot = lax.rem(t, RING)

        @pl.when(hands_on)
        def _():
            for g in range(2):
                remote(
                    r.z_out.at[0, 0], r.m_in.at[slot, g], r.z_send.at[t, 0], r.m_recv.at[t, g],
                    far, head,
                ).wait_recv()
                k = 2 * core + g
                r.z_out[slot, k] = (
                    r.z_out[slot, k].astype(f32) + r.m_in[slot, g].astype(f32)
                ).astype(low)
                far_copy(t, g).start()

            @pl.when(t + RING < STEPS)
            def _():
                pl.semaphore_signal(r.m_free, inc=1, device_id=(far, head), device_id_type=MESH)

    def out_copy(t, kind):
        slot = lax.rem(t, 2)
        at = pl.multiple_of(lax.rem(t, 9) * WIDE, WIDE)
        if kind == DOWN:
            return pltpu.make_async_copy(
                r.flat.at[slot], r.down_out.at[:, pl.ds(at, WIDE)], r.out_sem.at[t]
            )
        if kind == QUERY:
            return pltpu.make_async_copy(
                r.flat.at[slot], r.query_out.at[:, pl.ds(0, WIDE)], r.out_sem.at[t]
            )
        if kind == QUERY_END:
            return pltpu.make_async_copy(
                r.flat.at[slot, :, pl.ds(0, 128)], r.query_out.at[:, pl.ds(WIDE, 128)],
                r.out_sem.at[t],
            )
        if kind == OUT:
            return pltpu.make_async_copy(
                r.flat.at[slot, :, pl.ds(256, 128)], r.out_out.at[:, pl.ds(0, 128)],
                r.out_sem.at[t],
            )
        if kind == OUT_END:
            return pltpu.make_async_copy(
                r.flat.at[slot], r.out_out.at[:, pl.ds(128, WIDE)], r.out_sem.at[t]
            )
        target = r.gate_out if kind == GATE else r.up_out
        return pltpu.make_async_copy(
            r.flat.at[slot], target.at[:, pl.ds(at, WIDE)], r.out_sem.at[t]
        )

    KINDS = (
        (DOWN, 0, 9), (GATE, 9, 18), (UP, 18, 27), (QUERY, 27, 28), (QUERY_END, 28, 29),
        (OUT, 29, 30), (OUT_END, 30, 31),
    )

    def out_wait(t):
        for kind, first, end in KINDS:
            @pl.when((t >= first) & (t < end))
            def _():
                out_copy(t, kind).wait()

    def z_stage(t):
        for z in range(4):
            @pl.when((sources[z] != seq) & jnp.logical_not(unheard(z)))
            def _():
                z_arrival(t, z).wait_recv()

        total = r.z_in[t, 1].astype(f32) + r.z_in[t, 2].astype(f32)
        for z in (0, 3):
            total = total + jnp.where(unheard(z), 0.0, r.z_in[t, z].astype(f32))

        @pl.when(t >= 2)
        def _():
            out_wait(t - 2)

        r.flat[lax.rem(t, 2)] = total
        for kind, first, end in KINDS:
            @pl.when((t >= first) & (t < end))
            def _():
                out_copy(t, kind).start()

        @pl.when(t == FIRST_SIDE + 1)
        def _():
            r.kv_own[:, :256] = total[:, 128:]

        @pl.when(t == FIRST_SIDE + 2)
        def _():
            r.kv_own[:, 256:] = total[:, :256]

    def pump(i):
        @pl.when(i < STEPS)
        def _():
            produce(i)

        @pl.when((i >= 1) & (i - 1 < STEPS))
        def _():
            core_stage(i - 1)

        @pl.when((i >= LAG_X) & (i - LAG_X < STEPS))
        def _():
            x_stage(i - LAG_X)

        @pl.when((i >= LAG_M) & (i - LAG_M < STEPS))
        def _():
            m_stage(i - LAG_M)

        @pl.when((i >= LAG_Z) & (i - LAG_Z < STEPS))
        def _():
            z_stage(i - LAG_Z)

    def y_part(n, part):
        size = rows // Y_PARTS
        at = pl.ds(part * size, size)
        return remote(
            r.y_out.at[at, :], r.y_in.at[n, at, :], r.y_send.at[n, part], r.y_recv.at[n, part],
            seq, 1 - head,
        )

    def y_start(n, first):
        for part in (first, first + 1):
            y_part(n, part).start()

    def y_sent(n):
        for part in range(Y_PARTS):
            y_part(n, part).wait_send()

    def y_arrived(n):
        for part in range(Y_PARTS):
            y_part(n, part).wait_recv()

    def feed_forward(grad, wd, wg, wu, gate, up, acc):
        sems, grad_sem, left_sem = r.tile_sems, r.grad_sem, r.left_sem

        def copies(j):
            slot = lax.rem(j, 2)
            at = pl.ds(pl.multiple_of(j * WIDE, WIDE), WIDE)
            pairs = (
                (r.w_down.at[at, :], wd),
                (r.w_gate.at[:, at], wg),
                (r.w_up.at[:, at], wu),
                (r.gate_act.at[:, at], gate),
                (r.up_proj.at[:, at], up),
            )
            return [
                pltpu.make_async_copy(src, dst.at[slot], sems.at[n, slot])
                for n, (src, dst) in enumerate(pairs)
            ]

        def mixed_copy(j):
            slot = lax.rem(j, 2)
            at = pl.ds(pl.multiple_of(j * WIDE, WIDE), WIDE)
            return pltpu.make_async_copy(r.mixed.at[:, at], r.tiles.at[slot], sems.at[5, slot])

        first = [pltpu.make_async_copy(r.grad_ffn, grad, grad_sem)] + [
            pltpu.make_async_copy(left, r.lefts.at[n], left_sem.at[n])
            for n, left in enumerate((r.left_ffn, r.left_mid, r.left_in))
        ]
        for copy in (first[1], mixed_copy(0), first[0], *copies(0), *first[2:]):
            copy.start()
        first[1].wait()
        first[0].wait()
        acc[...] = jnp.zeros_like(acc)

        def step(i, carry):
            @pl.when(i + 1 < 9)
            def _():
                for copy in (mixed_copy(i + 1), *copies(i + 1)):
                    copy.start()

            mixed_copy(i).wait()
            pump(i)
            for copy in copies(i):
                copy.wait()
            slot = lax.rem(i, 2)
            grad_mixed = dot_nt(grad[...], wd[slot])
            v, u = gate[slot], up[slot]
            square = v * v
            curve = jnp.tanh(0.7978845608028654 * v * (1.0 + 0.044715 * square))
            gelu = 0.5 * v * (1.0 + curve)
            slope = 0.5 * (1.0 + curve) + 0.5 * v * (1.0 - curve * curve) * (
                0.7978845608028654 * (1.0 + 3.0 * 0.044715 * square)
            )
            grad_gate = (grad_mixed * u * slope).astype(low)
            grad_up = (grad_mixed * gelu).astype(low)
            r.tiles[2 + i] = grad_gate
            r.tiles[11 + i] = grad_up
            acc[...] += dot_nt(grad_gate, wg[slot])
            acc[...] += dot_nt(grad_up, wu[slot])
            return carry

        lax.fori_loop(0, 9, step, 0)
        for copy in first[2:]:
            copy.wait()
        r.y_out[...] = acc[...].astype(low)

    dma = pltpu.SemaphoreType.DMA
    pl.run_scoped(
        feed_forward,
        pltpu.VMEM((rows, width), low),
        pltpu.VMEM((2, WIDE, width), low),
        pltpu.VMEM((2, width, WIDE), low),
        pltpu.VMEM((2, width, WIDE), low),
        pltpu.VMEM((2, rows, WIDE), f32),
        pltpu.VMEM((2, rows, WIDE), f32),
        pltpu.VMEM((rows, width), f32),
    )

    def attention(loaded, names, *scoped):
        b = types.SimpleNamespace(**dict(zip(names, scoped)))
        made = {
            name: pltpu.make_async_copy(getattr(r, name), getattr(b, name), b.sems.at[n])
            for n, name in enumerate(loaded)
        }
        for copy in made.values():
            copy.start()
        loads = types.SimpleNamespace(**made)
        heads = r.queries.shape[1] // 256

        def gains_copy(n):
            to_seq, to_head = ((seq, 1 - head), (seq ^ 1, head), (seq ^ 2, head))[n]
            return remote(
                r.gains.at[n], r.gains_in.at[n], r.gains_send.at[n], r.gains_recv.at[n],
                to_seq, to_head,
            )

        def gains_level(z):
            return remote(
                r.gains.at[3], r.gains_z.at[level], r.level_send.at[z], r.level_recv.at[level],
                z * 4 + side * 2 + core, head,
            )

        def gains_from(z):
            return remote(
                r.gains.at[3], r.gains_z.at[z], r.level_send.at[z], r.level_recv.at[z],
                z * 4 + side * 2 + core, head,
            )

        def norms():
            y_arrived(0)
            y_sent(0)
            for copy in (loads.residual_mid, loads.attn_branch, loads.cotangent, loads.gain_rows, loads.head_gains):
                copy.wait()
            loads.gain_start.wait()
            gain_post, gain_pre = b.gain_rows[1:2, :], b.gain_rows[2:3, :]
            size = 128

            def chunk(c, sums):
                at = pl.ds(pl.multiple_of(c * size, size), size)
                grad_mid = r.y_out[at, :].astype(f32) + r.y_in[0, at, :].astype(f32)
                scale, normed = norm_parts(b.residual_mid[at, :])
                back, pre = norm_back(grad_mid, gain_pre, scale, normed)
                grad_residual = b.cotangent[at, :].astype(f32) + back
                b.residual_mid[at, :] = grad_residual
                scale, normed = norm_parts(b.attn_branch[at, :])
                back, post = norm_back(grad_residual, gain_post, scale, normed)
                r.y_out[at, :] = back.astype(low)
                return sums[0] + post, sums[1] + pre

            zero = jnp.zeros((1, width), f32)
            post, pre = lax.fori_loop(0, rows // size, chunk, (zero, zero))
            r.gains[0] = b.gain_start[...]
            r.gains[0, 1:2, :] = post
            r.gains[0, 2:3, :] = pre

        def through_out():
            for copy in (loads.w_out, loads.attended, loads.lse):
                copy.wait()
            b.grad_attended[...] = dot_nt(r.y_out[...], b.w_out[...]).astype(low)
            for h in range(heads):
                at = slice(256 * h, 256 * h + 256)
                delta = jnp.sum(
                    b.grad_attended[:, at].astype(f32) * b.attended[:, at], axis=1, keepdims=True
                )
                b.delta[h : h + 1, :] = jnp.broadcast_to(delta, (rows, 128)).T[:1]
            to_blocks(r.lefts.at[0], r.y_out[...], slice(0, rows))
            r.tiles[4, :, 256:] = b.attended[:, :128].astype(low)
            r.tiles[5] = b.attended[:, 128:].astype(low)

        def attend(block):
            if block == 0:
                for copy in (loads.queries, loads.keys, loads.values, loads.ids_out):
                    copy.wait()
                b.grad_queries[...] = jnp.zeros_like(b.grad_queries)
                b.ids_turned[...] = jnp.broadcast_to(b.ids_out[:1], (128, 3 * rows)).T
            size = 256

            def chunk(c, carry):
                local = pl.multiple_of(c * size, size)
                at = pl.ds(pl.multiple_of(block * rows + c * size, size), size)
                keys, values = b.keys[at, :], b.values[at, :]
                seen = b.ids_turned[at, :1] == b.ids_out[:1, 2 * rows :]
                if block == 2:
                    key_at = lax.broadcasted_iota(jnp.int32, (size, rows), 0) + local
                    query_at = lax.broadcasted_iota(jnp.int32, (size, rows), 1)
                    seen = seen & (key_at <= query_at)
                grad_keys = jnp.zeros((size, 256), f32)
                grad_values = jnp.zeros((size, 256), f32)
                for h in range(heads):
                    head_at = slice(256 * h, 256 * h + 256)
                    q, grad_out = b.queries[:, head_at], b.grad_attended[:, head_at]
                    probs = jnp.where(
                        seen, jnp.exp(dot_nt(keys, q) - b.lse[h : h + 1, :]), 0.0
                    )
                    grad_probs = dot_nt(values, grad_out)
                    grad_scores = (probs * (grad_probs - b.delta[h : h + 1, :])).astype(low)
                    grad_keys += jnp.dot(grad_scores, q, preferred_element_type=f32)
                    grad_values += jnp.dot(
                        probs.astype(low), grad_out, preferred_element_type=f32
                    )
                    b.grad_queries[:, head_at] += dot_tn(grad_scores, keys)
                to = pl.ds(local, size)
                if block == 2:
                    b.grad_own[0, to, :] = grad_keys
                    b.grad_own[1, to, :] = grad_values
                else:
                    r.halo_out[block, 0, to, :] = grad_keys.astype(low)
                    r.halo_out[block, 1, to, :] = grad_values.astype(low)
                return carry

            lax.fori_loop(0, rows // size, chunk, 0)
            if block == 0:
                @pl.when((seq >= 2) & (core == 1))
                def _():
                    relay_copy().start()

                halo_start(0, 0)

            if block == 1:
                @pl.when((core == 0) & (seq >= 2))
                def _():
                    remote(
                        r.halo_out.at[0], r.relay_in, r.relay_send, r.relay_recv, seq ^ 1, head
                    ).wait_recv()
                    for n in range(2):
                        r.halo_out[1, n] = (
                            r.halo_out[1, n].astype(f32) + r.relay_in[n].astype(f32)
                        ).astype(low)

        def relay_copy():
            return remote(
                r.halo_out.at[0], r.relay_in, r.relay_send, r.relay_recv, seq - 1, head
            )

        def halo_part(block, n, half):
            at = pl.ds(half * (rows // 2), rows // 2)
            return remote(
                r.halo_out.at[block, n, at, :], r.halo_in.at[block, n, at, :],
                r.halo_send.at[block, n, half], r.halo_recv.at[block, n, half],
                seq - (2 - block), head,
            )

        def halo_start(block, n):
            @pl.when((seq >= 1) if block == 1 else (seq >= 2) & (core == 0))
            def _():
                for half in range(2):
                    halo_part(block, n, half).start()

        def halo_parts(block):
            return [halo_part(block, n, half) for n in range(2) for half in range(2)]

        def query_side():
            for copy in (loads.query_proj, loads.cosine_out, loads.sine_out, loads.w_query):
                copy.wait()
            total = jnp.zeros((1, 256), f32)
            for h in range(heads):
                at = slice(256 * h, 256 * h + 256)
                grad = rotate_back(
                    b.grad_queries[:, at] * QUERY_SCALE, b.cosine_out[...], b.sine_out[...]
                )
                scale, normed = norm_parts(b.query_proj[:, at])
                back, gain = norm_back(grad, b.head_gains[0:1, :], scale, normed)
                total += gain
                back = back.astype(low)
                if h == 0:
                    r.tiles[2, :, :256] = back
                else:
                    r.tiles[2, :, 256:] = back[:, :128]
                    r.tiles[3, :, :128] = back[:, 128:]
                part = dot_nt(back, b.w_query[:, at])
                if h == 0:
                    b.attn_branch[...] = part
                else:
                    b.attn_branch[...] += part
            r.gains[0, 4:5, :256] = total

        def key_side():
            for copy in (loads.key_proj, loads.w_key, loads.w_value, loads.inputs):
                copy.wait()
            for block in range(2):
                heard = seq + (2 - block) <= last_seq

                @pl.when(heard & (core == 0) if block == 0 else heard)
                def _():
                    for copy in halo_parts(block):
                        copy.wait_recv()
                    for n in range(2):
                        b.grad_own[n] += r.halo_in[block, n].astype(f32)

            grad = rotate_back(b.grad_own[0], b.cosine_out[...], b.sine_out[...])
            scale, normed = norm_parts(b.key_proj[...])
            back, gain = norm_back(grad, b.head_gains[1:2, :], scale, normed)
            r.gains[0, 4:5, 256:512] = gain
            grad_key, grad_value = back.astype(low), b.grad_own[1].astype(low)
            r.tiles[3, :, 128:] = grad_key
            r.tiles[4, :, :256] = grad_value
            b.attn_branch[...] += dot_nt(grad_key, b.w_key[...])
            b.attn_branch[...] += dot_nt(grad_value, b.w_value[...])
            size = 128

            def chunk(c, total):
                at = pl.ds(pl.multiple_of(c * size, size), size)
                part = b.attn_branch[at, :]
                scale, normed = norm_parts(b.inputs[at, :].astype(f32))
                r.y_out[at, :] = part.astype(low)
                return total + jnp.sum(part * normed, axis=0, keepdims=True)

            zero = jnp.zeros((1, width), f32)
            r.gains[0, 0:1, :] = lax.fori_loop(0, rows // size, chunk, zero)
            gains_copy(0).start()

        def gains_stage(n):
            gains_copy(n).wait_recv()
            own, other = r.gains[n], r.gains_in[n]
            if n == 0:
                row = lax.broadcasted_iota(jnp.int32, own.shape, 0)
                other = jnp.where((row == 0) | (row == 4), other, 0.0)
            r.gains[n + 1] = own + other
            if n < 2:
                gains_copy(n + 1).start()
            else:
                for z in range(4):
                    @pl.when(level == z)
                    def _():
                        r.gains_z[z] = r.gains[3]

                    @pl.when(level != z)
                    def _():
                        gains_level(z).start()

        def gains_end():
            for z in range(4):
                @pl.when(level != z)
                def _():
                    gains_from(z).wait_recv()

            r.gains_out[...] = (r.gains_z[0] + r.gains_z[1]) + (r.gains_z[2] + r.gains_z[3])

        def finish_inputs():
            y_arrived(1)
            size = 128

            def chunk(c, carry):
                at = pl.ds(pl.multiple_of(c * size, size), size)
                grad = r.y_out[at, :].astype(f32) + r.y_in[1, at, :].astype(f32)
                scale, normed = norm_parts(b.inputs[at, :].astype(f32))
                back, _ = norm_back(grad, b.gain_rows[0:1, :], scale, normed)
                r.inputs_out[at, :] = (b.residual_mid[at, :] + back).astype(low)
                return carry

            lax.fori_loop(0, rows // size, chunk, 0)

        def kv_copy():
            return remote(r.kv_own, r.kv_in, r.kv_send, r.kv_recv, seq, 1 - head)

        pieces = (
            *((9 + n, functools.partial(y_start, 0, 2 * n)) for n in range(4)),
            (16, norms),
            (17, through_out),
            (18, lambda: attend(0)),
            (19, lambda: halo_start(0, 1)),
            (19, lambda: attend(1)),
            (20, lambda: halo_start(1, 0)),
            (20, lambda: attend(2)),
            (21, lambda: halo_start(1, 1)),
            (21, query_side),
            (24, key_side),
            *((24 + n, functools.partial(y_start, 1, 2 * n)) for n in range(4)),
            (25, lambda: gains_stage(0)),
            (26, lambda: gains_stage(1)),
            (27, lambda: gains_stage(2)),
            (29, gains_end),
            (32, finish_inputs),
            (FIRST_SIDE + 3 + LAG_Z, lambda: kv_copy().start()),
        )

        def step(i, carry):
            for k, piece in pieces:
                @pl.when(i == k)
                def _():
                    piece()

            pump(i)
            return carry

        lax.fori_loop(9, STEPS + LAG_Z, step, 0)
        kv_copy().wait()
        r.kv_out[...] = r.kv_own[...] + r.kv_in[...]
        y_sent(1)
        for n in range(3):
            gains_copy(n).wait_send()
        for z in range(4):
            @pl.when(level != z)
            def _():
                gains_level(z).wait_send()

        @pl.when((seq >= 2) & (core == 1))
        def _():
            relay_copy().wait_send()

        @pl.when((seq >= 2) & (core == 0))
        def _():
            for copy in halo_parts(0):
                copy.wait_send()

        @pl.when(seq >= 1)
        def _():
            for copy in halo_parts(1):
                copy.wait_send()

    heads_width = r.queries.shape[1]
    def shape(size, kind):
        return pltpu.VMEM(size, kind)

    loaded = dict(
        residual_mid=shape((rows, width), f32),
        attn_branch=shape((rows, width), f32),
        cotangent=shape((rows, width), low),
        inputs=shape((rows, width), low),
        gain_rows=shape((8, width), f32),
        head_gains=shape((8, 256), f32),
        gain_start=shape((8, width), f32),
        w_out=shape((heads_width, width), low),
        attended=shape((rows, heads_width), f32),
        lse=shape((8, rows), f32),
        queries=shape((rows, heads_width), low),
        keys=shape((3 * rows, 256), low),
        values=shape((3 * rows, 256), low),
        ids_out=shape((8, 3 * rows), f32),
        query_proj=shape((rows, heads_width), f32),
        key_proj=shape((rows, 256), f32),
        cosine_out=shape((rows, 128), f32),
        sine_out=shape((rows, 128), f32),
        w_query=shape((width, heads_width), low),
        w_key=shape((width, 256), low),
        w_value=shape((width, 256), low),
    )
    scoped = dict(
        loaded,
        grad_attended=shape((rows, heads_width), low),
        delta=shape((8, rows), f32),
        grad_queries=shape((rows, heads_width), f32),
        grad_own=shape((2, rows, 256), f32),
        ids_turned=shape((3 * rows, 128), f32),
        sems=dma((len(loaded),)),
    )
    pl.run_scoped(functools.partial(attention, tuple(loaded), tuple(scoped)), *scoped.values())

    def drain(i, carry):
        @pl.when(i >= STEPS - 2)
        def _():
            core_copy(i).wait_send()
            out_wait(i)

        x_copy(i).wait_send()
        for k in range(4):
            @pl.when(targets[k] != seq)
            def _():
                z_copy(i, k).wait_send()

        return carry

    lax.fori_loop(STEPS - RING, STEPS, drain, 0)


def backward(operands):
    low, f32 = jnp.bfloat16, jnp.float32
    dma = pltpu.SemaphoreType.DMA
    rows, width = operands["grad_ffn"].shape
    hidden = operands["w_gate"].shape[1]
    wide = operands["w_query"].shape[1]
    anywhere = pl.BlockSpec(memory_space=pl.ANY)
    vmem = pl.BlockSpec(memory_space=pltpu.VMEM)
    outs = dict(
        down_out=(jax.ShapeDtypeStruct((BLOCK, hidden), f32), anywhere),
        gate_out=(jax.ShapeDtypeStruct((BLOCK, hidden), f32), anywhere),
        up_out=(jax.ShapeDtypeStruct((BLOCK, hidden), f32), anywhere),
        query_out=(jax.ShapeDtypeStruct((BLOCK, wide), f32), anywhere),
        out_out=(jax.ShapeDtypeStruct((BLOCK, wide), f32), anywhere),
        kv_out=(jax.ShapeDtypeStruct((BLOCK, 512), f32), vmem),
        gains_out=(jax.ShapeDtypeStruct((8, width), f32), vmem),
        inputs_out=(jax.ShapeDtypeStruct((rows, width), low), vmem),
    )
    scratch = dict(
        held=pltpu.VMEM((RING, 2, 4, BLOCK, WIDE), low),
        sent=pltpu.VMEM((2, 2, 4, BLOCK, WIDE), low),
        core_in=pltpu.VMEM((RING, 2, 4, BLOCK, WIDE), low),
        x_in=pltpu.VMEM((RING, 4, BLOCK, WIDE), low),
        m_in=pltpu.VMEM((RING, 2, BLOCK, WIDE), low),
        z_out=pltpu.VMEM((RING, 4, BLOCK, WIDE), low),
        z_in=pltpu.VMEM((STEPS, 4, BLOCK, WIDE), low),
        tiles=pltpu.VMEM((20, rows, WIDE), low),
        lefts=pltpu.VMEM((3, width, rows), low),
        y_out=pltpu.VMEM((rows, width), low),
        y_in=pltpu.VMEM((2, rows, width), low),
        halo_out=pltpu.VMEM((2, 2, rows, 256), low),
        halo_in=pltpu.VMEM((2, 2, rows, 256), low),
        relay_in=pltpu.VMEM((2, rows, 256), low),
        gains=pltpu.VMEM((4, 8, width), f32),
        gains_in=pltpu.VMEM((3, 8, width), f32),
        gains_z=pltpu.VMEM((4, 8, width), f32),
        kv_own=pltpu.VMEM((BLOCK, 512), f32),
        kv_in=pltpu.VMEM((BLOCK, 512), f32),
        flat=pltpu.VMEM((2, BLOCK, WIDE), f32),
        core_send=dma((STEPS,)),
        core_recv=dma((STEPS,)),
        x_send=dma((STEPS,)),
        x_recv=dma((STEPS,)),
        z_send=dma((STEPS, 4)),
        z_recv=dma((STEPS, 4)),
        out_sem=dma((STEPS,)),
        y_send=dma((2, Y_PARTS)),
        y_recv=dma((2, Y_PARTS)),
        halo_send=dma((2, 2, 2)),
        halo_recv=dma((2, 2, 2)),
        gains_send=dma((3,)),
        gains_recv=dma((3,)),
        level_send=dma((4,)),
        level_recv=dma((4,)),
        kv_send=dma(()),
        kv_recv=dma(()),
        tile_sems=dma((6, 2)),
        grad_sem=dma(()),
        left_sem=dma((3,)),
        m_recv=dma((STEPS, 2)),
        m_free=pltpu.SemaphoreType.REGULAR,
        relay_send=dma(()),
        relay_recv=dma(()),
        core_free=pltpu.SemaphoreType.REGULAR,
        x_free=pltpu.SemaphoreType.REGULAR,
    )
    names = (*operands, *outs, *scratch)
    results = pl.pallas_call(
        functools.partial(backward_kernel, names),
        out_shape=[shape for shape, _ in outs.values()],
        in_specs=[anywhere] * len(operands),
        out_specs=[spec for _, spec in outs.values()],
        scratch_shapes=list(scratch.values()),
        compiler_params=pltpu.CompilerParams(
            collective_id=1, has_side_effects=True, vmem_limit_bytes=62 << 20
        ),
        name="backward",
    )(*operands.values())
    return dict(zip(outs, results))


def last_kernel(names, *refs):
    r = types.SimpleNamespace(**dict(zip(names, refs)))
    place = lax.axis_index("seq")
    pairs = (
        (r.output, r.output_held, r.output_end),
        (r.inputs_out, r.inputs_held, r.inputs_end),
        (r.gate_out, r.gate_held, r.gate_end),
        (r.up_out, r.up_held, r.up_end),
        (r.down_out, r.down_held, r.down_end),
        (r.query_out, r.query_held, r.query_end),
        (r.out_out, r.out_held, r.out_end),
        (r.kv_out.at[:, pl.ds(0, 256)], r.key_held, r.key_end),
        (r.kv_out.at[:, pl.ds(256, 256)], r.value_held, r.value_end),
    )
    loads = [
        pltpu.make_async_copy(src, held, r.sems.at[0, n]) for n, (src, held, _) in enumerate(pairs)
    ]
    copies = [
        pltpu.make_async_copy(held, dst, r.sems.at[1, n]) for n, (_, held, dst) in enumerate(pairs)
    ]
    for copy in loads:
        copy.start()
    width = r.gains_out.shape[1]
    rolled = pltpu.roll(r.gains_out[...], lax.rem(width - place * BLOCK, width), 1)
    for n, target in enumerate((r.in_end, r.post_attn_end, r.pre_ffn_end, r.post_ffn_end)):
        target[...] = rolled[n : n + 1, :BLOCK].reshape(BLOCK)
    own = r.gain_query_end.shape[0]
    for n, target in enumerate((r.gain_query_end, r.gain_key_end)):
        rolled = pltpu.roll(r.gains_out[...], lax.rem(2 * width - place * own - 256 * n, width), 1)
        target[...] = rolled[4:5, :own].reshape(own)
    for load, copy in zip(loads, copies):
        load.wait()
        copy.start()
    for copy in copies:
        copy.wait()


def last(operands):
    f32 = jnp.float32
    anywhere = pl.BlockSpec(memory_space=pl.ANY)
    vmem = pl.BlockSpec(memory_space=pltpu.VMEM)
    shape = jax.ShapeDtypeStruct
    like = types.SimpleNamespace(**operands)
    part = shape((BLOCK, 256), f32)
    gain = shape((BLOCK,), f32)
    small = shape((256 // lax.axis_size("seq"),), f32)
    outs = dict(
        output_end=like.output,
        inputs_end=like.inputs_out,
        query_end=like.query_out,
        key_end=part,
        value_end=part,
        out_end=like.out_out,
        gate_end=like.gate_out,
        up_end=like.up_out,
        down_end=like.down_out,
        in_end=gain,
        gain_query_end=small,
        gain_key_end=small,
        post_attn_end=gain,
        pre_ffn_end=gain,
        post_ffn_end=gain,
    )
    held = dict(
        output_held=like.output,
        inputs_held=like.inputs_out,
        gate_held=like.gate_out,
        up_held=like.up_out,
        down_held=like.down_out,
        query_held=like.query_out,
        out_held=like.out_out,
        key_held=part,
        value_held=part,
    )
    names = (*operands, *outs, *held, *dict(sems=0))
    return pl.pallas_call(
        functools.partial(last_kernel, names),
        out_shape=[shape(a.shape, a.dtype) for a in outs.values()],
        in_specs=[vmem if name == "gains_out" else anywhere for name in operands],
        out_specs=[vmem if len(a.shape) == 1 else anywhere for a in outs.values()],
        scratch_shapes=[pltpu.VMEM(a.shape, a.dtype) for a in held.values()]
        + [pltpu.SemaphoreType.DMA((2, len(held)))],
        name="last",
    )(*operands.values())


def fast_device(
    inputs,
    segment_ids,
    w_query,
    w_key,
    w_value,
    w_out,
    w_gate,
    w_up,
    w_down,
    gain_in,
    gain_query,
    gain_key,
    gain_post_attn,
    gain_pre_ffn,
    gain_post_ffn,
    cotangent,
):
    shared = dict(
        inputs=inputs, cotangent=cotangent, w_query=w_query, w_key=w_key, w_value=w_value,
        w_out=w_out, w_gate=w_gate, w_up=w_up, w_down=w_down,
    )
    first = forward(
        dict(
            shared,
            segment_ids=segment_ids, gain_in=gain_in, gain_query=gain_query, gain_key=gain_key,
            gain_post_attn=gain_post_attn, gain_pre_ffn=gain_pre_ffn, gain_post_ffn=gain_post_ffn,
        )
    )
    output = first.pop("output")
    results = last(dict(backward(dict(shared, **first)), output=output))
    return tuple(a.T if n in (5, 8) else a for n, a in enumerate(results))


def scatter_rows(grad):
    return lax.psum_scatter(grad, "seq", scatter_dimension=0, tiled=True).astype(jnp.float32)


def per_device(
    inputs,
    segment_ids,
    w_query,
    w_key,
    w_value,
    w_out,
    w_gate,
    w_up,
    w_down,
    gain_in,
    gain_query,
    gain_key,
    gain_post_attn,
    gain_pre_ffn,
    gain_post_ffn,
    cotangent,
):
    rows = inputs.shape[0]
    head_dim = w_key.shape[1]
    local_heads = w_query.shape[1] // head_dim
    place = lax.axis_index("seq")
    local_index = jnp.arange(rows, dtype=jnp.int32)
    ids_parts = [
        jnp.where(place >= distance, from_behind(segment_ids, "seq", distance), -1)
        for distance in (2, 1)
    ]
    window_ids = jnp.concatenate(ids_parts + [segment_ids], axis=0)
    window_index = jnp.arange(3 * rows, dtype=jnp.int32) - 2 * rows
    same = segment_ids[:, None] == window_ids[None, :]
    visible = same & (window_index[None, :] <= local_index[:, None])
    positions = jnp.sum(visible.astype(jnp.int32), axis=1) - 1
    cosine, sine = rope_angles(positions, head_dim)
    inputs_f = inputs.astype(jnp.float32)
    hidden_in = rms_scale(inputs_f, gain_in).astype(jnp.bfloat16)
    query_proj = jnp.dot(hidden_in, w_query, preferred_element_type=jnp.float32)
    key_proj = jnp.dot(hidden_in, w_key, preferred_element_type=jnp.float32)
    value_proj = jnp.dot(hidden_in, w_value, preferred_element_type=jnp.float32)

    def query_side(projection, gain):
        return prepare(
            projection.reshape(rows, local_heads, head_dim), gain, cosine, sine, QUERY_SCALE
        )

    def key_side(projection, gain):
        return prepare(projection[:, None, :], gain, cosine, sine, 1.0)[:, 0, :]

    queries = query_side(query_proj, gain_query).astype(jnp.bfloat16)
    own_keys = key_side(key_proj, gain_key).astype(jnp.bfloat16)
    own_values = value_proj.astype(jnp.bfloat16)
    key_parts = []
    value_parts = []
    for distance in (2, 1):
        moved_keys, moved_values = from_behind((own_keys, own_values), "seq", distance)
        key_parts.append(moved_keys)
        value_parts.append(moved_values)
    all_keys = jnp.concatenate(key_parts + [own_keys], axis=0)
    all_values = jnp.concatenate(value_parts + [own_values], axis=0)
    def raw_scores():
        return jnp.einsum("ihd,jd->hij", queries, all_keys, preferred_element_type=jnp.float32)

    scores = jnp.where(visible[None], raw_scores(), -1e30)
    row_max = jnp.max(scores, axis=-1, keepdims=True)
    expo = jnp.exp(scores - row_max)
    total = jnp.sum(expo, axis=-1, keepdims=True)
    attn_probs = expo / total
    log_total = row_max + jnp.log(total)
    attended = jnp.einsum(
        "hij,jd->ihd",
        attn_probs.astype(jnp.bfloat16),
        all_values,
        preferred_element_type=jnp.float32,
    )
    attended = attended.reshape(rows, local_heads * head_dim).astype(jnp.bfloat16)
    attn_branch = over_head(jnp.dot(attended, w_out, preferred_element_type=jnp.float32))
    residual_mid = inputs_f + rms_scale(attn_branch, gain_post_attn)
    hidden_mid = rms_scale(residual_mid, gain_pre_ffn).astype(jnp.bfloat16)
    gate_act = jnp.dot(hidden_mid, w_gate, preferred_element_type=jnp.float32)
    up_proj = jnp.dot(hidden_mid, w_up, preferred_element_type=jnp.float32)
    mixed_low = gated(gate_act, up_proj).astype(jnp.bfloat16)
    ffn_branch = over_head(jnp.dot(mixed_low, w_down, preferred_element_type=jnp.float32))
    output_f = residual_mid + rms_scale(ffn_branch, gain_post_ffn)
    grad_output = cotangent.astype(jnp.float32)
    unused_post, post_back = jax.vjp(rms_scale, ffn_branch, gain_post_ffn)
    grad_ffn, grad_g_post_ffn = post_back(grad_output)
    grad_ffn_low = grad_ffn.astype(jnp.bfloat16)
    grad_w_down = jnp.dot(grad_ffn_low.T, mixed_low, preferred_element_type=jnp.float32)
    summed_down = scatter_rows(grad_w_down.astype(jnp.bfloat16))
    grad_mixed = jnp.dot(grad_ffn_low, w_down.T, preferred_element_type=jnp.float32)
    unused_gate, gate_back = jax.vjp(gated, gate_act, up_proj)
    grad_gate, grad_up = gate_back(grad_mixed)
    grad_gate_low = grad_gate.astype(jnp.bfloat16)
    grad_up_low = grad_up.astype(jnp.bfloat16)
    grad_w_gate = jnp.dot(hidden_mid.T, grad_gate_low, preferred_element_type=jnp.float32)
    grad_w_up = jnp.dot(hidden_mid.T, grad_up_low, preferred_element_type=jnp.float32)
    summed_gate = scatter_rows(grad_w_gate.astype(jnp.bfloat16))
    summed_up = scatter_rows(grad_w_up.astype(jnp.bfloat16))
    grad_hidden_part = jnp.dot(
        grad_gate_low, w_gate.T, preferred_element_type=jnp.float32
    ) + jnp.dot(grad_up_low, w_up.T, preferred_element_type=jnp.float32)
    grad_hidden_mid = over_head(grad_hidden_part)
    unused_pre, pre_back = jax.vjp(rms_scale, residual_mid, gain_pre_ffn)
    grad_res_part, grad_g_pre_ffn = pre_back(grad_hidden_mid)
    grad_residual = grad_output + grad_res_part
    unused_attn, attn_post_back = jax.vjp(rms_scale, attn_branch, gain_post_attn)
    grad_attn, grad_g_post_attn = attn_post_back(grad_residual)
    grad_attn_low = grad_attn.astype(jnp.bfloat16)
    grad_w_out = jnp.dot(grad_attn_low.T, attended, preferred_element_type=jnp.float32)
    grad_attended = jnp.dot(grad_attn_low, w_out.T, preferred_element_type=jnp.float32).astype(
        jnp.bfloat16
    )
    grad_attended = grad_attended.reshape(rows, local_heads, head_dim)
    probs_again = jnp.where(visible[None], jnp.exp(raw_scores() - log_total), 0.0)
    grad_probs = jnp.einsum(
        "ihd,jd->hij", grad_attended, all_values, preferred_element_type=jnp.float32
    )
    grad_scores = (
        probs_again * (grad_probs - jnp.sum(probs_again * grad_probs, axis=-1, keepdims=True))
    ).astype(jnp.bfloat16)
    grad_queries = jnp.einsum(
        "hij,jd->ihd", grad_scores, all_keys, preferred_element_type=jnp.float32
    )
    grad_keys_all = jnp.einsum(
        "hij,ihd->jd", grad_scores, queries, preferred_element_type=jnp.float32
    )
    grad_values_all = jnp.einsum(
        "hij,ihd->jd",
        probs_again.astype(jnp.bfloat16),
        grad_attended,
        preferred_element_type=jnp.float32,
    )
    grad_keys = grad_keys_all[2 * rows :]
    grad_values = grad_values_all[2 * rows :]
    for distance in (2, 1):
        piece_begin = (2 - distance) * rows
        returned_keys, returned_values = (
            from_behind(
                grad_keys_all[piece_begin : piece_begin + rows].astype(jnp.bfloat16),
                "seq",
                -distance,
            ).astype(jnp.float32),
            from_behind(
                grad_values_all[piece_begin : piece_begin + rows].astype(jnp.bfloat16),
                "seq",
                -distance,
            ).astype(jnp.float32),
        )
        grad_keys = grad_keys + returned_keys
        grad_values = grad_values + returned_values
    unused_query, query_back = jax.vjp(query_side, query_proj, gain_query)
    grad_query_proj, grad_g_query_part = query_back(grad_queries)
    grad_query_low = grad_query_proj.astype(jnp.bfloat16)
    grad_w_query = jnp.dot(hidden_in.T, grad_query_low, preferred_element_type=jnp.float32)
    grad_hidden_query = jnp.dot(grad_query_low, w_query.T, preferred_element_type=jnp.float32)
    keys_summed, values_summed, hidden_summed, grad_g_query = (
        over_head(grad_keys),
        over_head(grad_values),
        over_head(grad_hidden_query),
        over_head(grad_g_query_part),
    )
    unused_key, key_back = jax.vjp(key_side, key_proj, gain_key)
    grad_key_proj, grad_g_key = key_back(keys_summed)
    grad_key_low = grad_key_proj.astype(jnp.bfloat16)
    grad_value_low = values_summed.astype(jnp.bfloat16)
    grad_w_key = jnp.dot(hidden_in.T, grad_key_low, preferred_element_type=jnp.float32)
    grad_w_value = jnp.dot(hidden_in.T, grad_value_low, preferred_element_type=jnp.float32)
    grad_hidden_in = (
        hidden_summed
        + jnp.dot(grad_key_low, w_key.T, preferred_element_type=jnp.float32)
        + jnp.dot(grad_value_low, w_value.T, preferred_element_type=jnp.float32)
    )
    unused_in, in_back = jax.vjp(rms_scale, inputs_f, gain_in)
    grad_in_part, grad_g_in = in_back(grad_hidden_in)
    grad_inputs = (grad_residual + grad_in_part).astype(jnp.bfloat16)
    count = lax.axis_size("seq")
    gain_columns = jnp.stack(
        [grad_g_in, grad_g_post_attn, grad_g_pre_ffn, grad_g_post_ffn], axis=1
    )
    side = jnp.concatenate(
        [grad_g_query.reshape(count, -1), grad_g_key.reshape(count, -1)], axis=1
    )
    side_rows = jnp.repeat(side, inputs.shape[1] // count, axis=0)
    extra = jnp.concatenate([gain_columns, side_rows], axis=1)
    extra = jnp.pad(extra, ((0, 0), (0, -extra.shape[1] % 128)))
    widths = [g.shape[1] for g in (grad_w_query, grad_w_out, grad_w_key, grad_w_value)]
    attn_sum = scatter_rows(
        jnp.concatenate(
            [
                g.astype(jnp.bfloat16)
                for g in (grad_w_query, grad_w_out, grad_w_key, grad_w_value, extra)
            ],
            axis=1,
        )
    )
    edges = [sum(widths[:i]) for i in range(5)]
    summed_query, summed_out, summed_key, summed_value = (
        attn_sum[:, edges[i] : edges[i + 1]] for i in range(4)
    )
    gain_sum = attn_sum[:, edges[4] :]
    summed_g_in, summed_g_post_attn, summed_g_pre_ffn, summed_g_post_ffn = (
        gain_sum[:, i] for i in range(4)
    )
    own = head_dim // count
    summed_g_query = gain_sum[0, 4 : 4 + own]
    summed_g_key = gain_sum[0, 4 + own : 4 + 2 * own]
    summed_out = summed_out.T
    summed_down = summed_down.T
    return (
        output_f.astype(jnp.bfloat16),
        grad_inputs,
        summed_query,
        summed_key,
        summed_value,
        summed_out,
        summed_gate,
        summed_up,
        summed_down,
        summed_g_in,
        summed_g_query,
        summed_g_key,
        summed_g_post_attn,
        summed_g_pre_ffn,
        summed_g_post_ffn,
    )


def solution(mesh):
    placed = (
        P("seq", None),
        P("seq"),
        P(None, "head"),
        P(),
        P(),
        P("head", None),
        P(None, "head"),
        P(None, "head"),
        P("head", None),
        P(),
        P(),
        P(),
        P(),
        P(),
        P(),
        P("seq", None),
    )
    return jax.shard_map(
        fast_device if mesh.shape["seq"] == 16 else per_device,
        mesh=mesh,
        in_specs=placed,
        out_specs=(
            P("seq", None),
            P("seq", None),
            P("seq", "head"),
            P("seq", None),
            P("seq", None),
            P("head", "seq"),
            P("seq", "head"),
            P("seq", "head"),
            P("head", "seq"),
            P("seq"),
            P("seq"),
            P("seq"),
            P("seq"),
            P("seq"),
            P("seq"),
        ),
        check_vma=False,
    )
```

```python
import functools
import math
import types

import jax
import jax.numpy as jnp
from jax import lax
from jax.experimental import pallas as pl
from jax.experimental.pallas import tpu as pltpu
from jax.sharding import PartitionSpec as P

MESH = pl.DeviceIdType.MESH
WIDE = 384
BLOCK = 72

EPS = 1e-06
QUERY_SCALE = 0.0625


def from_behind(block, axis, distance):
    devices = range(lax.axis_size(axis))
    route = [(i - distance, i) for i in devices if i - distance in devices]
    return lax.ppermute(block, axis, route)


def rms_scale(values, gain):
    return values * lax.rsqrt(jnp.mean(values * values, axis=-1, keepdims=True) + EPS) * gain


def rope_angles(positions, width):
    half_width = width // 2
    frequency = jnp.exp(
        jnp.arange(half_width, dtype=jnp.float32) * (-2.0 * math.log(1000000.0) / width)
    )
    angles = positions.astype(jnp.float32)[:, None] * frequency[None, :]
    return (jnp.cos(angles), jnp.sin(angles))


def rotate(values, cosine, sine):
    half_width = values.shape[-1] // 2
    first_half = values[..., :half_width]
    second_half = values[..., half_width:]
    cos_rows = cosine[:, None, :]
    sin_rows = sine[:, None, :]
    return jnp.concatenate(
        [
            first_half * cos_rows - second_half * sin_rows,
            second_half * cos_rows + first_half * sin_rows,
        ],
        axis=-1,
    )


def prepare(values, gain, cosine, sine, factor):
    return rotate(rms_scale(values, gain), cosine, sine) * factor


def gelu_tanh(values):
    return (
        0.5
        * values
        * (1.0 + jnp.tanh(0.7978845608028654 * (values + 0.044715 * values * values * values)))
    )


def gated(gate_act, up_proj):
    return gelu_tanh(gate_act) * up_proj


def over_head(part):
    low = part.astype(jnp.bfloat16)
    other = lax.ppermute(low, "head", [(0, 1), (1, 0)])
    return low.astype(jnp.float32) + other.astype(jnp.float32)


def place_of():
    seq = lax.axis_index("seq")
    return seq, lax.axis_index("head"), seq % 2, seq // 2 % 2, seq // 4


def dot_nt(left, right):
    return lax.dot_general(left, right, (((1,), (1,)), ((), ())), preferred_element_type=jnp.float32)


def dot_tn(left, right):
    return lax.dot_general(left, right, (((0,), (0,)), ((), ())), preferred_element_type=jnp.float32)


def rotate_back(grad, cosine, sine):
    half = grad.shape[-1] // 2
    first, second = grad[:, :half], grad[:, half:]
    return jnp.concatenate(
        [first * cosine + second * sine, second * cosine - first * sine], axis=-1
    )


def norm_parts(values):
    scale = lax.rsqrt(jnp.mean(values * values, axis=-1, keepdims=True) + EPS)
    return scale, values * scale


def norm_back(grad, gain, scale, normed):
    inner = grad * gain
    back = scale * (inner - normed * jnp.mean(inner * normed, axis=-1, keepdims=True))
    return back, jnp.sum(grad * normed, axis=0, keepdims=True)


CHUNKS = 4
FEEDS = 4
OUT_PARTS = 8


def turn(values, cosine, sine):
    half = values.shape[-1] // 2
    first, second = values[:, :half], values[:, half:]
    return jnp.concatenate(
        [first * cosine - second * sine, second * cosine + first * sine], axis=-1
    )


def to_blocks(target, values, columns):
    turned = values.astype(jnp.float32).T.astype(jnp.bfloat16)
    for half in range(2):
        for x in range(2):
            for f in range(2):
                source = 144 * ((2 * half + f) * 2 + x)
                to = 144 * (half * 4 + x * 2 + f)
                target[to : to + 144, columns] = turned[source : source + 144]


def forward_kernel(names, *refs):
    r = types.SimpleNamespace(**dict(zip(names, refs)))
    seq, head, core, side, level = place_of()
    last_seq = lax.axis_size("seq") - 1
    f32, low = jnp.float32, jnp.bfloat16
    rows, width = r.inputs.shape
    heads = r.w_query.shape[1] // 256
    hidden = r.w_gate.shape[1]
    size = rows // CHUNKS
    feed_size = rows // FEEDS
    even = core == 0

    barrier = pltpu.get_barrier_semaphore()

    def greet(to_seq, to_head):
        pl.semaphore_signal(barrier, inc=1, device_id=(to_seq, to_head), device_id_type=MESH)

    def load(n, src, dst):
        copy = pltpu.make_async_copy(src, dst, r.load_sem.at[n])
        copy.start()
        return copy

    in_copy = load(0, r.inputs, r.x)
    kv_copies = (load(2, r.w_key, r.wk), load(3, r.w_value, r.wv))
    query_copy = load(7, r.w_query, r.wq)
    out_copy = load(8, r.w_out, r.wo.at[head])
    steps = hidden // WIDE

    def tile_loads(j):
        at = pl.ds(pl.multiple_of(j * WIDE, WIDE), WIDE)
        gate_at = pl.ds(pl.multiple_of(2 * j * WIDE, WIDE), WIDE)
        up_at = pl.ds(pl.multiple_of((2 * j + 1) * WIDE, WIDE), WIDE)
        return (
            pltpu.make_async_copy(r.w_gate.at[:, at], r.wgu.at[:, gate_at], r.weight_sem.at[0, j]),
            pltpu.make_async_copy(r.w_up.at[:, at], r.wgu.at[:, up_at], r.weight_sem.at[1, j]),
        )

    for j in range(steps):
        for copy in tile_loads(j):
            copy.start()
    down_copy = load(11, r.w_down, r.wd)
    cot_copy = load(12, r.cotangent, r.cot)

    greet(seq ^ 1, head)
    greet(seq, 1 - head)
    expected = jnp.int32(2)
    for distance in (1, 2):
        @pl.when(seq >= distance)
        def _():
            greet(seq - distance, head)

        @pl.when(seq + distance <= last_seq)
        def _():
            greet(seq + distance, head)

        expected = (
            expected
            + (seq >= distance).astype(jnp.int32)
            + (seq + distance <= last_seq).astype(jnp.int32)
        )
    pl.semaphore_wait(barrier, expected)

    def remote(src, dst, send, recv, to_seq, to_head):
        return pltpu.make_async_remote_copy(
            src_ref=src,
            dst_ref=dst,
            send_sem=send,
            recv_sem=recv,
            device_id=(to_seq, to_head),
            device_id_type=MESH,
        )

    share = r.w_out.shape[0] // 2

    def out_share(which):
        return pl.ds(pl.multiple_of(which * share, share), share)

    def w_out_y(part):
        size = share // OUT_PARTS
        mine = pl.ds(pl.multiple_of(core * share + part * size, size), size)
        return remote(
            r.w_out.at[mine, :], r.wo.at[head, mine, :], r.out_send.at[part], r.out_recv.at[part],
            seq, 1 - head,
        )

    def w_out_start(first):
        for part in (first, first + 1):
            w_out_y(part).start()

    def w_out_core():
        mine = out_share(core)
        part = r.wo.at[1 - head, mine, :]
        return remote(part, part, r.wo_send, r.wo_recv, seq ^ 1, head)

    def ids_send(distance):
        return remote(
            r.ids.at[2], r.ids.at[2 - distance], r.ids_send.at[distance - 1],
            r.ids_recv.at[distance - 1], seq + distance, head,
        )

    def halo(n, distance, hand_on=False):
        kind = r.window.at[n]
        source = kind.at[pl.ds((1 if hand_on else 2) * rows, rows), :]
        target = kind.at[pl.ds((2 - distance) * rows, rows), :]
        place = 2 if hand_on else distance - 1
        return remote(
            source, target, r.halo_send.at[n, place], r.halo_recv.at[n, distance - 1],
            seq + (1 if hand_on else distance), head,
        )

    ids = r.segment_ids[...].astype(f32).reshape(1, rows)
    r.ids[2] = jnp.broadcast_to(ids, (8, rows))
    for distance in (1, 2):
        @pl.when(seq + distance <= last_seq)
        def _():
            ids_send(distance).start()

    w_out_start(0)

    r.gains[...] = jnp.zeros_like(r.gains)
    r.head_gain[...] = jnp.zeros_like(r.head_gain)
    for n, gain in enumerate((r.gain_in, r.gain_post_attn, r.gain_pre_ffn, r.gain_post_ffn)):
        r.gains[n : n + 1, :] = gain[...].reshape(1, width)
    for n, gain in enumerate((r.gain_query, r.gain_key)):
        r.head_gain[n : n + 1, :] = gain[...].reshape(1, 256)
    in_copy.wait()

    def norm_in(c, carry):
        at = pl.ds(pl.multiple_of(c * 128, 128), 128)
        _, normed = norm_parts(r.x[at, :].astype(f32))
        r.normed_in[at, :] = (normed * r.gains[0:1, :]).astype(low)
        return carry

    lax.fori_loop(0, rows // 128, norm_in, 0)
    w_out_start(2)
    for copy in kv_copies:
        copy.wait()
    r.key_raw[...] = jnp.dot(r.normed_in[...], r.wk[...], preferred_element_type=f32)
    r.window[1, 2 * rows :, :] = jnp.dot(
        r.normed_in[...], r.wv[...], preferred_element_type=f32
    ).astype(low)

    def value_halo(distance):
        return halo(1, distance)

    @pl.when(even & (seq + 2 <= last_seq))
    def _():
        value_halo(2).start()

    @pl.when(seq + 1 <= last_seq)
    def _():
        value_halo(1).start()

    w_out_start(4)

    for distance in (1, 2):
        @pl.when(seq >= distance)
        def _():
            remote(
                r.ids.at[2], r.ids.at[2 - distance], r.ids_send.at[distance - 1],
                r.ids_recv.at[distance - 1], seq ^ 1, head,
            ).wait_recv()

        @pl.when(seq < distance)
        def _():
            r.ids[2 - distance] = jnp.full((8, rows), -1.0, f32)

    ids_row = jnp.concatenate([r.ids[b][:1] for b in range(3)], axis=1)
    r.ids_flat[...] = jnp.broadcast_to(ids_row, (8, 3 * rows))
    ids_column = jnp.broadcast_to(r.ids[2][:1], (128, rows)).T
    r.ids_turned[...] = ids_column
    column = lax.broadcasted_iota(jnp.int32, (8, 128), 1).astype(f32)
    frequency = jnp.exp(column * (-2.0 * math.log(1000000.0) / 256))[:1]

    def angles(c, carry):
        at = pl.ds(pl.multiple_of(c * 128, 128), 128)
        here = lax.broadcasted_iota(jnp.int32, (128, 3 * rows), 0) + (2 * rows + c * 128)
        there = lax.broadcasted_iota(jnp.int32, (128, 3 * rows), 1)
        same = (r.ids_turned[at, :1] == r.ids_flat[:1, :]) & (there < here)
        position = jnp.sum(same.astype(f32), axis=1, keepdims=True)
        angle = position * frequency
        r.cosine[at, :] = jnp.cos(angle)
        r.sine[at, :] = jnp.sin(angle)
        return carry

    lax.fori_loop(0, rows // 128, angles, 0)
    _, normed = norm_parts(r.key_raw[...])
    r.window[0, 2 * rows :, :] = turn(
        normed * r.head_gain[1:2, :], r.cosine[...], r.sine[...]
    ).astype(low)

    @pl.when(even & (seq + 2 <= last_seq))
    def _():
        halo(0, 2).start()

    @pl.when(seq + 1 <= last_seq)
    def _():
        halo(0, 1).start()

    w_out_start(6)

    query_copy.wait()
    r.query_raw[...] = jnp.dot(r.normed_in[...], r.wq[...], preferred_element_type=f32)
    for h in range(heads):
        at = slice(256 * h, 256 * h + 256)
        _, normed = norm_parts(r.query_raw[:, at])
        r.q[:, at] = (
            turn(normed * r.head_gain[0:1, :], r.cosine[...], r.sine[...]) * QUERY_SCALE
        ).astype(low)

    def store(n, src, dst):
        copy = pltpu.make_async_copy(src, dst, r.store_sem.at[n])
        copy.start()
        return copy

    to_blocks(r.turned, r.normed_in[...], slice(0, rows))
    stores = [
        store(1, r.key_raw, r.key_proj),
        store(2, r.query_raw, r.query_proj),
        store(3, r.q, r.queries),
        store(4, r.cosine, r.cosine_out),
        store(5, r.sine, r.sine_out),
        store(6, r.ids_flat, r.ids_out),
        store(16, r.gains, r.gain_rows),
        store(17, r.head_gain, r.head_gains),
    ]
    turned_store = store(0, r.turned, r.left_in)

    out_copy.wait()
    for part in range(OUT_PARTS):
        w_out_y(part).wait()
    w_out_core().start()

    def arrival(n, distance):
        return halo(n, distance)

    for n in (1, 0):
        @pl.when(seq >= 1)
        def _():
            arrival(n, 1).wait_recv()

        @pl.when(even & (seq >= 2))
        def _():
            halo(n, 2, True).start()

    for n in (1, 0):
        @pl.when(seq >= 2)
        def _():
            arrival(n, 2).wait_recv()

    for distance in (1, 2):
        @pl.when(seq < distance)
        def _():
            for n in range(2):
                r.window[n, (2 - distance) * rows : (3 - distance) * rows, :] = jnp.zeros(
                    (rows, 256), low
                )

    def head_exchange(c):
        part = r.heads_all.at[head, pl.ds(pl.multiple_of(c * size, size), size), :]
        return remote(part, part, r.y_send.at[c], r.y_recv.at[c], seq, 1 - head)

    def branch_exchange(c):
        at = pl.ds(pl.multiple_of(c * feed_size, feed_size), feed_size)
        return remote(
            r.y_out.at[at, :], r.y_in.at[at, :], r.y_send.at[CHUNKS + c], r.y_recv.at[CHUNKS + c],
            seq, 1 - head,
        )

    def attend(c):
        first = c * size
        span = 2 * rows + size
        at = slice(first, first + size)
        key_at = slice(first, first + span)
        here = lax.broadcasted_iota(jnp.int32, (size, span), 0) + 2 * rows
        there = lax.broadcasted_iota(jnp.int32, (size, span), 1)
        seen = (r.ids_turned[at, :1] == r.ids_flat[:1, key_at]) & (there <= here)
        for h in range(heads):
            head_at = slice(256 * h, 256 * h + 256)
            scores = jnp.where(seen, dot_nt(r.q[at, head_at], r.window[0, key_at, :]), -1e30)
            top = jnp.max(scores, axis=1, keepdims=True)
            expo = jnp.exp(scores - top)
            total = jnp.sum(expo, axis=1, keepdims=True)
            probs = (expo / total).astype(low)
            out = jnp.dot(probs, r.window[1, key_at, :], preferred_element_type=f32)
            r.heads_f[at, head_at] = out
            r.heads_all[head, at, head_at] = out.astype(low)
            r.lse_rows[h : h + 1, at] = jnp.broadcast_to(top + jnp.log(total), (size, 128)).T[:1]
        head_exchange(c).start()

    for c in range(CHUNKS):
        attend(c)
    stores += [
        store(7, r.heads_f, r.attended),
        store(8, r.lse_rows, r.lse),
        store(9, r.window.at[0], r.keys),
        store(10, r.window.at[1], r.values),
    ]
    w_out_core().wait()
    turned_store.wait()

    def feed_rows(c):
        return pl.ds(pl.multiple_of(c * feed_size, feed_size), feed_size)

    def part_stores(c):
        slot = lax.rem(c, 2)
        return (
            pltpu.make_async_copy(
                r.gate_up_part.at[slot], r.gate_up.at[feed_rows(c), :], r.part_sem.at[0, slot]
            ),
            pltpu.make_async_copy(
                r.mixed_part.at[slot], r.mixed.at[feed_rows(c), :], r.part_sem.at[1, slot]
            ),
        )

    def feed(c, carry):
        at = feed_rows(c)
        slot = lax.rem(c, 2)
        head_exchange(c).wait_recv()
        branch = jnp.dot(r.heads_all[0, at, :], r.wo[0], preferred_element_type=f32) + jnp.dot(
            r.heads_all[1, at, :], r.wo[1], preferred_element_type=f32
        )
        r.branch[at, :] = branch
        _, normed = norm_parts(branch)
        middle = r.x[at, :].astype(f32) + normed * r.gains[1:2, :]
        r.middle[at, :] = middle
        _, normed = norm_parts(middle)
        left = (normed * r.gains[2:3, :]).astype(low)
        r.normed_mid[at, :] = left

        @pl.when(c >= 2)
        def _():
            for copy in part_stores(c - 2):
                copy.wait()

        def finish(j, both):
            double = slice(2 * j * WIDE, 2 * (j + 1) * WIDE)
            r.gate_up_part[slot, :, double] = both.astype(low)
            gate, up = both[:, :WIDE], both[:, WIDE:]
            curve = jnp.tanh(0.7978845608028654 * gate * (1.0 + 0.044715 * gate * gate))
            r.mixed_part[slot, :, j * WIDE : (j + 1) * WIDE] = (
                0.5 * gate * (1.0 + curve) * up
            ).astype(low)

        waiting = None
        for j in range(steps):
            double = slice(2 * j * WIDE, 2 * (j + 1) * WIDE)
            both = jnp.dot(left, r.wgu[:, double], preferred_element_type=f32)
            if waiting is not None:
                finish(j - 1, waiting)
            waiting = both
        finish(steps - 1, waiting)
        for copy in part_stores(c):
            copy.start()
        r.y_out[at, :] = jnp.dot(
            r.mixed_part[slot], r.wd[...], preferred_element_type=f32
        ).astype(low)
        branch_exchange(c).start()
        return carry

    for j in range(steps):
        for copy in tile_loads(j):
            copy.wait()
    down_copy.wait()
    lax.fori_loop(0, FEEDS, feed, 0)
    stores += [store(11, r.branch, r.attn_branch), store(12, r.middle, r.residual_mid)]
    to_blocks(r.turned, r.normed_mid[...], slice(0, rows))
    mid_store = store(0, r.turned, r.left_mid)
    cot_copy.wait()
    gain_sum = jnp.zeros((1, width), f32)
    for c in range(FEEDS):
        branch_exchange(c).wait_recv()

        def end(n, total):
            at = pl.ds(pl.multiple_of(c * feed_size + n * 128, 128), 128)
            branch = r.y_out[at, :].astype(f32) + r.y_in[at, :].astype(f32)
            scale, normed = norm_parts(branch)
            r.result[at, :] = (r.middle[at, :] + normed * r.gains[3:4, :]).astype(low)
            back, gain = norm_back(r.cot[at, :].astype(f32), r.gains[3:4, :], scale, normed)
            r.cot[at, :] = back.astype(low)
            return total + gain

        gain_sum = lax.fori_loop(0, feed_size // 128, end, gain_sum)
        if c == 0:
            mid_store.wait()
        at = slice(c * feed_size, (c + 1) * feed_size)
        to_blocks(r.turned, r.cot[at, :], at)
    stores += [
        store(0, r.turned, r.left_ffn),
        store(13, r.cot, r.grad_ffn),
        store(14, r.result, r.output),
    ]
    r.gain_tile[...] = jnp.zeros_like(r.gain_tile)
    r.gain_tile[3:4, :] = gain_sum
    stores.append(store(15, r.gain_tile, r.gain_start))
    for copy in stores:
        copy.wait()
    for distance in (1, 2):
        @pl.when(seq + distance <= last_seq)
        def _():
            ids_send(distance).wait_send()

    for n in range(2):
        @pl.when(seq + 1 <= last_seq)
        def _():
            halo(n, 1).wait_send()

        @pl.when(even & (seq + 2 <= last_seq))
        def _():
            halo(n, 2).wait_send()

        @pl.when(even & (seq >= 2))
        def _():
            halo(n, 2, True).wait_send()

    for c in (FEEDS - 2, FEEDS - 1):
        for copy in part_stores(jnp.int32(c)):
            copy.wait()
    for c in range(CHUNKS):
        head_exchange(c).wait_send()
    for c in range(FEEDS):
        branch_exchange(c).wait_send()


def forward(operands):
    low, f32 = jnp.bfloat16, jnp.float32
    dma = pltpu.SemaphoreType.DMA
    rows, width = operands["inputs"].shape
    hidden = operands["w_gate"].shape[1]
    wide = operands["w_query"].shape[1]
    shape = jax.ShapeDtypeStruct
    anywhere = pl.BlockSpec(memory_space=pl.ANY)
    outs = dict(
        left_in=shape((width, rows), low),
        left_mid=shape((width, rows), low),
        left_ffn=shape((width, rows), low),
        key_proj=shape((rows, 256), f32),
        query_proj=shape((rows, wide), f32),
        queries=shape((rows, wide), low),
        cosine_out=shape((rows, 128), f32),
        sine_out=shape((rows, 128), f32),
        ids_out=shape((8, 3 * rows), f32),
        attended=shape((rows, wide), f32),
        lse=shape((8, rows), f32),
        keys=shape((3 * rows, 256), low),
        values=shape((3 * rows, 256), low),
        attn_branch=shape((rows, width), f32),
        residual_mid=shape((rows, width), f32),
        gate_up=shape((rows, 2 * hidden), low),
        mixed=shape((rows, hidden), low),
        grad_ffn=shape((rows, width), low),
        output=shape((rows, width), low),
        gain_start=shape((8, width), f32),
        gain_rows=shape((8, width), f32),
        head_gains=shape((8, 256), f32),
    )
    feed_size = rows // FEEDS
    vmem = pltpu.VMEM
    scratch = dict(
        x=vmem((rows, width), low),
        gains=vmem((8, width), f32),
        wk=vmem((width, 256), low),
        wv=vmem((width, 256), low),
        head_gain=vmem((8, 256), f32),
        ids=vmem((3, 8, rows), f32),
        ids_flat=vmem((8, 3 * rows), f32),
        ids_turned=vmem((rows, 128), f32),
        wq=vmem((width, wide), low),
        wo=vmem((2, wide, width), low),
        wgu=vmem((width, 2 * hidden), low),
        wd=vmem((hidden, width), low),
        cot=vmem((rows, width), low),
        normed_in=vmem((rows, width), low),
        normed_mid=vmem((rows, width), low),
        key_raw=vmem((rows, 256), f32),
        query_raw=vmem((rows, wide), f32),
        q=vmem((rows, wide), low),
        window=vmem((2, 3 * rows, 256), low),
        cosine=vmem((rows, 128), f32),
        sine=vmem((rows, 128), f32),
        turned=vmem((width, rows), low),
        heads_f=vmem((rows, wide), f32),
        heads_all=vmem((2, rows, wide), low),
        lse_rows=vmem((8, rows), f32),
        branch=vmem((rows, width), f32),
        middle=vmem((rows, width), f32),
        gate_up_part=vmem((2, feed_size, 2 * hidden), low),
        mixed_part=vmem((2, feed_size, hidden), low),
        y_out=vmem((rows, width), low),
        y_in=vmem((rows, width), low),
        result=vmem((rows, width), low),
        gain_tile=vmem((8, width), f32),
        load_sem=dma((13,)),
        store_sem=dma((18,)),
        part_sem=dma((2, 2)),
        weight_sem=dma((2, hidden // WIDE)),
        wo_send=dma(()),
        wo_recv=dma(()),
        out_send=dma((OUT_PARTS,)),
        out_recv=dma((OUT_PARTS,)),
        ids_send=dma((2,)),
        ids_recv=dma((2,)),
        halo_send=dma((2, 3)),
        halo_recv=dma((2, 2)),
        y_send=dma((CHUNKS + FEEDS,)),
        y_recv=dma((CHUNKS + FEEDS,)),
    )
    names = (*operands, *outs, *scratch)
    results = pl.pallas_call(
        functools.partial(forward_kernel, names),
        out_shape=list(outs.values()),
        in_specs=[
            pl.BlockSpec(memory_space=pltpu.VMEM) if len(a.shape) == 1 else anywhere
            for a in operands.values()
        ],
        out_specs=[anywhere] * len(outs),
        scratch_shapes=list(scratch.values()),
        compiler_params=pltpu.CompilerParams(
            collective_id=2, has_side_effects=True, vmem_limit_bytes=62 << 20
        ),
        name="forward",
    )(*operands.values())
    return dict(zip(outs, results))


DOWN, GATE, UP, QUERY, QUERY_END, OUT, OUT_END = range(7)
RING = 6
Y_PARTS = 8
STEPS = 31
FIRST_SIDE = 27
LAG_X = 4
LAG_M = 6
LAG_Z = 8


def backward_kernel(names, *refs):
    r = types.SimpleNamespace(**dict(zip(names, refs)))
    seq, head, core, side, level = place_of()
    last_seq = lax.axis_size("seq") - 1
    f32, low = jnp.float32, jnp.bfloat16
    rows = r.grad_ffn.shape[0]
    width = r.grad_ffn.shape[1]

    barrier = pltpu.get_barrier_semaphore()

    def greet(to_seq, to_head):
        pl.semaphore_signal(barrier, inc=1, device_id=(to_seq, to_head), device_id_type=MESH)

    greet(seq ^ 1, head)
    greet(seq ^ 2, head)
    greet(seq, 1 - head)
    for z in range(4):
        for c in range(2):
            other = z * 4 + side * 2 + c

            @pl.when(other != seq)
            def _():
                greet(other, head)

    expected = jnp.int32(10)
    for distance in (1, 2):
        @pl.when(seq >= distance)
        def _():
            greet(seq - distance, head)

        @pl.when(seq + distance <= last_seq)
        def _():
            greet(seq + distance, head)

        expected = (
            expected
            + (seq >= distance).astype(jnp.int32)
            + (seq + distance <= last_seq).astype(jnp.int32)
        )
    pl.semaphore_wait(barrier, expected)

    def remote(src, dst, send, recv, to_seq, to_head):
        return pltpu.make_async_remote_copy(
            src_ref=src,
            dst_ref=dst,
            send_sem=send,
            recv_sem=recv,
            device_id=(to_seq, to_head),
            device_id_type=MESH,
        )

    targets = [((2 * core + k // 2) * 4 + side * 2 + k % 2) for k in range(4)]
    sources = [z * 4 + side * 2 + level // 2 for z in range(4)]
    starts_far = (level == 3 * (1 - core))
    hands_on = (level == 2 - core)
    near = (2 - core) * 4 + side * 2 + core
    far = (3 - 3 * core) * 4 + side * 2 + core
    far_level = 3 * core

    def is_far(k):
        return core == k // 2

    def unheard(z):
        return (level == 3 - z) if z in (0, 3) else False

    def core_copy(t):
        slot = lax.rem(t, RING)
        return remote(
            r.sent.at[lax.rem(t, 2)], r.core_in.at[slot], r.core_send.at[t], r.core_recv.at[t],
            seq ^ 1, head,
        )

    def x_copy(t):
        slot = lax.rem(t, RING)
        return remote(
            r.held.at[slot, 1 - side], r.x_in.at[slot], r.x_send.at[t], r.x_recv.at[t],
            seq ^ 2, head,
        )

    def z_copy(t, k):
        return remote(
            r.z_out.at[lax.rem(t, RING), k], r.z_in.at[t, level],
            r.z_send.at[t, k], r.z_recv.at[t, level], targets[k], head,
        )

    def near_copy(t, k):
        return remote(
            r.z_out.at[lax.rem(t, RING), k], r.m_in.at[lax.rem(t, RING), k % 2],
            r.z_send.at[t, k], r.m_recv.at[t, k % 2], near, head,
        )

    def far_copy(t, g):
        return remote(
            r.z_out.at[lax.rem(t, RING), 2 * core + g], r.z_in.at[t, level],
            r.z_send.at[t, 2 * core + g], r.z_recv.at[t, level],
            far_level * 4 + side * 2 + g, head,
        )

    def z_arrival(t, z):
        return remote(
            r.z_out.at[0, 0], r.z_in.at[t, z], r.z_send.at[t, 0], r.z_recv.at[t, z],
            sources[z], head,
        )

    def produce(t):
        @pl.when(t >= 2)
        def _():
            core_copy(t - 2).wait_send()

        @pl.when(t >= RING)
        def _():
            x_copy(t - RING).wait_send()

        which = jnp.where(t < 9, 0, jnp.where(t < FIRST_SIDE, 1, jnp.where(t < 30, 2, 0)))
        place = jnp.where(
            t < 9, lax.rem(t, 2), jnp.where(t < FIRST_SIDE, t - 7, t - (FIRST_SIDE - 2))
        )
        tile = r.tiles[place]

        def half(start):
            left = r.lefts[which, pl.ds(pl.multiple_of(start, 576), 576), :]
            return jnp.dot(left, tile, preferred_element_type=f32)

        away = half((1 - core) * 576)
        for k in range(8):
            r.sent[lax.rem(t, 2), k // 4, k % 4] = away[k * BLOCK : (k + 1) * BLOCK].astype(low)

        @pl.when(t >= RING)
        def _():
            pl.semaphore_wait(r.core_free, 1)

        def second(start):
            left = r.lefts[0, pl.ds(pl.multiple_of(start, 576), 576), :]
            return jnp.dot(left, tile[:, 256:], preferred_element_type=f32)

        @pl.when(t == FIRST_SIDE + 2)
        def _():
            more = second((1 - core) * 576)
            for k in range(8):
                r.sent[lax.rem(t, 2), k // 4, k % 4, :, 256:] = more[
                    k * BLOCK : (k + 1) * BLOCK
                ].astype(low)

        core_copy(t).start()
        home = half(core * 576)
        for k in range(8):
            r.held[lax.rem(t, RING), k // 4, k % 4] = home[k * BLOCK : (k + 1) * BLOCK].astype(low)

        @pl.when(t == FIRST_SIDE + 2)
        def _():
            more = second(core * 576)
            for k in range(8):
                r.held[lax.rem(t, RING), k // 4, k % 4, :, 256:] = more[
                    k * BLOCK : (k + 1) * BLOCK
                ].astype(low)

    def core_stage(t):
        core_copy(t).wait_recv()
        slot = lax.rem(t, RING)

        def add(part):
            for k in range(4):
                r.held[slot, part, k] = (
                    r.held[slot, part, k].astype(f32) + r.core_in[slot, part, k].astype(f32)
                ).astype(low)

        add(1 - side)

        @pl.when(t >= RING)
        def _():
            pl.semaphore_wait(r.x_free, 1)

        x_copy(t).start()
        add(side)

        @pl.when(t + RING < STEPS)
        def _():
            pl.semaphore_signal(r.core_free, inc=1, device_id=(seq ^ 1, head), device_id_type=MESH)

    def x_stage(t):
        x_copy(t).wait_recv()
        slot = lax.rem(t, RING)

        @pl.when(t >= RING)
        def _():
            for k in range(4):
                @pl.when(targets[k] != seq)
                def _():
                    z_copy(t - RING, k).wait_send()

        @pl.when(starts_far & (t >= RING))
        def _():
            pl.semaphore_wait(r.m_free, 1)

        for k in range(4):
            total = (r.held[slot, side, k].astype(f32) + r.x_in[slot, k].astype(f32)).astype(low)

            @pl.when(targets[k] == seq)
            def _():
                r.z_in[t, level] = total

            @pl.when(targets[k] != seq)
            def _():
                r.z_out[slot, k] = total

                @pl.when(starts_far & is_far(k))
                def _():
                    near_copy(t, k).start()

                @pl.when(jnp.logical_not((starts_far | hands_on) & is_far(k)))
                def _():
                    z_copy(t, k).start()

        @pl.when(t + RING < STEPS)
        def _():
            pl.semaphore_signal(r.x_free, inc=1, device_id=(seq ^ 2, head), device_id_type=MESH)

    def m_stage(t):
        slot = lax.rem(t, RING)

        @pl.when(hands_on)
        def _():
            for g in range(2):
                remote(
                    r.z_out.at[0, 0], r.m_in.at[slot, g], r.z_send.at[t, 0], r.m_recv.at[t, g],
                    far, head,
                ).wait_recv()
                k = 2 * core + g
                r.z_out[slot, k] = (
                    r.z_out[slot, k].astype(f32) + r.m_in[slot, g].astype(f32)
                ).astype(low)
                far_copy(t, g).start()

            @pl.when(t + RING < STEPS)
            def _():
                pl.semaphore_signal(r.m_free, inc=1, device_id=(far, head), device_id_type=MESH)

    def out_copy(t, kind):
        slot = lax.rem(t, 2)
        at = pl.multiple_of(lax.rem(t, 9) * WIDE, WIDE)
        if kind == DOWN:
            return pltpu.make_async_copy(
                r.flat.at[slot], r.down_out.at[:, pl.ds(at, WIDE)], r.out_sem.at[t]
            )
        if kind == QUERY:
            return pltpu.make_async_copy(
                r.flat.at[slot], r.query_out.at[:, pl.ds(0, WIDE)], r.out_sem.at[t]
            )
        if kind == QUERY_END:
            return pltpu.make_async_copy(
                r.flat.at[slot, :, pl.ds(0, 128)], r.query_out.at[:, pl.ds(WIDE, 128)],
                r.out_sem.at[t],
            )
        if kind == OUT:
            return pltpu.make_async_copy(
                r.flat.at[slot, :, pl.ds(256, 128)], r.out_out.at[:, pl.ds(0, 128)],
                r.out_sem.at[t],
            )
        if kind == OUT_END:
            return pltpu.make_async_copy(
                r.flat.at[slot], r.out_out.at[:, pl.ds(128, WIDE)], r.out_sem.at[t]
            )
        target = r.gate_out if kind == GATE else r.up_out
        return pltpu.make_async_copy(
            r.flat.at[slot], target.at[:, pl.ds(at, WIDE)], r.out_sem.at[t]
        )

    KINDS = (
        (DOWN, 0, 9), (GATE, 9, 18), (UP, 18, 27), (QUERY, 27, 28), (QUERY_END, 28, 29),
        (OUT, 29, 30), (OUT_END, 30, 31),
    )

    def out_wait(t):
        for kind, first, end in KINDS:
            @pl.when((t >= first) & (t < end))
            def _():
                out_copy(t, kind).wait()

    def z_stage(t):
        for z in range(4):
            @pl.when((sources[z] != seq) & jnp.logical_not(unheard(z)))
            def _():
                z_arrival(t, z).wait_recv()

        total = r.z_in[t, 1].astype(f32) + r.z_in[t, 2].astype(f32)
        for z in (0, 3):
            total = total + jnp.where(unheard(z), 0.0, r.z_in[t, z].astype(f32))

        @pl.when(t >= 2)
        def _():
            out_wait(t - 2)

        r.flat[lax.rem(t, 2)] = total
        for kind, first, end in KINDS:
            @pl.when((t >= first) & (t < end))
            def _():
                out_copy(t, kind).start()

        @pl.when(t == FIRST_SIDE + 1)
        def _():
            r.kv_own[:, :256] = total[:, 128:]

        @pl.when(t == FIRST_SIDE + 2)
        def _():
            r.kv_own[:, 256:] = total[:, :256]

    def pump(i):
        @pl.when(i < STEPS)
        def _():
            produce(i)

        @pl.when((i >= 1) & (i - 1 < STEPS))
        def _():
            core_stage(i - 1)

        @pl.when((i >= LAG_X) & (i - LAG_X < STEPS))
        def _():
            x_stage(i - LAG_X)

        @pl.when((i >= LAG_M) & (i - LAG_M < STEPS))
        def _():
            m_stage(i - LAG_M)

        @pl.when((i >= LAG_Z) & (i - LAG_Z < STEPS))
        def _():
            z_stage(i - LAG_Z)

    def y_part(n, part):
        size = rows // Y_PARTS
        at = pl.ds(part * size, size)
        return remote(
            r.y_out.at[at, :], r.y_in.at[n, at, :], r.y_send.at[n, part], r.y_recv.at[n, part],
            seq, 1 - head,
        )

    def y_start(n, first):
        for part in (first, first + 1):
            y_part(n, part).start()

    def y_sent(n):
        for part in range(Y_PARTS):
            y_part(n, part).wait_send()

    def y_arrived(n):
        for part in range(Y_PARTS):
            y_part(n, part).wait_recv()

    def feed_forward(grad, wd, wgu, gate_up, acc):
        sems, grad_sem, left_sem = r.tile_sems, r.grad_sem, r.left_sem

        def copies(j):
            slot = lax.rem(j, 2)
            at = pl.ds(pl.multiple_of(j * WIDE, WIDE), WIDE)
            double = pl.ds(pl.multiple_of(j * 2 * WIDE, 2 * WIDE), 2 * WIDE)
            pairs = (
                (r.w_down.at[at, :], wd),
                (r.gate_up.at[:, double], gate_up),
            )
            halves = (
                (r.w_gate.at[:, at], wgu.at[slot, :, pl.ds(0, WIDE)]),
                (r.w_up.at[:, at], wgu.at[slot, :, pl.ds(WIDE, WIDE)]),
            )
            return [
                pltpu.make_async_copy(src, dst.at[slot], sems.at[n, slot])
                for n, (src, dst) in enumerate(pairs)
            ] + [
                pltpu.make_async_copy(src, dst, sems.at[2 + n, slot])
                for n, (src, dst) in enumerate(halves)
            ]

        def mixed_copy(j):
            slot = lax.rem(j, 2)
            at = pl.ds(pl.multiple_of(j * WIDE, WIDE), WIDE)
            return pltpu.make_async_copy(r.mixed.at[:, at], r.tiles.at[slot], sems.at[5, slot])

        first = [pltpu.make_async_copy(r.grad_ffn, grad, grad_sem)] + [
            pltpu.make_async_copy(left, r.lefts.at[n], left_sem.at[n])
            for n, left in enumerate((r.left_ffn, r.left_mid, r.left_in))
        ]
        for copy in (first[1], mixed_copy(0), first[0], *copies(0), *first[2:]):
            copy.start()
        first[1].wait()
        first[0].wait()
        acc[...] = jnp.zeros_like(acc)

        def step(i, carry):
            @pl.when(i + 1 < 9)
            def _():
                for copy in (mixed_copy(i + 1), *copies(i + 1)):
                    copy.start()

            mixed_copy(i).wait()
            pump(i)
            for copy in copies(i):
                copy.wait()
            slot = lax.rem(i, 2)
            grad_mixed = dot_nt(grad[...], wd[slot])
            v = gate_up[slot, :, :WIDE].astype(f32)
            u = gate_up[slot, :, WIDE:].astype(f32)
            square = v * v
            curve = jnp.tanh(0.7978845608028654 * v * (1.0 + 0.044715 * square))
            gelu = 0.5 * v * (1.0 + curve)
            slope = 0.5 * (1.0 + curve) + 0.5 * v * (1.0 - curve * curve) * (
                0.7978845608028654 * (1.0 + 3.0 * 0.044715 * square)
            )
            grad_gate = (grad_mixed * u * slope).astype(low)
            grad_up = (grad_mixed * gelu).astype(low)
            r.tiles[2 + i] = grad_gate
            r.tiles[11 + i] = grad_up
            acc[...] += dot_nt(jnp.concatenate([grad_gate, grad_up], axis=1), wgu[slot])
            return carry

        lax.fori_loop(0, 9, step, 0)
        for copy in first[2:]:
            copy.wait()
        r.y_out[...] = acc[...].astype(low)

    dma = pltpu.SemaphoreType.DMA
    pl.run_scoped(
        feed_forward,
        pltpu.VMEM((rows, width), low),
        pltpu.VMEM((2, WIDE, width), low),
        pltpu.VMEM((2, width, 2 * WIDE), low),
        pltpu.VMEM((2, rows, 2 * WIDE), low),
        pltpu.VMEM((rows, width), f32),
    )

    def attention(loaded, names, *scoped):
        b = types.SimpleNamespace(**dict(zip(names, scoped)))
        made = {
            name: pltpu.make_async_copy(getattr(r, name), getattr(b, name), b.sems.at[n])
            for n, name in enumerate(loaded)
        }
        for copy in made.values():
            copy.start()
        loads = types.SimpleNamespace(**made)
        heads = r.queries.shape[1] // 256

        def gains_copy(n):
            to_seq, to_head = ((seq, 1 - head), (seq ^ 1, head), (seq ^ 2, head))[n]
            return remote(
                r.gains.at[n], r.gains_in.at[n], r.gains_send.at[n], r.gains_recv.at[n],
                to_seq, to_head,
            )

        def gains_level(z):
            return remote(
                r.gains.at[3], r.gains_z.at[level], r.level_send.at[z], r.level_recv.at[level],
                z * 4 + side * 2 + core, head,
            )

        def gains_from(z):
            return remote(
                r.gains.at[3], r.gains_z.at[z], r.level_send.at[z], r.level_recv.at[z],
                z * 4 + side * 2 + core, head,
            )

        def norms():
            y_arrived(0)
            y_sent(0)
            for copy in (loads.residual_mid, loads.attn_branch, loads.cotangent, loads.gain_rows, loads.head_gains):
                copy.wait()
            loads.gain_start.wait()
            gain_post, gain_pre = b.gain_rows[1:2, :], b.gain_rows[2:3, :]
            size = 128

            def chunk(c, sums):
                at = pl.ds(pl.multiple_of(c * size, size), size)
                grad_mid = r.y_out[at, :].astype(f32) + r.y_in[0, at, :].astype(f32)
                scale, normed = norm_parts(b.residual_mid[at, :])
                back, pre = norm_back(grad_mid, gain_pre, scale, normed)
                grad_residual = b.cotangent[at, :].astype(f32) + back
                b.residual_mid[at, :] = grad_residual
                scale, normed = norm_parts(b.attn_branch[at, :])
                back, post = norm_back(grad_residual, gain_post, scale, normed)
                r.y_out[at, :] = back.astype(low)
                return sums[0] + post, sums[1] + pre

            zero = jnp.zeros((1, width), f32)
            post, pre = lax.fori_loop(0, rows // size, chunk, (zero, zero))
            r.gains[0] = b.gain_start[...]
            r.gains[0, 1:2, :] = post
            r.gains[0, 2:3, :] = pre

        def through_out():
            for copy in (loads.w_out, loads.attended, loads.lse):
                copy.wait()
            b.grad_attended[...] = dot_nt(r.y_out[...], b.w_out[...]).astype(low)
            for h in range(heads):
                at = slice(256 * h, 256 * h + 256)
                delta = jnp.sum(
                    b.grad_attended[:, at].astype(f32) * b.attended[:, at], axis=1, keepdims=True
                )
                b.delta[h : h + 1, :] = jnp.broadcast_to(delta, (rows, 128)).T[:1]
            to_blocks(r.lefts.at[0], r.y_out[...], slice(0, rows))
            r.tiles[4, :, 256:] = b.attended[:, :128].astype(low)
            r.tiles[5] = b.attended[:, 128:].astype(low)

        def attend(block):
            if block == 0:
                for copy in (loads.queries, loads.keys, loads.values, loads.ids_out):
                    copy.wait()
                b.grad_queries[...] = jnp.zeros_like(b.grad_queries)
                b.ids_turned[...] = jnp.broadcast_to(b.ids_out[:1], (128, 3 * rows)).T
            size = 256

            def chunk(c, carry):
                local = pl.multiple_of(c * size, size)
                at = pl.ds(pl.multiple_of(block * rows + c * size, size), size)
                keys, values = b.keys[at, :], b.values[at, :]
                seen = b.ids_turned[at, :1] == b.ids_out[:1, 2 * rows :]
                if block == 2:
                    key_at = lax.broadcasted_iota(jnp.int32, (size, rows), 0) + local
                    query_at = lax.broadcasted_iota(jnp.int32, (size, rows), 1)
                    seen = seen & (key_at <= query_at)
                grad_keys = jnp.zeros((size, 256), f32)
                grad_values = jnp.zeros((size, 256), f32)
                for h in range(heads):
                    head_at = slice(256 * h, 256 * h + 256)
                    q, grad_out = b.queries[:, head_at], b.grad_attended[:, head_at]
                    probs = jnp.where(
                        seen, jnp.exp(dot_nt(keys, q) - b.lse[h : h + 1, :]), 0.0
                    )
                    grad_probs = dot_nt(values, grad_out)
                    grad_scores = (probs * (grad_probs - b.delta[h : h + 1, :])).astype(low)
                    grad_keys += jnp.dot(grad_scores, q, preferred_element_type=f32)
                    grad_values += jnp.dot(
                        probs.astype(low), grad_out, preferred_element_type=f32
                    )
                    b.grad_queries[:, head_at] += dot_tn(grad_scores, keys)
                to = pl.ds(local, size)
                if block == 2:
                    b.grad_own[0, to, :] = grad_keys
                    b.grad_own[1, to, :] = grad_values
                else:
                    r.halo_out[block, 0, to, :] = grad_keys.astype(low)
                    r.halo_out[block, 1, to, :] = grad_values.astype(low)
                return carry

            lax.fori_loop(0, rows // size, chunk, 0)
            if block == 0:
                @pl.when((seq >= 2) & (core == 1))
                def _():
                    relay_copy().start()

                halo_start(0, 0)

            if block == 1:
                @pl.when((core == 0) & (seq >= 2))
                def _():
                    remote(
                        r.halo_out.at[0], r.relay_in, r.relay_send, r.relay_recv, seq ^ 1, head
                    ).wait_recv()
                    for n in range(2):
                        r.halo_out[1, n] = (
                            r.halo_out[1, n].astype(f32) + r.relay_in[n].astype(f32)
                        ).astype(low)

        def relay_copy():
            return remote(
                r.halo_out.at[0], r.relay_in, r.relay_send, r.relay_recv, seq - 1, head
            )

        def halo_part(block, n, half):
            at = pl.ds(half * (rows // 2), rows // 2)
            return remote(
                r.halo_out.at[block, n, at, :], r.halo_in.at[block, n, at, :],
                r.halo_send.at[block, n, half], r.halo_recv.at[block, n, half],
                seq - (2 - block), head,
            )

        def halo_start(block, n):
            @pl.when((seq >= 1) if block == 1 else (seq >= 2) & (core == 0))
            def _():
                for half in range(2):
                    halo_part(block, n, half).start()

        def halo_parts(block):
            return [halo_part(block, n, half) for n in range(2) for half in range(2)]

        def query_side():
            for copy in (loads.query_proj, loads.cosine_out, loads.sine_out, loads.w_query):
                copy.wait()
            total = jnp.zeros((1, 256), f32)
            for h in range(heads):
                at = slice(256 * h, 256 * h + 256)
                grad = rotate_back(
                    b.grad_queries[:, at] * QUERY_SCALE, b.cosine_out[...], b.sine_out[...]
                )
                scale, normed = norm_parts(b.query_proj[:, at])
                back, gain = norm_back(grad, b.head_gains[0:1, :], scale, normed)
                total += gain
                back = back.astype(low)
                if h == 0:
                    r.tiles[2, :, :256] = back
                else:
                    r.tiles[2, :, 256:] = back[:, :128]
                    r.tiles[3, :, :128] = back[:, 128:]
                part = dot_nt(back, b.w_query[:, at])
                if h == 0:
                    b.attn_branch[...] = part
                else:
                    b.attn_branch[...] += part
            r.gains[0, 4:5, :256] = total

        def key_side():
            for copy in (loads.key_proj, loads.w_key, loads.w_value, loads.inputs):
                copy.wait()
            for block in range(2):
                heard = seq + (2 - block) <= last_seq

                @pl.when(heard & (core == 0) if block == 0 else heard)
                def _():
                    for copy in halo_parts(block):
                        copy.wait_recv()
                    for n in range(2):
                        b.grad_own[n] += r.halo_in[block, n].astype(f32)

            grad = rotate_back(b.grad_own[0], b.cosine_out[...], b.sine_out[...])
            scale, normed = norm_parts(b.key_proj[...])
            back, gain = norm_back(grad, b.head_gains[1:2, :], scale, normed)
            r.gains[0, 4:5, 256:512] = gain
            grad_key, grad_value = back.astype(low), b.grad_own[1].astype(low)
            r.tiles[3, :, 128:] = grad_key
            r.tiles[4, :, :256] = grad_value
            b.attn_branch[...] += dot_nt(grad_key, b.w_key[...])
            b.attn_branch[...] += dot_nt(grad_value, b.w_value[...])
            size = 128

            def chunk(c, total):
                at = pl.ds(pl.multiple_of(c * size, size), size)
                part = b.attn_branch[at, :]
                scale, normed = norm_parts(b.inputs[at, :].astype(f32))
                r.y_out[at, :] = part.astype(low)
                return total + jnp.sum(part * normed, axis=0, keepdims=True)

            zero = jnp.zeros((1, width), f32)
            r.gains[0, 0:1, :] = lax.fori_loop(0, rows // size, chunk, zero)
            gains_copy(0).start()

        def gains_stage(n):
            gains_copy(n).wait_recv()
            own, other = r.gains[n], r.gains_in[n]
            if n == 0:
                row = lax.broadcasted_iota(jnp.int32, own.shape, 0)
                other = jnp.where((row == 0) | (row == 4), other, 0.0)
            r.gains[n + 1] = own + other
            if n < 2:
                gains_copy(n + 1).start()
            else:
                for z in range(4):
                    @pl.when(level == z)
                    def _():
                        r.gains_z[z] = r.gains[3]

                    @pl.when(level != z)
                    def _():
                        gains_level(z).start()

        def gains_end():
            for z in range(4):
                @pl.when(level != z)
                def _():
                    gains_from(z).wait_recv()

            r.gains_out[...] = (r.gains_z[0] + r.gains_z[1]) + (r.gains_z[2] + r.gains_z[3])

        def finish_inputs():
            y_arrived(1)
            size = 128

            def chunk(c, carry):
                at = pl.ds(pl.multiple_of(c * size, size), size)
                grad = r.y_out[at, :].astype(f32) + r.y_in[1, at, :].astype(f32)
                scale, normed = norm_parts(b.inputs[at, :].astype(f32))
                back, _ = norm_back(grad, b.gain_rows[0:1, :], scale, normed)
                r.inputs_out[at, :] = (b.residual_mid[at, :] + back).astype(low)
                return carry

            lax.fori_loop(0, rows // size, chunk, 0)

        def kv_copy():
            return remote(r.kv_own, r.kv_in, r.kv_send, r.kv_recv, seq, 1 - head)

        pieces = (
            *((9 + n, functools.partial(y_start, 0, 2 * n)) for n in range(4)),
            (16, norms),
            (17, through_out),
            (18, lambda: attend(0)),
            (19, lambda: halo_start(0, 1)),
            (19, lambda: attend(1)),
            (20, lambda: halo_start(1, 0)),
            (20, lambda: attend(2)),
            (21, lambda: halo_start(1, 1)),
            (21, query_side),
            (24, key_side),
            *((24 + n, functools.partial(y_start, 1, 2 * n)) for n in range(4)),
            (25, lambda: gains_stage(0)),
            (26, lambda: gains_stage(1)),
            (27, lambda: gains_stage(2)),
            (29, gains_end),
            (32, finish_inputs),
            (FIRST_SIDE + 3 + LAG_Z, lambda: kv_copy().start()),
        )

        def step(i, carry):
            for k, piece in pieces:
                @pl.when(i == k)
                def _():
                    piece()

            pump(i)
            return carry

        lax.fori_loop(9, STEPS + LAG_Z, step, 0)
        kv_copy().wait()
        r.kv_out[...] = r.kv_own[...] + r.kv_in[...]
        y_sent(1)
        for n in range(3):
            gains_copy(n).wait_send()
        for z in range(4):
            @pl.when(level != z)
            def _():
                gains_level(z).wait_send()

        @pl.when((seq >= 2) & (core == 1))
        def _():
            relay_copy().wait_send()

        @pl.when((seq >= 2) & (core == 0))
        def _():
            for copy in halo_parts(0):
                copy.wait_send()

        @pl.when(seq >= 1)
        def _():
            for copy in halo_parts(1):
                copy.wait_send()

    heads_width = r.queries.shape[1]
    def shape(size, kind):
        return pltpu.VMEM(size, kind)

    loaded = dict(
        residual_mid=shape((rows, width), f32),
        attn_branch=shape((rows, width), f32),
        cotangent=shape((rows, width), low),
        inputs=shape((rows, width), low),
        gain_rows=shape((8, width), f32),
        head_gains=shape((8, 256), f32),
        gain_start=shape((8, width), f32),
        w_out=shape((heads_width, width), low),
        attended=shape((rows, heads_width), f32),
        lse=shape((8, rows), f32),
        queries=shape((rows, heads_width), low),
        keys=shape((3 * rows, 256), low),
        values=shape((3 * rows, 256), low),
        ids_out=shape((8, 3 * rows), f32),
        query_proj=shape((rows, heads_width), f32),
        key_proj=shape((rows, 256), f32),
        cosine_out=shape((rows, 128), f32),
        sine_out=shape((rows, 128), f32),
        w_query=shape((width, heads_width), low),
        w_key=shape((width, 256), low),
        w_value=shape((width, 256), low),
    )
    scoped = dict(
        loaded,
        grad_attended=shape((rows, heads_width), low),
        delta=shape((8, rows), f32),
        grad_queries=shape((rows, heads_width), f32),
        grad_own=shape((2, rows, 256), f32),
        ids_turned=shape((3 * rows, 128), f32),
        sems=dma((len(loaded),)),
    )
    pl.run_scoped(functools.partial(attention, tuple(loaded), tuple(scoped)), *scoped.values())

    def drain(i, carry):
        @pl.when(i >= STEPS - 2)
        def _():
            core_copy(i).wait_send()
            out_wait(i)

        x_copy(i).wait_send()
        for k in range(4):
            @pl.when(targets[k] != seq)
            def _():
                z_copy(i, k).wait_send()

        return carry

    lax.fori_loop(STEPS - RING, STEPS, drain, 0)


def backward(operands):
    low, f32 = jnp.bfloat16, jnp.float32
    dma = pltpu.SemaphoreType.DMA
    rows, width = operands["grad_ffn"].shape
    hidden = operands["w_gate"].shape[1]
    wide = operands["w_query"].shape[1]
    anywhere = pl.BlockSpec(memory_space=pl.ANY)
    vmem = pl.BlockSpec(memory_space=pltpu.VMEM)
    outs = dict(
        down_out=(jax.ShapeDtypeStruct((BLOCK, hidden), f32), anywhere),
        gate_out=(jax.ShapeDtypeStruct((BLOCK, hidden), f32), anywhere),
        up_out=(jax.ShapeDtypeStruct((BLOCK, hidden), f32), anywhere),
        query_out=(jax.ShapeDtypeStruct((BLOCK, wide), f32), anywhere),
        out_out=(jax.ShapeDtypeStruct((BLOCK, wide), f32), anywhere),
        kv_out=(jax.ShapeDtypeStruct((BLOCK, 512), f32), vmem),
        gains_out=(jax.ShapeDtypeStruct((8, width), f32), vmem),
        inputs_out=(jax.ShapeDtypeStruct((rows, width), low), vmem),
    )
    scratch = dict(
        held=pltpu.VMEM((RING, 2, 4, BLOCK, WIDE), low),
        sent=pltpu.VMEM((2, 2, 4, BLOCK, WIDE), low),
        core_in=pltpu.VMEM((RING, 2, 4, BLOCK, WIDE), low),
        x_in=pltpu.VMEM((RING, 4, BLOCK, WIDE), low),
        m_in=pltpu.VMEM((RING, 2, BLOCK, WIDE), low),
        z_out=pltpu.VMEM((RING, 4, BLOCK, WIDE), low),
        z_in=pltpu.VMEM((STEPS, 4, BLOCK, WIDE), low),
        tiles=pltpu.VMEM((20, rows, WIDE), low),
        lefts=pltpu.VMEM((3, width, rows), low),
        y_out=pltpu.VMEM((rows, width), low),
        y_in=pltpu.VMEM((2, rows, width), low),
        halo_out=pltpu.VMEM((2, 2, rows, 256), low),
        halo_in=pltpu.VMEM((2, 2, rows, 256), low),
        relay_in=pltpu.VMEM((2, rows, 256), low),
        gains=pltpu.VMEM((4, 8, width), f32),
        gains_in=pltpu.VMEM((3, 8, width), f32),
        gains_z=pltpu.VMEM((4, 8, width), f32),
        kv_own=pltpu.VMEM((BLOCK, 512), f32),
        kv_in=pltpu.VMEM((BLOCK, 512), f32),
        flat=pltpu.VMEM((2, BLOCK, WIDE), f32),
        core_send=dma((STEPS,)),
        core_recv=dma((STEPS,)),
        x_send=dma((STEPS,)),
        x_recv=dma((STEPS,)),
        z_send=dma((STEPS, 4)),
        z_recv=dma((STEPS, 4)),
        out_sem=dma((STEPS,)),
        y_send=dma((2, Y_PARTS)),
        y_recv=dma((2, Y_PARTS)),
        halo_send=dma((2, 2, 2)),
        halo_recv=dma((2, 2, 2)),
        gains_send=dma((3,)),
        gains_recv=dma((3,)),
        level_send=dma((4,)),
        level_recv=dma((4,)),
        kv_send=dma(()),
        kv_recv=dma(()),
        tile_sems=dma((6, 2)),
        grad_sem=dma(()),
        left_sem=dma((3,)),
        m_recv=dma((STEPS, 2)),
        m_free=pltpu.SemaphoreType.REGULAR,
        relay_send=dma(()),
        relay_recv=dma(()),
        core_free=pltpu.SemaphoreType.REGULAR,
        x_free=pltpu.SemaphoreType.REGULAR,
    )
    names = (*operands, *outs, *scratch)
    results = pl.pallas_call(
        functools.partial(backward_kernel, names),
        out_shape=[shape for shape, _ in outs.values()],
        in_specs=[anywhere] * len(operands),
        out_specs=[spec for _, spec in outs.values()],
        scratch_shapes=list(scratch.values()),
        compiler_params=pltpu.CompilerParams(
            collective_id=1, has_side_effects=True, vmem_limit_bytes=62 << 20
        ),
        name="backward",
    )(*operands.values())
    return dict(zip(outs, results))


def last_kernel(names, *refs):
    r = types.SimpleNamespace(**dict(zip(names, refs)))
    place = lax.axis_index("seq")
    pairs = (
        (r.output, r.output_held, r.output_end),
        (r.inputs_out, r.inputs_held, r.inputs_end),
        (r.gate_out, r.gate_held, r.gate_end),
        (r.up_out, r.up_held, r.up_end),
        (r.down_out, r.down_held, r.down_end),
        (r.query_out, r.query_held, r.query_end),
        (r.out_out, r.out_held, r.out_end),
        (r.kv_out.at[:, pl.ds(0, 256)], r.key_held, r.key_end),
        (r.kv_out.at[:, pl.ds(256, 256)], r.value_held, r.value_end),
    )
    loads = [
        pltpu.make_async_copy(src, held, r.sems.at[0, n]) for n, (src, held, _) in enumerate(pairs)
    ]
    copies = [
        pltpu.make_async_copy(held, dst, r.sems.at[1, n]) for n, (_, held, dst) in enumerate(pairs)
    ]
    for copy in loads:
        copy.start()
    width = r.gains_out.shape[1]
    rolled = pltpu.roll(r.gains_out[...], lax.rem(width - place * BLOCK, width), 1)
    for n, target in enumerate((r.in_end, r.post_attn_end, r.pre_ffn_end, r.post_ffn_end)):
        target[...] = rolled[n : n + 1, :BLOCK].reshape(BLOCK)
    own = r.gain_query_end.shape[0]
    for n, target in enumerate((r.gain_query_end, r.gain_key_end)):
        rolled = pltpu.roll(r.gains_out[...], lax.rem(2 * width - place * own - 256 * n, width), 1)
        target[...] = rolled[4:5, :own].reshape(own)
    for load, copy in zip(loads, copies):
        load.wait()
        copy.start()
    for copy in copies:
        copy.wait()


def last(operands):
    f32 = jnp.float32
    anywhere = pl.BlockSpec(memory_space=pl.ANY)
    vmem = pl.BlockSpec(memory_space=pltpu.VMEM)
    shape = jax.ShapeDtypeStruct
    like = types.SimpleNamespace(**operands)
    part = shape((BLOCK, 256), f32)
    gain = shape((BLOCK,), f32)
    small = shape((256 // lax.axis_size("seq"),), f32)
    outs = dict(
        output_end=like.output,
        inputs_end=like.inputs_out,
        query_end=like.query_out,
        key_end=part,
        value_end=part,
        out_end=like.out_out,
        gate_end=like.gate_out,
        up_end=like.up_out,
        down_end=like.down_out,
        in_end=gain,
        gain_query_end=small,
        gain_key_end=small,
        post_attn_end=gain,
        pre_ffn_end=gain,
        post_ffn_end=gain,
    )
    held = dict(
        output_held=like.output,
        inputs_held=like.inputs_out,
        gate_held=like.gate_out,
        up_held=like.up_out,
        down_held=like.down_out,
        query_held=like.query_out,
        out_held=like.out_out,
        key_held=part,
        value_held=part,
    )
    names = (*operands, *outs, *held, *dict(sems=0))
    return pl.pallas_call(
        functools.partial(last_kernel, names),
        out_shape=[shape(a.shape, a.dtype) for a in outs.values()],
        in_specs=[vmem if name == "gains_out" else anywhere for name in operands],
        out_specs=[vmem if len(a.shape) == 1 else anywhere for a in outs.values()],
        scratch_shapes=[pltpu.VMEM(a.shape, a.dtype) for a in held.values()]
        + [pltpu.SemaphoreType.DMA((2, len(held)))],
        name="last",
    )(*operands.values())


def fast_device(
    inputs,
    segment_ids,
    w_query,
    w_key,
    w_value,
    w_out,
    w_gate,
    w_up,
    w_down,
    gain_in,
    gain_query,
    gain_key,
    gain_post_attn,
    gain_pre_ffn,
    gain_post_ffn,
    cotangent,
):
    shared = dict(
        inputs=inputs, cotangent=cotangent, w_query=w_query, w_key=w_key, w_value=w_value,
        w_out=w_out, w_gate=w_gate, w_up=w_up, w_down=w_down,
    )
    first = forward(
        dict(
            shared,
            segment_ids=segment_ids, gain_in=gain_in, gain_query=gain_query, gain_key=gain_key,
            gain_post_attn=gain_post_attn, gain_pre_ffn=gain_pre_ffn, gain_post_ffn=gain_post_ffn,
        )
    )
    output = first.pop("output")
    results = last(dict(backward(dict(shared, **first)), output=output))
    return tuple(a.T if n in (5, 8) else a for n, a in enumerate(results))


def scatter_rows(grad):
    return lax.psum_scatter(grad, "seq", scatter_dimension=0, tiled=True).astype(jnp.float32)


def per_device(
    inputs,
    segment_ids,
    w_query,
    w_key,
    w_value,
    w_out,
    w_gate,
    w_up,
    w_down,
    gain_in,
    gain_query,
    gain_key,
    gain_post_attn,
    gain_pre_ffn,
    gain_post_ffn,
    cotangent,
):
    rows = inputs.shape[0]
    head_dim = w_key.shape[1]
    local_heads = w_query.shape[1] // head_dim
    place = lax.axis_index("seq")
    local_index = jnp.arange(rows, dtype=jnp.int32)
    ids_parts = [
        jnp.where(place >= distance, from_behind(segment_ids, "seq", distance), -1)
        for distance in (2, 1)
    ]
    window_ids = jnp.concatenate(ids_parts + [segment_ids], axis=0)
    window_index = jnp.arange(3 * rows, dtype=jnp.int32) - 2 * rows
    same = segment_ids[:, None] == window_ids[None, :]
    visible = same & (window_index[None, :] <= local_index[:, None])
    positions = jnp.sum(visible.astype(jnp.int32), axis=1) - 1
    cosine, sine = rope_angles(positions, head_dim)
    inputs_f = inputs.astype(jnp.float32)
    hidden_in = rms_scale(inputs_f, gain_in).astype(jnp.bfloat16)
    query_proj = jnp.dot(hidden_in, w_query, preferred_element_type=jnp.float32)
    key_proj = jnp.dot(hidden_in, w_key, preferred_element_type=jnp.float32)
    value_proj = jnp.dot(hidden_in, w_value, preferred_element_type=jnp.float32)

    def query_side(projection, gain):
        return prepare(
            projection.reshape(rows, local_heads, head_dim), gain, cosine, sine, QUERY_SCALE
        )

    def key_side(projection, gain):
        return prepare(projection[:, None, :], gain, cosine, sine, 1.0)[:, 0, :]

    queries = query_side(query_proj, gain_query).astype(jnp.bfloat16)
    own_keys = key_side(key_proj, gain_key).astype(jnp.bfloat16)
    own_values = value_proj.astype(jnp.bfloat16)
    key_parts = []
    value_parts = []
    for distance in (2, 1):
        moved_keys, moved_values = from_behind((own_keys, own_values), "seq", distance)
        key_parts.append(moved_keys)
        value_parts.append(moved_values)
    all_keys = jnp.concatenate(key_parts + [own_keys], axis=0)
    all_values = jnp.concatenate(value_parts + [own_values], axis=0)
    def raw_scores():
        return jnp.einsum("ihd,jd->hij", queries, all_keys, preferred_element_type=jnp.float32)

    scores = jnp.where(visible[None], raw_scores(), -1e30)
    row_max = jnp.max(scores, axis=-1, keepdims=True)
    expo = jnp.exp(scores - row_max)
    total = jnp.sum(expo, axis=-1, keepdims=True)
    attn_probs = expo / total
    log_total = row_max + jnp.log(total)
    attended = jnp.einsum(
        "hij,jd->ihd",
        attn_probs.astype(jnp.bfloat16),
        all_values,
        preferred_element_type=jnp.float32,
    )
    attended = attended.reshape(rows, local_heads * head_dim).astype(jnp.bfloat16)
    attn_branch = over_head(jnp.dot(attended, w_out, preferred_element_type=jnp.float32))
    residual_mid = inputs_f + rms_scale(attn_branch, gain_post_attn)
    hidden_mid = rms_scale(residual_mid, gain_pre_ffn).astype(jnp.bfloat16)
    gate_act = jnp.dot(hidden_mid, w_gate, preferred_element_type=jnp.float32)
    up_proj = jnp.dot(hidden_mid, w_up, preferred_element_type=jnp.float32)
    mixed_low = gated(gate_act, up_proj).astype(jnp.bfloat16)
    ffn_branch = over_head(jnp.dot(mixed_low, w_down, preferred_element_type=jnp.float32))
    output_f = residual_mid + rms_scale(ffn_branch, gain_post_ffn)
    grad_output = cotangent.astype(jnp.float32)
    unused_post, post_back = jax.vjp(rms_scale, ffn_branch, gain_post_ffn)
    grad_ffn, grad_g_post_ffn = post_back(grad_output)
    grad_ffn_low = grad_ffn.astype(jnp.bfloat16)
    grad_w_down = jnp.dot(grad_ffn_low.T, mixed_low, preferred_element_type=jnp.float32)
    summed_down = scatter_rows(grad_w_down.astype(jnp.bfloat16))
    grad_mixed = jnp.dot(grad_ffn_low, w_down.T, preferred_element_type=jnp.float32)
    unused_gate, gate_back = jax.vjp(gated, gate_act, up_proj)
    grad_gate, grad_up = gate_back(grad_mixed)
    grad_gate_low = grad_gate.astype(jnp.bfloat16)
    grad_up_low = grad_up.astype(jnp.bfloat16)
    grad_w_gate = jnp.dot(hidden_mid.T, grad_gate_low, preferred_element_type=jnp.float32)
    grad_w_up = jnp.dot(hidden_mid.T, grad_up_low, preferred_element_type=jnp.float32)
    summed_gate = scatter_rows(grad_w_gate.astype(jnp.bfloat16))
    summed_up = scatter_rows(grad_w_up.astype(jnp.bfloat16))
    grad_hidden_part = jnp.dot(
        grad_gate_low, w_gate.T, preferred_element_type=jnp.float32
    ) + jnp.dot(grad_up_low, w_up.T, preferred_element_type=jnp.float32)
    grad_hidden_mid = over_head(grad_hidden_part)
    unused_pre, pre_back = jax.vjp(rms_scale, residual_mid, gain_pre_ffn)
    grad_res_part, grad_g_pre_ffn = pre_back(grad_hidden_mid)
    grad_residual = grad_output + grad_res_part
    unused_attn, attn_post_back = jax.vjp(rms_scale, attn_branch, gain_post_attn)
    grad_attn, grad_g_post_attn = attn_post_back(grad_residual)
    grad_attn_low = grad_attn.astype(jnp.bfloat16)
    grad_w_out = jnp.dot(grad_attn_low.T, attended, preferred_element_type=jnp.float32)
    grad_attended = jnp.dot(grad_attn_low, w_out.T, preferred_element_type=jnp.float32).astype(
        jnp.bfloat16
    )
    grad_attended = grad_attended.reshape(rows, local_heads, head_dim)
    probs_again = jnp.where(visible[None], jnp.exp(raw_scores() - log_total), 0.0)
    grad_probs = jnp.einsum(
        "ihd,jd->hij", grad_attended, all_values, preferred_element_type=jnp.float32
    )
    grad_scores = (
        probs_again * (grad_probs - jnp.sum(probs_again * grad_probs, axis=-1, keepdims=True))
    ).astype(jnp.bfloat16)
    grad_queries = jnp.einsum(
        "hij,jd->ihd", grad_scores, all_keys, preferred_element_type=jnp.float32
    )
    grad_keys_all = jnp.einsum(
        "hij,ihd->jd", grad_scores, queries, preferred_element_type=jnp.float32
    )
    grad_values_all = jnp.einsum(
        "hij,ihd->jd",
        probs_again.astype(jnp.bfloat16),
        grad_attended,
        preferred_element_type=jnp.float32,
    )
    grad_keys = grad_keys_all[2 * rows :]
    grad_values = grad_values_all[2 * rows :]
    for distance in (2, 1):
        piece_begin = (2 - distance) * rows
        returned_keys, returned_values = (
            from_behind(
                grad_keys_all[piece_begin : piece_begin + rows].astype(jnp.bfloat16),
                "seq",
                -distance,
            ).astype(jnp.float32),
            from_behind(
                grad_values_all[piece_begin : piece_begin + rows].astype(jnp.bfloat16),
                "seq",
                -distance,
            ).astype(jnp.float32),
        )
        grad_keys = grad_keys + returned_keys
        grad_values = grad_values + returned_values
    unused_query, query_back = jax.vjp(query_side, query_proj, gain_query)
    grad_query_proj, grad_g_query_part = query_back(grad_queries)
    grad_query_low = grad_query_proj.astype(jnp.bfloat16)
    grad_w_query = jnp.dot(hidden_in.T, grad_query_low, preferred_element_type=jnp.float32)
    grad_hidden_query = jnp.dot(grad_query_low, w_query.T, preferred_element_type=jnp.float32)
    keys_summed, values_summed, hidden_summed, grad_g_query = (
        over_head(grad_keys),
        over_head(grad_values),
        over_head(grad_hidden_query),
        over_head(grad_g_query_part),
    )
    unused_key, key_back = jax.vjp(key_side, key_proj, gain_key)
    grad_key_proj, grad_g_key = key_back(keys_summed)
    grad_key_low = grad_key_proj.astype(jnp.bfloat16)
    grad_value_low = values_summed.astype(jnp.bfloat16)
    grad_w_key = jnp.dot(hidden_in.T, grad_key_low, preferred_element_type=jnp.float32)
    grad_w_value = jnp.dot(hidden_in.T, grad_value_low, preferred_element_type=jnp.float32)
    grad_hidden_in = (
        hidden_summed
        + jnp.dot(grad_key_low, w_key.T, preferred_element_type=jnp.float32)
        + jnp.dot(grad_value_low, w_value.T, preferred_element_type=jnp.float32)
    )
    unused_in, in_back = jax.vjp(rms_scale, inputs_f, gain_in)
    grad_in_part, grad_g_in = in_back(grad_hidden_in)
    grad_inputs = (grad_residual + grad_in_part).astype(jnp.bfloat16)
    count = lax.axis_size("seq")
    gain_columns = jnp.stack(
        [grad_g_in, grad_g_post_attn, grad_g_pre_ffn, grad_g_post_ffn], axis=1
    )
    side = jnp.concatenate(
        [grad_g_query.reshape(count, -1), grad_g_key.reshape(count, -1)], axis=1
    )
    side_rows = jnp.repeat(side, inputs.shape[1] // count, axis=0)
    extra = jnp.concatenate([gain_columns, side_rows], axis=1)
    extra = jnp.pad(extra, ((0, 0), (0, -extra.shape[1] % 128)))
    widths = [g.shape[1] for g in (grad_w_query, grad_w_out, grad_w_key, grad_w_value)]
    attn_sum = scatter_rows(
        jnp.concatenate(
            [
                g.astype(jnp.bfloat16)
                for g in (grad_w_query, grad_w_out, grad_w_key, grad_w_value, extra)
            ],
            axis=1,
        )
    )
    edges = [sum(widths[:i]) for i in range(5)]
    summed_query, summed_out, summed_key, summed_value = (
        attn_sum[:, edges[i] : edges[i + 1]] for i in range(4)
    )
    gain_sum = attn_sum[:, edges[4] :]
    summed_g_in, summed_g_post_attn, summed_g_pre_ffn, summed_g_post_ffn = (
        gain_sum[:, i] for i in range(4)
    )
    own = head_dim // count
    summed_g_query = gain_sum[0, 4 : 4 + own]
    summed_g_key = gain_sum[0, 4 + own : 4 + 2 * own]
    summed_out = summed_out.T
    summed_down = summed_down.T
    return (
        output_f.astype(jnp.bfloat16),
        grad_inputs,
        summed_query,
        summed_key,
        summed_value,
        summed_out,
        summed_gate,
        summed_up,
        summed_down,
        summed_g_in,
        summed_g_query,
        summed_g_key,
        summed_g_post_attn,
        summed_g_pre_ffn,
        summed_g_post_ffn,
    )


def solution(mesh):
    placed = (
        P("seq", None),
        P("seq"),
        P(None, "head"),
        P(),
        P(),
        P("head", None),
        P(None, "head"),
        P(None, "head"),
        P("head", None),
        P(),
        P(),
        P(),
        P(),
        P(),
        P(),
        P("seq", None),
    )
    return jax.shard_map(
        fast_device if mesh.shape["seq"] == 16 else per_device,
        mesh=mesh,
        in_specs=placed,
        out_specs=(
            P("seq", None),
            P("seq", None),
            P("seq", "head"),
            P("seq", None),
            P("seq", None),
            P("head", "seq"),
            P("seq", "head"),
            P("seq", "head"),
            P("head", "seq"),
            P("seq"),
            P("seq"),
            P("seq"),
            P("seq"),
            P("seq"),
            P("seq"),
        ),
        check_vma=False,
    )
```

```python
import functools
import math
import types

import jax
import jax.numpy as jnp
from jax import lax
from jax.experimental import pallas as pl
from jax.experimental.pallas import tpu as pltpu
from jax.sharding import PartitionSpec as P

MESH = pl.DeviceIdType.MESH
WIDE = 384
BLOCK = 72

EPS = 1e-06
QUERY_SCALE = 0.0625


def from_behind(block, axis, distance):
    devices = range(lax.axis_size(axis))
    route = [(i - distance, i) for i in devices if i - distance in devices]
    return lax.ppermute(block, axis, route)


def rms_scale(values, gain):
    return values * lax.rsqrt(jnp.mean(values * values, axis=-1, keepdims=True) + EPS) * gain


def rope_angles(positions, width):
    half_width = width // 2
    frequency = jnp.exp(
        jnp.arange(half_width, dtype=jnp.float32) * (-2.0 * math.log(1000000.0) / width)
    )
    angles = positions.astype(jnp.float32)[:, None] * frequency[None, :]
    return (jnp.cos(angles), jnp.sin(angles))


def rotate(values, cosine, sine):
    half_width = values.shape[-1] // 2
    first_half = values[..., :half_width]
    second_half = values[..., half_width:]
    cos_rows = cosine[:, None, :]
    sin_rows = sine[:, None, :]
    return jnp.concatenate(
        [
            first_half * cos_rows - second_half * sin_rows,
            second_half * cos_rows + first_half * sin_rows,
        ],
        axis=-1,
    )


def prepare(values, gain, cosine, sine, factor):
    return rotate(rms_scale(values, gain), cosine, sine) * factor


def gelu_tanh(values):
    return (
        0.5
        * values
        * (1.0 + jnp.tanh(0.7978845608028654 * (values + 0.044715 * values * values * values)))
    )


def gated(gate_act, up_proj):
    return gelu_tanh(gate_act) * up_proj


def over_head(part):
    low = part.astype(jnp.bfloat16)
    other = lax.ppermute(low, "head", [(0, 1), (1, 0)])
    return low.astype(jnp.float32) + other.astype(jnp.float32)


def place_of():
    seq = lax.axis_index("seq")
    return seq, lax.axis_index("head"), seq % 2, seq // 2 % 2, seq // 4


def dot_nt(left, right):
    return lax.dot_general(left, right, (((1,), (1,)), ((), ())), preferred_element_type=jnp.float32)


def dot_tn(left, right):
    return lax.dot_general(left, right, (((0,), (0,)), ((), ())), preferred_element_type=jnp.float32)


def rotate_back(grad, cosine, sine):
    half = grad.shape[-1] // 2
    first, second = grad[:, :half], grad[:, half:]
    return jnp.concatenate(
        [first * cosine + second * sine, second * cosine - first * sine], axis=-1
    )


def norm_parts(values):
    scale = lax.rsqrt(jnp.mean(values * values, axis=-1, keepdims=True) + EPS)
    return scale, values * scale


def norm_back(grad, gain, scale, normed):
    inner = grad * gain
    back = scale * (inner - normed * jnp.mean(inner * normed, axis=-1, keepdims=True))
    return back, jnp.sum(grad * normed, axis=0, keepdims=True)


CHUNKS = 4
FEEDS = 4
OUT_PARTS = 8


def turn(values, cosine, sine):
    half = values.shape[-1] // 2
    first, second = values[:, :half], values[:, half:]
    return jnp.concatenate(
        [first * cosine - second * sine, second * cosine + first * sine], axis=-1
    )


def to_blocks(target, values, columns):
    turned = values.astype(jnp.float32).T.astype(jnp.bfloat16)
    for half in range(2):
        for x in range(2):
            for f in range(2):
                source = 144 * ((2 * half + f) * 2 + x)
                to = 144 * (half * 4 + x * 2 + f)
                target[to : to + 144, columns] = turned[source : source + 144]


def forward_kernel(names, *refs):
    r = types.SimpleNamespace(**dict(zip(names, refs)))
    seq, head, core, side, level = place_of()
    last_seq = lax.axis_size("seq") - 1
    f32, low = jnp.float32, jnp.bfloat16
    rows, width = r.inputs.shape
    heads = r.w_query.shape[1] // 256
    hidden = r.w_gate.shape[1]
    size = rows // CHUNKS
    feed_size = rows // FEEDS
    even = core == 0

    barrier = pltpu.get_barrier_semaphore()

    def greet(to_seq, to_head):
        pl.semaphore_signal(barrier, inc=1, device_id=(to_seq, to_head), device_id_type=MESH)

    def load(n, src, dst):
        copy = pltpu.make_async_copy(src, dst, r.load_sem.at[n])
        copy.start()
        return copy

    in_copy = load(0, r.inputs, r.x)
    kv_copies = (load(2, r.w_key, r.wk), load(3, r.w_value, r.wv))
    query_copy = load(7, r.w_query, r.wq)
    out_copy = load(8, r.w_out, r.wo.at[head])
    steps = hidden // WIDE

    def tile_loads(j):
        at = pl.ds(pl.multiple_of(j * WIDE, WIDE), WIDE)
        gate_at = pl.ds(pl.multiple_of(2 * j * WIDE, WIDE), WIDE)
        up_at = pl.ds(pl.multiple_of((2 * j + 1) * WIDE, WIDE), WIDE)
        return (
            pltpu.make_async_copy(r.w_gate.at[:, at], r.wgu.at[:, gate_at], r.weight_sem.at[0, j]),
            pltpu.make_async_copy(r.w_up.at[:, at], r.wgu.at[:, up_at], r.weight_sem.at[1, j]),
        )

    for j in range(steps):
        for copy in tile_loads(j):
            copy.start()
    down_copy = load(11, r.w_down, r.wd)
    cot_copy = load(12, r.cotangent, r.cot)

    greet(seq ^ 1, head)
    greet(seq, 1 - head)
    expected = jnp.int32(2)
    for distance in (1, 2):
        @pl.when(seq >= distance)
        def _():
            greet(seq - distance, head)

        @pl.when(seq + distance <= last_seq)
        def _():
            greet(seq + distance, head)

        expected = (
            expected
            + (seq >= distance).astype(jnp.int32)
            + (seq + distance <= last_seq).astype(jnp.int32)
        )
    pl.semaphore_wait(barrier, expected)

    def remote(src, dst, send, recv, to_seq, to_head):
        return pltpu.make_async_remote_copy(
            src_ref=src,
            dst_ref=dst,
            send_sem=send,
            recv_sem=recv,
            device_id=(to_seq, to_head),
            device_id_type=MESH,
        )

    share = r.w_out.shape[0] // 2

    def out_share(which):
        return pl.ds(pl.multiple_of(which * share, share), share)

    def w_out_y(part):
        size = share // OUT_PARTS
        mine = pl.ds(pl.multiple_of(core * share + part * size, size), size)
        return remote(
            r.w_out.at[mine, :], r.wo.at[head, mine, :], r.out_send.at[part], r.out_recv.at[part],
            seq, 1 - head,
        )

    def w_out_start(first):
        for part in (first, first + 1):
            w_out_y(part).start()

    def w_out_core():
        mine = out_share(core)
        part = r.wo.at[1 - head, mine, :]
        return remote(part, part, r.wo_send, r.wo_recv, seq ^ 1, head)

    def ids_send(distance):
        return remote(
            r.ids.at[2], r.ids.at[2 - distance], r.ids_send.at[distance - 1],
            r.ids_recv.at[distance - 1], seq + distance, head,
        )

    def halo(n, distance, hand_on=False):
        kind = r.window.at[n]
        source = kind.at[pl.ds((1 if hand_on else 2) * rows, rows), :]
        target = kind.at[pl.ds((2 - distance) * rows, rows), :]
        place = 2 if hand_on else distance - 1
        return remote(
            source, target, r.halo_send.at[n, place], r.halo_recv.at[n, distance - 1],
            seq + (1 if hand_on else distance), head,
        )

    ids = r.segment_ids[...].astype(f32).reshape(1, rows)
    r.ids[2] = jnp.broadcast_to(ids, (8, rows))
    for distance in (1, 2):
        @pl.when(seq + distance <= last_seq)
        def _():
            ids_send(distance).start()

    w_out_start(0)

    r.gains[...] = jnp.zeros_like(r.gains)
    r.head_gain[...] = jnp.zeros_like(r.head_gain)
    for n, gain in enumerate((r.gain_in, r.gain_post_attn, r.gain_pre_ffn, r.gain_post_ffn)):
        r.gains[n : n + 1, :] = gain[...].reshape(1, width)
    for n, gain in enumerate((r.gain_query, r.gain_key)):
        r.head_gain[n : n + 1, :] = gain[...].reshape(1, 256)
    in_copy.wait()

    def norm_in(c, carry):
        at = pl.ds(pl.multiple_of(c * 128, 128), 128)
        _, normed = norm_parts(r.x[at, :].astype(f32))
        r.normed_in[at, :] = (normed * r.gains[0:1, :]).astype(low)
        return carry

    lax.fori_loop(0, rows // 128, norm_in, 0)
    w_out_start(2)
    for copy in kv_copies:
        copy.wait()
    r.key_raw[...] = jnp.dot(r.normed_in[...], r.wk[...], preferred_element_type=f32)
    r.window[1, 2 * rows :, :] = jnp.dot(
        r.normed_in[...], r.wv[...], preferred_element_type=f32
    ).astype(low)

    def value_halo(distance):
        return halo(1, distance)

    @pl.when(even & (seq + 2 <= last_seq))
    def _():
        value_halo(2).start()

    @pl.when(seq + 1 <= last_seq)
    def _():
        value_halo(1).start()

    w_out_start(4)

    for distance in (1, 2):
        @pl.when(seq >= distance)
        def _():
            remote(
                r.ids.at[2], r.ids.at[2 - distance], r.ids_send.at[distance - 1],
                r.ids_recv.at[distance - 1], seq ^ 1, head,
            ).wait_recv()

        @pl.when(seq < distance)
        def _():
            r.ids[2 - distance] = jnp.full((8, rows), -1.0, f32)

    ids_row = jnp.concatenate([r.ids[b][:1] for b in range(3)], axis=1)
    r.ids_flat[...] = jnp.broadcast_to(ids_row, (8, 3 * rows))
    ids_column = jnp.broadcast_to(r.ids[2][:1], (128, rows)).T
    r.ids_turned[...] = ids_column
    column = lax.broadcasted_iota(jnp.int32, (8, 128), 1).astype(f32)
    frequency = jnp.exp(column * (-2.0 * math.log(1000000.0) / 256))[:1]

    def angles(c, carry):
        at = pl.ds(pl.multiple_of(c * 128, 128), 128)
        here = lax.broadcasted_iota(jnp.int32, (128, 3 * rows), 0) + (2 * rows + c * 128)
        there = lax.broadcasted_iota(jnp.int32, (128, 3 * rows), 1)
        same = (r.ids_turned[at, :1] == r.ids_flat[:1, :]) & (there < here)
        position = jnp.sum(same.astype(f32), axis=1, keepdims=True)
        angle = position * frequency
        r.cosine[at, :] = jnp.cos(angle)
        r.sine[at, :] = jnp.sin(angle)
        return carry

    lax.fori_loop(0, rows // 128, angles, 0)
    _, normed = norm_parts(r.key_raw[...])
    r.window[0, 2 * rows :, :] = turn(
        normed * r.head_gain[1:2, :], r.cosine[...], r.sine[...]
    ).astype(low)

    @pl.when(even & (seq + 2 <= last_seq))
    def _():
        halo(0, 2).start()

    @pl.when(seq + 1 <= last_seq)
    def _():
        halo(0, 1).start()

    w_out_start(6)

    query_copy.wait()
    r.query_raw[...] = jnp.dot(r.normed_in[...], r.wq[...], preferred_element_type=f32)
    for h in range(heads):
        at = slice(256 * h, 256 * h + 256)
        _, normed = norm_parts(r.query_raw[:, at])
        r.q[:, at] = (
            turn(normed * r.head_gain[0:1, :], r.cosine[...], r.sine[...]) * QUERY_SCALE
        ).astype(low)

    def store(n, src, dst):
        copy = pltpu.make_async_copy(src, dst, r.store_sem.at[n])
        copy.start()
        return copy

    to_blocks(r.turned, r.normed_in[...], slice(0, rows))
    stores = [
        store(1, r.key_raw, r.key_proj),
        store(2, r.query_raw, r.query_proj),
        store(3, r.q, r.queries),
        store(4, r.cosine, r.cosine_out),
        store(5, r.sine, r.sine_out),
        store(6, r.ids_flat, r.ids_out),
        store(16, r.gains, r.gain_rows),
        store(17, r.head_gain, r.head_gains),
    ]
    turned_store = store(0, r.turned, r.left_in)

    out_copy.wait()
    for part in range(OUT_PARTS):
        w_out_y(part).wait()
    w_out_core().start()

    def arrival(n, distance):
        return halo(n, distance)

    for n in (1, 0):
        @pl.when(seq >= 1)
        def _():
            arrival(n, 1).wait_recv()

        @pl.when(even & (seq >= 2))
        def _():
            halo(n, 2, True).start()

    for n in (1, 0):
        @pl.when(seq >= 2)
        def _():
            arrival(n, 2).wait_recv()

    for distance in (1, 2):
        @pl.when(seq < distance)
        def _():
            for n in range(2):
                r.window[n, (2 - distance) * rows : (3 - distance) * rows, :] = jnp.zeros(
                    (rows, 256), low
                )

    def head_exchange(c):
        part = r.heads_all.at[head, pl.ds(pl.multiple_of(c * size, size), size), :]
        return remote(part, part, r.y_send.at[c], r.y_recv.at[c], seq, 1 - head)

    def branch_exchange(c):
        at = pl.ds(pl.multiple_of(c * feed_size, feed_size), feed_size)
        return remote(
            r.y_out.at[at, :], r.y_in.at[at, :], r.y_send.at[CHUNKS + c], r.y_recv.at[CHUNKS + c],
            seq, 1 - head,
        )

    def attend(c):
        first = c * size
        span = 2 * rows + size
        at = slice(first, first + size)
        key_at = slice(first, first + span)
        here = lax.broadcasted_iota(jnp.int32, (size, span), 0) + 2 * rows
        there = lax.broadcasted_iota(jnp.int32, (size, span), 1)
        seen = (r.ids_turned[at, :1] == r.ids_flat[:1, key_at]) & (there <= here)
        for h in range(heads):
            head_at = slice(256 * h, 256 * h + 256)
            scores = jnp.where(seen, dot_nt(r.q[at, head_at], r.window[0, key_at, :]), -1e30)
            top = jnp.max(scores, axis=1, keepdims=True)
            expo = jnp.exp(scores - top)
            total = jnp.sum(expo, axis=1, keepdims=True)
            probs = (expo / total).astype(low)
            out = jnp.dot(probs, r.window[1, key_at, :], preferred_element_type=f32)
            r.heads_f[at, head_at] = out
            r.heads_all[head, at, head_at] = out.astype(low)
            r.lse_rows[h : h + 1, at] = jnp.broadcast_to(top + jnp.log(total), (size, 128)).T[:1]
        head_exchange(c).start()

    for c in range(CHUNKS):
        attend(c)
    stores += [
        store(7, r.heads_f, r.attended),
        store(8, r.lse_rows, r.lse),
        store(9, r.window.at[0], r.keys),
        store(10, r.window.at[1], r.values),
    ]
    w_out_core().wait()
    turned_store.wait()

    def feed_rows(c):
        return pl.ds(pl.multiple_of(c * feed_size, feed_size), feed_size)

    def part_stores(c):
        slot = lax.rem(c, 2)
        return (
            pltpu.make_async_copy(
                r.gate_up_part.at[slot], r.gate_up.at[feed_rows(c), :], r.part_sem.at[0, slot]
            ),
            pltpu.make_async_copy(
                r.mixed_part.at[slot], r.mixed.at[feed_rows(c), :], r.part_sem.at[1, slot]
            ),
        )

    def feed(c, carry):
        at = feed_rows(c)
        slot = lax.rem(c, 2)
        head_exchange(c).wait_recv()
        branch = jnp.dot(r.heads_all[0, at, :], r.wo[0], preferred_element_type=f32) + jnp.dot(
            r.heads_all[1, at, :], r.wo[1], preferred_element_type=f32
        )
        r.branch[at, :] = branch
        _, normed = norm_parts(branch)
        middle = r.x[at, :].astype(f32) + normed * r.gains[1:2, :]
        r.middle[at, :] = middle
        _, normed = norm_parts(middle)
        left = (normed * r.gains[2:3, :]).astype(low)
        r.normed_mid[at, :] = left

        @pl.when(c >= 2)
        def _():
            for copy in part_stores(c - 2):
                copy.wait()

        def finish(j, both):
            double = slice(2 * j * WIDE, 2 * (j + 1) * WIDE)
            r.gate_up_part[slot, :, double] = both.astype(low)
            gate, up = both[:, :WIDE], both[:, WIDE:]
            curve = jnp.tanh(0.7978845608028654 * gate * (1.0 + 0.044715 * gate * gate))
            r.mixed_part[slot, :, j * WIDE : (j + 1) * WIDE] = (
                0.5 * gate * (1.0 + curve) * up
            ).astype(low)

        waiting = None
        for j in range(steps):
            double = slice(2 * j * WIDE, 2 * (j + 1) * WIDE)
            both = jnp.dot(left, r.wgu[:, double], preferred_element_type=f32)
            if waiting is not None:
                finish(j - 1, waiting)
            waiting = both
        finish(steps - 1, waiting)
        for copy in part_stores(c):
            copy.start()
        r.y_out[at, :] = jnp.dot(
            r.mixed_part[slot], r.wd[...], preferred_element_type=f32
        ).astype(low)
        branch_exchange(c).start()
        return carry

    for j in range(steps):
        for copy in tile_loads(j):
            copy.wait()
    down_copy.wait()
    lax.fori_loop(0, FEEDS, feed, 0)
    stores += [store(11, r.branch, r.attn_branch), store(12, r.middle, r.residual_mid)]
    to_blocks(r.turned, r.normed_mid[...], slice(0, rows))
    mid_store = store(0, r.turned, r.left_mid)
    cot_copy.wait()
    gain_sum = jnp.zeros((1, width), f32)
    for c in range(FEEDS):
        branch_exchange(c).wait_recv()

        def end(n, total):
            at = pl.ds(pl.multiple_of(c * feed_size + n * 128, 128), 128)
            branch = r.y_out[at, :].astype(f32) + r.y_in[at, :].astype(f32)
            scale, normed = norm_parts(branch)
            r.result[at, :] = (r.middle[at, :] + normed * r.gains[3:4, :]).astype(low)
            back, gain = norm_back(r.cot[at, :].astype(f32), r.gains[3:4, :], scale, normed)
            r.cot[at, :] = back.astype(low)
            return total + gain

        gain_sum = lax.fori_loop(0, feed_size // 128, end, gain_sum)
        if c == 0:
            mid_store.wait()
        at = slice(c * feed_size, (c + 1) * feed_size)
        to_blocks(r.turned, r.cot[at, :], at)
    stores += [
        store(0, r.turned, r.left_ffn),
        store(13, r.cot, r.grad_ffn),
        store(14, r.result, r.output),
    ]
    r.gain_tile[...] = jnp.zeros_like(r.gain_tile)
    r.gain_tile[3:4, :] = gain_sum
    stores.append(store(15, r.gain_tile, r.gain_start))
    for copy in stores:
        copy.wait()
    for distance in (1, 2):
        @pl.when(seq + distance <= last_seq)
        def _():
            ids_send(distance).wait_send()

    for n in range(2):
        @pl.when(seq + 1 <= last_seq)
        def _():
            halo(n, 1).wait_send()

        @pl.when(even & (seq + 2 <= last_seq))
        def _():
            halo(n, 2).wait_send()

        @pl.when(even & (seq >= 2))
        def _():
            halo(n, 2, True).wait_send()

    for c in (FEEDS - 2, FEEDS - 1):
        for copy in part_stores(jnp.int32(c)):
            copy.wait()
    for c in range(CHUNKS):
        head_exchange(c).wait_send()
    for c in range(FEEDS):
        branch_exchange(c).wait_send()


def forward(operands):
    low, f32 = jnp.bfloat16, jnp.float32
    dma = pltpu.SemaphoreType.DMA
    rows, width = operands["inputs"].shape
    hidden = operands["w_gate"].shape[1]
    wide = operands["w_query"].shape[1]
    shape = jax.ShapeDtypeStruct
    anywhere = pl.BlockSpec(memory_space=pl.ANY)
    outs = dict(
        left_in=shape((width, rows), low),
        left_mid=shape((width, rows), low),
        left_ffn=shape((width, rows), low),
        key_proj=shape((rows, 256), f32),
        query_proj=shape((rows, wide), f32),
        queries=shape((rows, wide), low),
        cosine_out=shape((rows, 128), f32),
        sine_out=shape((rows, 128), f32),
        ids_out=shape((8, 3 * rows), f32),
        attended=shape((rows, wide), f32),
        lse=shape((8, rows), f32),
        keys=shape((3 * rows, 256), low),
        values=shape((3 * rows, 256), low),
        attn_branch=shape((rows, width), f32),
        residual_mid=shape((rows, width), f32),
        gate_up=shape((rows, 2 * hidden), low),
        mixed=shape((rows, hidden), low),
        grad_ffn=shape((rows, width), low),
        output=shape((rows, width), low),
        gain_start=shape((8, width), f32),
        gain_rows=shape((8, width), f32),
        head_gains=shape((8, 256), f32),
    )
    feed_size = rows // FEEDS
    vmem = pltpu.VMEM
    scratch = dict(
        x=vmem((rows, width), low),
        gains=vmem((8, width), f32),
        wk=vmem((width, 256), low),
        wv=vmem((width, 256), low),
        head_gain=vmem((8, 256), f32),
        ids=vmem((3, 8, rows), f32),
        ids_flat=vmem((8, 3 * rows), f32),
        ids_turned=vmem((rows, 128), f32),
        wq=vmem((width, wide), low),
        wo=vmem((2, wide, width), low),
        wgu=vmem((width, 2 * hidden), low),
        wd=vmem((hidden, width), low),
        cot=vmem((rows, width), low),
        normed_in=vmem((rows, width), low),
        normed_mid=vmem((rows, width), low),
        key_raw=vmem((rows, 256), f32),
        query_raw=vmem((rows, wide), f32),
        q=vmem((rows, wide), low),
        window=vmem((2, 3 * rows, 256), low),
        cosine=vmem((rows, 128), f32),
        sine=vmem((rows, 128), f32),
        turned=vmem((width, rows), low),
        heads_f=vmem((rows, wide), f32),
        heads_all=vmem((2, rows, wide), low),
        lse_rows=vmem((8, rows), f32),
        branch=vmem((rows, width), f32),
        middle=vmem((rows, width), f32),
        gate_up_part=vmem((2, feed_size, 2 * hidden), low),
        mixed_part=vmem((2, feed_size, hidden), low),
        y_out=vmem((rows, width), low),
        y_in=vmem((rows, width), low),
        result=vmem((rows, width), low),
        gain_tile=vmem((8, width), f32),
        load_sem=dma((13,)),
        store_sem=dma((18,)),
        part_sem=dma((2, 2)),
        weight_sem=dma((2, hidden // WIDE)),
        wo_send=dma(()),
        wo_recv=dma(()),
        out_send=dma((OUT_PARTS,)),
        out_recv=dma((OUT_PARTS,)),
        ids_send=dma((2,)),
        ids_recv=dma((2,)),
        halo_send=dma((2, 3)),
        halo_recv=dma((2, 2)),
        y_send=dma((CHUNKS + FEEDS,)),
        y_recv=dma((CHUNKS + FEEDS,)),
    )
    names = (*operands, *outs, *scratch)
    results = pl.pallas_call(
        functools.partial(forward_kernel, names),
        out_shape=list(outs.values()),
        in_specs=[
            pl.BlockSpec(memory_space=pltpu.VMEM) if len(a.shape) == 1 else anywhere
            for a in operands.values()
        ],
        out_specs=[anywhere] * len(outs),
        scratch_shapes=list(scratch.values()),
        compiler_params=pltpu.CompilerParams(
            collective_id=2, has_side_effects=True, vmem_limit_bytes=62 << 20
        ),
        name="forward",
    )(*operands.values())
    return dict(zip(outs, results))


DOWN, GATE, UP, QUERY, QUERY_END, OUT, OUT_END = range(7)
RING = 6
Y_PARTS = 8
STEPS = 31
FIRST_SIDE = 27
LAG_X = 4
LAG_M = 6
LAG_Z = 8
LAG_END = 10
TURNED = 2


def backward_kernel(names, *refs):
    r = types.SimpleNamespace(**dict(zip(names, refs)))
    seq, head, core, side, level = place_of()
    last_seq = lax.axis_size("seq") - 1
    f32, low = jnp.float32, jnp.bfloat16
    rows = r.grad_ffn.shape[0]
    width = r.grad_ffn.shape[1]

    barrier = pltpu.get_barrier_semaphore()

    def greet(to_seq, to_head):
        pl.semaphore_signal(barrier, inc=1, device_id=(to_seq, to_head), device_id_type=MESH)

    greet(seq ^ 1, head)
    greet(seq ^ 2, head)
    greet(seq, 1 - head)
    for z in range(4):
        for c in range(2):
            other = z * 4 + side * 2 + c

            @pl.when(other != seq)
            def _():
                greet(other, head)

    expected = jnp.int32(10)
    for distance in (1, 2):
        @pl.when(seq >= distance)
        def _():
            greet(seq - distance, head)

        @pl.when(seq + distance <= last_seq)
        def _():
            greet(seq + distance, head)

        expected = (
            expected
            + (seq >= distance).astype(jnp.int32)
            + (seq + distance <= last_seq).astype(jnp.int32)
        )
    pl.semaphore_wait(barrier, expected)

    def remote(src, dst, send, recv, to_seq, to_head):
        return pltpu.make_async_remote_copy(
            src_ref=src,
            dst_ref=dst,
            send_sem=send,
            recv_sem=recv,
            device_id=(to_seq, to_head),
            device_id_type=MESH,
        )

    targets = [((2 * core + k // 2) * 4 + side * 2 + k % 2) for k in range(4)]
    sources = [z * 4 + side * 2 + level // 2 for z in range(4)]
    starts_far = (level == 3 * (1 - core))
    hands_on = (level == 2 - core)
    near = (2 - core) * 4 + side * 2 + core
    far = (3 - 3 * core) * 4 + side * 2 + core
    far_level = 3 * core

    def is_far(k):
        return core == k // 2

    def unheard(z):
        return (level == 3 - z) if z in (0, 3) else False

    def core_copy(t):
        slot = lax.rem(t, RING)
        return remote(
            r.sent.at[lax.rem(t, 2)], r.core_in.at[slot], r.core_send.at[t], r.core_recv.at[t],
            seq ^ 1, head,
        )

    def x_copy(t):
        slot = lax.rem(t, RING)
        return remote(
            r.held.at[slot, 1 - side], r.x_in.at[slot], r.x_send.at[t], r.x_recv.at[t],
            seq ^ 2, head,
        )

    def z_copy(t, k):
        return remote(
            r.z_out.at[lax.rem(t, RING), k], r.z_in.at[t, level],
            r.z_send.at[t, k], r.z_recv.at[t, level], targets[k], head,
        )

    def near_copy(t, k):
        return remote(
            r.z_out.at[lax.rem(t, RING), k], r.m_in.at[lax.rem(t, RING), k % 2],
            r.z_send.at[t, k], r.m_recv.at[t, k % 2], near, head,
        )

    def far_copy(t, g):
        return remote(
            r.z_out.at[lax.rem(t, RING), 2 * core + g], r.z_in.at[t, level],
            r.z_send.at[t, 2 * core + g], r.z_recv.at[t, level],
            far_level * 4 + side * 2 + g, head,
        )

    def z_first(t):
        return lax.rem(t, RING) == TURNED

    def zz_copy(t, x, k):
        n = t // RING
        return remote(
            r.held.at[TURNED, x, k], r.zz_in.at[n, level, x],
            r.zz_send.at[n, x, k], r.zz_recv.at[n, level, x], targets[k], head,
        )

    def zz_near(t, x, k):
        n = t // RING
        return remote(
            r.held.at[TURNED, x, k], r.mm_in.at[n, k % 2, x],
            r.zz_send.at[n, x, k], r.mm_recv.at[n, k % 2, x], near, head,
        )

    def zz_far(t, x, g):
        n = t // RING
        return remote(
            r.mm_in.at[n, g, x], r.zz_in.at[n, level, x],
            r.zz_send.at[n, x, 2 * core + g], r.zz_recv.at[n, level, x],
            far_level * 4 + side * 2 + g, head,
        )

    def xx_copy(t):
        n = t // RING
        return remote(
            r.xx_out.at[n], r.xx_in.at[n], r.xx_send.at[n], r.xx_recv.at[n], seq ^ 2, head
        )

    def zz_sent(t):
        for x in range(2):
            for k in range(4):
                @pl.when(targets[k] != seq)
                def _():
                    zz_copy(t, x, k).wait_send()

    def zz_start(t):
        n = t // RING
        for x in range(2):
            for k in range(4):
                @pl.when(targets[k] == seq)
                def _():
                    r.zz_in[n, level, x] = r.held[TURNED, x, k]

                @pl.when(starts_far & is_far(k))
                def _():
                    zz_near(t, x, k).start()

                @pl.when(
                    (targets[k] != seq) & jnp.logical_not((starts_far | hands_on) & is_far(k))
                )
                def _():
                    zz_copy(t, x, k).start()

    def zz_merge(t):
        n = t // RING

        @pl.when(hands_on)
        def _():
            for x in range(2):
                for g in range(2):
                    remote(
                        r.held.at[TURNED, x, g], r.mm_in.at[n, g, x], r.zz_send.at[n, x, g],
                        r.mm_recv.at[n, g, x], far, head,
                    ).wait_recv()
                    r.mm_in[n, g, x] = (
                        r.mm_in[n, g, x].astype(f32)
                        + r.held[TURNED, x, 2 * core + g].astype(f32)
                    ).astype(low)
                    zz_far(t, x, g).start()

    def zz_sum(t):
        n = t // RING
        for z in range(4):
            @pl.when((sources[z] != seq) & jnp.logical_not(unheard(z)))
            def _():
                for x in range(2):
                    remote(
                        r.held.at[TURNED, x, 0], r.zz_in.at[n, z, x], r.zz_send.at[n, x, 0],
                        r.zz_recv.at[n, z, x], sources[z], head,
                    ).wait_recv()

        def total(x):
            value = r.zz_in[n, 1, x].astype(f32) + r.zz_in[n, 2, x].astype(f32)
            for z in (0, 3):
                value = value + jnp.where(unheard(z), 0.0, r.zz_in[n, z, x].astype(f32))
            return value

        @pl.when(n >= 1)
        def _():
            out_wait(t - RING)

        r.xx_out[n] = total(1 - side).astype(low)
        xx_copy(t).start()
        r.kept[...] = total(side)

    def zz_end(t):
        xx_copy(t).wait()
        r.kept[...] += r.xx_in[t // RING].astype(f32)
        out_start(t)

    def z_arrival(t, z):
        return remote(
            r.z_out.at[0, 0], r.z_in.at[t, z], r.z_send.at[t, 0], r.z_recv.at[t, z],
            sources[z], head,
        )

    def produce(t):
        @pl.when(t >= 2)
        def _():
            core_copy(t - 2).wait_send()

        @pl.when((t >= RING) & jnp.logical_not(z_first(t)))
        def _():
            x_copy(t - RING).wait_send()

        @pl.when((t >= RING) & z_first(t))
        def _():
            zz_sent(t - RING)

        which = jnp.where(t < 9, 0, jnp.where(t < FIRST_SIDE, 1, jnp.where(t < 30, 2, 0)))
        place = jnp.where(
            t < 9, lax.rem(t, 2), jnp.where(t < FIRST_SIDE, t - 7, t - (FIRST_SIDE - 2))
        )
        tile = r.tiles[place]

        def half(start):
            left = r.lefts[which, pl.ds(pl.multiple_of(start, 576), 576), :]
            return jnp.dot(left, tile, preferred_element_type=f32)

        away = half((1 - core) * 576)
        for k in range(8):
            r.sent[lax.rem(t, 2), k // 4, k % 4] = away[k * BLOCK : (k + 1) * BLOCK].astype(low)

        @pl.when(t >= RING)
        def _():
            pl.semaphore_wait(r.core_free, 1)

        def second(start):
            left = r.lefts[0, pl.ds(pl.multiple_of(start, 576), 576), :]
            return jnp.dot(left, tile[:, 256:], preferred_element_type=f32)

        @pl.when(t == FIRST_SIDE + 2)
        def _():
            more = second((1 - core) * 576)
            for k in range(8):
                r.sent[lax.rem(t, 2), k // 4, k % 4, :, 256:] = more[
                    k * BLOCK : (k + 1) * BLOCK
                ].astype(low)

        core_copy(t).start()
        home = half(core * 576)
        for k in range(8):
            r.held[lax.rem(t, RING), k // 4, k % 4] = home[k * BLOCK : (k + 1) * BLOCK].astype(low)

        @pl.when(t == FIRST_SIDE + 2)
        def _():
            more = second(core * 576)
            for k in range(8):
                r.held[lax.rem(t, RING), k // 4, k % 4, :, 256:] = more[
                    k * BLOCK : (k + 1) * BLOCK
                ].astype(low)

    def core_stage(t):
        core_copy(t).wait_recv()
        slot = lax.rem(t, RING)

        def add(part):
            for k in range(4):
                r.held[slot, part, k] = (
                    r.held[slot, part, k].astype(f32) + r.core_in[slot, part, k].astype(f32)
                ).astype(low)

        add(1 - side)

        @pl.when(t >= RING)
        def _():
            pl.semaphore_wait(r.x_free, 1)

        @pl.when(jnp.logical_not(z_first(t)))
        def _():
            x_copy(t).start()

        add(side)

        @pl.when(z_first(t))
        def _():
            zz_start(t)

        @pl.when(t + RING < STEPS)
        def _():
            pl.semaphore_signal(r.core_free, inc=1, device_id=(seq ^ 1, head), device_id_type=MESH)

    def x_stage(t):
        @pl.when(z_first(t))
        def _():
            zz_merge(t)

        @pl.when(starts_far & (t >= RING))
        def _():
            pl.semaphore_wait(r.m_free, 1)

        @pl.when(jnp.logical_not(z_first(t)))
        def _():
            x_add(t)

        @pl.when(t + RING < STEPS)
        def _():
            pl.semaphore_signal(r.x_free, inc=1, device_id=(seq ^ 2, head), device_id_type=MESH)

    def x_add(t):
        x_copy(t).wait_recv()
        slot = lax.rem(t, RING)

        @pl.when(t >= RING)
        def _():
            for k in range(4):
                @pl.when(targets[k] != seq)
                def _():
                    z_copy(t - RING, k).wait_send()

        for k in range(4):
            total = (r.held[slot, side, k].astype(f32) + r.x_in[slot, k].astype(f32)).astype(low)

            @pl.when(targets[k] == seq)
            def _():
                r.z_in[t, level] = total

            @pl.when(targets[k] != seq)
            def _():
                r.z_out[slot, k] = total

                @pl.when(starts_far & is_far(k))
                def _():
                    near_copy(t, k).start()

                @pl.when(jnp.logical_not((starts_far | hands_on) & is_far(k)))
                def _():
                    z_copy(t, k).start()

    def m_stage(t):
        slot = lax.rem(t, RING)

        @pl.when(hands_on & jnp.logical_not(z_first(t)))
        def _():
            for g in range(2):
                remote(
                    r.z_out.at[0, 0], r.m_in.at[slot, g], r.z_send.at[t, 0], r.m_recv.at[t, g],
                    far, head,
                ).wait_recv()
                k = 2 * core + g
                r.z_out[slot, k] = (
                    r.z_out[slot, k].astype(f32) + r.m_in[slot, g].astype(f32)
                ).astype(low)
                far_copy(t, g).start()

        @pl.when(hands_on)
        def _():
            @pl.when(t + RING < STEPS)
            def _():
                pl.semaphore_signal(r.m_free, inc=1, device_id=(far, head), device_id_type=MESH)

    def out_copy(t, kind, source):
        at = pl.multiple_of(lax.rem(t, 9) * WIDE, WIDE)
        if kind == DOWN:
            return pltpu.make_async_copy(
                source, r.down_out.at[:, pl.ds(at, WIDE)], r.out_sem.at[t]
            )
        if kind == QUERY:
            return pltpu.make_async_copy(
                source, r.query_out.at[:, pl.ds(0, WIDE)], r.out_sem.at[t]
            )
        if kind == QUERY_END:
            return pltpu.make_async_copy(
                source.at[:, pl.ds(0, 128)], r.query_out.at[:, pl.ds(WIDE, 128)],
                r.out_sem.at[t],
            )
        if kind == OUT:
            return pltpu.make_async_copy(
                source.at[:, pl.ds(256, 128)], r.out_out.at[:, pl.ds(0, 128)],
                r.out_sem.at[t],
            )
        if kind == OUT_END:
            return pltpu.make_async_copy(
                source, r.out_out.at[:, pl.ds(128, WIDE)], r.out_sem.at[t]
            )
        target = r.gate_out if kind == GATE else r.up_out
        return pltpu.make_async_copy(
            source, target.at[:, pl.ds(at, WIDE)], r.out_sem.at[t]
        )

    KINDS = (
        (DOWN, 0, 9), (GATE, 9, 18), (UP, 18, 27), (QUERY, 27, 28), (QUERY_END, 28, 29),
        (OUT, 29, 30), (OUT_END, 30, 31),
    )

    def out_each(t, act):
        for kind, first, end in KINDS:
            @pl.when((t >= first) & (t < end) & jnp.logical_not(z_first(t)))
            def _():
                act(out_copy(t, kind, r.flat.at[lax.rem(t, 2)]))

            if kind in (DOWN, GATE, UP):
                @pl.when((t >= first) & (t < end) & z_first(t))
                def _():
                    act(out_copy(t, kind, r.kept))

    def out_wait(t):
        out_each(t, lambda copy: copy.wait())

    def out_start(t):
        out_each(t, lambda copy: copy.start())

    def z_stage(t):
        for z in range(4):
            @pl.when((sources[z] != seq) & jnp.logical_not(unheard(z)))
            def _():
                z_arrival(t, z).wait_recv()

        total = r.z_in[t, 1].astype(f32) + r.z_in[t, 2].astype(f32)
        for z in (0, 3):
            total = total + jnp.where(unheard(z), 0.0, r.z_in[t, z].astype(f32))

        before = jnp.where(z_first(t - 2), t - 4, t - 2)

        @pl.when(before >= 0)
        def _():
            out_wait(before)

        r.flat[lax.rem(t, 2)] = total
        out_start(t)

        @pl.when(t == FIRST_SIDE + 1)
        def _():
            r.kv_own[:, :256] = total[:, 128:]

        @pl.when(t == FIRST_SIDE + 2)
        def _():
            r.kv_own[:, 256:] = total[:, :256]

    def pump(i):
        @pl.when(i < STEPS)
        def _():
            produce(i)

        @pl.when((i >= 1) & (i - 1 < STEPS))
        def _():
            core_stage(i - 1)

        @pl.when((i >= LAG_X) & (i - LAG_X < STEPS))
        def _():
            x_stage(i - LAG_X)

        @pl.when((i >= LAG_M) & (i - LAG_M < STEPS))
        def _():
            m_stage(i - LAG_M)

        @pl.when((i >= LAG_Z) & (i - LAG_Z < STEPS))
        def _():
            t = i - LAG_Z

            @pl.when(z_first(t))
            def _():
                zz_sum(t)

            @pl.when(jnp.logical_not(z_first(t)))
            def _():
                z_stage(t)

        @pl.when((i >= LAG_END) & (i - LAG_END < STEPS) & z_first(i - LAG_END))
        def _():
            zz_end(i - LAG_END)

    def y_part(n, part):
        size = rows // Y_PARTS
        at = pl.ds(part * size, size)
        return remote(
            r.y_out.at[at, :], r.y_in.at[n, at, :], r.y_send.at[n, part], r.y_recv.at[n, part],
            seq, 1 - head,
        )

    def y_start(n, first):
        for part in (first, first + 1):
            y_part(n, part).start()

    def y_sent(n):
        for part in range(Y_PARTS):
            y_part(n, part).wait_send()

    def y_arrived(n):
        for part in range(Y_PARTS):
            y_part(n, part).wait_recv()

    def feed_forward(grad, wd, wgu, gate_up, acc):
        sems, grad_sem, left_sem = r.tile_sems, r.grad_sem, r.left_sem

        def copies(j):
            slot = lax.rem(j, 2)
            at = pl.ds(pl.multiple_of(j * WIDE, WIDE), WIDE)
            double = pl.ds(pl.multiple_of(j * 2 * WIDE, 2 * WIDE), 2 * WIDE)
            pairs = (
                (r.w_down.at[at, :], wd),
                (r.gate_up.at[:, double], gate_up),
            )
            halves = (
                (r.w_gate.at[:, at], wgu.at[slot, :, pl.ds(0, WIDE)]),
                (r.w_up.at[:, at], wgu.at[slot, :, pl.ds(WIDE, WIDE)]),
            )
            return [
                pltpu.make_async_copy(src, dst.at[slot], sems.at[n, slot])
                for n, (src, dst) in enumerate(pairs)
            ] + [
                pltpu.make_async_copy(src, dst, sems.at[2 + n, slot])
                for n, (src, dst) in enumerate(halves)
            ]

        def mixed_copy(j):
            slot = lax.rem(j, 2)
            at = pl.ds(pl.multiple_of(j * WIDE, WIDE), WIDE)
            return pltpu.make_async_copy(r.mixed.at[:, at], r.tiles.at[slot], sems.at[5, slot])

        first = [pltpu.make_async_copy(r.grad_ffn, grad, grad_sem)] + [
            pltpu.make_async_copy(left, r.lefts.at[n], left_sem.at[n])
            for n, left in enumerate((r.left_ffn, r.left_mid, r.left_in))
        ]
        for copy in (first[1], mixed_copy(0), first[0], *copies(0), *first[2:]):
            copy.start()
        first[1].wait()
        first[0].wait()
        acc[...] = jnp.zeros_like(acc)

        def step(i, carry):
            @pl.when(i + 1 < 9)
            def _():
                for copy in (mixed_copy(i + 1), *copies(i + 1)):
                    copy.start()

            mixed_copy(i).wait()
            pump(i)
            for copy in copies(i):
                copy.wait()
            slot = lax.rem(i, 2)
            grad_mixed = dot_nt(grad[...], wd[slot])
            v = gate_up[slot, :, :WIDE].astype(f32)
            u = gate_up[slot, :, WIDE:].astype(f32)
            square = v * v
            curve = jnp.tanh(0.7978845608028654 * v * (1.0 + 0.044715 * square))
            gelu = 0.5 * v * (1.0 + curve)
            slope = 0.5 * (1.0 + curve) + 0.5 * v * (1.0 - curve * curve) * (
                0.7978845608028654 * (1.0 + 3.0 * 0.044715 * square)
            )
            grad_gate = (grad_mixed * u * slope).astype(low)
            grad_up = (grad_mixed * gelu).astype(low)
            r.tiles[2 + i] = grad_gate
            r.tiles[11 + i] = grad_up
            acc[...] += dot_nt(jnp.concatenate([grad_gate, grad_up], axis=1), wgu[slot])
            return carry

        lax.fori_loop(0, 9, step, 0)
        for copy in first[2:]:
            copy.wait()
        r.y_out[...] = acc[...].astype(low)

    dma = pltpu.SemaphoreType.DMA
    pl.run_scoped(
        feed_forward,
        pltpu.VMEM((rows, width), low),
        pltpu.VMEM((2, WIDE, width), low),
        pltpu.VMEM((2, width, 2 * WIDE), low),
        pltpu.VMEM((2, rows, 2 * WIDE), low),
        pltpu.VMEM((rows, width), f32),
    )

    def attention(loaded, names, *scoped):
        b = types.SimpleNamespace(**dict(zip(names, scoped)))
        made = {
            name: pltpu.make_async_copy(getattr(r, name), getattr(b, name), b.sems.at[n])
            for n, name in enumerate(loaded)
        }
        for copy in made.values():
            copy.start()
        loads = types.SimpleNamespace(**made)
        heads = r.queries.shape[1] // 256

        def gains_copy(n):
            to_seq, to_head = ((seq, 1 - head), (seq ^ 1, head), (seq ^ 2, head))[n]
            return remote(
                r.gains.at[n], r.gains_in.at[n], r.gains_send.at[n], r.gains_recv.at[n],
                to_seq, to_head,
            )

        def gains_level(z):
            return remote(
                r.gains.at[3], r.gains_z.at[level], r.level_send.at[z], r.level_recv.at[level],
                z * 4 + side * 2 + core, head,
            )

        def gains_from(z):
            return remote(
                r.gains.at[3], r.gains_z.at[z], r.level_send.at[z], r.level_recv.at[z],
                z * 4 + side * 2 + core, head,
            )

        def norms():
            y_arrived(0)
            y_sent(0)
            for copy in (loads.residual_mid, loads.attn_branch, loads.cotangent, loads.gain_rows, loads.head_gains):
                copy.wait()
            loads.gain_start.wait()
            gain_post, gain_pre = b.gain_rows[1:2, :], b.gain_rows[2:3, :]
            size = 128

            def chunk(c, sums):
                at = pl.ds(pl.multiple_of(c * size, size), size)
                grad_mid = r.y_out[at, :].astype(f32) + r.y_in[0, at, :].astype(f32)
                scale, normed = norm_parts(b.residual_mid[at, :])
                back, pre = norm_back(grad_mid, gain_pre, scale, normed)
                grad_residual = b.cotangent[at, :].astype(f32) + back
                b.residual_mid[at, :] = grad_residual
                scale, normed = norm_parts(b.attn_branch[at, :])
                back, post = norm_back(grad_residual, gain_post, scale, normed)
                r.y_out[at, :] = back.astype(low)
                return sums[0] + post, sums[1] + pre

            zero = jnp.zeros((1, width), f32)
            post, pre = lax.fori_loop(0, rows // size, chunk, (zero, zero))
            r.gains[0] = b.gain_start[...]
            r.gains[0, 1:2, :] = post
            r.gains[0, 2:3, :] = pre

        def through_out():
            for copy in (loads.w_out, loads.attended, loads.lse):
                copy.wait()
            b.grad_attended[...] = dot_nt(r.y_out[...], b.w_out[...]).astype(low)
            for h in range(heads):
                at = slice(256 * h, 256 * h + 256)
                delta = jnp.sum(
                    b.grad_attended[:, at].astype(f32) * b.attended[:, at], axis=1, keepdims=True
                )
                b.delta[h : h + 1, :] = jnp.broadcast_to(delta, (rows, 128)).T[:1]
            to_blocks(r.lefts.at[0], r.y_out[...], slice(0, rows))
            r.tiles[4, :, 256:] = b.attended[:, :128].astype(low)
            r.tiles[5] = b.attended[:, 128:].astype(low)

        def attend(block):
            if block == 0:
                for copy in (loads.queries, loads.keys, loads.values, loads.ids_out):
                    copy.wait()
                b.grad_queries[...] = jnp.zeros_like(b.grad_queries)
                b.ids_turned[...] = jnp.broadcast_to(b.ids_out[:1], (128, 3 * rows)).T
            size = 256

            def chunk(c, carry):
                local = pl.multiple_of(c * size, size)
                at = pl.ds(pl.multiple_of(block * rows + c * size, size), size)
                keys, values = b.keys[at, :], b.values[at, :]
                seen = b.ids_turned[at, :1] == b.ids_out[:1, 2 * rows :]
                if block == 2:
                    key_at = lax.broadcasted_iota(jnp.int32, (size, rows), 0) + local
                    query_at = lax.broadcasted_iota(jnp.int32, (size, rows), 1)
                    seen = seen & (key_at <= query_at)
                grad_keys = jnp.zeros((size, 256), f32)
                grad_values = jnp.zeros((size, 256), f32)
                for h in range(heads):
                    head_at = slice(256 * h, 256 * h + 256)
                    q, grad_out = b.queries[:, head_at], b.grad_attended[:, head_at]
                    probs = jnp.where(
                        seen, jnp.exp(dot_nt(keys, q) - b.lse[h : h + 1, :]), 0.0
                    )
                    grad_probs = dot_nt(values, grad_out)
                    grad_scores = (probs * (grad_probs - b.delta[h : h + 1, :])).astype(low)
                    grad_keys += jnp.dot(grad_scores, q, preferred_element_type=f32)
                    grad_values += jnp.dot(
                        probs.astype(low), grad_out, preferred_element_type=f32
                    )
                    b.grad_queries[:, head_at] += dot_tn(grad_scores, keys)
                to = pl.ds(local, size)
                if block == 2:
                    b.grad_own[0, to, :] = grad_keys
                    b.grad_own[1, to, :] = grad_values
                else:
                    r.halo_out[block, 0, to, :] = grad_keys.astype(low)
                    r.halo_out[block, 1, to, :] = grad_values.astype(low)
                return carry

            lax.fori_loop(0, rows // size, chunk, 0)
            if block == 0:
                @pl.when((seq >= 2) & (core == 1))
                def _():
                    relay_copy().start()

                halo_start(0, 0)

            if block == 1:
                @pl.when((core == 0) & (seq >= 2))
                def _():
                    remote(
                        r.halo_out.at[0], r.relay_in, r.relay_send, r.relay_recv, seq ^ 1, head
                    ).wait_recv()
                    for n in range(2):
                        r.halo_out[1, n] = (
                            r.halo_out[1, n].astype(f32) + r.relay_in[n].astype(f32)
                        ).astype(low)

        def relay_copy():
            return remote(
                r.halo_out.at[0], r.relay_in, r.relay_send, r.relay_recv, seq - 1, head
            )

        def halo_part(block, n, half):
            at = pl.ds(half * (rows // 2), rows // 2)
            return remote(
                r.halo_out.at[block, n, at, :], r.halo_in.at[block, n, at, :],
                r.halo_send.at[block, n, half], r.halo_recv.at[block, n, half],
                seq - (2 - block), head,
            )

        def halo_start(block, n):
            @pl.when((seq >= 1) if block == 1 else (seq >= 2) & (core == 0))
            def _():
                for half in range(2):
                    halo_part(block, n, half).start()

        def halo_parts(block):
            return [halo_part(block, n, half) for n in range(2) for half in range(2)]

        def query_side():
            for copy in (loads.query_proj, loads.cosine_out, loads.sine_out, loads.w_query):
                copy.wait()
            total = jnp.zeros((1, 256), f32)
            for h in range(heads):
                at = slice(256 * h, 256 * h + 256)
                grad = rotate_back(
                    b.grad_queries[:, at] * QUERY_SCALE, b.cosine_out[...], b.sine_out[...]
                )
                scale, normed = norm_parts(b.query_proj[:, at])
                back, gain = norm_back(grad, b.head_gains[0:1, :], scale, normed)
                total += gain
                back = back.astype(low)
                if h == 0:
                    r.tiles[2, :, :256] = back
                else:
                    r.tiles[2, :, 256:] = back[:, :128]
                    r.tiles[3, :, :128] = back[:, 128:]
                part = dot_nt(back, b.w_query[:, at])
                if h == 0:
                    b.attn_branch[...] = part
                else:
                    b.attn_branch[...] += part
            r.gains[0, 4:5, :256] = total

        def key_side():
            for copy in (loads.key_proj, loads.w_key, loads.w_value, loads.inputs):
                copy.wait()
            for block in range(2):
                heard = seq + (2 - block) <= last_seq

                @pl.when(heard & (core == 0) if block == 0 else heard)
                def _():
                    for copy in halo_parts(block):
                        copy.wait_recv()
                    for n in range(2):
                        b.grad_own[n] += r.halo_in[block, n].astype(f32)

            grad = rotate_back(b.grad_own[0], b.cosine_out[...], b.sine_out[...])
            scale, normed = norm_parts(b.key_proj[...])
            back, gain = norm_back(grad, b.head_gains[1:2, :], scale, normed)
            r.gains[0, 4:5, 256:512] = gain
            grad_key, grad_value = back.astype(low), b.grad_own[1].astype(low)
            r.tiles[3, :, 128:] = grad_key
            r.tiles[4, :, :256] = grad_value
            b.attn_branch[...] += dot_nt(grad_key, b.w_key[...])
            b.attn_branch[...] += dot_nt(grad_value, b.w_value[...])
            size = 128

            def chunk(c, total):
                at = pl.ds(pl.multiple_of(c * size, size), size)
                part = b.attn_branch[at, :]
                scale, normed = norm_parts(b.inputs[at, :].astype(f32))
                r.y_out[at, :] = part.astype(low)
                return total + jnp.sum(part * normed, axis=0, keepdims=True)

            zero = jnp.zeros((1, width), f32)
            r.gains[0, 0:1, :] = lax.fori_loop(0, rows // size, chunk, zero)
            gains_copy(0).start()

        def gains_stage(n):
            gains_copy(n).wait_recv()
            own, other = r.gains[n], r.gains_in[n]
            if n == 0:
                row = lax.broadcasted_iota(jnp.int32, own.shape, 0)
                other = jnp.where((row == 0) | (row == 4), other, 0.0)
            r.gains[n + 1] = own + other
            if n < 2:
                gains_copy(n + 1).start()
            else:
                for z in range(4):
                    @pl.when(level == z)
                    def _():
                        r.gains_z[z] = r.gains[3]

                    @pl.when(level != z)
                    def _():
                        gains_level(z).start()

        def gains_end():
            for z in range(4):
                @pl.when(level != z)
                def _():
                    gains_from(z).wait_recv()

            r.gains_out[...] = (r.gains_z[0] + r.gains_z[1]) + (r.gains_z[2] + r.gains_z[3])

        def finish_inputs():
            y_arrived(1)
            size = 128

            def chunk(c, carry):
                at = pl.ds(pl.multiple_of(c * size, size), size)
                grad = r.y_out[at, :].astype(f32) + r.y_in[1, at, :].astype(f32)
                scale, normed = norm_parts(b.inputs[at, :].astype(f32))
                back, _ = norm_back(grad, b.gain_rows[0:1, :], scale, normed)
                r.inputs_out[at, :] = (b.residual_mid[at, :] + back).astype(low)
                return carry

            lax.fori_loop(0, rows // size, chunk, 0)

        def kv_copy():
            return remote(r.kv_own, r.kv_in, r.kv_send, r.kv_recv, seq, 1 - head)

        pieces = (
            *((9 + n, functools.partial(y_start, 0, 2 * n)) for n in range(4)),
            (16, norms),
            (17, through_out),
            (18, lambda: attend(0)),
            (19, lambda: halo_start(0, 1)),
            (19, lambda: attend(1)),
            (20, lambda: halo_start(1, 0)),
            (20, lambda: attend(2)),
            (21, lambda: halo_start(1, 1)),
            (21, query_side),
            (24, key_side),
            *((24 + n, functools.partial(y_start, 1, 2 * n)) for n in range(4)),
            (25, lambda: gains_stage(0)),
            (26, lambda: gains_stage(1)),
            (27, lambda: gains_stage(2)),
            (29, gains_end),
            (32, finish_inputs),
            (FIRST_SIDE + 3 + LAG_Z, lambda: kv_copy().start()),
        )

        def step(i, carry):
            for k, piece in pieces:
                @pl.when(i == k)
                def _():
                    piece()

            pump(i)
            return carry

        lax.fori_loop(9, STEPS + LAG_Z, step, 0)
        kv_copy().wait()
        r.kv_out[...] = r.kv_own[...] + r.kv_in[...]
        y_sent(1)
        for n in range(3):
            gains_copy(n).wait_send()
        for z in range(4):
            @pl.when(level != z)
            def _():
                gains_level(z).wait_send()

        @pl.when((seq >= 2) & (core == 1))
        def _():
            relay_copy().wait_send()

        @pl.when((seq >= 2) & (core == 0))
        def _():
            for copy in halo_parts(0):
                copy.wait_send()

        @pl.when(seq >= 1)
        def _():
            for copy in halo_parts(1):
                copy.wait_send()

    heads_width = r.queries.shape[1]
    def shape(size, kind):
        return pltpu.VMEM(size, kind)

    loaded = dict(
        residual_mid=shape((rows, width), f32),
        attn_branch=shape((rows, width), f32),
        cotangent=shape((rows, width), low),
        inputs=shape((rows, width), low),
        gain_rows=shape((8, width), f32),
        head_gains=shape((8, 256), f32),
        gain_start=shape((8, width), f32),
        w_out=shape((heads_width, width), low),
        attended=shape((rows, heads_width), f32),
        lse=shape((8, rows), f32),
        queries=shape((rows, heads_width), low),
        keys=shape((3 * rows, 256), low),
        values=shape((3 * rows, 256), low),
        ids_out=shape((8, 3 * rows), f32),
        query_proj=shape((rows, heads_width), f32),
        key_proj=shape((rows, 256), f32),
        cosine_out=shape((rows, 128), f32),
        sine_out=shape((rows, 128), f32),
        w_query=shape((width, heads_width), low),
        w_key=shape((width, 256), low),
        w_value=shape((width, 256), low),
    )
    scoped = dict(
        loaded,
        grad_attended=shape((rows, heads_width), low),
        delta=shape((8, rows), f32),
        grad_queries=shape((rows, heads_width), f32),
        grad_own=shape((2, rows, 256), f32),
        ids_turned=shape((3 * rows, 128), f32),
        sems=dma((len(loaded),)),
    )
    pl.run_scoped(functools.partial(attention, tuple(loaded), tuple(scoped)), *scoped.values())

    def drain(i, carry):
        @pl.when(i >= STEPS - 2)
        def _():
            core_copy(i).wait_send()
            out_wait(i)

        @pl.when(z_first(i))
        def _():
            zz_sent(i)
            out_wait(i)

        @pl.when(jnp.logical_not(z_first(i)))
        def _():
            x_copy(i).wait_send()
            for k in range(4):
                @pl.when(targets[k] != seq)
                def _():
                    z_copy(i, k).wait_send()

        return carry

    lax.fori_loop(STEPS - RING, STEPS, drain, 0)


def backward(operands):
    low, f32 = jnp.bfloat16, jnp.float32
    dma = pltpu.SemaphoreType.DMA
    rows, width = operands["grad_ffn"].shape
    hidden = operands["w_gate"].shape[1]
    wide = operands["w_query"].shape[1]
    turned = (STEPS - TURNED + RING - 1) // RING
    anywhere = pl.BlockSpec(memory_space=pl.ANY)
    vmem = pl.BlockSpec(memory_space=pltpu.VMEM)
    outs = dict(
        down_out=(jax.ShapeDtypeStruct((BLOCK, hidden), f32), anywhere),
        gate_out=(jax.ShapeDtypeStruct((BLOCK, hidden), f32), anywhere),
        up_out=(jax.ShapeDtypeStruct((BLOCK, hidden), f32), anywhere),
        query_out=(jax.ShapeDtypeStruct((BLOCK, wide), f32), anywhere),
        out_out=(jax.ShapeDtypeStruct((BLOCK, wide), f32), anywhere),
        kv_out=(jax.ShapeDtypeStruct((BLOCK, 512), f32), vmem),
        gains_out=(jax.ShapeDtypeStruct((8, width), f32), vmem),
        inputs_out=(jax.ShapeDtypeStruct((rows, width), low), vmem),
    )
    scratch = dict(
        held=pltpu.VMEM((RING, 2, 4, BLOCK, WIDE), low),
        sent=pltpu.VMEM((2, 2, 4, BLOCK, WIDE), low),
        core_in=pltpu.VMEM((RING, 2, 4, BLOCK, WIDE), low),
        x_in=pltpu.VMEM((RING, 4, BLOCK, WIDE), low),
        m_in=pltpu.VMEM((RING, 2, BLOCK, WIDE), low),
        zz_in=pltpu.VMEM((turned, 4, 2, BLOCK, WIDE), low),
        mm_in=pltpu.VMEM((turned, 2, 2, BLOCK, WIDE), low),
        xx_out=pltpu.VMEM((turned, BLOCK, WIDE), low),
        xx_in=pltpu.VMEM((turned, BLOCK, WIDE), low),
        kept=pltpu.VMEM((BLOCK, WIDE), f32),
        z_out=pltpu.VMEM((RING, 4, BLOCK, WIDE), low),
        z_in=pltpu.VMEM((STEPS, 4, BLOCK, WIDE), low),
        tiles=pltpu.VMEM((20, rows, WIDE), low),
        lefts=pltpu.VMEM((3, width, rows), low),
        y_out=pltpu.VMEM((rows, width), low),
        y_in=pltpu.VMEM((2, rows, width), low),
        halo_out=pltpu.VMEM((2, 2, rows, 256), low),
        halo_in=pltpu.VMEM((2, 2, rows, 256), low),
        relay_in=pltpu.VMEM((2, rows, 256), low),
        gains=pltpu.VMEM((4, 8, width), f32),
        gains_in=pltpu.VMEM((3, 8, width), f32),
        gains_z=pltpu.VMEM((4, 8, width), f32),
        kv_own=pltpu.VMEM((BLOCK, 512), f32),
        kv_in=pltpu.VMEM((BLOCK, 512), f32),
        flat=pltpu.VMEM((2, BLOCK, WIDE), f32),
        core_send=dma((STEPS,)),
        core_recv=dma((STEPS,)),
        x_send=dma((STEPS,)),
        x_recv=dma((STEPS,)),
        z_send=dma((STEPS, 4)),
        z_recv=dma((STEPS, 4)),
        out_sem=dma((STEPS,)),
        y_send=dma((2, Y_PARTS)),
        y_recv=dma((2, Y_PARTS)),
        halo_send=dma((2, 2, 2)),
        halo_recv=dma((2, 2, 2)),
        gains_send=dma((3,)),
        gains_recv=dma((3,)),
        level_send=dma((4,)),
        level_recv=dma((4,)),
        kv_send=dma(()),
        kv_recv=dma(()),
        tile_sems=dma((6, 2)),
        grad_sem=dma(()),
        left_sem=dma((3,)),
        m_recv=dma((STEPS, 2)),
        zz_send=dma((turned, 2, 4)),
        zz_recv=dma((turned, 4, 2)),
        mm_recv=dma((turned, 2, 2)),
        xx_send=dma((turned,)),
        xx_recv=dma((turned,)),
        m_free=pltpu.SemaphoreType.REGULAR,
        relay_send=dma(()),
        relay_recv=dma(()),
        core_free=pltpu.SemaphoreType.REGULAR,
        x_free=pltpu.SemaphoreType.REGULAR,
    )
    names = (*operands, *outs, *scratch)
    results = pl.pallas_call(
        functools.partial(backward_kernel, names),
        out_shape=[shape for shape, _ in outs.values()],
        in_specs=[anywhere] * len(operands),
        out_specs=[spec for _, spec in outs.values()],
        scratch_shapes=list(scratch.values()),
        compiler_params=pltpu.CompilerParams(
            collective_id=1, has_side_effects=True, vmem_limit_bytes=62 << 20
        ),
        name="backward",
    )(*operands.values())
    return dict(zip(outs, results))


def last_kernel(names, *refs):
    r = types.SimpleNamespace(**dict(zip(names, refs)))
    place = lax.axis_index("seq")
    pairs = (
        (r.output, r.output_held, r.output_end),
        (r.inputs_out, r.inputs_held, r.inputs_end),
        (r.gate_out, r.gate_held, r.gate_end),
        (r.up_out, r.up_held, r.up_end),
        (r.down_out, r.down_held, r.down_end),
        (r.query_out, r.query_held, r.query_end),
        (r.out_out, r.out_held, r.out_end),
        (r.kv_out.at[:, pl.ds(0, 256)], r.key_held, r.key_end),
        (r.kv_out.at[:, pl.ds(256, 256)], r.value_held, r.value_end),
    )
    loads = [
        pltpu.make_async_copy(src, held, r.sems.at[0, n]) for n, (src, held, _) in enumerate(pairs)
    ]
    copies = [
        pltpu.make_async_copy(held, dst, r.sems.at[1, n]) for n, (_, held, dst) in enumerate(pairs)
    ]
    for copy in loads:
        copy.start()
    width = r.gains_out.shape[1]
    rolled = pltpu.roll(r.gains_out[...], lax.rem(width - place * BLOCK, width), 1)
    for n, target in enumerate((r.in_end, r.post_attn_end, r.pre_ffn_end, r.post_ffn_end)):
        target[...] = rolled[n : n + 1, :BLOCK].reshape(BLOCK)
    own = r.gain_query_end.shape[0]
    for n, target in enumerate((r.gain_query_end, r.gain_key_end)):
        rolled = pltpu.roll(r.gains_out[...], lax.rem(2 * width - place * own - 256 * n, width), 1)
        target[...] = rolled[4:5, :own].reshape(own)
    for load, copy in zip(loads, copies):
        load.wait()
        copy.start()
    for copy in copies:
        copy.wait()


def last(operands):
    f32 = jnp.float32
    anywhere = pl.BlockSpec(memory_space=pl.ANY)
    vmem = pl.BlockSpec(memory_space=pltpu.VMEM)
    shape = jax.ShapeDtypeStruct
    like = types.SimpleNamespace(**operands)
    part = shape((BLOCK, 256), f32)
    gain = shape((BLOCK,), f32)
    small = shape((256 // lax.axis_size("seq"),), f32)
    outs = dict(
        output_end=like.output,
        inputs_end=like.inputs_out,
        query_end=like.query_out,
        key_end=part,
        value_end=part,
        out_end=like.out_out,
        gate_end=like.gate_out,
        up_end=like.up_out,
        down_end=like.down_out,
        in_end=gain,
        gain_query_end=small,
        gain_key_end=small,
        post_attn_end=gain,
        pre_ffn_end=gain,
        post_ffn_end=gain,
    )
    held = dict(
        output_held=like.output,
        inputs_held=like.inputs_out,
        gate_held=like.gate_out,
        up_held=like.up_out,
        down_held=like.down_out,
        query_held=like.query_out,
        out_held=like.out_out,
        key_held=part,
        value_held=part,
    )
    names = (*operands, *outs, *held, *dict(sems=0))
    return pl.pallas_call(
        functools.partial(last_kernel, names),
        out_shape=[shape(a.shape, a.dtype) for a in outs.values()],
        in_specs=[vmem if name == "gains_out" else anywhere for name in operands],
        out_specs=[vmem if len(a.shape) == 1 else anywhere for a in outs.values()],
        scratch_shapes=[pltpu.VMEM(a.shape, a.dtype) for a in held.values()]
        + [pltpu.SemaphoreType.DMA((2, len(held)))],
        name="last",
    )(*operands.values())


def fast_device(
    inputs,
    segment_ids,
    w_query,
    w_key,
    w_value,
    w_out,
    w_gate,
    w_up,
    w_down,
    gain_in,
    gain_query,
    gain_key,
    gain_post_attn,
    gain_pre_ffn,
    gain_post_ffn,
    cotangent,
):
    shared = dict(
        inputs=inputs, cotangent=cotangent, w_query=w_query, w_key=w_key, w_value=w_value,
        w_out=w_out, w_gate=w_gate, w_up=w_up, w_down=w_down,
    )
    first = forward(
        dict(
            shared,
            segment_ids=segment_ids, gain_in=gain_in, gain_query=gain_query, gain_key=gain_key,
            gain_post_attn=gain_post_attn, gain_pre_ffn=gain_pre_ffn, gain_post_ffn=gain_post_ffn,
        )
    )
    output = first.pop("output")
    results = last(dict(backward(dict(shared, **first)), output=output))
    return tuple(a.T if n in (5, 8) else a for n, a in enumerate(results))


def scatter_rows(grad):
    return lax.psum_scatter(grad, "seq", scatter_dimension=0, tiled=True).astype(jnp.float32)


def per_device(
    inputs,
    segment_ids,
    w_query,
    w_key,
    w_value,
    w_out,
    w_gate,
    w_up,
    w_down,
    gain_in,
    gain_query,
    gain_key,
    gain_post_attn,
    gain_pre_ffn,
    gain_post_ffn,
    cotangent,
):
    rows = inputs.shape[0]
    head_dim = w_key.shape[1]
    local_heads = w_query.shape[1] // head_dim
    place = lax.axis_index("seq")
    local_index = jnp.arange(rows, dtype=jnp.int32)
    ids_parts = [
        jnp.where(place >= distance, from_behind(segment_ids, "seq", distance), -1)
        for distance in (2, 1)
    ]
    window_ids = jnp.concatenate(ids_parts + [segment_ids], axis=0)
    window_index = jnp.arange(3 * rows, dtype=jnp.int32) - 2 * rows
    same = segment_ids[:, None] == window_ids[None, :]
    visible = same & (window_index[None, :] <= local_index[:, None])
    positions = jnp.sum(visible.astype(jnp.int32), axis=1) - 1
    cosine, sine = rope_angles(positions, head_dim)
    inputs_f = inputs.astype(jnp.float32)
    hidden_in = rms_scale(inputs_f, gain_in).astype(jnp.bfloat16)
    query_proj = jnp.dot(hidden_in, w_query, preferred_element_type=jnp.float32)
    key_proj = jnp.dot(hidden_in, w_key, preferred_element_type=jnp.float32)
    value_proj = jnp.dot(hidden_in, w_value, preferred_element_type=jnp.float32)

    def query_side(projection, gain):
        return prepare(
            projection.reshape(rows, local_heads, head_dim), gain, cosine, sine, QUERY_SCALE
        )

    def key_side(projection, gain):
        return prepare(projection[:, None, :], gain, cosine, sine, 1.0)[:, 0, :]

    queries = query_side(query_proj, gain_query).astype(jnp.bfloat16)
    own_keys = key_side(key_proj, gain_key).astype(jnp.bfloat16)
    own_values = value_proj.astype(jnp.bfloat16)
    key_parts = []
    value_parts = []
    for distance in (2, 1):
        moved_keys, moved_values = from_behind((own_keys, own_values), "seq", distance)
        key_parts.append(moved_keys)
        value_parts.append(moved_values)
    all_keys = jnp.concatenate(key_parts + [own_keys], axis=0)
    all_values = jnp.concatenate(value_parts + [own_values], axis=0)
    def raw_scores():
        return jnp.einsum("ihd,jd->hij", queries, all_keys, preferred_element_type=jnp.float32)

    scores = jnp.where(visible[None], raw_scores(), -1e30)
    row_max = jnp.max(scores, axis=-1, keepdims=True)
    expo = jnp.exp(scores - row_max)
    total = jnp.sum(expo, axis=-1, keepdims=True)
    attn_probs = expo / total
    log_total = row_max + jnp.log(total)
    attended = jnp.einsum(
        "hij,jd->ihd",
        attn_probs.astype(jnp.bfloat16),
        all_values,
        preferred_element_type=jnp.float32,
    )
    attended = attended.reshape(rows, local_heads * head_dim).astype(jnp.bfloat16)
    attn_branch = over_head(jnp.dot(attended, w_out, preferred_element_type=jnp.float32))
    residual_mid = inputs_f + rms_scale(attn_branch, gain_post_attn)
    hidden_mid = rms_scale(residual_mid, gain_pre_ffn).astype(jnp.bfloat16)
    gate_act = jnp.dot(hidden_mid, w_gate, preferred_element_type=jnp.float32)
    up_proj = jnp.dot(hidden_mid, w_up, preferred_element_type=jnp.float32)
    mixed_low = gated(gate_act, up_proj).astype(jnp.bfloat16)
    ffn_branch = over_head(jnp.dot(mixed_low, w_down, preferred_element_type=jnp.float32))
    output_f = residual_mid + rms_scale(ffn_branch, gain_post_ffn)
    grad_output = cotangent.astype(jnp.float32)
    unused_post, post_back = jax.vjp(rms_scale, ffn_branch, gain_post_ffn)
    grad_ffn, grad_g_post_ffn = post_back(grad_output)
    grad_ffn_low = grad_ffn.astype(jnp.bfloat16)
    grad_w_down = jnp.dot(grad_ffn_low.T, mixed_low, preferred_element_type=jnp.float32)
    summed_down = scatter_rows(grad_w_down.astype(jnp.bfloat16))
    grad_mixed = jnp.dot(grad_ffn_low, w_down.T, preferred_element_type=jnp.float32)
    unused_gate, gate_back = jax.vjp(gated, gate_act, up_proj)
    grad_gate, grad_up = gate_back(grad_mixed)
    grad_gate_low = grad_gate.astype(jnp.bfloat16)
    grad_up_low = grad_up.astype(jnp.bfloat16)
    grad_w_gate = jnp.dot(hidden_mid.T, grad_gate_low, preferred_element_type=jnp.float32)
    grad_w_up = jnp.dot(hidden_mid.T, grad_up_low, preferred_element_type=jnp.float32)
    summed_gate = scatter_rows(grad_w_gate.astype(jnp.bfloat16))
    summed_up = scatter_rows(grad_w_up.astype(jnp.bfloat16))
    grad_hidden_part = jnp.dot(
        grad_gate_low, w_gate.T, preferred_element_type=jnp.float32
    ) + jnp.dot(grad_up_low, w_up.T, preferred_element_type=jnp.float32)
    grad_hidden_mid = over_head(grad_hidden_part)
    unused_pre, pre_back = jax.vjp(rms_scale, residual_mid, gain_pre_ffn)
    grad_res_part, grad_g_pre_ffn = pre_back(grad_hidden_mid)
    grad_residual = grad_output + grad_res_part
    unused_attn, attn_post_back = jax.vjp(rms_scale, attn_branch, gain_post_attn)
    grad_attn, grad_g_post_attn = attn_post_back(grad_residual)
    grad_attn_low = grad_attn.astype(jnp.bfloat16)
    grad_w_out = jnp.dot(grad_attn_low.T, attended, preferred_element_type=jnp.float32)
    grad_attended = jnp.dot(grad_attn_low, w_out.T, preferred_element_type=jnp.float32).astype(
        jnp.bfloat16
    )
    grad_attended = grad_attended.reshape(rows, local_heads, head_dim)
    probs_again = jnp.where(visible[None], jnp.exp(raw_scores() - log_total), 0.0)
    grad_probs = jnp.einsum(
        "ihd,jd->hij", grad_attended, all_values, preferred_element_type=jnp.float32
    )
    grad_scores = (
        probs_again * (grad_probs - jnp.sum(probs_again * grad_probs, axis=-1, keepdims=True))
    ).astype(jnp.bfloat16)
    grad_queries = jnp.einsum(
        "hij,jd->ihd", grad_scores, all_keys, preferred_element_type=jnp.float32
    )
    grad_keys_all = jnp.einsum(
        "hij,ihd->jd", grad_scores, queries, preferred_element_type=jnp.float32
    )
    grad_values_all = jnp.einsum(
        "hij,ihd->jd",
        probs_again.astype(jnp.bfloat16),
        grad_attended,
        preferred_element_type=jnp.float32,
    )
    grad_keys = grad_keys_all[2 * rows :]
    grad_values = grad_values_all[2 * rows :]
    for distance in (2, 1):
        piece_begin = (2 - distance) * rows
        returned_keys, returned_values = (
            from_behind(
                grad_keys_all[piece_begin : piece_begin + rows].astype(jnp.bfloat16),
                "seq",
                -distance,
            ).astype(jnp.float32),
            from_behind(
                grad_values_all[piece_begin : piece_begin + rows].astype(jnp.bfloat16),
                "seq",
                -distance,
            ).astype(jnp.float32),
        )
        grad_keys = grad_keys + returned_keys
        grad_values = grad_values + returned_values
    unused_query, query_back = jax.vjp(query_side, query_proj, gain_query)
    grad_query_proj, grad_g_query_part = query_back(grad_queries)
    grad_query_low = grad_query_proj.astype(jnp.bfloat16)
    grad_w_query = jnp.dot(hidden_in.T, grad_query_low, preferred_element_type=jnp.float32)
    grad_hidden_query = jnp.dot(grad_query_low, w_query.T, preferred_element_type=jnp.float32)
    keys_summed, values_summed, hidden_summed, grad_g_query = (
        over_head(grad_keys),
        over_head(grad_values),
        over_head(grad_hidden_query),
        over_head(grad_g_query_part),
    )
    unused_key, key_back = jax.vjp(key_side, key_proj, gain_key)
    grad_key_proj, grad_g_key = key_back(keys_summed)
    grad_key_low = grad_key_proj.astype(jnp.bfloat16)
    grad_value_low = values_summed.astype(jnp.bfloat16)
    grad_w_key = jnp.dot(hidden_in.T, grad_key_low, preferred_element_type=jnp.float32)
    grad_w_value = jnp.dot(hidden_in.T, grad_value_low, preferred_element_type=jnp.float32)
    grad_hidden_in = (
        hidden_summed
        + jnp.dot(grad_key_low, w_key.T, preferred_element_type=jnp.float32)
        + jnp.dot(grad_value_low, w_value.T, preferred_element_type=jnp.float32)
    )
    unused_in, in_back = jax.vjp(rms_scale, inputs_f, gain_in)
    grad_in_part, grad_g_in = in_back(grad_hidden_in)
    grad_inputs = (grad_residual + grad_in_part).astype(jnp.bfloat16)
    count = lax.axis_size("seq")
    gain_columns = jnp.stack(
        [grad_g_in, grad_g_post_attn, grad_g_pre_ffn, grad_g_post_ffn], axis=1
    )
    side = jnp.concatenate(
        [grad_g_query.reshape(count, -1), grad_g_key.reshape(count, -1)], axis=1
    )
    side_rows = jnp.repeat(side, inputs.shape[1] // count, axis=0)
    extra = jnp.concatenate([gain_columns, side_rows], axis=1)
    extra = jnp.pad(extra, ((0, 0), (0, -extra.shape[1] % 128)))
    widths = [g.shape[1] for g in (grad_w_query, grad_w_out, grad_w_key, grad_w_value)]
    attn_sum = scatter_rows(
        jnp.concatenate(
            [
                g.astype(jnp.bfloat16)
                for g in (grad_w_query, grad_w_out, grad_w_key, grad_w_value, extra)
            ],
            axis=1,
        )
    )
    edges = [sum(widths[:i]) for i in range(5)]
    summed_query, summed_out, summed_key, summed_value = (
        attn_sum[:, edges[i] : edges[i + 1]] for i in range(4)
    )
    gain_sum = attn_sum[:, edges[4] :]
    summed_g_in, summed_g_post_attn, summed_g_pre_ffn, summed_g_post_ffn = (
        gain_sum[:, i] for i in range(4)
    )
    own = head_dim // count
    summed_g_query = gain_sum[0, 4 : 4 + own]
    summed_g_key = gain_sum[0, 4 + own : 4 + 2 * own]
    summed_out = summed_out.T
    summed_down = summed_down.T
    return (
        output_f.astype(jnp.bfloat16),
        grad_inputs,
        summed_query,
        summed_key,
        summed_value,
        summed_out,
        summed_gate,
        summed_up,
        summed_down,
        summed_g_in,
        summed_g_query,
        summed_g_key,
        summed_g_post_attn,
        summed_g_pre_ffn,
        summed_g_post_ffn,
    )


def solution(mesh):
    placed = (
        P("seq", None),
        P("seq"),
        P(None, "head"),
        P(),
        P(),
        P("head", None),
        P(None, "head"),
        P(None, "head"),
        P("head", None),
        P(),
        P(),
        P(),
        P(),
        P(),
        P(),
        P("seq", None),
    )
    return jax.shard_map(
        fast_device if mesh.shape["seq"] == 16 else per_device,
        mesh=mesh,
        in_specs=placed,
        out_specs=(
            P("seq", None),
            P("seq", None),
            P("seq", "head"),
            P("seq", None),
            P("seq", None),
            P("head", "seq"),
            P("seq", "head"),
            P("seq", "head"),
            P("head", "seq"),
            P("seq"),
            P("seq"),
            P("seq"),
            P("seq"),
            P("seq"),
            P("seq"),
        ),
        check_vma=False,
    )
```

```python
import functools
import math
import types

import jax
import jax.numpy as jnp
from jax import lax
from jax.experimental import pallas as pl
from jax.experimental.pallas import tpu as pltpu
from jax.sharding import PartitionSpec as P

MESH = pl.DeviceIdType.MESH
WIDE = 384
BLOCK = 72

EPS = 1e-06
QUERY_SCALE = 0.0625


def from_behind(block, axis, distance):
    devices = range(lax.axis_size(axis))
    route = [(i - distance, i) for i in devices if i - distance in devices]
    return lax.ppermute(block, axis, route)


def rms_scale(values, gain):
    return values * lax.rsqrt(jnp.mean(values * values, axis=-1, keepdims=True) + EPS) * gain


def rope_angles(positions, width):
    half_width = width // 2
    frequency = jnp.exp(
        jnp.arange(half_width, dtype=jnp.float32) * (-2.0 * math.log(1000000.0) / width)
    )
    angles = positions.astype(jnp.float32)[:, None] * frequency[None, :]
    return (jnp.cos(angles), jnp.sin(angles))


def rotate(values, cosine, sine):
    half_width = values.shape[-1] // 2
    first_half = values[..., :half_width]
    second_half = values[..., half_width:]
    cos_rows = cosine[:, None, :]
    sin_rows = sine[:, None, :]
    return jnp.concatenate(
        [
            first_half * cos_rows - second_half * sin_rows,
            second_half * cos_rows + first_half * sin_rows,
        ],
        axis=-1,
    )


def prepare(values, gain, cosine, sine, factor):
    return rotate(rms_scale(values, gain), cosine, sine) * factor


def gelu_tanh(values):
    return (
        0.5
        * values
        * (1.0 + jnp.tanh(0.7978845608028654 * (values + 0.044715 * values * values * values)))
    )


def gated(gate_act, up_proj):
    return gelu_tanh(gate_act) * up_proj


def over_head(part):
    low = part.astype(jnp.bfloat16)
    other = lax.ppermute(low, "head", [(0, 1), (1, 0)])
    return low.astype(jnp.float32) + other.astype(jnp.float32)


def place_of():
    seq = lax.axis_index("seq")
    return seq, lax.axis_index("head"), seq % 2, seq // 2 % 2, seq // 4


def dot_nt(left, right):
    return lax.dot_general(left, right, (((1,), (1,)), ((), ())), preferred_element_type=jnp.float32)


def dot_tn(left, right):
    return lax.dot_general(left, right, (((0,), (0,)), ((), ())), preferred_element_type=jnp.float32)


def rotate_back(grad, cosine, sine):
    half = grad.shape[-1] // 2
    first, second = grad[:, :half], grad[:, half:]
    return jnp.concatenate(
        [first * cosine + second * sine, second * cosine - first * sine], axis=-1
    )


def norm_parts(values):
    scale = lax.rsqrt(jnp.mean(values * values, axis=-1, keepdims=True) + EPS)
    return scale, values * scale


def norm_back(grad, gain, scale, normed):
    inner = grad * gain
    back = scale * (inner - normed * jnp.mean(inner * normed, axis=-1, keepdims=True))
    return back, jnp.sum(grad * normed, axis=0, keepdims=True)


CHUNKS = 4
FEEDS = 4
OUT_PARTS = 8


def turn(values, cosine, sine):
    half = values.shape[-1] // 2
    first, second = values[:, :half], values[:, half:]
    return jnp.concatenate(
        [first * cosine - second * sine, second * cosine + first * sine], axis=-1
    )


def to_blocks(target, values, columns):
    turned = values.astype(jnp.float32).T.astype(jnp.bfloat16)
    for half in range(2):
        for x in range(2):
            for f in range(2):
                source = 144 * ((2 * half + f) * 2 + x)
                to = 144 * (half * 4 + x * 2 + f)
                target[to : to + 144, columns] = turned[source : source + 144]


def forward_kernel(names, *refs):
    r = types.SimpleNamespace(**dict(zip(names, refs)))
    seq, head, core, side, level = place_of()
    last_seq = lax.axis_size("seq") - 1
    f32, low = jnp.float32, jnp.bfloat16
    rows, width = r.inputs.shape
    heads = r.w_query.shape[1] // 256
    hidden = r.w_gate.shape[1]
    size = rows // CHUNKS
    feed_size = rows // FEEDS
    even = core == 0

    barrier = pltpu.get_barrier_semaphore()

    def greet(to_seq, to_head):
        pl.semaphore_signal(barrier, inc=1, device_id=(to_seq, to_head), device_id_type=MESH)

    def load(n, src, dst):
        copy = pltpu.make_async_copy(src, dst, r.load_sem.at[n])
        copy.start()
        return copy

    in_copy = load(0, r.inputs, r.x)
    kv_copies = (load(2, r.w_key, r.wk), load(3, r.w_value, r.wv))
    query_copy = load(7, r.w_query, r.wq)
    out_copy = load(8, r.w_out, r.wo.at[head])
    steps = hidden // WIDE

    def tile_loads(j):
        at = pl.ds(pl.multiple_of(j * WIDE, WIDE), WIDE)
        gate_at = pl.ds(pl.multiple_of(2 * j * WIDE, WIDE), WIDE)
        up_at = pl.ds(pl.multiple_of((2 * j + 1) * WIDE, WIDE), WIDE)
        return (
            pltpu.make_async_copy(r.w_gate.at[:, at], r.wgu.at[:, gate_at], r.weight_sem.at[0, j]),
            pltpu.make_async_copy(r.w_up.at[:, at], r.wgu.at[:, up_at], r.weight_sem.at[1, j]),
        )

    for j in range(steps):
        for copy in tile_loads(j):
            copy.start()
    down_copy = load(11, r.w_down, r.wd)
    cot_copy = load(12, r.cotangent, r.cot)

    greet(seq ^ 1, head)
    greet(seq, 1 - head)
    expected = jnp.int32(2)
    for distance in (1, 2):
        @pl.when(seq >= distance)
        def _():
            greet(seq - distance, head)

        @pl.when(seq + distance <= last_seq)
        def _():
            greet(seq + distance, head)

        expected = (
            expected
            + (seq >= distance).astype(jnp.int32)
            + (seq + distance <= last_seq).astype(jnp.int32)
        )
    pl.semaphore_wait(barrier, expected)

    def remote(src, dst, send, recv, to_seq, to_head):
        return pltpu.make_async_remote_copy(
            src_ref=src,
            dst_ref=dst,
            send_sem=send,
            recv_sem=recv,
            device_id=(to_seq, to_head),
            device_id_type=MESH,
        )

    share = r.w_out.shape[0] // 2

    def out_share(which):
        return pl.ds(pl.multiple_of(which * share, share), share)

    def w_out_y(part):
        size = share // OUT_PARTS
        mine = pl.ds(pl.multiple_of(core * share + part * size, size), size)
        return remote(
            r.w_out.at[mine, :], r.wo.at[head, mine, :], r.out_send.at[part], r.out_recv.at[part],
            seq, 1 - head,
        )

    def w_out_start(first):
        for part in (first, first + 1):
            w_out_y(part).start()

    def w_out_core():
        mine = out_share(core)
        part = r.wo.at[1 - head, mine, :]
        return remote(part, part, r.wo_send, r.wo_recv, seq ^ 1, head)

    def ids_send(distance):
        return remote(
            r.ids.at[2], r.ids.at[2 - distance], r.ids_send.at[distance - 1],
            r.ids_recv.at[distance - 1], seq + distance, head,
        )

    def halo(n, distance, hand_on=False):
        kind = r.window.at[n]
        source = kind.at[pl.ds((1 if hand_on else 2) * rows, rows), :]
        target = kind.at[pl.ds((2 - distance) * rows, rows), :]
        place = 2 if hand_on else distance - 1
        return remote(
            source, target, r.halo_send.at[n, place], r.halo_recv.at[n, distance - 1],
            seq + (1 if hand_on else distance), head,
        )

    ids = r.segment_ids[...].astype(f32).reshape(1, rows)
    r.ids[2] = jnp.broadcast_to(ids, (8, rows))
    for distance in (1, 2):
        @pl.when(seq + distance <= last_seq)
        def _():
            ids_send(distance).start()

    w_out_start(0)

    r.gains[...] = jnp.zeros_like(r.gains)
    r.head_gain[...] = jnp.zeros_like(r.head_gain)
    for n, gain in enumerate((r.gain_in, r.gain_post_attn, r.gain_pre_ffn, r.gain_post_ffn)):
        r.gains[n : n + 1, :] = gain[...].reshape(1, width)
    for n, gain in enumerate((r.gain_query, r.gain_key)):
        r.head_gain[n : n + 1, :] = gain[...].reshape(1, 256)
    in_copy.wait()

    def norm_in(c, carry):
        at = pl.ds(pl.multiple_of(c * 128, 128), 128)
        _, normed = norm_parts(r.x[at, :].astype(f32))
        r.normed_in[at, :] = (normed * r.gains[0:1, :]).astype(low)
        return carry

    lax.fori_loop(0, rows // 128, norm_in, 0)
    w_out_start(2)
    for copy in kv_copies:
        copy.wait()
    r.key_raw[...] = jnp.dot(r.normed_in[...], r.wk[...], preferred_element_type=f32)
    r.window[1, 2 * rows :, :] = jnp.dot(
        r.normed_in[...], r.wv[...], preferred_element_type=f32
    ).astype(low)

    def value_halo(distance):
        return halo(1, distance)

    @pl.when(even & (seq + 2 <= last_seq))
    def _():
        value_halo(2).start()

    @pl.when(seq + 1 <= last_seq)
    def _():
        value_halo(1).start()

    w_out_start(4)

    for distance in (1, 2):
        @pl.when(seq >= distance)
        def _():
            remote(
                r.ids.at[2], r.ids.at[2 - distance], r.ids_send.at[distance - 1],
                r.ids_recv.at[distance - 1], seq ^ 1, head,
            ).wait_recv()

        @pl.when(seq < distance)
        def _():
            r.ids[2 - distance] = jnp.full((8, rows), -1.0, f32)

    ids_row = jnp.concatenate([r.ids[b][:1] for b in range(3)], axis=1)
    r.ids_flat[...] = jnp.broadcast_to(ids_row, (8, 3 * rows))
    ids_column = jnp.broadcast_to(r.ids[2][:1], (128, rows)).T
    r.ids_turned[...] = ids_column
    column = lax.broadcasted_iota(jnp.int32, (8, 128), 1).astype(f32)
    frequency = jnp.exp(column * (-2.0 * math.log(1000000.0) / 256))[:1]

    def angles(c, carry):
        at = pl.ds(pl.multiple_of(c * 128, 128), 128)
        here = lax.broadcasted_iota(jnp.int32, (128, 3 * rows), 0) + (2 * rows + c * 128)
        there = lax.broadcasted_iota(jnp.int32, (128, 3 * rows), 1)
        same = (r.ids_turned[at, :1] == r.ids_flat[:1, :]) & (there < here)
        position = jnp.sum(same.astype(f32), axis=1, keepdims=True)
        angle = position * frequency
        r.cosine[at, :] = jnp.cos(angle)
        r.sine[at, :] = jnp.sin(angle)
        return carry

    lax.fori_loop(0, rows // 128, angles, 0)
    _, normed = norm_parts(r.key_raw[...])
    r.window[0, 2 * rows :, :] = turn(
        normed * r.head_gain[1:2, :], r.cosine[...], r.sine[...]
    ).astype(low)

    @pl.when(even & (seq + 2 <= last_seq))
    def _():
        halo(0, 2).start()

    @pl.when(seq + 1 <= last_seq)
    def _():
        halo(0, 1).start()

    w_out_start(6)

    query_copy.wait()
    r.query_raw[...] = jnp.dot(r.normed_in[...], r.wq[...], preferred_element_type=f32)
    for h in range(heads):
        at = slice(256 * h, 256 * h + 256)
        _, normed = norm_parts(r.query_raw[:, at])
        r.q[:, at] = (
            turn(normed * r.head_gain[0:1, :], r.cosine[...], r.sine[...]) * QUERY_SCALE
        ).astype(low)

    def store(n, src, dst):
        copy = pltpu.make_async_copy(src, dst, r.store_sem.at[n])
        copy.start()
        return copy

    to_blocks(r.turned, r.normed_in[...], slice(0, rows))
    stores = [
        store(1, r.key_raw, r.key_proj),
        store(2, r.query_raw, r.query_proj),
        store(3, r.q, r.queries),
        store(4, r.cosine, r.cosine_out),
        store(5, r.sine, r.sine_out),
        store(6, r.ids_flat, r.ids_out),
        store(16, r.gains, r.gain_rows),
        store(17, r.head_gain, r.head_gains),
    ]
    turned_store = store(0, r.turned, r.left_in)

    out_copy.wait()
    for part in range(OUT_PARTS):
        w_out_y(part).wait()
    w_out_core().start()

    def arrival(n, distance):
        return halo(n, distance)

    for n in (1, 0):
        @pl.when(seq >= 1)
        def _():
            arrival(n, 1).wait_recv()

        @pl.when(even & (seq >= 2))
        def _():
            halo(n, 2, True).start()

    for n in (1, 0):
        @pl.when(seq >= 2)
        def _():
            arrival(n, 2).wait_recv()

    for distance in (1, 2):
        @pl.when(seq < distance)
        def _():
            for n in range(2):
                r.window[n, (2 - distance) * rows : (3 - distance) * rows, :] = jnp.zeros(
                    (rows, 256), low
                )

    def head_exchange(c):
        part = r.heads_all.at[head, pl.ds(pl.multiple_of(c * size, size), size), :]
        return remote(part, part, r.y_send.at[c], r.y_recv.at[c], seq, 1 - head)

    def branch_exchange(c):
        at = pl.ds(pl.multiple_of(c * feed_size, feed_size), feed_size)
        return remote(
            r.y_out.at[at, :], r.y_in.at[at, :], r.y_send.at[CHUNKS + c], r.y_recv.at[CHUNKS + c],
            seq, 1 - head,
        )

    def attend(c):
        first = c * size
        span = 2 * rows + size
        at = slice(first, first + size)
        key_at = slice(first, first + span)
        here = lax.broadcasted_iota(jnp.int32, (size, span), 0) + 2 * rows
        there = lax.broadcasted_iota(jnp.int32, (size, span), 1)
        seen = (r.ids_turned[at, :1] == r.ids_flat[:1, key_at]) & (there <= here)
        for h in range(heads):
            head_at = slice(256 * h, 256 * h + 256)
            scores = jnp.where(seen, dot_nt(r.q[at, head_at], r.window[0, key_at, :]), -1e30)
            top = jnp.max(scores, axis=1, keepdims=True)
            expo = jnp.exp(scores - top)
            total = jnp.sum(expo, axis=1, keepdims=True)
            probs = (expo / total).astype(low)
            out = jnp.dot(probs, r.window[1, key_at, :], preferred_element_type=f32)
            r.heads_f[at, head_at] = out
            r.heads_all[head, at, head_at] = out.astype(low)
            r.lse_rows[h : h + 1, at] = jnp.broadcast_to(top + jnp.log(total), (size, 128)).T[:1]
        head_exchange(c).start()

    for c in range(CHUNKS):
        attend(c)
    stores += [
        store(7, r.heads_f, r.attended),
        store(8, r.lse_rows, r.lse),
        store(9, r.window.at[0], r.keys),
        store(10, r.window.at[1], r.values),
    ]
    w_out_core().wait()
    turned_store.wait()

    def feed_rows(c):
        return pl.ds(pl.multiple_of(c * feed_size, feed_size), feed_size)

    def part_stores(c):
        slot = lax.rem(c, 2)
        return (
            pltpu.make_async_copy(
                r.gate_up_part.at[slot], r.gate_up.at[feed_rows(c), :], r.part_sem.at[0, slot]
            ),
            pltpu.make_async_copy(
                r.mixed_part.at[slot], r.mixed.at[feed_rows(c), :], r.part_sem.at[1, slot]
            ),
        )

    def feed(c, carry):
        at = feed_rows(c)
        slot = lax.rem(c, 2)
        head_exchange(c).wait_recv()
        branch = jnp.dot(r.heads_all[0, at, :], r.wo[0], preferred_element_type=f32) + jnp.dot(
            r.heads_all[1, at, :], r.wo[1], preferred_element_type=f32
        )
        r.branch[at, :] = branch
        _, normed = norm_parts(branch)
        middle = r.x[at, :].astype(f32) + normed * r.gains[1:2, :]
        r.middle[at, :] = middle
        _, normed = norm_parts(middle)
        left = (normed * r.gains[2:3, :]).astype(low)
        r.normed_mid[at, :] = left

        @pl.when(c >= 2)
        def _():
            for copy in part_stores(c - 2):
                copy.wait()

        def finish(j, both):
            double = slice(2 * j * WIDE, 2 * (j + 1) * WIDE)
            r.gate_up_part[slot, :, double] = both.astype(low)
            gate, up = both[:, :WIDE], both[:, WIDE:]
            curve = jnp.tanh(0.7978845608028654 * gate * (1.0 + 0.044715 * gate * gate))
            r.mixed_part[slot, :, j * WIDE : (j + 1) * WIDE] = (
                0.5 * gate * (1.0 + curve) * up
            ).astype(low)

        waiting = None
        for j in range(steps):
            double = slice(2 * j * WIDE, 2 * (j + 1) * WIDE)
            both = jnp.dot(left, r.wgu[:, double], preferred_element_type=f32)
            if waiting is not None:
                finish(j - 1, waiting)
            waiting = both
        finish(steps - 1, waiting)
        for copy in part_stores(c):
            copy.start()
        r.y_out[at, :] = jnp.dot(
            r.mixed_part[slot], r.wd[...], preferred_element_type=f32
        ).astype(low)
        branch_exchange(c).start()
        return carry

    for j in range(steps):
        for copy in tile_loads(j):
            copy.wait()
    down_copy.wait()
    lax.fori_loop(0, FEEDS, feed, 0)
    stores += [store(11, r.branch, r.attn_branch), store(12, r.middle, r.residual_mid)]
    to_blocks(r.turned, r.normed_mid[...], slice(0, rows))
    mid_store = store(0, r.turned, r.left_mid)
    cot_copy.wait()
    gain_sum = jnp.zeros((1, width), f32)
    for c in range(FEEDS):
        branch_exchange(c).wait_recv()

        def end(n, total):
            at = pl.ds(pl.multiple_of(c * feed_size + n * 128, 128), 128)
            branch = r.y_out[at, :].astype(f32) + r.y_in[at, :].astype(f32)
            scale, normed = norm_parts(branch)
            r.result[at, :] = (r.middle[at, :] + normed * r.gains[3:4, :]).astype(low)
            back, gain = norm_back(r.cot[at, :].astype(f32), r.gains[3:4, :], scale, normed)
            r.cot[at, :] = back.astype(low)
            return total + gain

        gain_sum = lax.fori_loop(0, feed_size // 128, end, gain_sum)
        if c == 0:
            mid_store.wait()
        at = slice(c * feed_size, (c + 1) * feed_size)
        to_blocks(r.turned, r.cot[at, :], at)
    stores += [
        store(0, r.turned, r.left_ffn),
        store(13, r.cot, r.grad_ffn),
        store(14, r.result, r.output),
    ]
    r.gain_tile[...] = jnp.zeros_like(r.gain_tile)
    r.gain_tile[3:4, :] = gain_sum
    stores.append(store(15, r.gain_tile, r.gain_start))
    for copy in stores:
        copy.wait()
    for distance in (1, 2):
        @pl.when(seq + distance <= last_seq)
        def _():
            ids_send(distance).wait_send()

    for n in range(2):
        @pl.when(seq + 1 <= last_seq)
        def _():
            halo(n, 1).wait_send()

        @pl.when(even & (seq + 2 <= last_seq))
        def _():
            halo(n, 2).wait_send()

        @pl.when(even & (seq >= 2))
        def _():
            halo(n, 2, True).wait_send()

    for c in (FEEDS - 2, FEEDS - 1):
        for copy in part_stores(jnp.int32(c)):
            copy.wait()
    for c in range(CHUNKS):
        head_exchange(c).wait_send()
    for c in range(FEEDS):
        branch_exchange(c).wait_send()


def forward(operands):
    low, f32 = jnp.bfloat16, jnp.float32
    dma = pltpu.SemaphoreType.DMA
    rows, width = operands["inputs"].shape
    hidden = operands["w_gate"].shape[1]
    wide = operands["w_query"].shape[1]
    shape = jax.ShapeDtypeStruct
    anywhere = pl.BlockSpec(memory_space=pl.ANY)
    outs = dict(
        left_in=shape((width, rows), low),
        left_mid=shape((width, rows), low),
        left_ffn=shape((width, rows), low),
        key_proj=shape((rows, 256), f32),
        query_proj=shape((rows, wide), f32),
        queries=shape((rows, wide), low),
        cosine_out=shape((rows, 128), f32),
        sine_out=shape((rows, 128), f32),
        ids_out=shape((8, 3 * rows), f32),
        attended=shape((rows, wide), f32),
        lse=shape((8, rows), f32),
        keys=shape((3 * rows, 256), low),
        values=shape((3 * rows, 256), low),
        attn_branch=shape((rows, width), f32),
        residual_mid=shape((rows, width), f32),
        gate_up=shape((rows, 2 * hidden), low),
        mixed=shape((rows, hidden), low),
        grad_ffn=shape((rows, width), low),
        output=shape((rows, width), low),
        gain_start=shape((8, width), f32),
        gain_rows=shape((8, width), f32),
        head_gains=shape((8, 256), f32),
    )
    feed_size = rows // FEEDS
    vmem = pltpu.VMEM
    scratch = dict(
        x=vmem((rows, width), low),
        gains=vmem((8, width), f32),
        wk=vmem((width, 256), low),
        wv=vmem((width, 256), low),
        head_gain=vmem((8, 256), f32),
        ids=vmem((3, 8, rows), f32),
        ids_flat=vmem((8, 3 * rows), f32),
        ids_turned=vmem((rows, 128), f32),
        wq=vmem((width, wide), low),
        wo=vmem((2, wide, width), low),
        wgu=vmem((width, 2 * hidden), low),
        wd=vmem((hidden, width), low),
        cot=vmem((rows, width), low),
        normed_in=vmem((rows, width), low),
        normed_mid=vmem((rows, width), low),
        key_raw=vmem((rows, 256), f32),
        query_raw=vmem((rows, wide), f32),
        q=vmem((rows, wide), low),
        window=vmem((2, 3 * rows, 256), low),
        cosine=vmem((rows, 128), f32),
        sine=vmem((rows, 128), f32),
        turned=vmem((width, rows), low),
        heads_f=vmem((rows, wide), f32),
        heads_all=vmem((2, rows, wide), low),
        lse_rows=vmem((8, rows), f32),
        branch=vmem((rows, width), f32),
        middle=vmem((rows, width), f32),
        gate_up_part=vmem((2, feed_size, 2 * hidden), low),
        mixed_part=vmem((2, feed_size, hidden), low),
        y_out=vmem((rows, width), low),
        y_in=vmem((rows, width), low),
        result=vmem((rows, width), low),
        gain_tile=vmem((8, width), f32),
        load_sem=dma((13,)),
        store_sem=dma((18,)),
        part_sem=dma((2, 2)),
        weight_sem=dma((2, hidden // WIDE)),
        wo_send=dma(()),
        wo_recv=dma(()),
        out_send=dma((OUT_PARTS,)),
        out_recv=dma((OUT_PARTS,)),
        ids_send=dma((2,)),
        ids_recv=dma((2,)),
        halo_send=dma((2, 3)),
        halo_recv=dma((2, 2)),
        y_send=dma((CHUNKS + FEEDS,)),
        y_recv=dma((CHUNKS + FEEDS,)),
    )
    names = (*operands, *outs, *scratch)
    results = pl.pallas_call(
        functools.partial(forward_kernel, names),
        out_shape=list(outs.values()),
        in_specs=[
            pl.BlockSpec(memory_space=pltpu.VMEM) if len(a.shape) == 1 else anywhere
            for a in operands.values()
        ],
        out_specs=[anywhere] * len(outs),
        scratch_shapes=list(scratch.values()),
        compiler_params=pltpu.CompilerParams(
            collective_id=2, has_side_effects=True, vmem_limit_bytes=62 << 20
        ),
        name="forward",
    )(*operands.values())
    return dict(zip(outs, results))


DOWN, GATE, UP, QUERY, QUERY_END, OUT, OUT_END = range(7)
RING = 7
Y_PARTS = 8
STEPS = 31
FIRST_SIDE = 27
LAG_X = 4
LAG_M = 6
LAG_Z = 8
LAG_END = 10
AHEAD = 2
TURNED = 2
LAST_TURNED = 23


def backward_kernel(names, *refs):
    r = types.SimpleNamespace(**dict(zip(names, refs)))
    seq, head, core, side, level = place_of()
    last_seq = lax.axis_size("seq") - 1
    f32, low = jnp.float32, jnp.bfloat16
    rows = r.grad_ffn.shape[0]
    width = r.grad_ffn.shape[1]

    barrier = pltpu.get_barrier_semaphore()

    def greet(to_seq, to_head):
        pl.semaphore_signal(barrier, inc=1, device_id=(to_seq, to_head), device_id_type=MESH)

    greet(seq ^ 1, head)
    greet(seq ^ 2, head)
    greet(seq, 1 - head)
    for z in range(4):
        for c in range(2):
            other = z * 4 + side * 2 + c

            @pl.when(other != seq)
            def _():
                greet(other, head)

    expected = jnp.int32(10)
    for distance in (1, 2):
        @pl.when(seq >= distance)
        def _():
            greet(seq - distance, head)

        @pl.when(seq + distance <= last_seq)
        def _():
            greet(seq + distance, head)

        expected = (
            expected
            + (seq >= distance).astype(jnp.int32)
            + (seq + distance <= last_seq).astype(jnp.int32)
        )
    pl.semaphore_wait(barrier, expected)

    def remote(src, dst, send, recv, to_seq, to_head):
        return pltpu.make_async_remote_copy(
            src_ref=src,
            dst_ref=dst,
            send_sem=send,
            recv_sem=recv,
            device_id=(to_seq, to_head),
            device_id_type=MESH,
        )

    targets = [((2 * core + k // 2) * 4 + side * 2 + k % 2) for k in range(4)]
    sources = [z * 4 + side * 2 + level // 2 for z in range(4)]
    starts_far = (level == 3 * (1 - core))
    hands_on = (level == 2 - core)
    near = (2 - core) * 4 + side * 2 + core
    far = (3 - 3 * core) * 4 + side * 2 + core
    far_level = 3 * core

    def is_far(k):
        return core == k // 2

    def unheard(z):
        return (level == 3 - z) if z in (0, 3) else False

    def core_copy(t):
        slot = lax.rem(t, RING)
        return remote(
            r.sent.at[lax.rem(t, 2)], r.core_in.at[slot], r.core_send.at[t], r.core_recv.at[t],
            seq ^ 1, head,
        )

    def x_copy(t):
        slot = lax.rem(t, RING)
        return remote(
            r.held.at[slot, 1 - side], r.x_in.at[slot], r.x_send.at[t], r.x_recv.at[t],
            seq ^ 2, head,
        )

    def z_copy(t, k):
        return remote(
            r.z_out.at[lax.rem(t, RING), k], r.z_in.at[t, level],
            r.z_send.at[t, k], r.z_recv.at[t, level], targets[k], head,
        )

    def near_copy(t, k):
        return remote(
            r.z_out.at[lax.rem(t, RING), k], r.m_in.at[lax.rem(t, RING), k % 2],
            r.z_send.at[t, k], r.m_recv.at[t, k % 2], near, head,
        )

    def far_copy(t, g):
        return remote(
            r.z_out.at[lax.rem(t, RING), 2 * core + g], r.z_in.at[t, level],
            r.z_send.at[t, 2 * core + g], r.z_recv.at[t, level],
            far_level * 4 + side * 2 + g, head,
        )

    def z_first(t):
        return (lax.rem(t, RING) == TURNED) & (t < LAST_TURNED + 1)

    def zz_copy(t, x, k):
        n = t // RING
        return remote(
            r.held.at[TURNED, x, k], r.zz_in.at[n, level, x],
            r.zz_send.at[n, x, k], r.zz_recv.at[n, level, x], targets[k], head,
        )

    def zz_near(t, x, k):
        n = t // RING
        return remote(
            r.held.at[TURNED, x, k], r.mm_in.at[n, k % 2, x],
            r.zz_send.at[n, x, k], r.mm_recv.at[n, k % 2, x], near, head,
        )

    def zz_far(t, x, g):
        n = t // RING
        return remote(
            r.mm_in.at[n, g, x], r.zz_in.at[n, level, x],
            r.zz_send.at[n, x, 2 * core + g], r.zz_recv.at[n, level, x],
            far_level * 4 + side * 2 + g, head,
        )

    def xx_copy(t):
        n = t // RING
        return remote(
            r.xx_out.at[n], r.xx_in.at[n], r.xx_send.at[n], r.xx_recv.at[n], seq ^ 2, head
        )

    def zz_sent(t):
        for x in range(2):
            for k in range(4):
                @pl.when(targets[k] != seq)
                def _():
                    zz_copy(t, x, k).wait_send()

    def zz_start(t):
        n = t // RING
        for x in range(2):
            for k in range(4):
                @pl.when(targets[k] == seq)
                def _():
                    r.zz_in[n, level, x] = r.held[TURNED, x, k]

                @pl.when(starts_far & is_far(k))
                def _():
                    zz_near(t, x, k).start()

                @pl.when(
                    (targets[k] != seq) & jnp.logical_not((starts_far | hands_on) & is_far(k))
                )
                def _():
                    zz_copy(t, x, k).start()

    def zz_merge(t):
        n = t // RING

        @pl.when(hands_on)
        def _():
            for x in range(2):
                for g in range(2):
                    remote(
                        r.held.at[TURNED, x, g], r.mm_in.at[n, g, x], r.zz_send.at[n, x, g],
                        r.mm_recv.at[n, g, x], far, head,
                    ).wait_recv()
                    r.mm_in[n, g, x] = (
                        r.mm_in[n, g, x].astype(f32)
                        + r.held[TURNED, x, 2 * core + g].astype(f32)
                    ).astype(low)
                    zz_far(t, x, g).start()

    def zz_sum(t):
        n = t // RING
        for z in range(4):
            @pl.when((sources[z] != seq) & jnp.logical_not(unheard(z)))
            def _():
                for x in range(2):
                    remote(
                        r.held.at[TURNED, x, 0], r.zz_in.at[n, z, x], r.zz_send.at[n, x, 0],
                        r.zz_recv.at[n, z, x], sources[z], head,
                    ).wait_recv()

        def total(x):
            value = r.zz_in[n, 1, x].astype(f32) + r.zz_in[n, 2, x].astype(f32)
            for z in (0, 3):
                value = value + jnp.where(unheard(z), 0.0, r.zz_in[n, z, x].astype(f32))
            return value

        @pl.when(n >= 1)
        def _():
            out_wait(t - RING)

        r.xx_out[n] = total(1 - side).astype(low)
        xx_copy(t).start()
        r.kept[...] = total(side)

    def zz_end(t):
        xx_copy(t).wait()
        r.kept[...] += r.xx_in[t // RING].astype(f32)
        out_start(t)

    def z_arrival(t, z):
        return remote(
            r.z_out.at[0, 0], r.z_in.at[t, z], r.z_send.at[t, 0], r.z_recv.at[t, z],
            sources[z], head,
        )

    def produce(t):
        @pl.when(t >= 2)
        def _():
            core_copy(t - 2).wait_send()

        @pl.when((t >= RING) & jnp.logical_not(z_first(t - RING)))
        def _():
            x_copy(t - RING).wait_send()

        @pl.when((t >= RING) & z_first(t - RING))
        def _():
            zz_sent(t - RING)

        which = jnp.where(t < 9, 0, jnp.where(t < FIRST_SIDE, 1, jnp.where(t < 30, 2, 0)))
        place = jnp.where(
            t < 9, lax.rem(t, 2), jnp.where(t < FIRST_SIDE, t - 7, t - (FIRST_SIDE - 2))
        )
        tile = r.tiles[place]

        def half(start):
            left = r.lefts[which, pl.ds(pl.multiple_of(start, 576), 576), :]
            return jnp.dot(left, tile, preferred_element_type=f32)

        away = half((1 - core) * 576)
        for k in range(8):
            r.sent[lax.rem(t, 2), k // 4, k % 4] = away[k * BLOCK : (k + 1) * BLOCK].astype(low)

        @pl.when(t >= RING)
        def _():
            pl.semaphore_wait(r.core_free, 1)

        def second(start):
            left = r.lefts[0, pl.ds(pl.multiple_of(start, 576), 576), :]
            return jnp.dot(left, tile[:, 256:], preferred_element_type=f32)

        @pl.when(t == FIRST_SIDE + 2)
        def _():
            more = second((1 - core) * 576)
            for k in range(8):
                r.sent[lax.rem(t, 2), k // 4, k % 4, :, 256:] = more[
                    k * BLOCK : (k + 1) * BLOCK
                ].astype(low)

        core_copy(t).start()
        home = half(core * 576)
        for k in range(8):
            r.held[lax.rem(t, RING), k // 4, k % 4] = home[k * BLOCK : (k + 1) * BLOCK].astype(low)

        @pl.when(t == FIRST_SIDE + 2)
        def _():
            more = second(core * 576)
            for k in range(8):
                r.held[lax.rem(t, RING), k // 4, k % 4, :, 256:] = more[
                    k * BLOCK : (k + 1) * BLOCK
                ].astype(low)

    def core_stage(t):
        core_copy(t).wait_recv()
        slot = lax.rem(t, RING)

        def add(part):
            for k in range(4):
                r.held[slot, part, k] = (
                    r.held[slot, part, k].astype(f32) + r.core_in[slot, part, k].astype(f32)
                ).astype(low)

        add(1 - side)

        @pl.when(t >= RING)
        def _():
            pl.semaphore_wait(r.x_free, 1)

        @pl.when(jnp.logical_not(z_first(t)))
        def _():
            x_copy(t).start()

        add(side)

        @pl.when(z_first(t))
        def _():
            zz_start(t)

        @pl.when(t + RING < STEPS)
        def _():
            pl.semaphore_signal(r.core_free, inc=1, device_id=(seq ^ 1, head), device_id_type=MESH)

    def x_stage(t):
        @pl.when(z_first(t))
        def _():
            zz_merge(t)

        @pl.when(starts_far & (t >= RING))
        def _():
            pl.semaphore_wait(r.m_free, 1)

        @pl.when(jnp.logical_not(z_first(t)))
        def _():
            x_add(t)

        @pl.when(t + RING < STEPS)
        def _():
            pl.semaphore_signal(r.x_free, inc=1, device_id=(seq ^ 2, head), device_id_type=MESH)

    def x_add(t):
        x_copy(t).wait_recv()
        slot = lax.rem(t, RING)

        @pl.when((t >= RING) & jnp.logical_not(z_first(t - RING)))
        def _():
            for k in range(4):
                @pl.when(targets[k] != seq)
                def _():
                    z_copy(t - RING, k).wait_send()

        for k in range(4):
            total = (r.held[slot, side, k].astype(f32) + r.x_in[slot, k].astype(f32)).astype(low)

            @pl.when(targets[k] == seq)
            def _():
                r.z_in[t, level] = total

            @pl.when(targets[k] != seq)
            def _():
                r.z_out[slot, k] = total

                @pl.when(starts_far & is_far(k))
                def _():
                    near_copy(t, k).start()

                @pl.when(jnp.logical_not((starts_far | hands_on) & is_far(k)))
                def _():
                    z_copy(t, k).start()

    def m_stage(t):
        slot = lax.rem(t, RING)

        @pl.when(hands_on & jnp.logical_not(z_first(t)))
        def _():
            for g in range(2):
                remote(
                    r.z_out.at[0, 0], r.m_in.at[slot, g], r.z_send.at[t, 0], r.m_recv.at[t, g],
                    far, head,
                ).wait_recv()
                k = 2 * core + g
                r.z_out[slot, k] = (
                    r.z_out[slot, k].astype(f32) + r.m_in[slot, g].astype(f32)
                ).astype(low)
                far_copy(t, g).start()

        @pl.when(hands_on)
        def _():
            @pl.when(t + RING < STEPS)
            def _():
                pl.semaphore_signal(r.m_free, inc=1, device_id=(far, head), device_id_type=MESH)

    def out_copy(t, kind, source):
        at = pl.multiple_of(lax.rem(t, 9) * WIDE, WIDE)
        if kind == DOWN:
            return pltpu.make_async_copy(
                source, r.down_out.at[:, pl.ds(at, WIDE)], r.out_sem.at[t]
            )
        if kind == QUERY:
            return pltpu.make_async_copy(
                source, r.query_out.at[:, pl.ds(0, WIDE)], r.out_sem.at[t]
            )
        if kind == QUERY_END:
            return pltpu.make_async_copy(
                source.at[:, pl.ds(0, 128)], r.query_out.at[:, pl.ds(WIDE, 128)],
                r.out_sem.at[t],
            )
        if kind == OUT:
            return pltpu.make_async_copy(
                source.at[:, pl.ds(256, 128)], r.out_out.at[:, pl.ds(0, 128)],
                r.out_sem.at[t],
            )
        if kind == OUT_END:
            return pltpu.make_async_copy(
                source, r.out_out.at[:, pl.ds(128, WIDE)], r.out_sem.at[t]
            )
        target = r.gate_out if kind == GATE else r.up_out
        return pltpu.make_async_copy(
            source, target.at[:, pl.ds(at, WIDE)], r.out_sem.at[t]
        )

    KINDS = (
        (DOWN, 0, 9), (GATE, 9, 18), (UP, 18, 27), (QUERY, 27, 28), (QUERY_END, 28, 29),
        (OUT, 29, 30), (OUT_END, 30, 31),
    )

    def out_each(t, act):
        for kind, first, end in KINDS:
            @pl.when((t >= first) & (t < end) & jnp.logical_not(z_first(t)))
            def _():
                act(out_copy(t, kind, r.flat.at[lax.rem(t, 2)]))

            if kind in (DOWN, GATE, UP):
                @pl.when((t >= first) & (t < end) & z_first(t))
                def _():
                    act(out_copy(t, kind, r.kept))

    def out_wait(t):
        out_each(t, lambda copy: copy.wait())

    def out_start(t):
        out_each(t, lambda copy: copy.start())

    def z_stage(t):
        for z in range(4):
            @pl.when((sources[z] != seq) & jnp.logical_not(unheard(z)))
            def _():
                z_arrival(t, z).wait_recv()

        total = r.z_in[t, 1].astype(f32) + r.z_in[t, 2].astype(f32)
        for z in (0, 3):
            total = total + jnp.where(unheard(z), 0.0, r.z_in[t, z].astype(f32))

        before = jnp.where(z_first(t - 2), t - 4, t - 2)

        @pl.when(before >= 0)
        def _():
            out_wait(before)

        r.flat[lax.rem(t, 2)] = total
        out_start(t)

        @pl.when(t == FIRST_SIDE + 1)
        def _():
            r.kv_own[:, :256] = total[:, 128:]

        @pl.when(t == FIRST_SIDE + 2)
        def _():
            r.kv_own[:, 256:] = total[:, :256]

    def pump(i):
        @pl.when(i < STEPS)
        def _():
            produce(i)

        @pl.when((i >= 1) & (i - 1 < STEPS))
        def _():
            core_stage(i - 1)

        @pl.when((i >= LAG_X) & (i - LAG_X < STEPS))
        def _():
            x_stage(i - LAG_X)

        @pl.when((i >= LAG_M) & (i - LAG_M < STEPS))
        def _():
            m_stage(i - LAG_M)

        @pl.when((i >= LAG_Z) & (i - LAG_Z < STEPS))
        def _():
            t = i - LAG_Z

            @pl.when(z_first(t))
            def _():
                zz_sum(t)

            @pl.when(jnp.logical_not(z_first(t)))
            def _():
                z_stage(t)

        @pl.when((i >= LAG_END) & (i - LAG_END < STEPS) & z_first(i - LAG_END))
        def _():
            zz_end(i - LAG_END)

    def y_part(n, part):
        size = rows // Y_PARTS
        at = pl.ds(part * size, size)
        return remote(
            r.y_out.at[at, :], r.y_in.at[n, at, :], r.y_send.at[n, part], r.y_recv.at[n, part],
            seq, 1 - head,
        )

    def y_start(n, first):
        for part in (first, first + 1):
            y_part(n, part).start()

    def y_sent(n):
        for part in range(Y_PARTS):
            y_part(n, part).wait_send()

    def y_arrived(n):
        for part in range(Y_PARTS):
            y_part(n, part).wait_recv()

    def feed_forward(grad, wd, wgu, gate_up, acc):
        sems, grad_sem, left_sem = r.tile_sems, r.grad_sem, r.left_sem

        def copies(j):
            slot = lax.rem(j, 2)
            at = pl.ds(pl.multiple_of(j * WIDE, WIDE), WIDE)
            double = pl.ds(pl.multiple_of(j * 2 * WIDE, 2 * WIDE), 2 * WIDE)
            pairs = (
                (r.w_down.at[at, :], wd),
                (r.gate_up.at[:, double], gate_up),
            )
            halves = (
                (r.w_gate.at[:, at], wgu.at[slot, :, pl.ds(0, WIDE)]),
                (r.w_up.at[:, at], wgu.at[slot, :, pl.ds(WIDE, WIDE)]),
            )
            return [
                pltpu.make_async_copy(src, dst.at[slot], sems.at[n, slot])
                for n, (src, dst) in enumerate(pairs)
            ] + [
                pltpu.make_async_copy(src, dst, sems.at[2 + n, slot])
                for n, (src, dst) in enumerate(halves)
            ]

        def mixed_copy(j):
            slot = lax.rem(j, 2)
            at = pl.ds(pl.multiple_of(j * WIDE, WIDE), WIDE)
            return pltpu.make_async_copy(r.mixed.at[:, at], r.tiles.at[slot], sems.at[5, slot])

        first = [pltpu.make_async_copy(r.grad_ffn, grad, grad_sem)] + [
            pltpu.make_async_copy(left, r.lefts.at[n], left_sem.at[n])
            for n, left in enumerate((r.left_ffn, r.left_mid, r.left_in))
        ]
        for copy in (first[1], mixed_copy(0), mixed_copy(1), first[0], *copies(0), *first[2:]):
            copy.start()
        first[1].wait()

        for i in range(AHEAD):
            mixed_copy(i).wait()
            pump(jnp.int32(i))
            if i + 2 < AHEAD + 1:
                mixed_copy(i + 2).start()

        first[0].wait()
        acc[...] = jnp.zeros_like(acc)

        def step(i, carry):
            @pl.when(i + 1 < 9)
            def _():
                for copy in copies(i + 1):
                    copy.start()

            @pl.when(i + AHEAD + 1 < 9)
            def _():
                mixed_copy(i + AHEAD + 1).start()

            for copy in copies(i):
                copy.wait()
            slot = lax.rem(i, 2)
            grad_mixed = dot_nt(grad[...], wd[slot])
            v = gate_up[slot, :, :WIDE].astype(f32)
            u = gate_up[slot, :, WIDE:].astype(f32)
            square = v * v
            curve = jnp.tanh(0.7978845608028654 * v * (1.0 + 0.044715 * square))
            gelu = 0.5 * v * (1.0 + curve)
            slope = 0.5 * (1.0 + curve) + 0.5 * v * (1.0 - curve * curve) * (
                0.7978845608028654 * (1.0 + 3.0 * 0.044715 * square)
            )
            grad_gate = (grad_mixed * u * slope).astype(low)
            grad_up = (grad_mixed * gelu).astype(low)
            r.tiles[2 + i] = grad_gate
            r.tiles[11 + i] = grad_up
            acc[...] += dot_nt(jnp.concatenate([grad_gate, grad_up], axis=1), wgu[slot])

            @pl.when(i + AHEAD < 9)
            def _():
                mixed_copy(i + AHEAD).wait()

            @pl.when(i + AHEAD == 9)
            def _():
                first[2].wait()

            pump(i + AHEAD)
            return carry

        lax.fori_loop(0, 9, step, 0)
        first[3].wait()
        r.y_out[...] = acc[...].astype(low)

    dma = pltpu.SemaphoreType.DMA
    pl.run_scoped(
        feed_forward,
        pltpu.VMEM((rows, width), low),
        pltpu.VMEM((2, WIDE, width), low),
        pltpu.VMEM((2, width, 2 * WIDE), low),
        pltpu.VMEM((2, rows, 2 * WIDE), low),
        pltpu.VMEM((rows, width), f32),
    )

    def attention(loaded, names, *scoped):
        b = types.SimpleNamespace(**dict(zip(names, scoped)))
        made = {
            name: pltpu.make_async_copy(getattr(r, name), getattr(b, name), b.sems.at[n])
            for n, name in enumerate(loaded)
        }
        for copy in made.values():
            copy.start()
        loads = types.SimpleNamespace(**made)
        heads = r.queries.shape[1] // 256

        def gains_copy(n):
            to_seq, to_head = ((seq, 1 - head), (seq ^ 1, head), (seq ^ 2, head))[n]
            return remote(
                r.gains.at[n], r.gains_in.at[n], r.gains_send.at[n], r.gains_recv.at[n],
                to_seq, to_head,
            )

        def gains_level(z):
            return remote(
                r.gains.at[3], r.gains_z.at[level], r.level_send.at[z], r.level_recv.at[level],
                z * 4 + side * 2 + core, head,
            )

        def gains_from(z):
            return remote(
                r.gains.at[3], r.gains_z.at[z], r.level_send.at[z], r.level_recv.at[z],
                z * 4 + side * 2 + core, head,
            )

        def norms():
            y_arrived(0)
            y_sent(0)
            for copy in (loads.residual_mid, loads.attn_branch, loads.cotangent, loads.gain_rows, loads.head_gains):
                copy.wait()
            loads.gain_start.wait()
            gain_post, gain_pre = b.gain_rows[1:2, :], b.gain_rows[2:3, :]
            size = 128

            def chunk(c, sums):
                at = pl.ds(pl.multiple_of(c * size, size), size)
                grad_mid = r.y_out[at, :].astype(f32) + r.y_in[0, at, :].astype(f32)
                scale, normed = norm_parts(b.residual_mid[at, :])
                back, pre = norm_back(grad_mid, gain_pre, scale, normed)
                grad_residual = b.cotangent[at, :].astype(f32) + back
                b.residual_mid[at, :] = grad_residual
                scale, normed = norm_parts(b.attn_branch[at, :])
                back, post = norm_back(grad_residual, gain_post, scale, normed)
                r.y_out[at, :] = back.astype(low)
                return sums[0] + post, sums[1] + pre

            zero = jnp.zeros((1, width), f32)
            post, pre = lax.fori_loop(0, rows // size, chunk, (zero, zero))
            r.gains[0] = b.gain_start[...]
            r.gains[0, 1:2, :] = post
            r.gains[0, 2:3, :] = pre

        def through_out():
            for copy in (loads.w_out, loads.attended, loads.lse):
                copy.wait()
            b.grad_attended[...] = dot_nt(r.y_out[...], b.w_out[...]).astype(low)
            for h in range(heads):
                at = slice(256 * h, 256 * h + 256)
                delta = jnp.sum(
                    b.grad_attended[:, at].astype(f32) * b.attended[:, at], axis=1, keepdims=True
                )
                b.delta[h : h + 1, :] = jnp.broadcast_to(delta, (rows, 128)).T[:1]
            to_blocks(r.lefts.at[0], r.y_out[...], slice(0, rows))
            r.tiles[4, :, 256:] = b.attended[:, :128].astype(low)
            r.tiles[5] = b.attended[:, 128:].astype(low)

        def attend(block):
            if block == 0:
                for copy in (loads.queries, loads.keys, loads.values, loads.ids_out):
                    copy.wait()
                b.grad_queries[...] = jnp.zeros_like(b.grad_queries)
                b.ids_turned[...] = jnp.broadcast_to(b.ids_out[:1], (128, 3 * rows)).T
            size = 256

            def chunk(c, carry):
                local = pl.multiple_of(c * size, size)
                at = pl.ds(pl.multiple_of(block * rows + c * size, size), size)
                keys, values = b.keys[at, :], b.values[at, :]
                seen = b.ids_turned[at, :1] == b.ids_out[:1, 2 * rows :]
                if block == 2:
                    key_at = lax.broadcasted_iota(jnp.int32, (size, rows), 0) + local
                    query_at = lax.broadcasted_iota(jnp.int32, (size, rows), 1)
                    seen = seen & (key_at <= query_at)
                grad_keys = jnp.zeros((size, 256), f32)
                grad_values = jnp.zeros((size, 256), f32)
                for h in range(heads):
                    head_at = slice(256 * h, 256 * h + 256)
                    q, grad_out = b.queries[:, head_at], b.grad_attended[:, head_at]
                    probs = jnp.where(
                        seen, jnp.exp(dot_nt(keys, q) - b.lse[h : h + 1, :]), 0.0
                    )
                    grad_probs = dot_nt(values, grad_out)
                    grad_scores = (probs * (grad_probs - b.delta[h : h + 1, :])).astype(low)
                    grad_keys += jnp.dot(grad_scores, q, preferred_element_type=f32)
                    grad_values += jnp.dot(
                        probs.astype(low), grad_out, preferred_element_type=f32
                    )
                    b.grad_queries[:, head_at] += dot_tn(grad_scores, keys)
                to = pl.ds(local, size)
                if block == 2:
                    b.grad_own[0, to, :] = grad_keys
                    b.grad_own[1, to, :] = grad_values
                else:
                    r.halo_out[block, 0, to, :] = grad_keys.astype(low)
                    r.halo_out[block, 1, to, :] = grad_values.astype(low)
                return carry

            lax.fori_loop(0, rows // size, chunk, 0)
            if block == 0:
                @pl.when((seq >= 2) & (core == 1))
                def _():
                    relay_copy().start()

                halo_start(0, 0)

            if block == 1:
                @pl.when((core == 0) & (seq >= 2))
                def _():
                    remote(
                        r.halo_out.at[0], r.relay_in, r.relay_send, r.relay_recv, seq ^ 1, head
                    ).wait_recv()
                    for n in range(2):
                        r.halo_out[1, n] = (
                            r.halo_out[1, n].astype(f32) + r.relay_in[n].astype(f32)
                        ).astype(low)

        def relay_copy():
            return remote(
                r.halo_out.at[0], r.relay_in, r.relay_send, r.relay_recv, seq - 1, head
            )

        def halo_part(block, n, half):
            at = pl.ds(half * (rows // 2), rows // 2)
            return remote(
                r.halo_out.at[block, n, at, :], r.halo_in.at[block, n, at, :],
                r.halo_send.at[block, n, half], r.halo_recv.at[block, n, half],
                seq - (2 - block), head,
            )

        def halo_start(block, n):
            @pl.when((seq >= 1) if block == 1 else (seq >= 2) & (core == 0))
            def _():
                for half in range(2):
                    halo_part(block, n, half).start()

        def halo_parts(block):
            return [halo_part(block, n, half) for n in range(2) for half in range(2)]

        def query_side():
            for copy in (loads.query_proj, loads.cosine_out, loads.sine_out, loads.w_query):
                copy.wait()
            total = jnp.zeros((1, 256), f32)
            for h in range(heads):
                at = slice(256 * h, 256 * h + 256)
                grad = rotate_back(
                    b.grad_queries[:, at] * QUERY_SCALE, b.cosine_out[...], b.sine_out[...]
                )
                scale, normed = norm_parts(b.query_proj[:, at])
                back, gain = norm_back(grad, b.head_gains[0:1, :], scale, normed)
                total += gain
                back = back.astype(low)
                if h == 0:
                    r.tiles[2, :, :256] = back
                else:
                    r.tiles[2, :, 256:] = back[:, :128]
                    r.tiles[3, :, :128] = back[:, 128:]
                part = dot_nt(back, b.w_query[:, at])
                if h == 0:
                    b.attn_branch[...] = part
                else:
                    b.attn_branch[...] += part
            r.gains[0, 4:5, :256] = total

        def key_side():
            for copy in (loads.key_proj, loads.w_key, loads.w_value, loads.inputs):
                copy.wait()
            for block in range(2):
                heard = seq + (2 - block) <= last_seq

                @pl.when(heard & (core == 0) if block == 0 else heard)
                def _():
                    for copy in halo_parts(block):
                        copy.wait_recv()
                    for n in range(2):
                        b.grad_own[n] += r.halo_in[block, n].astype(f32)

            grad = rotate_back(b.grad_own[0], b.cosine_out[...], b.sine_out[...])
            scale, normed = norm_parts(b.key_proj[...])
            back, gain = norm_back(grad, b.head_gains[1:2, :], scale, normed)
            r.gains[0, 4:5, 256:512] = gain
            grad_key, grad_value = back.astype(low), b.grad_own[1].astype(low)
            r.tiles[3, :, 128:] = grad_key
            r.tiles[4, :, :256] = grad_value
            b.attn_branch[...] += dot_nt(grad_key, b.w_key[...])
            b.attn_branch[...] += dot_nt(grad_value, b.w_value[...])
            size = 128

            def chunk(c, total):
                at = pl.ds(pl.multiple_of(c * size, size), size)
                part = b.attn_branch[at, :]
                scale, normed = norm_parts(b.inputs[at, :].astype(f32))
                r.y_out[at, :] = part.astype(low)
                return total + jnp.sum(part * normed, axis=0, keepdims=True)

            zero = jnp.zeros((1, width), f32)
            r.gains[0, 0:1, :] = lax.fori_loop(0, rows // size, chunk, zero)
            gains_copy(0).start()

        def gains_stage(n):
            gains_copy(n).wait_recv()
            own, other = r.gains[n], r.gains_in[n]
            if n == 0:
                row = lax.broadcasted_iota(jnp.int32, own.shape, 0)
                other = jnp.where((row == 0) | (row == 4), other, 0.0)
            r.gains[n + 1] = own + other
            if n < 2:
                gains_copy(n + 1).start()
            else:
                for z in range(4):
                    @pl.when(level == z)
                    def _():
                        r.gains_z[z] = r.gains[3]

                    @pl.when(level != z)
                    def _():
                        gains_level(z).start()

        def gains_end():
            for z in range(4):
                @pl.when(level != z)
                def _():
                    gains_from(z).wait_recv()

            r.gains_out[...] = (r.gains_z[0] + r.gains_z[1]) + (r.gains_z[2] + r.gains_z[3])

        def finish_inputs():
            y_arrived(1)
            size = 128

            def chunk(c, carry):
                at = pl.ds(pl.multiple_of(c * size, size), size)
                grad = r.y_out[at, :].astype(f32) + r.y_in[1, at, :].astype(f32)
                scale, normed = norm_parts(b.inputs[at, :].astype(f32))
                back, _ = norm_back(grad, b.gain_rows[0:1, :], scale, normed)
                r.inputs_out[at, :] = (b.residual_mid[at, :] + back).astype(low)
                return carry

            lax.fori_loop(0, rows // size, chunk, 0)

        def kv_copy():
            return remote(r.kv_own, r.kv_in, r.kv_send, r.kv_recv, seq, 1 - head)

        pieces = (
            *((11 + n, functools.partial(y_start, 0, 2 * n)) for n in range(4)),
            (17, norms),
            (18, through_out),
            (19, lambda: attend(0)),
            (20, lambda: halo_start(0, 1)),
            (20, lambda: attend(1)),
            (21, lambda: halo_start(1, 0)),
            (21, lambda: attend(2)),
            (22, lambda: halo_start(1, 1)),
            (22, query_side),
            (25, key_side),
            *((25 + n, functools.partial(y_start, 1, 2 * n)) for n in range(4)),
            (26, lambda: gains_stage(0)),
            (27, lambda: gains_stage(1)),
            (28, lambda: gains_stage(2)),
            (30, gains_end),
            (33, finish_inputs),
            (FIRST_SIDE + 3 + LAG_Z, lambda: kv_copy().start()),
        )

        def step(i, carry):
            for k, piece in pieces:
                @pl.when(i == k)
                def _():
                    piece()

            pump(i)
            return carry

        lax.fori_loop(9 + AHEAD, STEPS + LAG_Z, step, 0)
        kv_copy().wait()
        r.kv_out[...] = r.kv_own[...] + r.kv_in[...]
        y_sent(1)
        for n in range(3):
            gains_copy(n).wait_send()
        for z in range(4):
            @pl.when(level != z)
            def _():
                gains_level(z).wait_send()

        @pl.when((seq >= 2) & (core == 1))
        def _():
            relay_copy().wait_send()

        @pl.when((seq >= 2) & (core == 0))
        def _():
            for copy in halo_parts(0):
                copy.wait_send()

        @pl.when(seq >= 1)
        def _():
            for copy in halo_parts(1):
                copy.wait_send()

    heads_width = r.queries.shape[1]
    def shape(size, kind):
        return pltpu.VMEM(size, kind)

    loaded = dict(
        residual_mid=shape((rows, width), f32),
        attn_branch=shape((rows, width), f32),
        cotangent=shape((rows, width), low),
        inputs=shape((rows, width), low),
        gain_rows=shape((8, width), f32),
        head_gains=shape((8, 256), f32),
        gain_start=shape((8, width), f32),
        w_out=shape((heads_width, width), low),
        attended=shape((rows, heads_width), f32),
        lse=shape((8, rows), f32),
        queries=shape((rows, heads_width), low),
        keys=shape((3 * rows, 256), low),
        values=shape((3 * rows, 256), low),
        ids_out=shape((8, 3 * rows), f32),
        query_proj=shape((rows, heads_width), f32),
        key_proj=shape((rows, 256), f32),
        cosine_out=shape((rows, 128), f32),
        sine_out=shape((rows, 128), f32),
        w_query=shape((width, heads_width), low),
        w_key=shape((width, 256), low),
        w_value=shape((width, 256), low),
    )
    scoped = dict(
        loaded,
        grad_attended=shape((rows, heads_width), low),
        delta=shape((8, rows), f32),
        grad_queries=shape((rows, heads_width), f32),
        grad_own=shape((2, rows, 256), f32),
        ids_turned=shape((3 * rows, 128), f32),
        sems=dma((len(loaded),)),
    )
    pl.run_scoped(functools.partial(attention, tuple(loaded), tuple(scoped)), *scoped.values())

    def drain(i, carry):
        @pl.when(i >= STEPS - 2)
        def _():
            core_copy(i).wait_send()
            out_wait(i)

        @pl.when(z_first(i))
        def _():
            zz_sent(i)

        @pl.when(jnp.logical_not(z_first(i)))
        def _():
            x_copy(i).wait_send()
            for k in range(4):
                @pl.when(targets[k] != seq)
                def _():
                    z_copy(i, k).wait_send()

        return carry

    lax.fori_loop(STEPS - RING, STEPS, drain, 0)
    out_wait(jnp.int32(LAST_TURNED))


def backward(operands):
    low, f32 = jnp.bfloat16, jnp.float32
    dma = pltpu.SemaphoreType.DMA
    rows, width = operands["grad_ffn"].shape
    hidden = operands["w_gate"].shape[1]
    wide = operands["w_query"].shape[1]
    turned = LAST_TURNED // RING + 1
    anywhere = pl.BlockSpec(memory_space=pl.ANY)
    vmem = pl.BlockSpec(memory_space=pltpu.VMEM)
    outs = dict(
        down_out=(jax.ShapeDtypeStruct((BLOCK, hidden), f32), anywhere),
        gate_out=(jax.ShapeDtypeStruct((BLOCK, hidden), f32), anywhere),
        up_out=(jax.ShapeDtypeStruct((BLOCK, hidden), f32), anywhere),
        query_out=(jax.ShapeDtypeStruct((BLOCK, wide), f32), anywhere),
        out_out=(jax.ShapeDtypeStruct((BLOCK, wide), f32), anywhere),
        kv_out=(jax.ShapeDtypeStruct((BLOCK, 512), f32), vmem),
        gains_out=(jax.ShapeDtypeStruct((8, width), f32), vmem),
        inputs_out=(jax.ShapeDtypeStruct((rows, width), low), vmem),
    )
    scratch = dict(
        held=pltpu.VMEM((RING, 2, 4, BLOCK, WIDE), low),
        sent=pltpu.VMEM((2, 2, 4, BLOCK, WIDE), low),
        core_in=pltpu.VMEM((RING, 2, 4, BLOCK, WIDE), low),
        x_in=pltpu.VMEM((RING, 4, BLOCK, WIDE), low),
        m_in=pltpu.VMEM((RING, 2, BLOCK, WIDE), low),
        zz_in=pltpu.VMEM((turned, 4, 2, BLOCK, WIDE), low),
        mm_in=pltpu.VMEM((turned, 2, 2, BLOCK, WIDE), low),
        xx_out=pltpu.VMEM((turned, BLOCK, WIDE), low),
        xx_in=pltpu.VMEM((turned, BLOCK, WIDE), low),
        kept=pltpu.VMEM((BLOCK, WIDE), f32),
        z_out=pltpu.VMEM((RING, 4, BLOCK, WIDE), low),
        z_in=pltpu.VMEM((STEPS, 4, BLOCK, WIDE), low),
        tiles=pltpu.VMEM((20, rows, WIDE), low),
        lefts=pltpu.VMEM((3, width, rows), low),
        y_out=pltpu.VMEM((rows, width), low),
        y_in=pltpu.VMEM((2, rows, width), low),
        halo_out=pltpu.VMEM((2, 2, rows, 256), low),
        halo_in=pltpu.VMEM((2, 2, rows, 256), low),
        relay_in=pltpu.VMEM((2, rows, 256), low),
        gains=pltpu.VMEM((4, 8, width), f32),
        gains_in=pltpu.VMEM((3, 8, width), f32),
        gains_z=pltpu.VMEM((4, 8, width), f32),
        kv_own=pltpu.VMEM((BLOCK, 512), f32),
        kv_in=pltpu.VMEM((BLOCK, 512), f32),
        flat=pltpu.VMEM((2, BLOCK, WIDE), f32),
        core_send=dma((STEPS,)),
        core_recv=dma((STEPS,)),
        x_send=dma((STEPS,)),
        x_recv=dma((STEPS,)),
        z_send=dma((STEPS, 4)),
        z_recv=dma((STEPS, 4)),
        out_sem=dma((STEPS,)),
        y_send=dma((2, Y_PARTS)),
        y_recv=dma((2, Y_PARTS)),
        halo_send=dma((2, 2, 2)),
        halo_recv=dma((2, 2, 2)),
        gains_send=dma((3,)),
        gains_recv=dma((3,)),
        level_send=dma((4,)),
        level_recv=dma((4,)),
        kv_send=dma(()),
        kv_recv=dma(()),
        tile_sems=dma((6, 2)),
        grad_sem=dma(()),
        left_sem=dma((3,)),
        m_recv=dma((STEPS, 2)),
        zz_send=dma((turned, 2, 4)),
        zz_recv=dma((turned, 4, 2)),
        mm_recv=dma((turned, 2, 2)),
        xx_send=dma((turned,)),
        xx_recv=dma((turned,)),
        m_free=pltpu.SemaphoreType.REGULAR,
        relay_send=dma(()),
        relay_recv=dma(()),
        core_free=pltpu.SemaphoreType.REGULAR,
        x_free=pltpu.SemaphoreType.REGULAR,
    )
    names = (*operands, *outs, *scratch)
    results = pl.pallas_call(
        functools.partial(backward_kernel, names),
        out_shape=[shape for shape, _ in outs.values()],
        in_specs=[anywhere] * len(operands),
        out_specs=[spec for _, spec in outs.values()],
        scratch_shapes=list(scratch.values()),
        compiler_params=pltpu.CompilerParams(
            collective_id=1, has_side_effects=True, vmem_limit_bytes=62 << 20
        ),
        name="backward",
    )(*operands.values())
    return dict(zip(outs, results))


def last_kernel(names, *refs):
    r = types.SimpleNamespace(**dict(zip(names, refs)))
    place = lax.axis_index("seq")
    pairs = (
        (r.output, r.output_held, r.output_end),
        (r.inputs_out, r.inputs_held, r.inputs_end),
        (r.gate_out, r.gate_held, r.gate_end),
        (r.up_out, r.up_held, r.up_end),
        (r.down_out, r.down_held, r.down_end),
        (r.query_out, r.query_held, r.query_end),
        (r.out_out, r.out_held, r.out_end),
        (r.kv_out.at[:, pl.ds(0, 256)], r.key_held, r.key_end),
        (r.kv_out.at[:, pl.ds(256, 256)], r.value_held, r.value_end),
    )
    loads = [
        pltpu.make_async_copy(src, held, r.sems.at[0, n]) for n, (src, held, _) in enumerate(pairs)
    ]
    copies = [
        pltpu.make_async_copy(held, dst, r.sems.at[1, n]) for n, (_, held, dst) in enumerate(pairs)
    ]
    for copy in loads:
        copy.start()
    width = r.gains_out.shape[1]
    rolled = pltpu.roll(r.gains_out[...], lax.rem(width - place * BLOCK, width), 1)
    for n, target in enumerate((r.in_end, r.post_attn_end, r.pre_ffn_end, r.post_ffn_end)):
        target[...] = rolled[n : n + 1, :BLOCK].reshape(BLOCK)
    own = r.gain_query_end.shape[0]
    for n, target in enumerate((r.gain_query_end, r.gain_key_end)):
        rolled = pltpu.roll(r.gains_out[...], lax.rem(2 * width - place * own - 256 * n, width), 1)
        target[...] = rolled[4:5, :own].reshape(own)
    for load, copy in zip(loads, copies):
        load.wait()
        copy.start()
    for copy in copies:
        copy.wait()


def last(operands):
    f32 = jnp.float32
    anywhere = pl.BlockSpec(memory_space=pl.ANY)
    vmem = pl.BlockSpec(memory_space=pltpu.VMEM)
    shape = jax.ShapeDtypeStruct
    like = types.SimpleNamespace(**operands)
    part = shape((BLOCK, 256), f32)
    gain = shape((BLOCK,), f32)
    small = shape((256 // lax.axis_size("seq"),), f32)
    outs = dict(
        output_end=like.output,
        inputs_end=like.inputs_out,
        query_end=like.query_out,
        key_end=part,
        value_end=part,
        out_end=like.out_out,
        gate_end=like.gate_out,
        up_end=like.up_out,
        down_end=like.down_out,
        in_end=gain,
        gain_query_end=small,
        gain_key_end=small,
        post_attn_end=gain,
        pre_ffn_end=gain,
        post_ffn_end=gain,
    )
    held = dict(
        output_held=like.output,
        inputs_held=like.inputs_out,
        gate_held=like.gate_out,
        up_held=like.up_out,
        down_held=like.down_out,
        query_held=like.query_out,
        out_held=like.out_out,
        key_held=part,
        value_held=part,
    )
    names = (*operands, *outs, *held, *dict(sems=0))
    return pl.pallas_call(
        functools.partial(last_kernel, names),
        out_shape=[shape(a.shape, a.dtype) for a in outs.values()],
        in_specs=[vmem if name == "gains_out" else anywhere for name in operands],
        out_specs=[vmem if len(a.shape) == 1 else anywhere for a in outs.values()],
        scratch_shapes=[pltpu.VMEM(a.shape, a.dtype) for a in held.values()]
        + [pltpu.SemaphoreType.DMA((2, len(held)))],
        name="last",
    )(*operands.values())


def fast_device(
    inputs,
    segment_ids,
    w_query,
    w_key,
    w_value,
    w_out,
    w_gate,
    w_up,
    w_down,
    gain_in,
    gain_query,
    gain_key,
    gain_post_attn,
    gain_pre_ffn,
    gain_post_ffn,
    cotangent,
):
    shared = dict(
        inputs=inputs, cotangent=cotangent, w_query=w_query, w_key=w_key, w_value=w_value,
        w_out=w_out, w_gate=w_gate, w_up=w_up, w_down=w_down,
    )
    first = forward(
        dict(
            shared,
            segment_ids=segment_ids, gain_in=gain_in, gain_query=gain_query, gain_key=gain_key,
            gain_post_attn=gain_post_attn, gain_pre_ffn=gain_pre_ffn, gain_post_ffn=gain_post_ffn,
        )
    )
    output = first.pop("output")
    results = last(dict(backward(dict(shared, **first)), output=output))
    return tuple(a.T if n in (5, 8) else a for n, a in enumerate(results))


def scatter_rows(grad):
    return lax.psum_scatter(grad, "seq", scatter_dimension=0, tiled=True).astype(jnp.float32)


def per_device(
    inputs,
    segment_ids,
    w_query,
    w_key,
    w_value,
    w_out,
    w_gate,
    w_up,
    w_down,
    gain_in,
    gain_query,
    gain_key,
    gain_post_attn,
    gain_pre_ffn,
    gain_post_ffn,
    cotangent,
):
    rows = inputs.shape[0]
    head_dim = w_key.shape[1]
    local_heads = w_query.shape[1] // head_dim
    place = lax.axis_index("seq")
    local_index = jnp.arange(rows, dtype=jnp.int32)
    ids_parts = [
        jnp.where(place >= distance, from_behind(segment_ids, "seq", distance), -1)
        for distance in (2, 1)
    ]
    window_ids = jnp.concatenate(ids_parts + [segment_ids], axis=0)
    window_index = jnp.arange(3 * rows, dtype=jnp.int32) - 2 * rows
    same = segment_ids[:, None] == window_ids[None, :]
    visible = same & (window_index[None, :] <= local_index[:, None])
    positions = jnp.sum(visible.astype(jnp.int32), axis=1) - 1
    cosine, sine = rope_angles(positions, head_dim)
    inputs_f = inputs.astype(jnp.float32)
    hidden_in = rms_scale(inputs_f, gain_in).astype(jnp.bfloat16)
    query_proj = jnp.dot(hidden_in, w_query, preferred_element_type=jnp.float32)
    key_proj = jnp.dot(hidden_in, w_key, preferred_element_type=jnp.float32)
    value_proj = jnp.dot(hidden_in, w_value, preferred_element_type=jnp.float32)

    def query_side(projection, gain):
        return prepare(
            projection.reshape(rows, local_heads, head_dim), gain, cosine, sine, QUERY_SCALE
        )

    def key_side(projection, gain):
        return prepare(projection[:, None, :], gain, cosine, sine, 1.0)[:, 0, :]

    queries = query_side(query_proj, gain_query).astype(jnp.bfloat16)
    own_keys = key_side(key_proj, gain_key).astype(jnp.bfloat16)
    own_values = value_proj.astype(jnp.bfloat16)
    key_parts = []
    value_parts = []
    for distance in (2, 1):
        moved_keys, moved_values = from_behind((own_keys, own_values), "seq", distance)
        key_parts.append(moved_keys)
        value_parts.append(moved_values)
    all_keys = jnp.concatenate(key_parts + [own_keys], axis=0)
    all_values = jnp.concatenate(value_parts + [own_values], axis=0)
    def raw_scores():
        return jnp.einsum("ihd,jd->hij", queries, all_keys, preferred_element_type=jnp.float32)

    scores = jnp.where(visible[None], raw_scores(), -1e30)
    row_max = jnp.max(scores, axis=-1, keepdims=True)
    expo = jnp.exp(scores - row_max)
    total = jnp.sum(expo, axis=-1, keepdims=True)
    attn_probs = expo / total
    log_total = row_max + jnp.log(total)
    attended = jnp.einsum(
        "hij,jd->ihd",
        attn_probs.astype(jnp.bfloat16),
        all_values,
        preferred_element_type=jnp.float32,
    )
    attended = attended.reshape(rows, local_heads * head_dim).astype(jnp.bfloat16)
    attn_branch = over_head(jnp.dot(attended, w_out, preferred_element_type=jnp.float32))
    residual_mid = inputs_f + rms_scale(attn_branch, gain_post_attn)
    hidden_mid = rms_scale(residual_mid, gain_pre_ffn).astype(jnp.bfloat16)
    gate_act = jnp.dot(hidden_mid, w_gate, preferred_element_type=jnp.float32)
    up_proj = jnp.dot(hidden_mid, w_up, preferred_element_type=jnp.float32)
    mixed_low = gated(gate_act, up_proj).astype(jnp.bfloat16)
    ffn_branch = over_head(jnp.dot(mixed_low, w_down, preferred_element_type=jnp.float32))
    output_f = residual_mid + rms_scale(ffn_branch, gain_post_ffn)
    grad_output = cotangent.astype(jnp.float32)
    unused_post, post_back = jax.vjp(rms_scale, ffn_branch, gain_post_ffn)
    grad_ffn, grad_g_post_ffn = post_back(grad_output)
    grad_ffn_low = grad_ffn.astype(jnp.bfloat16)
    grad_w_down = jnp.dot(grad_ffn_low.T, mixed_low, preferred_element_type=jnp.float32)
    summed_down = scatter_rows(grad_w_down.astype(jnp.bfloat16))
    grad_mixed = jnp.dot(grad_ffn_low, w_down.T, preferred_element_type=jnp.float32)
    unused_gate, gate_back = jax.vjp(gated, gate_act, up_proj)
    grad_gate, grad_up = gate_back(grad_mixed)
    grad_gate_low = grad_gate.astype(jnp.bfloat16)
    grad_up_low = grad_up.astype(jnp.bfloat16)
    grad_w_gate = jnp.dot(hidden_mid.T, grad_gate_low, preferred_element_type=jnp.float32)
    grad_w_up = jnp.dot(hidden_mid.T, grad_up_low, preferred_element_type=jnp.float32)
    summed_gate = scatter_rows(grad_w_gate.astype(jnp.bfloat16))
    summed_up = scatter_rows(grad_w_up.astype(jnp.bfloat16))
    grad_hidden_part = jnp.dot(
        grad_gate_low, w_gate.T, preferred_element_type=jnp.float32
    ) + jnp.dot(grad_up_low, w_up.T, preferred_element_type=jnp.float32)
    grad_hidden_mid = over_head(grad_hidden_part)
    unused_pre, pre_back = jax.vjp(rms_scale, residual_mid, gain_pre_ffn)
    grad_res_part, grad_g_pre_ffn = pre_back(grad_hidden_mid)
    grad_residual = grad_output + grad_res_part
    unused_attn, attn_post_back = jax.vjp(rms_scale, attn_branch, gain_post_attn)
    grad_attn, grad_g_post_attn = attn_post_back(grad_residual)
    grad_attn_low = grad_attn.astype(jnp.bfloat16)
    grad_w_out = jnp.dot(grad_attn_low.T, attended, preferred_element_type=jnp.float32)
    grad_attended = jnp.dot(grad_attn_low, w_out.T, preferred_element_type=jnp.float32).astype(
        jnp.bfloat16
    )
    grad_attended = grad_attended.reshape(rows, local_heads, head_dim)
    probs_again = jnp.where(visible[None], jnp.exp(raw_scores() - log_total), 0.0)
    grad_probs = jnp.einsum(
        "ihd,jd->hij", grad_attended, all_values, preferred_element_type=jnp.float32
    )
    grad_scores = (
        probs_again * (grad_probs - jnp.sum(probs_again * grad_probs, axis=-1, keepdims=True))
    ).astype(jnp.bfloat16)
    grad_queries = jnp.einsum(
        "hij,jd->ihd", grad_scores, all_keys, preferred_element_type=jnp.float32
    )
    grad_keys_all = jnp.einsum(
        "hij,ihd->jd", grad_scores, queries, preferred_element_type=jnp.float32
    )
    grad_values_all = jnp.einsum(
        "hij,ihd->jd",
        probs_again.astype(jnp.bfloat16),
        grad_attended,
        preferred_element_type=jnp.float32,
    )
    grad_keys = grad_keys_all[2 * rows :]
    grad_values = grad_values_all[2 * rows :]
    for distance in (2, 1):
        piece_begin = (2 - distance) * rows
        returned_keys, returned_values = (
            from_behind(
                grad_keys_all[piece_begin : piece_begin + rows].astype(jnp.bfloat16),
                "seq",
                -distance,
            ).astype(jnp.float32),
            from_behind(
                grad_values_all[piece_begin : piece_begin + rows].astype(jnp.bfloat16),
                "seq",
                -distance,
            ).astype(jnp.float32),
        )
        grad_keys = grad_keys + returned_keys
        grad_values = grad_values + returned_values
    unused_query, query_back = jax.vjp(query_side, query_proj, gain_query)
    grad_query_proj, grad_g_query_part = query_back(grad_queries)
    grad_query_low = grad_query_proj.astype(jnp.bfloat16)
    grad_w_query = jnp.dot(hidden_in.T, grad_query_low, preferred_element_type=jnp.float32)
    grad_hidden_query = jnp.dot(grad_query_low, w_query.T, preferred_element_type=jnp.float32)
    keys_summed, values_summed, hidden_summed, grad_g_query = (
        over_head(grad_keys),
        over_head(grad_values),
        over_head(grad_hidden_query),
        over_head(grad_g_query_part),
    )
    unused_key, key_back = jax.vjp(key_side, key_proj, gain_key)
    grad_key_proj, grad_g_key = key_back(keys_summed)
    grad_key_low = grad_key_proj.astype(jnp.bfloat16)
    grad_value_low = values_summed.astype(jnp.bfloat16)
    grad_w_key = jnp.dot(hidden_in.T, grad_key_low, preferred_element_type=jnp.float32)
    grad_w_value = jnp.dot(hidden_in.T, grad_value_low, preferred_element_type=jnp.float32)
    grad_hidden_in = (
        hidden_summed
        + jnp.dot(grad_key_low, w_key.T, preferred_element_type=jnp.float32)
        + jnp.dot(grad_value_low, w_value.T, preferred_element_type=jnp.float32)
    )
    unused_in, in_back = jax.vjp(rms_scale, inputs_f, gain_in)
    grad_in_part, grad_g_in = in_back(grad_hidden_in)
    grad_inputs = (grad_residual + grad_in_part).astype(jnp.bfloat16)
    count = lax.axis_size("seq")
    gain_columns = jnp.stack(
        [grad_g_in, grad_g_post_attn, grad_g_pre_ffn, grad_g_post_ffn], axis=1
    )
    side = jnp.concatenate(
        [grad_g_query.reshape(count, -1), grad_g_key.reshape(count, -1)], axis=1
    )
    side_rows = jnp.repeat(side, inputs.shape[1] // count, axis=0)
    extra = jnp.concatenate([gain_columns, side_rows], axis=1)
    extra = jnp.pad(extra, ((0, 0), (0, -extra.shape[1] % 128)))
    widths = [g.shape[1] for g in (grad_w_query, grad_w_out, grad_w_key, grad_w_value)]
    attn_sum = scatter_rows(
        jnp.concatenate(
            [
                g.astype(jnp.bfloat16)
                for g in (grad_w_query, grad_w_out, grad_w_key, grad_w_value, extra)
            ],
            axis=1,
        )
    )
    edges = [sum(widths[:i]) for i in range(5)]
    summed_query, summed_out, summed_key, summed_value = (
        attn_sum[:, edges[i] : edges[i + 1]] for i in range(4)
    )
    gain_sum = attn_sum[:, edges[4] :]
    summed_g_in, summed_g_post_attn, summed_g_pre_ffn, summed_g_post_ffn = (
        gain_sum[:, i] for i in range(4)
    )
    own = head_dim // count
    summed_g_query = gain_sum[0, 4 : 4 + own]
    summed_g_key = gain_sum[0, 4 + own : 4 + 2 * own]
    summed_out = summed_out.T
    summed_down = summed_down.T
    return (
        output_f.astype(jnp.bfloat16),
        grad_inputs,
        summed_query,
        summed_key,
        summed_value,
        summed_out,
        summed_gate,
        summed_up,
        summed_down,
        summed_g_in,
        summed_g_query,
        summed_g_key,
        summed_g_post_attn,
        summed_g_pre_ffn,
        summed_g_post_ffn,
    )


def solution(mesh):
    placed = (
        P("seq", None),
        P("seq"),
        P(None, "head"),
        P(),
        P(),
        P("head", None),
        P(None, "head"),
        P(None, "head"),
        P("head", None),
        P(),
        P(),
        P(),
        P(),
        P(),
        P(),
        P("seq", None),
    )
    return jax.shard_map(
        fast_device if mesh.shape["seq"] == 16 else per_device,
        mesh=mesh,
        in_specs=placed,
        out_specs=(
            P("seq", None),
            P("seq", None),
            P("seq", "head"),
            P("seq", None),
            P("seq", None),
            P("head", "seq"),
            P("seq", "head"),
            P("seq", "head"),
            P("head", "seq"),
            P("seq"),
            P("seq"),
            P("seq"),
            P("seq"),
            P("seq"),
            P("seq"),
        ),
        check_vma=False,
    )
```

```python
import functools
import math
import types

import jax
import jax.numpy as jnp
from jax import lax
from jax.experimental import pallas as pl
from jax.experimental.pallas import tpu as pltpu
from jax.sharding import PartitionSpec as P

MESH = pl.DeviceIdType.MESH
WIDE = 384
BLOCK = 72

EPS = 1e-06
QUERY_SCALE = 0.0625


def from_behind(block, axis, distance):
    devices = range(lax.axis_size(axis))
    route = [(i - distance, i) for i in devices if i - distance in devices]
    return lax.ppermute(block, axis, route)


def rms_scale(values, gain):
    return values * lax.rsqrt(jnp.mean(values * values, axis=-1, keepdims=True) + EPS) * gain


def rope_angles(positions, width):
    half_width = width // 2
    frequency = jnp.exp(
        jnp.arange(half_width, dtype=jnp.float32) * (-2.0 * math.log(1000000.0) / width)
    )
    angles = positions.astype(jnp.float32)[:, None] * frequency[None, :]
    return (jnp.cos(angles), jnp.sin(angles))


def rotate(values, cosine, sine):
    half_width = values.shape[-1] // 2
    first_half = values[..., :half_width]
    second_half = values[..., half_width:]
    cos_rows = cosine[:, None, :]
    sin_rows = sine[:, None, :]
    return jnp.concatenate(
        [
            first_half * cos_rows - second_half * sin_rows,
            second_half * cos_rows + first_half * sin_rows,
        ],
        axis=-1,
    )


def prepare(values, gain, cosine, sine, factor):
    return rotate(rms_scale(values, gain), cosine, sine) * factor


def gelu_tanh(values):
    return (
        0.5
        * values
        * (1.0 + jnp.tanh(0.7978845608028654 * (values + 0.044715 * values * values * values)))
    )


def gated(gate_act, up_proj):
    return gelu_tanh(gate_act) * up_proj


def over_head(part):
    low = part.astype(jnp.bfloat16)
    other = lax.ppermute(low, "head", [(0, 1), (1, 0)])
    return low.astype(jnp.float32) + other.astype(jnp.float32)


def place_of():
    seq = lax.axis_index("seq")
    return seq, lax.axis_index("head"), seq % 2, seq // 2 % 2, seq // 4


def dot_nt(left, right):
    return lax.dot_general(left, right, (((1,), (1,)), ((), ())), preferred_element_type=jnp.float32)


def dot_tn(left, right):
    return lax.dot_general(left, right, (((0,), (0,)), ((), ())), preferred_element_type=jnp.float32)


def rotate_back(grad, cosine, sine):
    half = grad.shape[-1] // 2
    first, second = grad[:, :half], grad[:, half:]
    return jnp.concatenate(
        [first * cosine + second * sine, second * cosine - first * sine], axis=-1
    )


def norm_parts(values):
    scale = lax.rsqrt(jnp.mean(values * values, axis=-1, keepdims=True) + EPS)
    return scale, values * scale


def norm_back(grad, gain, scale, normed):
    inner = grad * gain
    back = scale * (inner - normed * jnp.mean(inner * normed, axis=-1, keepdims=True))
    return back, jnp.sum(grad * normed, axis=0, keepdims=True)


CHUNKS = 4
FEEDS = 4
OUT_PARTS = 8


def turn(values, cosine, sine):
    half = values.shape[-1] // 2
    first, second = values[:, :half], values[:, half:]
    return jnp.concatenate(
        [first * cosine - second * sine, second * cosine + first * sine], axis=-1
    )


def to_blocks(target, values, columns):
    turned = values.astype(jnp.float32).T.astype(jnp.bfloat16)
    for half in range(2):
        for x in range(2):
            for f in range(2):
                source = 144 * ((2 * half + f) * 2 + x)
                to = 144 * (half * 4 + x * 2 + f)
                target[to : to + 144, columns] = turned[source : source + 144]


def forward_kernel(names, *refs):
    r = types.SimpleNamespace(**dict(zip(names, refs)))
    seq, head, core, side, level = place_of()
    last_seq = lax.axis_size("seq") - 1
    f32, low = jnp.float32, jnp.bfloat16
    rows, width = r.inputs.shape
    heads = r.w_query.shape[1] // 256
    hidden = r.w_gate.shape[1]
    size = rows // CHUNKS
    feed_size = rows // FEEDS
    even = core == 0

    barrier = pltpu.get_barrier_semaphore()

    def greet(to_seq, to_head):
        pl.semaphore_signal(barrier, inc=1, device_id=(to_seq, to_head), device_id_type=MESH)

    def load(n, src, dst):
        copy = pltpu.make_async_copy(src, dst, r.load_sem.at[n])
        copy.start()
        return copy

    in_copy = load(0, r.inputs, r.x)
    kv_copies = (load(2, r.w_key, r.wk), load(3, r.w_value, r.wv))
    query_copy = load(7, r.w_query, r.wq)
    out_copy = load(8, r.w_out, r.wo.at[head])
    steps = hidden // WIDE

    def tile_loads(j):
        at = pl.ds(pl.multiple_of(j * WIDE, WIDE), WIDE)
        gate_at = pl.ds(pl.multiple_of(2 * j * WIDE, WIDE), WIDE)
        up_at = pl.ds(pl.multiple_of((2 * j + 1) * WIDE, WIDE), WIDE)
        return (
            pltpu.make_async_copy(r.w_gate.at[:, at], r.wgu.at[:, gate_at], r.weight_sem.at[0, j]),
            pltpu.make_async_copy(r.w_up.at[:, at], r.wgu.at[:, up_at], r.weight_sem.at[1, j]),
        )

    for j in range(steps):
        for copy in tile_loads(j):
            copy.start()
    down_copy = load(11, r.w_down, r.wd)
    cot_copy = load(12, r.cotangent, r.cot)

    greet(seq ^ 1, head)
    greet(seq, 1 - head)
    expected = jnp.int32(2)
    for distance in (1, 2):
        @pl.when(seq >= distance)
        def _():
            greet(seq - distance, head)

        @pl.when(seq + distance <= last_seq)
        def _():
            greet(seq + distance, head)

        expected = (
            expected
            + (seq >= distance).astype(jnp.int32)
            + (seq + distance <= last_seq).astype(jnp.int32)
        )
    pl.semaphore_wait(barrier, expected)

    def remote(src, dst, send, recv, to_seq, to_head):
        return pltpu.make_async_remote_copy(
            src_ref=src,
            dst_ref=dst,
            send_sem=send,
            recv_sem=recv,
            device_id=(to_seq, to_head),
            device_id_type=MESH,
        )

    share = r.w_out.shape[0] // 2

    def out_share(which):
        return pl.ds(pl.multiple_of(which * share, share), share)

    def w_out_y(part):
        size = share // OUT_PARTS
        mine = pl.ds(pl.multiple_of(core * share + part * size, size), size)
        return remote(
            r.w_out.at[mine, :], r.wo.at[head, mine, :], r.out_send.at[part], r.out_recv.at[part],
            seq, 1 - head,
        )

    def w_out_start(first):
        for part in (first, first + 1):
            w_out_y(part).start()

    def w_out_core():
        mine = out_share(core)
        part = r.wo.at[1 - head, mine, :]
        return remote(part, part, r.wo_send, r.wo_recv, seq ^ 1, head)

    def ids_send(distance):
        return remote(
            r.ids.at[2], r.ids.at[2 - distance], r.ids_send.at[distance - 1],
            r.ids_recv.at[distance - 1], seq + distance, head,
        )

    def halo(n, distance, hand_on=False):
        kind = r.window.at[n]
        source = kind.at[pl.ds((1 if hand_on else 2) * rows, rows), :]
        target = kind.at[pl.ds((2 - distance) * rows, rows), :]
        place = 2 if hand_on else distance - 1
        return remote(
            source, target, r.halo_send.at[n, place], r.halo_recv.at[n, distance - 1],
            seq + (1 if hand_on else distance), head,
        )

    ids = r.segment_ids[...].astype(f32).reshape(1, rows)
    r.ids[2] = jnp.broadcast_to(ids, (8, rows))
    for distance in (1, 2):
        @pl.when(seq + distance <= last_seq)
        def _():
            ids_send(distance).start()

    w_out_start(0)

    r.gains[...] = jnp.zeros_like(r.gains)
    r.head_gain[...] = jnp.zeros_like(r.head_gain)
    for n, gain in enumerate((r.gain_in, r.gain_post_attn, r.gain_pre_ffn, r.gain_post_ffn)):
        r.gains[n : n + 1, :] = gain[...].reshape(1, width)
    for n, gain in enumerate((r.gain_query, r.gain_key)):
        r.head_gain[n : n + 1, :] = gain[...].reshape(1, 256)
    in_copy.wait()

    def norm_in(c, carry):
        at = pl.ds(pl.multiple_of(c * 128, 128), 128)
        _, normed = norm_parts(r.x[at, :].astype(f32))
        r.normed_in[at, :] = (normed * r.gains[0:1, :]).astype(low)
        return carry

    lax.fori_loop(0, rows // 128, norm_in, 0)
    w_out_start(2)
    for copy in kv_copies:
        copy.wait()
    r.key_raw[...] = jnp.dot(r.normed_in[...], r.wk[...], preferred_element_type=f32)
    r.window[1, 2 * rows :, :] = jnp.dot(
        r.normed_in[...], r.wv[...], preferred_element_type=f32
    ).astype(low)

    def value_halo(distance):
        return halo(1, distance)

    @pl.when(even & (seq + 2 <= last_seq))
    def _():
        value_halo(2).start()

    @pl.when(seq + 1 <= last_seq)
    def _():
        value_halo(1).start()

    w_out_start(4)

    for distance in (1, 2):
        @pl.when(seq >= distance)
        def _():
            remote(
                r.ids.at[2], r.ids.at[2 - distance], r.ids_send.at[distance - 1],
                r.ids_recv.at[distance - 1], seq ^ 1, head,
            ).wait_recv()

        @pl.when(seq < distance)
        def _():
            r.ids[2 - distance] = jnp.full((8, rows), -1.0, f32)

    ids_row = jnp.concatenate([r.ids[b][:1] for b in range(3)], axis=1)
    r.ids_flat[...] = jnp.broadcast_to(ids_row, (8, 3 * rows))
    ids_column = jnp.broadcast_to(r.ids[2][:1], (128, rows)).T
    r.ids_turned[...] = ids_column
    column = lax.broadcasted_iota(jnp.int32, (8, 128), 1).astype(f32)
    frequency = jnp.exp(column * (-2.0 * math.log(1000000.0) / 256))[:1]

    def angles(c, carry):
        at = pl.ds(pl.multiple_of(c * 128, 128), 128)
        here = lax.broadcasted_iota(jnp.int32, (128, 3 * rows), 0) + (2 * rows + c * 128)
        there = lax.broadcasted_iota(jnp.int32, (128, 3 * rows), 1)
        same = (r.ids_turned[at, :1] == r.ids_flat[:1, :]) & (there < here)
        position = jnp.sum(same.astype(f32), axis=1, keepdims=True)
        angle = position * frequency
        r.cosine[at, :] = jnp.cos(angle)
        r.sine[at, :] = jnp.sin(angle)
        return carry

    lax.fori_loop(0, rows // 128, angles, 0)
    _, normed = norm_parts(r.key_raw[...])
    r.window[0, 2 * rows :, :] = turn(
        normed * r.head_gain[1:2, :], r.cosine[...], r.sine[...]
    ).astype(low)

    @pl.when(even & (seq + 2 <= last_seq))
    def _():
        halo(0, 2).start()

    @pl.when(seq + 1 <= last_seq)
    def _():
        halo(0, 1).start()

    w_out_start(6)

    query_copy.wait()
    r.query_raw[...] = jnp.dot(r.normed_in[...], r.wq[...], preferred_element_type=f32)
    for h in range(heads):
        at = slice(256 * h, 256 * h + 256)
        _, normed = norm_parts(r.query_raw[:, at])
        r.q[:, at] = (
            turn(normed * r.head_gain[0:1, :], r.cosine[...], r.sine[...]) * QUERY_SCALE
        ).astype(low)

    def store(n, src, dst):
        copy = pltpu.make_async_copy(src, dst, r.store_sem.at[n])
        copy.start()
        return copy

    to_blocks(r.turned, r.normed_in[...], slice(0, rows))
    stores = [
        store(1, r.key_raw, r.key_proj),
        store(2, r.query_raw, r.query_proj),
        store(3, r.q, r.queries),
        store(4, r.cosine, r.cosine_out),
        store(5, r.sine, r.sine_out),
        store(6, r.ids_flat, r.ids_out),
        store(16, r.gains, r.gain_rows),
        store(17, r.head_gain, r.head_gains),
    ]
    turned_store = store(0, r.turned, r.left_in)

    out_copy.wait()
    for part in range(OUT_PARTS):
        w_out_y(part).wait()
    w_out_core().start()

    def arrival(n, distance):
        return halo(n, distance)

    for n in (1, 0):
        @pl.when(seq >= 1)
        def _():
            arrival(n, 1).wait_recv()

        @pl.when(even & (seq >= 2))
        def _():
            halo(n, 2, True).start()

    for n in (1, 0):
        @pl.when(seq >= 2)
        def _():
            arrival(n, 2).wait_recv()

    for distance in (1, 2):
        @pl.when(seq < distance)
        def _():
            for n in range(2):
                r.window[n, (2 - distance) * rows : (3 - distance) * rows, :] = jnp.zeros(
                    (rows, 256), low
                )

    def head_exchange(c):
        part = r.heads_all.at[head, pl.ds(pl.multiple_of(c * size, size), size), :]
        return remote(part, part, r.y_send.at[c], r.y_recv.at[c], seq, 1 - head)

    def branch_exchange(c):
        at = pl.ds(pl.multiple_of(c * feed_size, feed_size), feed_size)
        return remote(
            r.y_out.at[at, :], r.y_in.at[at, :], r.y_send.at[CHUNKS + c], r.y_recv.at[CHUNKS + c],
            seq, 1 - head,
        )

    def attend(c):
        first = c * size
        span = 2 * rows + size
        at = slice(first, first + size)
        key_at = slice(first, first + span)
        here = lax.broadcasted_iota(jnp.int32, (size, span), 0) + 2 * rows
        there = lax.broadcasted_iota(jnp.int32, (size, span), 1)
        seen = (r.ids_turned[at, :1] == r.ids_flat[:1, key_at]) & (there <= here)
        for h in range(heads):
            head_at = slice(256 * h, 256 * h + 256)
            scores = jnp.where(seen, dot_nt(r.q[at, head_at], r.window[0, key_at, :]), -1e30)
            top = jnp.max(scores, axis=1, keepdims=True)
            expo = jnp.exp(scores - top)
            total = jnp.sum(expo, axis=1, keepdims=True)
            probs = (expo / total).astype(low)
            out = jnp.dot(probs, r.window[1, key_at, :], preferred_element_type=f32)
            r.heads_f[at, head_at] = out
            r.heads_all[head, at, head_at] = out.astype(low)
            r.lse_rows[h : h + 1, at] = jnp.broadcast_to(top + jnp.log(total), (size, 128)).T[:1]
        head_exchange(c).start()

    for c in range(CHUNKS):
        attend(c)
    stores += [
        store(7, r.heads_f, r.attended),
        store(8, r.lse_rows, r.lse),
        store(9, r.window.at[0], r.keys),
        store(10, r.window.at[1], r.values),
    ]
    w_out_core().wait()
    turned_store.wait()

    def feed_rows(c):
        return pl.ds(pl.multiple_of(c * feed_size, feed_size), feed_size)

    def part_stores(c):
        slot = lax.rem(c, 2)
        return (
            pltpu.make_async_copy(
                r.gate_up_part.at[slot], r.gate_up.at[feed_rows(c), :], r.part_sem.at[0, slot]
            ),
            pltpu.make_async_copy(
                r.mixed_part.at[slot], r.mixed.at[feed_rows(c), :], r.part_sem.at[1, slot]
            ),
        )

    def feed(c, carry):
        at = feed_rows(c)
        slot = lax.rem(c, 2)
        head_exchange(c).wait_recv()
        branch = jnp.dot(r.heads_all[0, at, :], r.wo[0], preferred_element_type=f32) + jnp.dot(
            r.heads_all[1, at, :], r.wo[1], preferred_element_type=f32
        )
        r.branch[at, :] = branch
        _, normed = norm_parts(branch)
        middle = r.x[at, :].astype(f32) + normed * r.gains[1:2, :]
        r.middle[at, :] = middle
        _, normed = norm_parts(middle)
        left = (normed * r.gains[2:3, :]).astype(low)
        r.normed_mid[at, :] = left

        @pl.when(c >= 2)
        def _():
            for copy in part_stores(c - 2):
                copy.wait()

        def finish(j, both):
            double = slice(2 * j * WIDE, 2 * (j + 1) * WIDE)
            r.gate_up_part[slot, :, double] = both.astype(low)
            gate, up = both[:, :WIDE], both[:, WIDE:]
            curve = jnp.tanh(0.7978845608028654 * gate * (1.0 + 0.044715 * gate * gate))
            r.mixed_part[slot, :, j * WIDE : (j + 1) * WIDE] = (
                0.5 * gate * (1.0 + curve) * up
            ).astype(low)

        waiting = None
        for j in range(steps):
            double = slice(2 * j * WIDE, 2 * (j + 1) * WIDE)
            both = jnp.dot(left, r.wgu[:, double], preferred_element_type=f32)
            if waiting is not None:
                finish(j - 1, waiting)
            waiting = both
        finish(steps - 1, waiting)
        for copy in part_stores(c):
            copy.start()
        r.y_out[at, :] = jnp.dot(
            r.mixed_part[slot], r.wd[...], preferred_element_type=f32
        ).astype(low)
        branch_exchange(c).start()
        return carry

    for j in range(steps):
        for copy in tile_loads(j):
            copy.wait()
    down_copy.wait()
    lax.fori_loop(0, FEEDS, feed, 0)
    stores += [store(11, r.branch, r.attn_branch), store(12, r.middle, r.residual_mid)]
    to_blocks(r.turned, r.normed_mid[...], slice(0, rows))
    mid_store = store(0, r.turned, r.left_mid)
    cot_copy.wait()
    gain_sum = jnp.zeros((1, width), f32)
    for c in range(FEEDS):
        branch_exchange(c).wait_recv()

        def end(n, total):
            at = pl.ds(pl.multiple_of(c * feed_size + n * 128, 128), 128)
            branch = r.y_out[at, :].astype(f32) + r.y_in[at, :].astype(f32)
            scale, normed = norm_parts(branch)
            r.result[at, :] = (r.middle[at, :] + normed * r.gains[3:4, :]).astype(low)
            back, gain = norm_back(r.cot[at, :].astype(f32), r.gains[3:4, :], scale, normed)
            r.cot[at, :] = back.astype(low)
            return total + gain

        gain_sum = lax.fori_loop(0, feed_size // 128, end, gain_sum)
        if c == 0:
            mid_store.wait()
        at = slice(c * feed_size, (c + 1) * feed_size)
        to_blocks(r.turned, r.cot[at, :], at)
    stores += [
        store(0, r.turned, r.left_ffn),
        store(13, r.cot, r.grad_ffn),
        store(14, r.result, r.output),
    ]
    r.gain_tile[...] = jnp.zeros_like(r.gain_tile)
    r.gain_tile[3:4, :] = gain_sum
    stores.append(store(15, r.gain_tile, r.gain_start))
    for copy in stores:
        copy.wait()
    for distance in (1, 2):
        @pl.when(seq + distance <= last_seq)
        def _():
            ids_send(distance).wait_send()

    for n in range(2):
        @pl.when(seq + 1 <= last_seq)
        def _():
            halo(n, 1).wait_send()

        @pl.when(even & (seq + 2 <= last_seq))
        def _():
            halo(n, 2).wait_send()

        @pl.when(even & (seq >= 2))
        def _():
            halo(n, 2, True).wait_send()

    for c in (FEEDS - 2, FEEDS - 1):
        for copy in part_stores(jnp.int32(c)):
            copy.wait()
    for c in range(CHUNKS):
        head_exchange(c).wait_send()
    for c in range(FEEDS):
        branch_exchange(c).wait_send()


def forward(operands):
    low, f32 = jnp.bfloat16, jnp.float32
    dma = pltpu.SemaphoreType.DMA
    rows, width = operands["inputs"].shape
    hidden = operands["w_gate"].shape[1]
    wide = operands["w_query"].shape[1]
    shape = jax.ShapeDtypeStruct
    anywhere = pl.BlockSpec(memory_space=pl.ANY)
    outs = dict(
        left_in=shape((width, rows), low),
        left_mid=shape((width, rows), low),
        left_ffn=shape((width, rows), low),
        key_proj=shape((rows, 256), f32),
        query_proj=shape((rows, wide), f32),
        queries=shape((rows, wide), low),
        cosine_out=shape((rows, 128), f32),
        sine_out=shape((rows, 128), f32),
        ids_out=shape((8, 3 * rows), f32),
        attended=shape((rows, wide), f32),
        lse=shape((8, rows), f32),
        keys=shape((3 * rows, 256), low),
        values=shape((3 * rows, 256), low),
        attn_branch=shape((rows, width), f32),
        residual_mid=shape((rows, width), f32),
        gate_up=shape((rows, 2 * hidden), low),
        mixed=shape((rows, hidden), low),
        grad_ffn=shape((rows, width), low),
        output=shape((rows, width), low),
        gain_start=shape((8, width), f32),
        gain_rows=shape((8, width), f32),
        head_gains=shape((8, 256), f32),
    )
    feed_size = rows // FEEDS
    vmem = pltpu.VMEM
    scratch = dict(
        x=vmem((rows, width), low),
        gains=vmem((8, width), f32),
        wk=vmem((width, 256), low),
        wv=vmem((width, 256), low),
        head_gain=vmem((8, 256), f32),
        ids=vmem((3, 8, rows), f32),
        ids_flat=vmem((8, 3 * rows), f32),
        ids_turned=vmem((rows, 128), f32),
        wq=vmem((width, wide), low),
        wo=vmem((2, wide, width), low),
        wgu=vmem((width, 2 * hidden), low),
        wd=vmem((hidden, width), low),
        cot=vmem((rows, width), low),
        normed_in=vmem((rows, width), low),
        normed_mid=vmem((rows, width), low),
        key_raw=vmem((rows, 256), f32),
        query_raw=vmem((rows, wide), f32),
        q=vmem((rows, wide), low),
        window=vmem((2, 3 * rows, 256), low),
        cosine=vmem((rows, 128), f32),
        sine=vmem((rows, 128), f32),
        turned=vmem((width, rows), low),
        heads_f=vmem((rows, wide), f32),
        heads_all=vmem((2, rows, wide), low),
        lse_rows=vmem((8, rows), f32),
        branch=vmem((rows, width), f32),
        middle=vmem((rows, width), f32),
        gate_up_part=vmem((2, feed_size, 2 * hidden), low),
        mixed_part=vmem((2, feed_size, hidden), low),
        y_out=vmem((rows, width), low),
        y_in=vmem((rows, width), low),
        result=vmem((rows, width), low),
        gain_tile=vmem((8, width), f32),
        load_sem=dma((13,)),
        store_sem=dma((18,)),
        part_sem=dma((2, 2)),
        weight_sem=dma((2, hidden // WIDE)),
        wo_send=dma(()),
        wo_recv=dma(()),
        out_send=dma((OUT_PARTS,)),
        out_recv=dma((OUT_PARTS,)),
        ids_send=dma((2,)),
        ids_recv=dma((2,)),
        halo_send=dma((2, 3)),
        halo_recv=dma((2, 2)),
        y_send=dma((CHUNKS + FEEDS,)),
        y_recv=dma((CHUNKS + FEEDS,)),
    )
    names = (*operands, *outs, *scratch)
    results = pl.pallas_call(
        functools.partial(forward_kernel, names),
        out_shape=list(outs.values()),
        in_specs=[
            pl.BlockSpec(memory_space=pltpu.VMEM) if len(a.shape) == 1 else anywhere
            for a in operands.values()
        ],
        out_specs=[anywhere] * len(outs),
        scratch_shapes=list(scratch.values()),
        compiler_params=pltpu.CompilerParams(
            collective_id=2, has_side_effects=True, vmem_limit_bytes=62 << 20
        ),
        name="forward",
    )(*operands.values())
    return dict(zip(outs, results))


DOWN, GATE, UP, QUERY, QUERY_END, OUT, OUT_END = range(7)
RING = 7
Y_PARTS = 8
STEPS = 31
FIRST_SIDE = 27
LAG_X = 4
LAG_M = 6
LAG_Z = 8
LAG_END = 10
AHEAD = 2
TURNED = 2
LAST_TURNED = 23


def backward_kernel(names, *refs):
    r = types.SimpleNamespace(**dict(zip(names, refs)))
    seq, head, core, side, level = place_of()
    last_seq = lax.axis_size("seq") - 1
    f32, low = jnp.float32, jnp.bfloat16
    rows = r.grad_ffn.shape[0]
    width = r.grad_ffn.shape[1]

    barrier = pltpu.get_barrier_semaphore()

    def greet(to_seq, to_head):
        pl.semaphore_signal(barrier, inc=1, device_id=(to_seq, to_head), device_id_type=MESH)

    greet(seq ^ 1, head)
    greet(seq ^ 2, head)
    greet(seq, 1 - head)
    for z in range(4):
        for c in range(2):
            other = z * 4 + side * 2 + c

            @pl.when(other != seq)
            def _():
                greet(other, head)

    expected = jnp.int32(10)
    for distance in (1, 2):
        @pl.when(seq >= distance)
        def _():
            greet(seq - distance, head)

        @pl.when(seq + distance <= last_seq)
        def _():
            greet(seq + distance, head)

        expected = (
            expected
            + (seq >= distance).astype(jnp.int32)
            + (seq + distance <= last_seq).astype(jnp.int32)
        )
    pl.semaphore_wait(barrier, expected)

    def remote(src, dst, send, recv, to_seq, to_head):
        return pltpu.make_async_remote_copy(
            src_ref=src,
            dst_ref=dst,
            send_sem=send,
            recv_sem=recv,
            device_id=(to_seq, to_head),
            device_id_type=MESH,
        )

    targets = [((2 * core + k // 2) * 4 + side * 2 + k % 2) for k in range(4)]
    sources = [z * 4 + side * 2 + level // 2 for z in range(4)]
    starts_far = (level == 3 * (1 - core))
    hands_on = (level == 2 - core)
    near = (2 - core) * 4 + side * 2 + core
    far = (3 - 3 * core) * 4 + side * 2 + core
    far_level = 3 * core

    def is_far(k):
        return core == k // 2

    def unheard(z):
        return (level == 3 - z) if z in (0, 3) else False

    def core_copy(t):
        slot = lax.rem(t, RING)
        return remote(
            r.sent.at[lax.rem(t, 2)], r.core_in.at[slot], r.core_send.at[t], r.core_recv.at[t],
            seq ^ 1, head,
        )

    def x_copy(t):
        slot = lax.rem(t, RING)
        return remote(
            r.held.at[slot, 1 - side], r.x_in.at[slot], r.x_send.at[t], r.x_recv.at[t],
            seq ^ 2, head,
        )

    def z_copy(t, k):
        return remote(
            r.z_out.at[lax.rem(t, RING), k], r.z_in.at[t, level],
            r.z_send.at[t, k], r.z_recv.at[t, level], targets[k], head,
        )

    def near_copy(t, k):
        return remote(
            r.z_out.at[lax.rem(t, RING), k], r.m_in.at[lax.rem(t, RING), k % 2],
            r.z_send.at[t, k], r.m_recv.at[t, k % 2], near, head,
        )

    def far_copy(t, g):
        return remote(
            r.z_out.at[lax.rem(t, RING), 2 * core + g], r.z_in.at[t, level],
            r.z_send.at[t, 2 * core + g], r.z_recv.at[t, level],
            far_level * 4 + side * 2 + g, head,
        )

    def z_first(t):
        return (lax.rem(t, RING) == TURNED) & (t < LAST_TURNED + 1)

    def zz_copy(t, x, k):
        n = t // RING
        return remote(
            r.held.at[TURNED, x, k], r.zz_in.at[n, level, x],
            r.zz_send.at[n, x, k], r.zz_recv.at[n, level, x], targets[k], head,
        )

    def zz_near(t, x, k):
        n = t // RING
        return remote(
            r.held.at[TURNED, x, k], r.mm_in.at[n, k % 2, x],
            r.zz_send.at[n, x, k], r.mm_recv.at[n, k % 2, x], near, head,
        )

    def zz_far(t, x, g):
        n = t // RING
        return remote(
            r.mm_in.at[n, g, x], r.zz_in.at[n, level, x],
            r.zz_send.at[n, x, 2 * core + g], r.zz_recv.at[n, level, x],
            far_level * 4 + side * 2 + g, head,
        )

    def xx_copy(t):
        n = t // RING
        return remote(
            r.xx_out.at[n], r.xx_in.at[n], r.xx_send.at[n], r.xx_recv.at[n], seq ^ 2, head
        )

    def zz_sent(t):
        for x in range(2):
            for k in range(4):
                @pl.when(targets[k] != seq)
                def _():
                    zz_copy(t, x, k).wait_send()

    def zz_start(t):
        n = t // RING
        for x in range(2):
            for k in range(4):
                @pl.when(targets[k] == seq)
                def _():
                    r.zz_in[n, level, x] = r.held[TURNED, x, k]

                @pl.when(starts_far & is_far(k))
                def _():
                    zz_near(t, x, k).start()

                @pl.when(
                    (targets[k] != seq) & jnp.logical_not((starts_far | hands_on) & is_far(k))
                )
                def _():
                    zz_copy(t, x, k).start()

    def zz_merge(t):
        n = t // RING

        @pl.when(hands_on)
        def _():
            for x in range(2):
                for g in range(2):
                    remote(
                        r.held.at[TURNED, x, g], r.mm_in.at[n, g, x], r.zz_send.at[n, x, g],
                        r.mm_recv.at[n, g, x], far, head,
                    ).wait_recv()
                    r.mm_in[n, g, x] = (
                        r.mm_in[n, g, x].astype(f32)
                        + r.held[TURNED, x, 2 * core + g].astype(f32)
                    ).astype(low)
                    zz_far(t, x, g).start()

    def zz_sum(t):
        n = t // RING
        for z in range(4):
            @pl.when((sources[z] != seq) & jnp.logical_not(unheard(z)))
            def _():
                for x in range(2):
                    remote(
                        r.held.at[TURNED, x, 0], r.zz_in.at[n, z, x], r.zz_send.at[n, x, 0],
                        r.zz_recv.at[n, z, x], sources[z], head,
                    ).wait_recv()

        def total(x):
            value = r.zz_in[n, 1, x].astype(f32) + r.zz_in[n, 2, x].astype(f32)
            for z in (0, 3):
                value = value + jnp.where(unheard(z), 0.0, r.zz_in[n, z, x].astype(f32))
            return value

        @pl.when(n >= 1)
        def _():
            out_wait(t - RING)

        r.xx_out[n] = total(1 - side).astype(low)
        xx_copy(t).start()
        r.kept[...] = total(side)

    def zz_end(t):
        xx_copy(t).wait()
        r.kept[...] += r.xx_in[t // RING].astype(f32)
        out_start(t)

    def z_arrival(t, z):
        return remote(
            r.z_out.at[0, 0], r.z_in.at[t, z], r.z_send.at[t, 0], r.z_recv.at[t, z],
            sources[z], head,
        )

    def produce(t):
        @pl.when(t >= 2)
        def _():
            core_copy(t - 2).wait_send()

        @pl.when((t >= RING) & jnp.logical_not(z_first(t - RING)))
        def _():
            x_copy(t - RING).wait_send()

        @pl.when((t >= RING) & z_first(t - RING))
        def _():
            zz_sent(t - RING)

        which = jnp.where(t < 9, 0, jnp.where(t < FIRST_SIDE, 1, jnp.where(t < 30, 2, 0)))
        place = jnp.where(
            t < 9, lax.rem(t, 2), jnp.where(t < FIRST_SIDE, t - 7, t - (FIRST_SIDE - 2))
        )
        tile = r.tiles[place]

        def half(start):
            left = r.lefts[which, pl.ds(pl.multiple_of(start, 576), 576), :]
            return jnp.dot(left, tile, preferred_element_type=f32)

        away = half((1 - core) * 576)
        for k in range(8):
            r.sent[lax.rem(t, 2), k // 4, k % 4] = away[k * BLOCK : (k + 1) * BLOCK].astype(low)

        @pl.when(t >= RING)
        def _():
            pl.semaphore_wait(r.core_free, 1)

        def second(start):
            left = r.lefts[0, pl.ds(pl.multiple_of(start, 576), 576), :]
            return jnp.dot(left, tile[:, 256:], preferred_element_type=f32)

        @pl.when(t == FIRST_SIDE + 2)
        def _():
            more = second((1 - core) * 576)
            for k in range(8):
                r.sent[lax.rem(t, 2), k // 4, k % 4, :, 256:] = more[
                    k * BLOCK : (k + 1) * BLOCK
                ].astype(low)

        core_copy(t).start()
        home = half(core * 576)
        for k in range(8):
            r.held[lax.rem(t, RING), k // 4, k % 4] = home[k * BLOCK : (k + 1) * BLOCK].astype(low)

        @pl.when(t == FIRST_SIDE + 2)
        def _():
            more = second(core * 576)
            for k in range(8):
                r.held[lax.rem(t, RING), k // 4, k % 4, :, 256:] = more[
                    k * BLOCK : (k + 1) * BLOCK
                ].astype(low)

    def core_stage(t):
        core_copy(t).wait_recv()
        slot = lax.rem(t, RING)

        def add(part):
            for k in range(4):
                r.held[slot, part, k] = (
                    r.held[slot, part, k].astype(f32) + r.core_in[slot, part, k].astype(f32)
                ).astype(low)

        add(1 - side)

        @pl.when(t >= RING)
        def _():
            pl.semaphore_wait(r.x_free, 1)

        @pl.when(jnp.logical_not(z_first(t)))
        def _():
            x_copy(t).start()

        add(side)

        @pl.when(z_first(t))
        def _():
            zz_start(t)

        @pl.when(t + RING < STEPS)
        def _():
            pl.semaphore_signal(r.core_free, inc=1, device_id=(seq ^ 1, head), device_id_type=MESH)

    def x_stage(t):
        @pl.when(z_first(t))
        def _():
            zz_merge(t)

        @pl.when(starts_far & (t >= RING))
        def _():
            pl.semaphore_wait(r.m_free, 1)

        @pl.when(jnp.logical_not(z_first(t)))
        def _():
            x_add(t)

        @pl.when(t + RING < STEPS)
        def _():
            pl.semaphore_signal(r.x_free, inc=1, device_id=(seq ^ 2, head), device_id_type=MESH)

    def x_add(t):
        x_copy(t).wait_recv()
        slot = lax.rem(t, RING)

        @pl.when((t >= RING) & jnp.logical_not(z_first(t - RING)))
        def _():
            for k in range(4):
                @pl.when(targets[k] != seq)
                def _():
                    z_copy(t - RING, k).wait_send()

        for k in range(4):
            total = (r.held[slot, side, k].astype(f32) + r.x_in[slot, k].astype(f32)).astype(low)

            @pl.when(targets[k] == seq)
            def _():
                r.z_in[t, level] = total

            @pl.when(targets[k] != seq)
            def _():
                r.z_out[slot, k] = total

                @pl.when(starts_far & is_far(k))
                def _():
                    near_copy(t, k).start()

                @pl.when(jnp.logical_not((starts_far | hands_on) & is_far(k)))
                def _():
                    z_copy(t, k).start()

    def m_stage(t):
        slot = lax.rem(t, RING)

        @pl.when(hands_on & jnp.logical_not(z_first(t)))
        def _():
            for g in range(2):
                remote(
                    r.z_out.at[0, 0], r.m_in.at[slot, g], r.z_send.at[t, 0], r.m_recv.at[t, g],
                    far, head,
                ).wait_recv()
                k = 2 * core + g
                r.z_out[slot, k] = (
                    r.z_out[slot, k].astype(f32) + r.m_in[slot, g].astype(f32)
                ).astype(low)
                far_copy(t, g).start()

        @pl.when(hands_on)
        def _():
            @pl.when(t + RING < STEPS)
            def _():
                pl.semaphore_signal(r.m_free, inc=1, device_id=(far, head), device_id_type=MESH)

    def out_copy(t, kind, source):
        at = pl.multiple_of(lax.rem(t, 9) * WIDE, WIDE)
        if kind == DOWN:
            return pltpu.make_async_copy(
                source, r.down_out.at[:, pl.ds(at, WIDE)], r.out_sem.at[t]
            )
        if kind == QUERY:
            return pltpu.make_async_copy(
                source, r.query_out.at[:, pl.ds(0, WIDE)], r.out_sem.at[t]
            )
        if kind == QUERY_END:
            return pltpu.make_async_copy(
                source.at[:, pl.ds(0, 128)], r.query_out.at[:, pl.ds(WIDE, 128)],
                r.out_sem.at[t],
            )
        if kind == OUT:
            return pltpu.make_async_copy(
                source.at[:, pl.ds(256, 128)], r.out_out.at[:, pl.ds(0, 128)],
                r.out_sem.at[t],
            )
        if kind == OUT_END:
            return pltpu.make_async_copy(
                source, r.out_out.at[:, pl.ds(128, WIDE)], r.out_sem.at[t]
            )
        target = r.gate_out if kind == GATE else r.up_out
        return pltpu.make_async_copy(
            source, target.at[:, pl.ds(at, WIDE)], r.out_sem.at[t]
        )

    KINDS = (
        (DOWN, 0, 9), (GATE, 9, 18), (UP, 18, 27), (QUERY, 27, 28), (QUERY_END, 28, 29),
        (OUT, 29, 30), (OUT_END, 30, 31),
    )

    def out_each(t, act):
        for kind, first, end in KINDS:
            @pl.when((t >= first) & (t < end) & jnp.logical_not(z_first(t)))
            def _():
                act(out_copy(t, kind, r.flat.at[lax.rem(t, 2)]))

            if kind in (DOWN, GATE, UP):
                @pl.when((t >= first) & (t < end) & z_first(t))
                def _():
                    act(out_copy(t, kind, r.kept))

    def out_wait(t):
        out_each(t, lambda copy: copy.wait())

    def out_start(t):
        out_each(t, lambda copy: copy.start())

    def z_stage(t):
        for z in range(4):
            @pl.when((sources[z] != seq) & jnp.logical_not(unheard(z)))
            def _():
                z_arrival(t, z).wait_recv()

        total = r.z_in[t, 1].astype(f32) + r.z_in[t, 2].astype(f32)
        for z in (0, 3):
            total = total + jnp.where(unheard(z), 0.0, r.z_in[t, z].astype(f32))

        before = jnp.where(z_first(t - 2), t - 4, t - 2)

        @pl.when(before >= 0)
        def _():
            out_wait(before)

        r.flat[lax.rem(t, 2)] = total
        out_start(t)

        @pl.when(t == FIRST_SIDE + 1)
        def _():
            r.kv_own[:, :256] = total[:, 128:]

        @pl.when(t == FIRST_SIDE + 2)
        def _():
            r.kv_own[:, 256:] = total[:, :256]

    def pump(i):
        @pl.when(i < STEPS)
        def _():
            produce(i)

        @pl.when((i >= 1) & (i - 1 < STEPS))
        def _():
            core_stage(i - 1)

        @pl.when((i >= LAG_X) & (i - LAG_X < STEPS))
        def _():
            x_stage(i - LAG_X)

        @pl.when((i >= LAG_M) & (i - LAG_M < STEPS))
        def _():
            m_stage(i - LAG_M)

        @pl.when((i >= LAG_Z) & (i - LAG_Z < STEPS))
        def _():
            t = i - LAG_Z

            @pl.when(z_first(t))
            def _():
                zz_sum(t)

            @pl.when(jnp.logical_not(z_first(t)))
            def _():
                z_stage(t)

        @pl.when((i >= LAG_END) & (i - LAG_END < STEPS) & z_first(i - LAG_END))
        def _():
            zz_end(i - LAG_END)

    def y_part(n, part):
        size = rows // Y_PARTS
        at = pl.ds(part * size, size)
        return remote(
            r.y_out.at[at, :], r.y_in.at[n, at, :], r.y_send.at[n, part], r.y_recv.at[n, part],
            seq, 1 - head,
        )

    def y_start(n, first):
        for part in (first, first + 1):
            y_part(n, part).start()

    def y_sent(n):
        for part in range(Y_PARTS):
            y_part(n, part).wait_send()

    def y_arrived(n):
        for part in range(Y_PARTS):
            y_part(n, part).wait_recv()

    def feed_forward(grad, wd, wgu, gate_up, acc):
        sems, grad_sem, left_sem = r.tile_sems, r.grad_sem, r.left_sem

        def copies(j):
            slot = lax.rem(j, 2)
            at = pl.ds(pl.multiple_of(j * WIDE, WIDE), WIDE)
            double = pl.ds(pl.multiple_of(j * 2 * WIDE, 2 * WIDE), 2 * WIDE)
            pairs = (
                (r.w_down.at[at, :], wd),
                (r.gate_up.at[:, double], gate_up),
            )
            halves = (
                (r.w_gate.at[:, at], wgu.at[slot, :, pl.ds(0, WIDE)]),
                (r.w_up.at[:, at], wgu.at[slot, :, pl.ds(WIDE, WIDE)]),
            )
            return [
                pltpu.make_async_copy(src, dst.at[slot], sems.at[n, slot])
                for n, (src, dst) in enumerate(pairs)
            ] + [
                pltpu.make_async_copy(src, dst, sems.at[2 + n, slot])
                for n, (src, dst) in enumerate(halves)
            ]

        def mixed_copy(j):
            slot = lax.rem(j, 2)
            at = pl.ds(pl.multiple_of(j * WIDE, WIDE), WIDE)
            return pltpu.make_async_copy(r.mixed.at[:, at], r.tiles.at[slot], sems.at[5, slot])

        first = [pltpu.make_async_copy(r.grad_ffn, grad, grad_sem)] + [
            pltpu.make_async_copy(left, r.lefts.at[n], left_sem.at[n])
            for n, left in enumerate((r.left_ffn, r.left_mid, r.left_in))
        ]
        for copy in (first[1], mixed_copy(0), mixed_copy(1), first[0], *copies(0), *first[2:]):
            copy.start()
        first[1].wait()

        for i in range(AHEAD):
            mixed_copy(i).wait()
            pump(jnp.int32(i))
            if i + 2 < AHEAD + 1:
                mixed_copy(i + 2).start()

        first[0].wait()
        acc[...] = jnp.zeros_like(acc)

        def step(i, carry):
            @pl.when(i + 1 < 9)
            def _():
                for copy in copies(i + 1):
                    copy.start()

            @pl.when(i + AHEAD + 1 < 9)
            def _():
                mixed_copy(i + AHEAD + 1).start()

            for copy in copies(i):
                copy.wait()
            slot = lax.rem(i, 2)
            grad_mixed = dot_nt(grad[...], wd[slot])
            v = gate_up[slot, :, :WIDE].astype(f32)
            u = gate_up[slot, :, WIDE:].astype(f32)
            square = v * v
            curve = jnp.tanh(0.7978845608028654 * v * (1.0 + 0.044715 * square))
            gelu = 0.5 * v * (1.0 + curve)
            slope = 0.5 * (1.0 + curve) + 0.5 * v * (1.0 - curve * curve) * (
                0.7978845608028654 * (1.0 + 3.0 * 0.044715 * square)
            )
            grad_gate = (grad_mixed * u * slope).astype(low)
            grad_up = (grad_mixed * gelu).astype(low)
            r.tiles[2 + i] = grad_gate
            r.tiles[11 + i] = grad_up
            acc[...] += dot_nt(jnp.concatenate([grad_gate, grad_up], axis=1), wgu[slot])

            @pl.when(i + AHEAD < 9)
            def _():
                mixed_copy(i + AHEAD).wait()

            @pl.when(i + AHEAD == 9)
            def _():
                first[2].wait()

            pump(i + AHEAD)
            return carry

        lax.fori_loop(0, 9, step, 0)
        first[3].wait()
        r.y_out[...] = acc[...].astype(low)

    dma = pltpu.SemaphoreType.DMA
    pl.run_scoped(
        feed_forward,
        pltpu.VMEM((rows, width), low),
        pltpu.VMEM((2, WIDE, width), low),
        pltpu.VMEM((2, width, 2 * WIDE), low),
        pltpu.VMEM((2, rows, 2 * WIDE), low),
        pltpu.VMEM((rows, width), f32),
    )

    def attention(loaded, names, *scoped):
        b = types.SimpleNamespace(**dict(zip(names, scoped)))
        made = {
            name: pltpu.make_async_copy(getattr(r, name), getattr(b, name), b.sems.at[n])
            for n, name in enumerate(loaded)
        }
        for copy in made.values():
            copy.start()
        loads = types.SimpleNamespace(**made)
        heads = r.queries.shape[1] // 256

        def gains_copy(n):
            to_seq, to_head = ((seq, 1 - head), (seq ^ 1, head), (seq ^ 2, head))[n]
            return remote(
                r.gains.at[n], r.gains_in.at[n], r.gains_send.at[n], r.gains_recv.at[n],
                to_seq, to_head,
            )

        def gains_level(z):
            return remote(
                r.gains.at[3], r.gains_z.at[level], r.level_send.at[z], r.level_recv.at[level],
                z * 4 + side * 2 + core, head,
            )

        def gains_from(z):
            return remote(
                r.gains.at[3], r.gains_z.at[z], r.level_send.at[z], r.level_recv.at[z],
                z * 4 + side * 2 + core, head,
            )

        def norms():
            y_arrived(0)
            y_sent(0)
            for copy in (loads.residual_mid, loads.attn_branch, loads.cotangent, loads.gain_rows, loads.head_gains):
                copy.wait()
            loads.gain_start.wait()
            gain_post, gain_pre = b.gain_rows[1:2, :], b.gain_rows[2:3, :]
            size = 128

            def chunk(c, sums):
                at = pl.ds(pl.multiple_of(c * size, size), size)
                grad_mid = r.y_out[at, :].astype(f32) + r.y_in[0, at, :].astype(f32)
                scale, normed = norm_parts(b.residual_mid[at, :])
                back, pre = norm_back(grad_mid, gain_pre, scale, normed)
                grad_residual = b.cotangent[at, :].astype(f32) + back
                b.residual_mid[at, :] = grad_residual
                scale, normed = norm_parts(b.attn_branch[at, :])
                back, post = norm_back(grad_residual, gain_post, scale, normed)
                r.y_out[at, :] = back.astype(low)
                return sums[0] + post, sums[1] + pre

            zero = jnp.zeros((1, width), f32)
            post, pre = lax.fori_loop(0, rows // size, chunk, (zero, zero))
            r.gains[0] = b.gain_start[...]
            r.gains[0, 1:2, :] = post
            r.gains[0, 2:3, :] = pre

        def through_out():
            for copy in (loads.w_out, loads.attended, loads.lse):
                copy.wait()
            b.grad_attended[...] = dot_nt(r.y_out[...], b.w_out[...]).astype(low)
            for h in range(heads):
                at = slice(256 * h, 256 * h + 256)
                delta = jnp.sum(
                    b.grad_attended[:, at].astype(f32) * b.attended[:, at], axis=1, keepdims=True
                )
                b.delta[h : h + 1, :] = jnp.broadcast_to(delta, (rows, 128)).T[:1]
            to_blocks(r.lefts.at[0], r.y_out[...], slice(0, rows))
            r.tiles[4, :, 256:] = b.attended[:, :128].astype(low)
            r.tiles[5] = b.attended[:, 128:].astype(low)

        def attend(block):
            if block == 0:
                for copy in (loads.queries, loads.keys, loads.values, loads.ids_out):
                    copy.wait()
                b.grad_queries[...] = jnp.zeros_like(b.grad_queries)
                b.ids_turned[...] = jnp.broadcast_to(b.ids_out[:1], (128, 3 * rows)).T
            size = 256

            for c in range(rows // size):
                local = c * size
                at = slice(block * rows + local, block * rows + local + size)
                begin = local if block == 2 else 0
                end = local + size if block == 0 else rows
                span = slice(begin, end)
                keys, values = b.keys[at, :], b.values[at, :]
                seen = b.ids_turned[at, :1] == b.ids_out[:1, 2 * rows + begin : 2 * rows + end]
                if block == 2:
                    key_at = lax.broadcasted_iota(jnp.int32, seen.shape, 0) + local
                    query_at = lax.broadcasted_iota(jnp.int32, seen.shape, 1) + begin
                    seen = seen & (key_at <= query_at)
                grad_keys = jnp.zeros((size, 256), f32)
                grad_values = jnp.zeros((size, 256), f32)
                for h in range(heads):
                    head_at = slice(256 * h, 256 * h + 256)
                    q, grad_out = b.queries[span, head_at], b.grad_attended[span, head_at]
                    probs = jnp.where(
                        seen, jnp.exp(dot_nt(keys, q) - b.lse[h : h + 1, span]), 0.0
                    )
                    grad_probs = dot_nt(values, grad_out)
                    grad_scores = (probs * (grad_probs - b.delta[h : h + 1, span])).astype(low)
                    grad_keys += jnp.dot(grad_scores, q, preferred_element_type=f32)
                    grad_values += jnp.dot(
                        probs.astype(low), grad_out, preferred_element_type=f32
                    )
                    b.grad_queries[span, head_at] += dot_tn(grad_scores, keys)
                to = slice(local, local + size)
                if block == 2:
                    b.grad_own[0, to, :] = grad_keys
                    b.grad_own[1, to, :] = grad_values
                else:
                    r.halo_out[block, 0, to, :] = grad_keys.astype(low)
                    r.halo_out[block, 1, to, :] = grad_values.astype(low)

            if block == 0:
                @pl.when((seq >= 2) & (core == 1))
                def _():
                    relay_copy().start()

                halo_start(0, 0)

            if block == 1:
                @pl.when((core == 0) & (seq >= 2))
                def _():
                    remote(
                        r.halo_out.at[0], r.relay_in, r.relay_send, r.relay_recv, seq ^ 1, head
                    ).wait_recv()
                    for n in range(2):
                        r.halo_out[1, n] = (
                            r.halo_out[1, n].astype(f32) + r.relay_in[n].astype(f32)
                        ).astype(low)

        def relay_copy():
            return remote(
                r.halo_out.at[0], r.relay_in, r.relay_send, r.relay_recv, seq - 1, head
            )

        def halo_part(block, n, half):
            at = pl.ds(half * (rows // 2), rows // 2)
            return remote(
                r.halo_out.at[block, n, at, :], r.halo_in.at[block, n, at, :],
                r.halo_send.at[block, n, half], r.halo_recv.at[block, n, half],
                seq - (2 - block), head,
            )

        def halo_start(block, n):
            @pl.when((seq >= 1) if block == 1 else (seq >= 2) & (core == 0))
            def _():
                for half in range(2):
                    halo_part(block, n, half).start()

        def halo_parts(block):
            return [halo_part(block, n, half) for n in range(2) for half in range(2)]

        def query_side():
            for copy in (loads.query_proj, loads.cosine_out, loads.sine_out, loads.w_query):
                copy.wait()
            total = jnp.zeros((1, 256), f32)
            for h in range(heads):
                at = slice(256 * h, 256 * h + 256)
                grad = rotate_back(
                    b.grad_queries[:, at] * QUERY_SCALE, b.cosine_out[...], b.sine_out[...]
                )
                scale, normed = norm_parts(b.query_proj[:, at])
                back, gain = norm_back(grad, b.head_gains[0:1, :], scale, normed)
                total += gain
                back = back.astype(low)
                if h == 0:
                    r.tiles[2, :, :256] = back
                else:
                    r.tiles[2, :, 256:] = back[:, :128]
                    r.tiles[3, :, :128] = back[:, 128:]
                part = dot_nt(back, b.w_query[:, at])
                if h == 0:
                    b.attn_branch[...] = part
                else:
                    b.attn_branch[...] += part
            r.gains[0, 4:5, :256] = total

        def key_side():
            for copy in (loads.key_proj, loads.w_key, loads.w_value, loads.inputs):
                copy.wait()
            for block in range(2):
                heard = seq + (2 - block) <= last_seq

                @pl.when(heard & (core == 0) if block == 0 else heard)
                def _():
                    for copy in halo_parts(block):
                        copy.wait_recv()
                    for n in range(2):
                        b.grad_own[n] += r.halo_in[block, n].astype(f32)

            grad = rotate_back(b.grad_own[0], b.cosine_out[...], b.sine_out[...])
            scale, normed = norm_parts(b.key_proj[...])
            back, gain = norm_back(grad, b.head_gains[1:2, :], scale, normed)
            r.gains[0, 4:5, 256:512] = gain
            grad_key, grad_value = back.astype(low), b.grad_own[1].astype(low)
            r.tiles[3, :, 128:] = grad_key
            r.tiles[4, :, :256] = grad_value
            b.attn_branch[...] += dot_nt(grad_key, b.w_key[...])
            b.attn_branch[...] += dot_nt(grad_value, b.w_value[...])
            size = 128

            def chunk(c, total):
                at = pl.ds(pl.multiple_of(c * size, size), size)
                part = b.attn_branch[at, :]
                scale, normed = norm_parts(b.inputs[at, :].astype(f32))
                r.y_out[at, :] = part.astype(low)
                return total + jnp.sum(part * normed, axis=0, keepdims=True)

            zero = jnp.zeros((1, width), f32)
            r.gains[0, 0:1, :] = lax.fori_loop(0, rows // size, chunk, zero)
            gains_copy(0).start()

        def gains_stage(n):
            gains_copy(n).wait_recv()
            own, other = r.gains[n], r.gains_in[n]
            if n == 0:
                row = lax.broadcasted_iota(jnp.int32, own.shape, 0)
                other = jnp.where((row == 0) | (row == 4), other, 0.0)
            r.gains[n + 1] = own + other
            if n < 2:
                gains_copy(n + 1).start()
            else:
                for z in range(4):
                    @pl.when(level == z)
                    def _():
                        r.gains_z[z] = r.gains[3]

                    @pl.when(level != z)
                    def _():
                        gains_level(z).start()

        def gains_end():
            for z in range(4):
                @pl.when(level != z)
                def _():
                    gains_from(z).wait_recv()

            r.gains_out[...] = (r.gains_z[0] + r.gains_z[1]) + (r.gains_z[2] + r.gains_z[3])

        def finish_inputs():
            y_arrived(1)
            size = 128

            def chunk(c, carry):
                at = pl.ds(pl.multiple_of(c * size, size), size)
                grad = r.y_out[at, :].astype(f32) + r.y_in[1, at, :].astype(f32)
                scale, normed = norm_parts(b.inputs[at, :].astype(f32))
                back, _ = norm_back(grad, b.gain_rows[0:1, :], scale, normed)
                r.inputs_out[at, :] = (b.residual_mid[at, :] + back).astype(low)
                return carry

            lax.fori_loop(0, rows // size, chunk, 0)

        def kv_copy():
            return remote(r.kv_own, r.kv_in, r.kv_send, r.kv_recv, seq, 1 - head)

        pieces = (
            *((11 + n, functools.partial(y_start, 0, 2 * n)) for n in range(4)),
            (17, norms),
            (18, through_out),
            (19, lambda: attend(0)),
            (20, lambda: halo_start(0, 1)),
            (20, lambda: attend(1)),
            (21, lambda: halo_start(1, 0)),
            (21, lambda: attend(2)),
            (22, lambda: halo_start(1, 1)),
            (22, query_side),
            (25, key_side),
            *((25 + n, functools.partial(y_start, 1, 2 * n)) for n in range(4)),
            (26, lambda: gains_stage(0)),
            (27, lambda: gains_stage(1)),
            (28, lambda: gains_stage(2)),
            (30, gains_end),
            (33, finish_inputs),
            (FIRST_SIDE + 3 + LAG_Z, lambda: kv_copy().start()),
        )

        def step(i, carry):
            for k, piece in pieces:
                @pl.when(i == k)
                def _():
                    piece()

            pump(i)
            return carry

        lax.fori_loop(9 + AHEAD, STEPS + LAG_Z, step, 0)
        kv_copy().wait()
        r.kv_out[...] = r.kv_own[...] + r.kv_in[...]
        y_sent(1)
        for n in range(3):
            gains_copy(n).wait_send()
        for z in range(4):
            @pl.when(level != z)
            def _():
                gains_level(z).wait_send()

        @pl.when((seq >= 2) & (core == 1))
        def _():
            relay_copy().wait_send()

        @pl.when((seq >= 2) & (core == 0))
        def _():
            for copy in halo_parts(0):
                copy.wait_send()

        @pl.when(seq >= 1)
        def _():
            for copy in halo_parts(1):
                copy.wait_send()

    heads_width = r.queries.shape[1]
    def shape(size, kind):
        return pltpu.VMEM(size, kind)

    loaded = dict(
        residual_mid=shape((rows, width), f32),
        attn_branch=shape((rows, width), f32),
        cotangent=shape((rows, width), low),
        inputs=shape((rows, width), low),
        gain_rows=shape((8, width), f32),
        head_gains=shape((8, 256), f32),
        gain_start=shape((8, width), f32),
        w_out=shape((heads_width, width), low),
        attended=shape((rows, heads_width), f32),
        lse=shape((8, rows), f32),
        queries=shape((rows, heads_width), low),
        keys=shape((3 * rows, 256), low),
        values=shape((3 * rows, 256), low),
        ids_out=shape((8, 3 * rows), f32),
        query_proj=shape((rows, heads_width), f32),
        key_proj=shape((rows, 256), f32),
        cosine_out=shape((rows, 128), f32),
        sine_out=shape((rows, 128), f32),
        w_query=shape((width, heads_width), low),
        w_key=shape((width, 256), low),
        w_value=shape((width, 256), low),
    )
    scoped = dict(
        loaded,
        grad_attended=shape((rows, heads_width), low),
        delta=shape((8, rows), f32),
        grad_queries=shape((rows, heads_width), f32),
        grad_own=shape((2, rows, 256), f32),
        ids_turned=shape((3 * rows, 128), f32),
        sems=dma((len(loaded),)),
    )
    pl.run_scoped(functools.partial(attention, tuple(loaded), tuple(scoped)), *scoped.values())

    def drain(i, carry):
        @pl.when(i >= STEPS - 2)
        def _():
            core_copy(i).wait_send()
            out_wait(i)

        @pl.when(z_first(i))
        def _():
            zz_sent(i)

        @pl.when(jnp.logical_not(z_first(i)))
        def _():
            x_copy(i).wait_send()
            for k in range(4):
                @pl.when(targets[k] != seq)
                def _():
                    z_copy(i, k).wait_send()

        return carry

    lax.fori_loop(STEPS - RING, STEPS, drain, 0)
    out_wait(jnp.int32(LAST_TURNED))


def backward(operands):
    low, f32 = jnp.bfloat16, jnp.float32
    dma = pltpu.SemaphoreType.DMA
    rows, width = operands["grad_ffn"].shape
    hidden = operands["w_gate"].shape[1]
    wide = operands["w_query"].shape[1]
    turned = LAST_TURNED // RING + 1
    anywhere = pl.BlockSpec(memory_space=pl.ANY)
    vmem = pl.BlockSpec(memory_space=pltpu.VMEM)
    outs = dict(
        down_out=(jax.ShapeDtypeStruct((BLOCK, hidden), f32), anywhere),
        gate_out=(jax.ShapeDtypeStruct((BLOCK, hidden), f32), anywhere),
        up_out=(jax.ShapeDtypeStruct((BLOCK, hidden), f32), anywhere),
        query_out=(jax.ShapeDtypeStruct((BLOCK, wide), f32), anywhere),
        out_out=(jax.ShapeDtypeStruct((BLOCK, wide), f32), anywhere),
        kv_out=(jax.ShapeDtypeStruct((BLOCK, 512), f32), vmem),
        gains_out=(jax.ShapeDtypeStruct((8, width), f32), vmem),
        inputs_out=(jax.ShapeDtypeStruct((rows, width), low), vmem),
    )
    scratch = dict(
        held=pltpu.VMEM((RING, 2, 4, BLOCK, WIDE), low),
        sent=pltpu.VMEM((2, 2, 4, BLOCK, WIDE), low),
        core_in=pltpu.VMEM((RING, 2, 4, BLOCK, WIDE), low),
        x_in=pltpu.VMEM((RING, 4, BLOCK, WIDE), low),
        m_in=pltpu.VMEM((RING, 2, BLOCK, WIDE), low),
        zz_in=pltpu.VMEM((turned, 4, 2, BLOCK, WIDE), low),
        mm_in=pltpu.VMEM((turned, 2, 2, BLOCK, WIDE), low),
        xx_out=pltpu.VMEM((turned, BLOCK, WIDE), low),
        xx_in=pltpu.VMEM((turned, BLOCK, WIDE), low),
        kept=pltpu.VMEM((BLOCK, WIDE), f32),
        z_out=pltpu.VMEM((RING, 4, BLOCK, WIDE), low),
        z_in=pltpu.VMEM((STEPS, 4, BLOCK, WIDE), low),
        tiles=pltpu.VMEM((20, rows, WIDE), low),
        lefts=pltpu.VMEM((3, width, rows), low),
        y_out=pltpu.VMEM((rows, width), low),
        y_in=pltpu.VMEM((2, rows, width), low),
        halo_out=pltpu.VMEM((2, 2, rows, 256), low),
        halo_in=pltpu.VMEM((2, 2, rows, 256), low),
        relay_in=pltpu.VMEM((2, rows, 256), low),
        gains=pltpu.VMEM((4, 8, width), f32),
        gains_in=pltpu.VMEM((3, 8, width), f32),
        gains_z=pltpu.VMEM((4, 8, width), f32),
        kv_own=pltpu.VMEM((BLOCK, 512), f32),
        kv_in=pltpu.VMEM((BLOCK, 512), f32),
        flat=pltpu.VMEM((2, BLOCK, WIDE), f32),
        core_send=dma((STEPS,)),
        core_recv=dma((STEPS,)),
        x_send=dma((STEPS,)),
        x_recv=dma((STEPS,)),
        z_send=dma((STEPS, 4)),
        z_recv=dma((STEPS, 4)),
        out_sem=dma((STEPS,)),
        y_send=dma((2, Y_PARTS)),
        y_recv=dma((2, Y_PARTS)),
        halo_send=dma((2, 2, 2)),
        halo_recv=dma((2, 2, 2)),
        gains_send=dma((3,)),
        gains_recv=dma((3,)),
        level_send=dma((4,)),
        level_recv=dma((4,)),
        kv_send=dma(()),
        kv_recv=dma(()),
        tile_sems=dma((6, 2)),
        grad_sem=dma(()),
        left_sem=dma((3,)),
        m_recv=dma((STEPS, 2)),
        zz_send=dma((turned, 2, 4)),
        zz_recv=dma((turned, 4, 2)),
        mm_recv=dma((turned, 2, 2)),
        xx_send=dma((turned,)),
        xx_recv=dma((turned,)),
        m_free=pltpu.SemaphoreType.REGULAR,
        relay_send=dma(()),
        relay_recv=dma(()),
        core_free=pltpu.SemaphoreType.REGULAR,
        x_free=pltpu.SemaphoreType.REGULAR,
    )
    names = (*operands, *outs, *scratch)
    results = pl.pallas_call(
        functools.partial(backward_kernel, names),
        out_shape=[shape for shape, _ in outs.values()],
        in_specs=[anywhere] * len(operands),
        out_specs=[spec for _, spec in outs.values()],
        scratch_shapes=list(scratch.values()),
        compiler_params=pltpu.CompilerParams(
            collective_id=1, has_side_effects=True, vmem_limit_bytes=62 << 20
        ),
        name="backward",
    )(*operands.values())
    return dict(zip(outs, results))


def last_kernel(names, *refs):
    r = types.SimpleNamespace(**dict(zip(names, refs)))
    place = lax.axis_index("seq")
    pairs = (
        (r.output, r.output_held, r.output_end),
        (r.inputs_out, r.inputs_held, r.inputs_end),
        (r.gate_out, r.gate_held, r.gate_end),
        (r.up_out, r.up_held, r.up_end),
        (r.down_out, r.down_held, r.down_end),
        (r.query_out, r.query_held, r.query_end),
        (r.out_out, r.out_held, r.out_end),
        (r.kv_out.at[:, pl.ds(0, 256)], r.key_held, r.key_end),
        (r.kv_out.at[:, pl.ds(256, 256)], r.value_held, r.value_end),
    )
    loads = [
        pltpu.make_async_copy(src, held, r.sems.at[0, n]) for n, (src, held, _) in enumerate(pairs)
    ]
    copies = [
        pltpu.make_async_copy(held, dst, r.sems.at[1, n]) for n, (_, held, dst) in enumerate(pairs)
    ]
    for copy in loads:
        copy.start()
    width = r.gains_out.shape[1]
    rolled = pltpu.roll(r.gains_out[...], lax.rem(width - place * BLOCK, width), 1)
    for n, target in enumerate((r.in_end, r.post_attn_end, r.pre_ffn_end, r.post_ffn_end)):
        target[...] = rolled[n : n + 1, :BLOCK].reshape(BLOCK)
    own = r.gain_query_end.shape[0]
    for n, target in enumerate((r.gain_query_end, r.gain_key_end)):
        rolled = pltpu.roll(r.gains_out[...], lax.rem(2 * width - place * own - 256 * n, width), 1)
        target[...] = rolled[4:5, :own].reshape(own)
    for load, copy in zip(loads, copies):
        load.wait()
        copy.start()
    for copy in copies:
        copy.wait()


def last(operands):
    f32 = jnp.float32
    anywhere = pl.BlockSpec(memory_space=pl.ANY)
    vmem = pl.BlockSpec(memory_space=pltpu.VMEM)
    shape = jax.ShapeDtypeStruct
    like = types.SimpleNamespace(**operands)
    part = shape((BLOCK, 256), f32)
    gain = shape((BLOCK,), f32)
    small = shape((256 // lax.axis_size("seq"),), f32)
    outs = dict(
        output_end=like.output,
        inputs_end=like.inputs_out,
        query_end=like.query_out,
        key_end=part,
        value_end=part,
        out_end=like.out_out,
        gate_end=like.gate_out,
        up_end=like.up_out,
        down_end=like.down_out,
        in_end=gain,
        gain_query_end=small,
        gain_key_end=small,
        post_attn_end=gain,
        pre_ffn_end=gain,
        post_ffn_end=gain,
    )
    held = dict(
        output_held=like.output,
        inputs_held=like.inputs_out,
        gate_held=like.gate_out,
        up_held=like.up_out,
        down_held=like.down_out,
        query_held=like.query_out,
        out_held=like.out_out,
        key_held=part,
        value_held=part,
    )
    names = (*operands, *outs, *held, *dict(sems=0))
    return pl.pallas_call(
        functools.partial(last_kernel, names),
        out_shape=[shape(a.shape, a.dtype) for a in outs.values()],
        in_specs=[vmem if name == "gains_out" else anywhere for name in operands],
        out_specs=[vmem if len(a.shape) == 1 else anywhere for a in outs.values()],
        scratch_shapes=[pltpu.VMEM(a.shape, a.dtype) for a in held.values()]
        + [pltpu.SemaphoreType.DMA((2, len(held)))],
        name="last",
    )(*operands.values())


def fast_device(
    inputs,
    segment_ids,
    w_query,
    w_key,
    w_value,
    w_out,
    w_gate,
    w_up,
    w_down,
    gain_in,
    gain_query,
    gain_key,
    gain_post_attn,
    gain_pre_ffn,
    gain_post_ffn,
    cotangent,
):
    shared = dict(
        inputs=inputs, cotangent=cotangent, w_query=w_query, w_key=w_key, w_value=w_value,
        w_out=w_out, w_gate=w_gate, w_up=w_up, w_down=w_down,
    )
    first = forward(
        dict(
            shared,
            segment_ids=segment_ids, gain_in=gain_in, gain_query=gain_query, gain_key=gain_key,
            gain_post_attn=gain_post_attn, gain_pre_ffn=gain_pre_ffn, gain_post_ffn=gain_post_ffn,
        )
    )
    output = first.pop("output")
    results = last(dict(backward(dict(shared, **first)), output=output))
    return tuple(a.T if n in (5, 8) else a for n, a in enumerate(results))


def scatter_rows(grad):
    return lax.psum_scatter(grad, "seq", scatter_dimension=0, tiled=True).astype(jnp.float32)


def per_device(
    inputs,
    segment_ids,
    w_query,
    w_key,
    w_value,
    w_out,
    w_gate,
    w_up,
    w_down,
    gain_in,
    gain_query,
    gain_key,
    gain_post_attn,
    gain_pre_ffn,
    gain_post_ffn,
    cotangent,
):
    rows = inputs.shape[0]
    head_dim = w_key.shape[1]
    local_heads = w_query.shape[1] // head_dim
    place = lax.axis_index("seq")
    local_index = jnp.arange(rows, dtype=jnp.int32)
    ids_parts = [
        jnp.where(place >= distance, from_behind(segment_ids, "seq", distance), -1)
        for distance in (2, 1)
    ]
    window_ids = jnp.concatenate(ids_parts + [segment_ids], axis=0)
    window_index = jnp.arange(3 * rows, dtype=jnp.int32) - 2 * rows
    same = segment_ids[:, None] == window_ids[None, :]
    visible = same & (window_index[None, :] <= local_index[:, None])
    positions = jnp.sum(visible.astype(jnp.int32), axis=1) - 1
    cosine, sine = rope_angles(positions, head_dim)
    inputs_f = inputs.astype(jnp.float32)
    hidden_in = rms_scale(inputs_f, gain_in).astype(jnp.bfloat16)
    query_proj = jnp.dot(hidden_in, w_query, preferred_element_type=jnp.float32)
    key_proj = jnp.dot(hidden_in, w_key, preferred_element_type=jnp.float32)
    value_proj = jnp.dot(hidden_in, w_value, preferred_element_type=jnp.float32)

    def query_side(projection, gain):
        return prepare(
            projection.reshape(rows, local_heads, head_dim), gain, cosine, sine, QUERY_SCALE
        )

    def key_side(projection, gain):
        return prepare(projection[:, None, :], gain, cosine, sine, 1.0)[:, 0, :]

    queries = query_side(query_proj, gain_query).astype(jnp.bfloat16)
    own_keys = key_side(key_proj, gain_key).astype(jnp.bfloat16)
    own_values = value_proj.astype(jnp.bfloat16)
    key_parts = []
    value_parts = []
    for distance in (2, 1):
        moved_keys, moved_values = from_behind((own_keys, own_values), "seq", distance)
        key_parts.append(moved_keys)
        value_parts.append(moved_values)
    all_keys = jnp.concatenate(key_parts + [own_keys], axis=0)
    all_values = jnp.concatenate(value_parts + [own_values], axis=0)
    def raw_scores():
        return jnp.einsum("ihd,jd->hij", queries, all_keys, preferred_element_type=jnp.float32)

    scores = jnp.where(visible[None], raw_scores(), -1e30)
    row_max = jnp.max(scores, axis=-1, keepdims=True)
    expo = jnp.exp(scores - row_max)
    total = jnp.sum(expo, axis=-1, keepdims=True)
    attn_probs = expo / total
    log_total = row_max + jnp.log(total)
    attended = jnp.einsum(
        "hij,jd->ihd",
        attn_probs.astype(jnp.bfloat16),
        all_values,
        preferred_element_type=jnp.float32,
    )
    attended = attended.reshape(rows, local_heads * head_dim).astype(jnp.bfloat16)
    attn_branch = over_head(jnp.dot(attended, w_out, preferred_element_type=jnp.float32))
    residual_mid = inputs_f + rms_scale(attn_branch, gain_post_attn)
    hidden_mid = rms_scale(residual_mid, gain_pre_ffn).astype(jnp.bfloat16)
    gate_act = jnp.dot(hidden_mid, w_gate, preferred_element_type=jnp.float32)
    up_proj = jnp.dot(hidden_mid, w_up, preferred_element_type=jnp.float32)
    mixed_low = gated(gate_act, up_proj).astype(jnp.bfloat16)
    ffn_branch = over_head(jnp.dot(mixed_low, w_down, preferred_element_type=jnp.float32))
    output_f = residual_mid + rms_scale(ffn_branch, gain_post_ffn)
    grad_output = cotangent.astype(jnp.float32)
    unused_post, post_back = jax.vjp(rms_scale, ffn_branch, gain_post_ffn)
    grad_ffn, grad_g_post_ffn = post_back(grad_output)
    grad_ffn_low = grad_ffn.astype(jnp.bfloat16)
    grad_w_down = jnp.dot(grad_ffn_low.T, mixed_low, preferred_element_type=jnp.float32)
    summed_down = scatter_rows(grad_w_down.astype(jnp.bfloat16))
    grad_mixed = jnp.dot(grad_ffn_low, w_down.T, preferred_element_type=jnp.float32)
    unused_gate, gate_back = jax.vjp(gated, gate_act, up_proj)
    grad_gate, grad_up = gate_back(grad_mixed)
    grad_gate_low = grad_gate.astype(jnp.bfloat16)
    grad_up_low = grad_up.astype(jnp.bfloat16)
    grad_w_gate = jnp.dot(hidden_mid.T, grad_gate_low, preferred_element_type=jnp.float32)
    grad_w_up = jnp.dot(hidden_mid.T, grad_up_low, preferred_element_type=jnp.float32)
    summed_gate = scatter_rows(grad_w_gate.astype(jnp.bfloat16))
    summed_up = scatter_rows(grad_w_up.astype(jnp.bfloat16))
    grad_hidden_part = jnp.dot(
        grad_gate_low, w_gate.T, preferred_element_type=jnp.float32
    ) + jnp.dot(grad_up_low, w_up.T, preferred_element_type=jnp.float32)
    grad_hidden_mid = over_head(grad_hidden_part)
    unused_pre, pre_back = jax.vjp(rms_scale, residual_mid, gain_pre_ffn)
    grad_res_part, grad_g_pre_ffn = pre_back(grad_hidden_mid)
    grad_residual = grad_output + grad_res_part
    unused_attn, attn_post_back = jax.vjp(rms_scale, attn_branch, gain_post_attn)
    grad_attn, grad_g_post_attn = attn_post_back(grad_residual)
    grad_attn_low = grad_attn.astype(jnp.bfloat16)
    grad_w_out = jnp.dot(grad_attn_low.T, attended, preferred_element_type=jnp.float32)
    grad_attended = jnp.dot(grad_attn_low, w_out.T, preferred_element_type=jnp.float32).astype(
        jnp.bfloat16
    )
    grad_attended = grad_attended.reshape(rows, local_heads, head_dim)
    probs_again = jnp.where(visible[None], jnp.exp(raw_scores() - log_total), 0.0)
    grad_probs = jnp.einsum(
        "ihd,jd->hij", grad_attended, all_values, preferred_element_type=jnp.float32
    )
    grad_scores = (
        probs_again * (grad_probs - jnp.sum(probs_again * grad_probs, axis=-1, keepdims=True))
    ).astype(jnp.bfloat16)
    grad_queries = jnp.einsum(
        "hij,jd->ihd", grad_scores, all_keys, preferred_element_type=jnp.float32
    )
    grad_keys_all = jnp.einsum(
        "hij,ihd->jd", grad_scores, queries, preferred_element_type=jnp.float32
    )
    grad_values_all = jnp.einsum(
        "hij,ihd->jd",
        probs_again.astype(jnp.bfloat16),
        grad_attended,
        preferred_element_type=jnp.float32,
    )
    grad_keys = grad_keys_all[2 * rows :]
    grad_values = grad_values_all[2 * rows :]
    for distance in (2, 1):
        piece_begin = (2 - distance) * rows
        returned_keys, returned_values = (
            from_behind(
                grad_keys_all[piece_begin : piece_begin + rows].astype(jnp.bfloat16),
                "seq",
                -distance,
            ).astype(jnp.float32),
            from_behind(
                grad_values_all[piece_begin : piece_begin + rows].astype(jnp.bfloat16),
                "seq",
                -distance,
            ).astype(jnp.float32),
        )
        grad_keys = grad_keys + returned_keys
        grad_values = grad_values + returned_values
    unused_query, query_back = jax.vjp(query_side, query_proj, gain_query)
    grad_query_proj, grad_g_query_part = query_back(grad_queries)
    grad_query_low = grad_query_proj.astype(jnp.bfloat16)
    grad_w_query = jnp.dot(hidden_in.T, grad_query_low, preferred_element_type=jnp.float32)
    grad_hidden_query = jnp.dot(grad_query_low, w_query.T, preferred_element_type=jnp.float32)
    keys_summed, values_summed, hidden_summed, grad_g_query = (
        over_head(grad_keys),
        over_head(grad_values),
        over_head(grad_hidden_query),
        over_head(grad_g_query_part),
    )
    unused_key, key_back = jax.vjp(key_side, key_proj, gain_key)
    grad_key_proj, grad_g_key = key_back(keys_summed)
    grad_key_low = grad_key_proj.astype(jnp.bfloat16)
    grad_value_low = values_summed.astype(jnp.bfloat16)
    grad_w_key = jnp.dot(hidden_in.T, grad_key_low, preferred_element_type=jnp.float32)
    grad_w_value = jnp.dot(hidden_in.T, grad_value_low, preferred_element_type=jnp.float32)
    grad_hidden_in = (
        hidden_summed
        + jnp.dot(grad_key_low, w_key.T, preferred_element_type=jnp.float32)
        + jnp.dot(grad_value_low, w_value.T, preferred_element_type=jnp.float32)
    )
    unused_in, in_back = jax.vjp(rms_scale, inputs_f, gain_in)
    grad_in_part, grad_g_in = in_back(grad_hidden_in)
    grad_inputs = (grad_residual + grad_in_part).astype(jnp.bfloat16)
    count = lax.axis_size("seq")
    gain_columns = jnp.stack(
        [grad_g_in, grad_g_post_attn, grad_g_pre_ffn, grad_g_post_ffn], axis=1
    )
    side = jnp.concatenate(
        [grad_g_query.reshape(count, -1), grad_g_key.reshape(count, -1)], axis=1
    )
    side_rows = jnp.repeat(side, inputs.shape[1] // count, axis=0)
    extra = jnp.concatenate([gain_columns, side_rows], axis=1)
    extra = jnp.pad(extra, ((0, 0), (0, -extra.shape[1] % 128)))
    widths = [g.shape[1] for g in (grad_w_query, grad_w_out, grad_w_key, grad_w_value)]
    attn_sum = scatter_rows(
        jnp.concatenate(
            [
                g.astype(jnp.bfloat16)
                for g in (grad_w_query, grad_w_out, grad_w_key, grad_w_value, extra)
            ],
            axis=1,
        )
    )
    edges = [sum(widths[:i]) for i in range(5)]
    summed_query, summed_out, summed_key, summed_value = (
        attn_sum[:, edges[i] : edges[i + 1]] for i in range(4)
    )
    gain_sum = attn_sum[:, edges[4] :]
    summed_g_in, summed_g_post_attn, summed_g_pre_ffn, summed_g_post_ffn = (
        gain_sum[:, i] for i in range(4)
    )
    own = head_dim // count
    summed_g_query = gain_sum[0, 4 : 4 + own]
    summed_g_key = gain_sum[0, 4 + own : 4 + 2 * own]
    summed_out = summed_out.T
    summed_down = summed_down.T
    return (
        output_f.astype(jnp.bfloat16),
        grad_inputs,
        summed_query,
        summed_key,
        summed_value,
        summed_out,
        summed_gate,
        summed_up,
        summed_down,
        summed_g_in,
        summed_g_query,
        summed_g_key,
        summed_g_post_attn,
        summed_g_pre_ffn,
        summed_g_post_ffn,
    )


def solution(mesh):
    placed = (
        P("seq", None),
        P("seq"),
        P(None, "head"),
        P(),
        P(),
        P("head", None),
        P(None, "head"),
        P(None, "head"),
        P("head", None),
        P(),
        P(),
        P(),
        P(),
        P(),
        P(),
        P("seq", None),
    )
    return jax.shard_map(
        fast_device if mesh.shape["seq"] == 16 else per_device,
        mesh=mesh,
        in_specs=placed,
        out_specs=(
            P("seq", None),
            P("seq", None),
            P("seq", "head"),
            P("seq", None),
            P("seq", None),
            P("head", "seq"),
            P("seq", "head"),
            P("seq", "head"),
            P("head", "seq"),
            P("seq"),
            P("seq"),
            P("seq"),
            P("seq"),
            P("seq"),
            P("seq"),
        ),
        check_vma=False,
    )
```
